32 devices in a mesh: dp: 16 (over z, y, x), fsdp: 2 (over core).
Axes of the slice: x: 2, y: 2, z: 4, core: 2. Of those that a mesh axis runs over, the one named last changes fastest.
Arguments:
- hidden_in: bfloat16 [16, 1024, 1536], P('dp', 'fsdp'), may hold values from -6 to 6
- text_state: bfloat16 [16, 256, 4096], P('dp', 'fsdp'), may hold values from -6 to 6
- caption_lengths: int32 [16], P('dp'), may hold values from 8 to 256, as said below
- timesteps: int32 [16], P('dp'), may hold values from 0 to 999
- patch_positions: int32 [16, 2, 1024], P('dp', None, 'fsdp'), may hold values from 0 to 127, as said below
- cotangent: bfloat16 [16, 1024, 1536], P('dp', 'fsdp'), may hold values from -6 to 6
- w_ada: bfloat16 [1024, 4, 1536], P('fsdp'), may hold values from -0.1875 to 0.1875
- w_text: bfloat16 [4096, 2, 1536], P('fsdp'), may hold values from -0.09375 to 0.09375
- w_qkv: bfloat16 [1536, 3, 1536], P('fsdp'), may hold values from -0.15625 to 0.15625
- w_out: bfloat16 [1536, 1536], P('fsdp'), may hold values from -3.5 to 3.5
- gains: bfloat16 [5, 1536], P(None, 'fsdp'), may hold values from 0.5 to 1.5
- cross_gate: bfloat16 [24], P('fsdp'), may hold values from 0.25 to 0.75
- w_gate_up: bfloat16 [1536, 2, 4096], P(None, None, 'fsdp'), may hold values from -0.15625 to 0.15625
- w_down: bfloat16 [4096, 1536], P('fsdp'), may hold values from -0.1875 to 0.1875
Outputs:
- output: bfloat16 [16, 1024, 1536], P('dp', 'fsdp')
- grad_input: bfloat16 [16, 1024, 1536], P('dp', 'fsdp')
- grad_text: bfloat16 [16, 256, 4096], P('dp', 'fsdp')
- grad_ada: float32 [1024, 4, 1536], P('fsdp', None, 'dp')
- grad_text_proj: float32 [4096, 2, 1536], P('fsdp', None, 'dp')
- grad_qkv: float32 [1536, 3, 1536], P('fsdp', None, 'dp')
- grad_out: float32 [1536, 1536], P('fsdp', 'dp')
- grad_gains: float32 [5, 1536], P(None, 'fsdp')
- grad_cross_gate: float32 [24], P('fsdp')
- grad_gate_up: float32 [1536, 2, 4096], P('dp', None, 'fsdp')
- grad_down: float32 [4096, 1536], P('fsdp', 'dp')
The draws below stay inside these ranges and needn't reach their ends.
Inputs may be any that keep to these rules, and one draw needn't show every extreme that they name: `caption_lengths`: each image's caption has at least 8 tokens; in every draw one image's caption fills all 256 slots and another's has exactly 8. `patch_positions`: each image's patches lie row by row on a grid whose width w is 8, 16 or 32: patch p sits at row p // w and column p % w. In every draw some image has width 8 and another width 32.
All inputs are finite; a program needn't handle non-finite values.
Results may differ from the reference program's by a relative error of at most 0.023.
Values may be sent and summed in bfloat16 or wider, within the bound.
A program may use at most 576 MiB of HBM per device.

```python
import math
import jax
import jax.numpy as jnp
from jax import lax

D = 1536
HEADS = 24
HD = 64
FF = 4096
TW = 4096
TE = 1024
PATCHES = 1024
TEXT = 256
IMAGES = 16


def draw_caption_lengths(key, part):
    key_band, key_offset, key_top, key_bottom = jax.random.split(key, 4)
    levels = TEXT.bit_length() - 4
    exponent = jax.random.randint(key_band, (IMAGES,), 0, levels)
    base_length = 8 * jnp.power(2, exponent)
    extra_tokens = jax.random.randint(key_offset, (IMAGES,), 0, 1 << 30) % base_length
    lengths = base_length + extra_tokens
    top_index = jax.random.randint(key_top, (), 0, IMAGES)
    short_index = (top_index + 1 + jax.random.randint(key_bottom, (), 0, IMAGES - 1)) % IMAGES
    image_index = jnp.arange(IMAGES, dtype=jnp.int32)
    lengths = jnp.where(image_index == top_index, TEXT, lengths)
    lengths = jnp.where(image_index == short_index, 8, lengths)
    return lengths.astype(jnp.int32)


def draw_patch_positions(key, part):
    key_width, key_narrow, key_broad = jax.random.split(jax.random.fold_in(key, 7), 3)
    shift_bits = 3 + jax.random.randint(key_width, (IMAGES,), 0, 3)
    narrow_index = jax.random.randint(key_narrow, (), 0, IMAGES)
    broad_index = (narrow_index + 1 + jax.random.randint(key_broad, (), 0, IMAGES - 1)) % IMAGES
    image_index = jnp.arange(IMAGES, dtype=jnp.int32)
    shift_bits = jnp.where(image_index == narrow_index, 3, shift_bits)
    shift_bits = jnp.where(image_index == broad_index, 5, shift_bits)
    widths = jnp.power(2, shift_bits).astype(jnp.int32)
    patch_index = jnp.arange(PATCHES, dtype=jnp.int32)
    row_index = patch_index[None, :] // widths[:, None]
    column_index = patch_index[None, :] % widths[:, None]
    return jnp.stack([row_index, column_index], axis=1).astype(jnp.int32)


def set_ends(entries, rng, smallest, high):
    dims = entries.shape
    place = [jax.random.randint(jax.random.fold_in(rng, axis), (), 0, dims[axis]) for axis in range(len(dims))]
    entries = entries.at[tuple(place)].set(smallest)
    longest = dims.index(max(dims))
    place[longest] = (place[longest] + 1) % dims[longest]
    return entries.at[tuple(place)].set(high)


def steps_of(own_key, shape, pieces, low, top_value):
    def one(axis_at, blocks):
        heights = jax.random.uniform(jax.random.fold_in(jax.random.fold_in(own_key, 6), axis_at), (blocks,), jnp.float32, low / len(pieces), top_value / len(pieces))
        return jnp.repeat(jnp.exp(heights), shape[axis_at] // blocks).reshape((-1,) + (1,) * (len(shape) - axis_at - 1))

    factor_of = one(*pieces[0])
    for cut in pieces[1:]:
        factor_of = factor_of * one(*cut)
    return factor_of


def centred(own_key, shape, width, limit, cuts=(), kind=jnp.bfloat16):
    values = jax.random.normal(own_key, shape, jnp.float32) * width
    if len(cuts) > 0:
        values = steps_of(own_key, shape, cuts, -0.22, 0.18) * values
    return jnp.clip(values, min=-limit, max=limit).astype(kind)


def setup_inputs(seed: int = 0) -> dict:
    seeds = jax.random.split(jax.random.key(seed), 15)
    hidden_in = centred(seeds[0], (IMAGES, PATCHES, D), 1.0, 6.0, ((0, 16), (1, 2)))
    text_state = centred(seeds[1], (IMAGES, TEXT, TW), 1.0, 6.0, ((0, 16), (1, 2)))
    caption_lengths = draw_caption_lengths(jax.random.fold_in(seeds[14], 71), 0)
    timesteps = set_ends(jax.random.randint(seeds[3], (IMAGES,), 0, 1000), jax.random.fold_in(seeds[3], 1), 0, 999).astype(jnp.int32)
    patch_positions = draw_patch_positions(jax.random.fold_in(seeds[14], 71), 0)
    cotangent = centred(seeds[5], (IMAGES, PATCHES, D), 1.0, 6.0, ((0, 16), (1, 2)))
    w_ada = centred(seeds[6], (TE, 4, D), TE ** -0.5, 0.1875, ((0, 2),))
    w_text = centred(seeds[7], (TW, 2, D), TW ** -0.5, 0.09375, ((0, 2),))
    w_qkv = centred(seeds[8], (D, 3, D), D ** -0.5, 0.15625, ((0, 2),))
    w_out = centred(seeds[9], (D, D), (max(D * 2 // PATCHES, 1)) ** -0.5, 3.5, ((0, 2),))
    gains = jnp.clip(1.0 + 0.1 * jax.random.normal(seeds[10], (5, D), jnp.float32), 0.5, 1.5).astype(jnp.bfloat16)
    cross_gate = jnp.clip(0.25 + 0.5 * jax.random.uniform(seeds[11], (HEADS,), jnp.float32) ** steps_of(seeds[11], (HEADS,), ((0, 2),), -0.2, 0.2), 0.25, 0.75).astype(jnp.bfloat16)
    w_gate_up = centred(seeds[12], (D, 2, FF), D ** -0.5, 0.15625, ((2, 2),))
    w_down = centred(seeds[13], (FF, D), (FF // 4) ** -0.5, 0.1875, ((0, 2),))
    return {"hidden_in": hidden_in, "text_state": text_state, "caption_lengths": caption_lengths, "timesteps": timesteps, "patch_positions": patch_positions, "cotangent": cotangent, "w_ada": w_ada, "w_text": w_text, "w_qkv": w_qkv, "w_out": w_out, "gains": gains, "cross_gate": cross_gate, "w_gate_up": w_gate_up, "w_down": w_down}


@jax.custom_vjp
def low(v):
    return lax.optimization_barrier(v.astype(jnp.bfloat16)).astype(jnp.float32)

@jax.custom_vjp
def low_back(v):
    return v

def low_keep(v):
    return (low(v), None)

def low_pass(kept, grad):
    return (grad,)

def back_keep(v):
    return (v, None)

def back_low(kept, grad):
    return (low(grad),)
low.defvjp(low_keep, low_pass)
low_back.defvjp(back_keep, back_low)
EPSILON = 1e-06
PRECISE = lax.Precision.HIGHEST

def time_embed(timesteps):
    half_width = TE // 2
    frequencies = jnp.exp(-math.log(10000.0) * jnp.arange(half_width, dtype=jnp.float32) / half_width)
    angles = timesteps.astype(jnp.float32)[..., None] * frequencies
    return jnp.concatenate([jnp.cos(angles), jnp.sin(angles)], axis=-1)

def rope_tables(positions):
    quarter = HD // 4
    frequencies = 10000.0 ** (-jnp.arange(quarter, dtype=jnp.float32) / quarter)
    angles = jnp.swapaxes(positions.astype(jnp.float32), -1, -2)[..., None] * frequencies
    return (jnp.cos(angles), jnp.sin(angles))

def rotate(values, cosine_rows, sine_rows):
    lead_shape = values.shape[:-1]
    quarters = values.reshape(lead_shape + (HEADS, 2, 2, HD // 4))
    first_half = quarters[..., 0, :]
    second_half = quarters[..., 1, :]
    cosine_b = cosine_rows[..., None, :, :]
    sine_b = sine_rows[..., None, :, :]
    turned = jnp.stack([first_half * cosine_b - second_half * sine_b, second_half * cosine_b + first_half * sine_b], axis=-2)
    return turned.reshape(values.shape)

def normalize(values, gain_row):
    return values * lax.rsqrt(lax.optimization_barrier(jnp.mean(values * values, axis=-1, keepdims=True)) + EPSILON) * gain_row

def attend(queries, keys_in, values_in, valid_keys):
    query_heads = queries.reshape(queries.shape[0], HEADS, HD)
    key_heads = keys_in.reshape(keys_in.shape[0], HEADS, HD)
    value_heads = values_in.reshape(values_in.shape[0], HEADS, HD)
    scores = low_back(jnp.einsum('qhd,khd->hqk', query_heads, key_heads, precision=PRECISE) * HD ** (-0.5))
    if valid_keys is not None:
        scores = jnp.where(valid_keys[None, None, :], scores, -1e+30)
    attn_probs = jax.nn.softmax(scores, axis=-1)
    context = jnp.einsum('hqk,khd->qhd', low(attn_probs), value_heads, precision=PRECISE)
    return context.reshape(queries.shape[0], D)

def layer(params, image_in, text_in, length, timestep, positions):
    w_ada, w_text, w_qkv, w_out, gains, cross_gate, w_gate_up, w_down = params
    time_low = low(jax.nn.silu(time_embed(timestep)))
    modulation = jnp.dot(time_low, w_ada.reshape(TE, 4 * D), precision=PRECISE).reshape(4, D)
    cosine_rows, sine_rows = rope_tables(positions)
    first_norm = low(normalize(image_in, gains[0]) * (1.0 + modulation[0]))
    projected = jnp.dot(first_norm, w_qkv.reshape(D, 3 * D), precision=PRECISE).reshape(-1, 3, D)
    queries = low(rotate(normalize(low_back(projected[:, 0]), gains[2]), cosine_rows, sine_rows))
    keys_self = low(rotate(normalize(low_back(projected[:, 1]), gains[3]), cosine_rows, sine_rows))
    values_self = low(low_back(projected[:, 2]))
    text_proj = jnp.dot(text_in, w_text.reshape(TW, 2 * D), precision=PRECISE).reshape(-1, 2, D)
    keys_text = low(normalize(low_back(text_proj[:, 0]), gains[4]))
    values_text = low(low_back(text_proj[:, 1]))
    valid_text = jnp.arange(text_in.shape[0]) < length
    self_out = low_back(attend(queries, keys_self, values_self, None))
    cross_out = low_back(attend(queries, keys_text, values_text, valid_text))
    head_gates = jnp.repeat(jnp.tanh(cross_gate), HD)
    mixed = low(self_out + head_gates * cross_out)
    attn_branch = low_back(jnp.dot(mixed, w_out, precision=PRECISE))
    after_attn = image_in + jnp.tanh(modulation[1]) * attn_branch
    second_norm = low(normalize(after_attn, gains[1]) * (1.0 + modulation[2]))
    gate_up_pre = jnp.dot(second_norm, w_gate_up.reshape(D, 2 * FF), precision=PRECISE).reshape(-1, 2, FF)
    hidden = low(jax.nn.silu(low_back(gate_up_pre[:, 0])) * low_back(gate_up_pre[:, 1]))
    ffn_branch = low_back(jnp.dot(hidden, w_down, precision=PRECISE))
    return after_attn + jnp.tanh(modulation[3]) * ffn_branch

def reference(hidden_in, text_state, caption_lengths, timesteps, patch_positions, cotangent, w_ada, w_text, w_qkv, w_out, gains, cross_gate, w_gate_up, w_down):
    params = tuple((weight.astype(jnp.float32) for weight in (w_ada, w_text, w_qkv, w_out, gains, cross_gate, w_gate_up, w_down)))
    initial = tuple((jnp.zeros(weight.shape, jnp.float32) for weight in params))

    def one_image(running, slices_in):
        image_in, text_in, length, timestep, positions, grad_in = slices_in

        def apply_layer(weights, image_val, text_val):
            return layer(weights, image_val, text_val, length, timestep, positions)
        result, pullback = jax.vjp(apply_layer, params, image_in.astype(jnp.float32), text_in.astype(jnp.float32))
        weight_grads, image_grad, text_grad = pullback(grad_in.astype(jnp.float32))
        running = tuple((acc_value + piece_grad for acc_value, piece_grad in zip(running, weight_grads)))
        return (running, (result.astype(jnp.bfloat16), image_grad.astype(jnp.bfloat16), text_grad.astype(jnp.bfloat16)))
    totals, (output, grad_input, grad_text) = lax.scan(one_image, initial, (hidden_in, text_state, caption_lengths, timesteps, patch_positions, cotangent))
    return (output, grad_input, grad_text) + totals
```

```python
import functools
import math

import jax
import jax.numpy as jnp
from jax import lax
from jax.experimental import pallas as pl
from jax.experimental.pallas import tpu as pltpu
from jax.sharding import PartitionSpec as P

D = 1536
HEADS = 24
HD = 64
TW = 4096
TE = 1024
PATCHES = 1024
TEXT = 256
EPSILON = 1e-06
F32 = jnp.float32
BF16 = jnp.bfloat16
QC = 256


def dot(a, b, ca=1, cb=0):
    return lax.dot_general(a, b, (((ca,), (cb,)), ((), ())), preferred_element_type=F32)


def from_behind(value, step):
    n = lax.axis_size("fsdp")
    return lax.ppermute(value, "fsdp", [(i, (i + step) % n) for i in range(n)])


def gather_rot(value):
    return [value] + [from_behind(value, r) for r in range(1, lax.axis_size("fsdp"))]


def pair_sum(value):
    return functools.reduce(lambda a, b: a + b, gather_rot(value))


def row_sum(value):
    n = lax.axis_size("fsdp")
    rows = value.shape[-1] // n
    total = value
    for r in range(1, n):
        total = total + jnp.roll(from_behind(value, r), r * rows, axis=-1)
    return total


def scatter_rot(blocks):
    n = lax.axis_size("fsdp")
    total = blocks[0].astype(F32)
    for r in range(1, n):
        got = lax.ppermute(blocks[r], "fsdp", [(i, (i - r) % n) for i in range(n)])
        total = total + got.astype(F32)
    return total


def rot_blocks(value, axis):
    n, f = lax.axis_size("fsdp"), lax.axis_index("fsdp")
    return [lax.dynamic_index_in_dim(value, (f - r) % n, axis, keepdims=False) for r in range(n)]


def dp_bits():
    return int(lax.axis_size("dp")).bit_length() - 1


def dp_swap(value, bit):
    n = lax.axis_size("dp")
    return lax.ppermute(value, "dp", [(i, i ^ (1 << bit)) for i in range(n)])


def orders():
    bits = list(range(dp_bits()))
    return bits, bits[:2][::-1] + bits[2:], bits[2:] + bits[:2]


def split_bit(value, axis, bit):
    mine = (lax.axis_index("dp") >> bit) & 1
    keep = lax.dynamic_index_in_dim(value, mine, axis, keepdims=False)
    send = lax.dynamic_index_in_dim(value, 1 - mine, axis, keepdims=False)
    return keep, send


def dp_scatter(value, order):
    nb = dp_bits()
    rows = value.shape[0] >> nb
    cur = value.reshape((2,) * nb + (rows, value.shape[1]))
    labels = list(range(nb))[::-1]
    for i, bit in enumerate(order):
        keep, send = split_bit(cur, labels.index(bit), bit)
        labels.remove(bit)
        total = keep.astype(F32) + dp_swap(send, bit).astype(F32)
        cur = total if i == nb - 1 else total.astype(BF16)
    return cur


def dp_exchange(value, order):
    nb = dp_bits()
    cur = value.reshape((2,) * nb + value.shape[1:])
    for bit in order:
        axis = nb - 1 - bit
        keep, send = split_bit(cur, axis, bit)
        cur = jnp.stack([keep, dp_swap(send, bit)], axis=axis)
    return cur.reshape(value.shape)


def dp_total(value):
    for bit in range(dp_bits()):
        value = value + dp_swap(value, bit)
    return value


def dp_gather(value, order):
    pieces = [([0], value[None])]
    for bit in order[::-1]:
        pieces = pieces + [([p ^ (1 << bit) for p in pos], dp_swap(a, bit)) for pos, a in pieces]
    return pieces


def rope_block(value, cosine, sine, sign):
    width = value.shape[1]
    lane = lax.broadcasted_iota(jnp.int32, value.shape, 1)
    partner = jnp.where(
        lane % 32 < 16, pltpu.roll(value, width - 16, 1), pltpu.roll(value, 16, 1)
    )
    return value * cosine + sign * (partner * sine)


def masked(value, head):
    lane = lax.broadcasted_iota(jnp.int32, value.shape, 1)
    return jnp.where(lane // HD == head, value, jnp.zeros_like(value))


def attn_fwd_kernel(
    len_ref, qp_ref, kp_ref, vp_ref, iq_ref, ik_ref, gq_ref, gk_ref, cos_ref, sin_ref,
    tk_ref, tv_ref, gate_ref,
    q_ref, k_ref, v_ref, mixed_ref, so_ref, co_ref, ls_ref, lc_ref, vt_ref, tvt_ref,
):
    tokens, width = qp_ref.shape
    heads = width // HD
    q = rope_block(qp_ref[...] * iq_ref[...] * gq_ref[...], cos_ref[...], sin_ref[...], 1.0)
    q_ref[...] = q.astype(BF16)
    k = rope_block(kp_ref[...] * ik_ref[...] * gk_ref[...], cos_ref[...], sin_ref[...], 1.0)
    k_ref[...] = k.astype(BF16)
    v_ref[...] = vp_ref[...].astype(BF16)
    vt_ref[...] = vp_ref[...].T.astype(BF16)
    tvt_ref[...] = tv_ref[...].astype(F32).T.astype(BF16)
    length = len_ref[0]

    def one(keys, values_t, qm, head, limit):
        s = dot(keys, qm, 1, 1)
        if limit is not None:
            slot = lax.broadcasted_iota(jnp.int32, s.shape, 0)
            s = jnp.where(slot < limit, s, -1e30)
        peak = jnp.max(s, axis=0, keepdims=True)
        e = jnp.exp(s - peak)
        total = jnp.sum(e, axis=0, keepdims=True)
        o = dot(values_t[head * HD : (head + 1) * HD, :], e.astype(BF16))
        return o * (1.0 / total), peak + jnp.log(total)

    def chunk(c, carry):
        rows = pl.ds(pl.multiple_of(c * QC, QC), QC)
        qc = q_ref[rows, :] * jnp.asarray(HD**-0.5, BF16)
        selfs, crosses = [], []
        for h in range(heads):
            qm = masked(qc, h)
            o, lse = one(k_ref[...], vt_ref, qm, h, None)
            selfs.append(o)
            ls_ref[0, h : h + 1, rows] = lse
            o, lse = one(tk_ref[...], tvt_ref, qm, h, length)
            crosses.append(o)
            lc_ref[0, h : h + 1, rows] = lse
        so = jnp.concatenate(selfs, axis=0)
        co = jnp.concatenate(crosses, axis=0)
        so_ref[:, rows] = so
        co_ref[:, rows] = co
        mixed_ref[rows, :] = (so + gate_ref[...] * co).T.astype(BF16)
        return carry

    lax.fori_loop(0, tokens // QC, chunk, 0)


def attn_bwd_kernel(
    len_ref, q_ref, k_ref, v_ref, tk_ref, tv_ref, g_ref, so_ref, co_ref, ls_ref, lc_ref,
    qp_ref, kp_ref, iq_ref, ik_ref, gq_ref, gk_ref, cos_ref, sin_ref, gate_ref, gate_row_ref,
    dq_ref, dk_ref, dv_ref, dtk_ref, dtv_ref, rq_ref, rk_ref, gainq_ref, gaink_ref, gateg_ref,
    gs_ref, gc_ref, ds_ref, dc_ref, kt_ref, tkt_ref, dqt_ref, dk_acc, dv_acc,
):
    tokens, width = q_ref.shape
    heads = width // HD
    scale = jnp.asarray(HD**-0.5, BF16)

    @pl.when(pl.program_id(0) == 0)
    def _():
        rq_ref[...] = jnp.zeros_like(rq_ref)
        rk_ref[...] = jnp.zeros_like(rk_ref)

    g = g_ref[...]
    gs_ref[...] = g.astype(BF16)
    gc_ref[...] = (g * gate_row_ref[...]).astype(BF16)
    gt = g.T
    co = co_ref[...]
    prod_c = gt * co
    gateg_ref[...] = jnp.sum(prod_c, axis=1, keepdims=True)
    prod_s = gt * so_ref[...]
    prod_c = prod_c * gate_ref[...]
    for h in range(heads):
        ds_ref[h : h + 1, :] = jnp.sum(prod_s[h * HD : (h + 1) * HD], axis=0, keepdims=True)
        dc_ref[h : h + 1, :] = jnp.sum(prod_c[h * HD : (h + 1) * HD], axis=0, keepdims=True)
    kt_ref[...] = k_ref[...].astype(F32).T.astype(BF16)
    tkt_ref[...] = tk_ref[...].astype(F32).T.astype(BF16)
    dk_acc[...] = jnp.zeros_like(dk_acc)
    dv_acc[...] = jnp.zeros_like(dv_acc)
    dtk_ref[...] = jnp.zeros_like(dtk_ref)
    dtv_ref[...] = jnp.zeros_like(dtv_ref)
    length = len_ref[0]

    def one(keys, keys_t, values, qm, gm, lse, delta, head, limit):
        s = dot(keys, qm, 1, 1)
        p = jnp.exp(s - lse)
        if limit is not None:
            slot = lax.broadcasted_iota(jnp.int32, s.shape, 0)
            p = jnp.where(slot < limit, p, 0.0)
        dp = dot(values, gm, 1, 1)
        ds = (p * (dp - delta)).astype(BF16)
        dq = dot(keys_t[head * HD : (head + 1) * HD, :], ds)
        return dq, dot(ds, qm), dot(p.astype(BF16), gm)

    def chunk(c, carry):
        rows = pl.ds(pl.multiple_of(c * QC, QC), QC)
        qc = q_ref[rows, :] * scale
        for h in range(heads):
            qm = masked(qc, h)
            dq, dk, dv = one(
                k_ref[...], kt_ref, v_ref[...], qm, masked(gs_ref[rows, :], h),
                ls_ref[0, h : h + 1, rows], ds_ref[h : h + 1, rows], h, None,
            )
            dk_acc[...] += dk
            dv_acc[...] += dv
            dq2, dk, dv = one(
                tk_ref[...], tkt_ref, tv_ref[...], qm, masked(gc_ref[rows, :], h),
                lc_ref[0, h : h + 1, rows], dc_ref[h : h + 1, rows], h, length,
            )
            dtk_ref[...] += dk
            dtv_ref[...] += dv
            dqt_ref[h * HD : (h + 1) * HD, rows] = (dq + dq2) * HD**-0.5
        return carry

    lax.fori_loop(0, tokens // QC, chunk, 0)
    dq = rope_block(dqt_ref[...].T, cos_ref[...], sin_ref[...], -1.0)
    dq_ref[...] = dq
    prod = dq * (qp_ref[...] * iq_ref[...])
    gainq_ref[...] = jnp.sum(prod, axis=0, keepdims=True)
    rq_ref[...] += prod * gq_ref[...]
    dk = rope_block(dk_acc[...], cos_ref[...], sin_ref[...], -1.0)
    dk_ref[...] = dk
    prod = dk * (kp_ref[...] * ik_ref[...])
    gaink_ref[...] = jnp.sum(prod, axis=0, keepdims=True)
    rk_ref[...] += prod * gk_ref[...]
    dv_ref[...] = dv_acc[...].astype(BF16)


def specs(tokens, text, width, heads):
    col = pl.BlockSpec((tokens, width), lambda i: (0, i))
    tcol = pl.BlockSpec((text, width), lambda i: (0, i))
    row = pl.BlockSpec((width, tokens), lambda i: (i, 0))
    stat = pl.BlockSpec((tokens, 1), lambda i: (0, 0))
    gain = pl.BlockSpec((1, width), lambda i: (0, i))
    gcol = pl.BlockSpec((width, 1), lambda i: (i, 0))
    table = pl.BlockSpec((tokens, width), lambda i: (0, 0))
    lse = pl.BlockSpec((1, heads, tokens), lambda i: (i, 0, 0))
    scalar = pl.BlockSpec(memory_space=pltpu.SMEM)
    return col, tcol, row, stat, gain, gcol, table, lse, scalar


def sds(shape, dtype=F32):
    return jax.ShapeDtypeStruct(shape, dtype)


def attn_forward(length, qp, kp, vp, iq, ik, gq, gk, cosine, sine, tk, tv, gate):
    tokens, columns = qp.shape
    text, width = tk.shape[0], cosine.shape[1]
    heads, blocks = width // HD, columns // width
    col, tcol, row, stat, gain, gcol, table, lse, scalar = specs(tokens, text, width, heads)
    pairs = columns // HD * tokens * (tokens + text)
    return pl.pallas_call(
        attn_fwd_kernel,
        grid=(blocks,),
        in_specs=[scalar, col, col, col, stat, stat, gain, gain, table, table, tcol, tcol, gcol],
        out_specs=[col, col, col, col, row, row, lse, lse],
        out_shape=[
            sds(qp.shape, BF16), sds(qp.shape, BF16), sds(qp.shape, BF16), sds(qp.shape, BF16),
            sds((columns, tokens)), sds((columns, tokens)),
            sds((blocks, heads, tokens)), sds((blocks, heads, tokens)),
        ],
        scratch_shapes=[pltpu.VMEM((width, tokens), BF16), pltpu.VMEM((width, text), BF16)],
        cost_estimate=pl.CostEstimate(
            flops=16 * pairs * HD, transcendentals=pairs, bytes_accessed=28 * tokens * columns
        ),
    )(length, qp, kp, vp, iq, ik, gq, gk, cosine, sine, tk, tv, gate)


def attn_backward(length, q, k, v, tk, tv, g, so, co, ls, lc, qp, kp, iq, ik, gq, gk, cosine, sine, gate):
    tokens, columns = q.shape
    text, width = tk.shape[0], cosine.shape[1]
    heads, blocks = width // HD, columns // width
    col, tcol, row, stat, gain, gcol, table, lse, scalar = specs(tokens, text, width, heads)
    pairs = columns // HD * tokens * (tokens + text)
    return pl.pallas_call(
        attn_bwd_kernel,
        grid=(blocks,),
        in_specs=[scalar, col, col, col, tcol, tcol, col, row, row, lse, lse,
                  col, col, stat, stat, gain, gain, table, table, gcol, gain],
        out_specs=[col, col, col, tcol, tcol, table, table, gain, gain, gcol],
        out_shape=[
            sds(q.shape), sds(q.shape), sds(q.shape, BF16), sds(tk.shape), sds(tk.shape),
            sds((tokens, width)), sds((tokens, width)),
            sds((1, columns)), sds((1, columns)), sds((columns, 1)),
        ],
        scratch_shapes=[
            pltpu.VMEM((tokens, width), BF16), pltpu.VMEM((tokens, width), BF16),
            pltpu.VMEM((heads, tokens), F32), pltpu.VMEM((heads, tokens), F32),
            pltpu.VMEM((width, tokens), BF16), pltpu.VMEM((width, text), BF16),
            pltpu.VMEM((width, tokens), F32),
            pltpu.VMEM((tokens, width), F32), pltpu.VMEM((tokens, width), F32),
        ],
        cost_estimate=pl.CostEstimate(
            flops=40 * pairs * HD, transcendentals=pairs, bytes_accessed=44 * tokens * columns
        ),
    )(length, q, k, v, tk, tv, g, so, co, ls, lc, qp, kp, iq, ik, gq, gk, cosine, sine,
      gate, gate.reshape(1, columns))


def time_embed(timesteps):
    half = TE // 2
    frequencies = jnp.exp(-math.log(10000.0) * jnp.arange(half, dtype=F32) / half)
    angles = timesteps.astype(F32)[:, None] * frequencies
    waves = jnp.concatenate([jnp.cos(angles), jnp.sin(angles)], axis=-1)
    return jax.nn.silu(waves).astype(BF16)


def rope_tables(positions, width):
    lane = jnp.arange(width)
    quarter = HD // 4
    frequencies = 10000.0 ** (-(lane % quarter).astype(F32) / quarter)
    place = jnp.where(lane % HD < HD // 2, positions[0][:, None], positions[1][:, None])
    angles = place.astype(F32) * frequencies
    return jnp.cos(angles), jnp.where(lane % 32 < 16, -1.0, 1.0) * jnp.sin(angles)


def inverse_rms(values):
    return lax.rsqrt(jnp.mean(values * values, axis=-1, keepdims=True) + EPSILON)


def rms_back(grad_hat, normed, inverse):
    return inverse * (grad_hat - normed * jnp.mean(grad_hat * normed, axis=-1, keepdims=True))


def pad_cols(value, width):
    extra = -value.shape[-1] % width
    return value if extra == 0 else jnp.pad(value, [(0, 0)] * (value.ndim - 1) + [(0, extra)])


def on_device(
    hidden_in, text_state, caption_lengths, timesteps, patch_positions, cotangent,
    w_ada, w_text, w_qkv, w_out, gains, cross_gate, w_gate_up, w_down,
):
    n, f = lax.axis_size("fsdp"), lax.axis_index("fsdp")
    dpn, me = lax.axis_size("dp"), lax.axis_index("dp")
    order_a, order_b, order_c = orders()
    own_d = D // n
    local = hidden_in.shape[1]
    width = 2 * HD
    x_bf, dy_bf = hidden_in[0], cotangent[0]

    x_all = jnp.concatenate(gather_rot(x_bf), axis=0)
    dy_all = jnp.concatenate(gather_rot(dy_bf), axis=0)
    places = jnp.concatenate(gather_rot(patch_positions[0]), axis=1)
    w_heads = lax.all_to_all(w_qkv, "fsdp", split_axis=2, concat_axis=0, tiled=True)
    text_cols = lax.all_to_all(text_state[0], "fsdp", split_axis=1, concat_axis=0, tiled=True)
    gain_full = lax.all_gather(gains, "fsdp", axis=1, tiled=True).astype(F32)
    gain_own = gains.astype(F32)
    times_all = lax.all_gather(timesteps, "dp", axis=0, tiled=True)

    time_low = time_embed(timesteps)
    own_te = TE // n
    time_own = lax.dynamic_slice_in_dim(time_low[0], f * own_te, own_te, 0)
    modulation = pair_sum(
        jnp.einsum("k,kjd->jd", time_own, w_ada, preferred_element_type=F32)
    )
    scale_attn, gate_attn = modulation[0:1], jnp.tanh(modulation[1:2])
    scale_ffn, gate_ffn = modulation[2:3], jnp.tanh(modulation[3:4])

    x_f = x_all.astype(F32)
    normed_all = x_f * inverse_rms(x_f)
    first_all = (normed_all * gain_full[0] * (1.0 + scale_attn)).astype(BF16)
    q_pre, k_pre, v_pre = (dot(first_all, w_heads[:, j]) for j in range(3))
    squares = row_sum(jnp.stack([jnp.sum(q_pre * q_pre, -1), jnp.sum(k_pre * k_pre, -1)]))
    inverse = lax.rsqrt(squares / D + EPSILON)
    inv_q, inv_k = inverse[0][:, None], inverse[1][:, None]

    text_part = jnp.stack([dot(text_cols, w_text[:, j]) for j in range(2)])
    text_pre = scatter_rot(rot_blocks(text_part.reshape(2, TEXT, n, own_d), 2))
    inv_t = lax.rsqrt(
        pair_sum(jnp.sum(text_pre[0] * text_pre[0], -1, keepdims=True)) / D + EPSILON
    )
    normed_t = text_pre[0] * inv_t
    tk = (normed_t * gain_own[4]).astype(BF16)
    tv = text_pre[1].astype(BF16)
    half = text_cols.shape[1] // 2
    text_a = dp_gather(text_cols[:, :half], order_a)
    text_b = dp_gather(text_cols[:, half:], order_b)

    head_tanh = jnp.tanh(cross_gate.astype(F32))
    gate_col = pad_cols(jnp.repeat(head_tanh, HD)[None], width).T
    cosine, sine = rope_tables(places, width)
    gq, gk = pad_cols(gain_own[2:3], width), pad_cols(gain_own[3:4], width)
    qp, kp, vp = (pad_cols(v, width) for v in (q_pre, k_pre, v_pre))
    tkp, tvp = pad_cols(tk, width), pad_cols(tv, width)
    q, k, v, mixed_p, so, co, ls, lc = attn_forward(
        caption_lengths, qp, kp, vp, inv_q, inv_k, gq, gk, cosine, sine, tkp, tvp, gate_col
    )
    mixed = mixed_p[:, :own_d]
    parts = [dot(mixed[r * local : (r + 1) * local], w_out) for r in range(n)]
    attn_branch = scatter_rot([parts[0]] + [p.astype(BF16) for p in parts[1:]])
    x_own = x_bf.astype(F32)
    after_attn = x_own + gate_attn * attn_branch
    inverse_two = inverse_rms(after_attn)
    normed_two = after_attn * inverse_two
    second = (normed_two * gain_full[1] * (1.0 + scale_ffn)).astype(BF16)

    second_all = jnp.concatenate(gather_rot(second), axis=0)
    branch_all = (gate_ffn * dy_all.astype(F32)).astype(BF16)
    w_gate, w_up = w_gate_up[:, 0], w_gate_up[:, 1]
    gate_pre = dot(second_all, w_gate)
    up_pre = dot(second_all, w_up)
    grad_hidden = dot(branch_all, w_down, 1, 1)
    sig = jax.nn.sigmoid(gate_pre)
    hidden = (gate_pre * sig * up_pre).astype(BF16)
    grad_gate = (grad_hidden * up_pre * (sig + gate_pre * sig * (1.0 - sig))).astype(BF16)
    grad_up = (grad_hidden * gate_pre * sig).astype(BF16)
    down_grad = dp_scatter(dot(branch_all, hidden, 0, 0).astype(BF16), order_c)
    gate_grad = dp_scatter(dot(second_all, grad_gate, 0, 0).astype(BF16), order_a)
    up_grad = dp_scatter(dot(second_all, grad_up, 0, 0).astype(BF16), order_b)

    def rows(value, r):
        return value[r * local : (r + 1) * local]

    back = [
        dot(rows(grad_gate, r), w_gate, 1, 1) + dot(rows(grad_up, r), w_up, 1, 1) for r in range(n)
    ]
    grad_second = scatter_rot([back[0]] + [b.astype(BF16) for b in back[1:]])
    parts = [dot(rows(hidden, r), w_down) for r in range(n)]
    ffn_branch = scatter_rot([parts[0]] + [p.astype(BF16) for p in parts[1:]])
    output = (after_attn + gate_ffn * ffn_branch).astype(BF16)
    dy = dy_bf.astype(F32)
    d_gate_ffn = jnp.sum(dy * ffn_branch, axis=0) * (1.0 - gate_ffn[0] * gate_ffn[0])

    scaled = grad_second * normed_two
    d_scale_ffn = jnp.sum(scaled * gain_full[1], axis=0)
    gain_two = jnp.sum(scaled * (1.0 + scale_ffn), axis=0)
    grad_after = dy + rms_back(
        grad_second * gain_full[1] * (1.0 + scale_ffn), normed_two, inverse_two
    )
    d_gate_attn = jnp.sum(grad_after * attn_branch, axis=0) * (1.0 - gate_attn[0] * gate_attn[0])
    grad_attn = (gate_attn * grad_after).astype(BF16)
    grad_attn_all = jnp.concatenate(gather_rot(grad_attn), axis=0)
    grad_mixed = dot(grad_attn_all, w_out, 1, 1)
    out_local = dot(grad_attn_all, mixed, 0, 0).astype(BF16)
    half_d = own_d // 2
    out_grad = jnp.concatenate(
        [dp_scatter(out_local[:, :half_d], order_a), dp_scatter(out_local[:, half_d:], order_b)],
        axis=1,
    )
    dq, dk, dv, dtk, dtv, rq, rk, gain_q, gain_k, gate_g = attn_backward(
        caption_lengths, q, k, v, tkp, tvp, pad_cols(grad_mixed, width), so, co, ls, lc, qp, kp,
        inv_q, inv_k, gq, gk, cosine, sine, gate_col,
    )
    dq, dk, dv, dtk, dtv = (v_[:, :own_d] for v_ in (dq, dk, dv, dtk, dtv))
    gate_total = jnp.sum(gate_g[:own_d].reshape(HEADS // n, HD), axis=1) * (
        1.0 - head_tanh * head_tanh
    )
    text_hat = dtk * gain_own[4]
    gain_text = jnp.sum(dtk * normed_t, axis=0, keepdims=True)
    means = row_sum(jnp.stack([jnp.sum(rq, -1), jnp.sum(rk, -1)])) / D
    mean_t = pair_sum(jnp.sum(text_hat * normed_t, -1, keepdims=True)) / D
    grad_q = (inv_q * (dq * gain_own[2] - q_pre * inv_q * means[0][:, None])).astype(BF16)
    grad_k = (inv_k * (dk * gain_own[3] - k_pre * inv_k * means[1][:, None])).astype(BF16)

    grads = (grad_q, grad_k, dv)
    wide = jnp.stack([dot(g, first_all, 0, 0).astype(BF16) for g in grads])
    wide = lax.all_to_all(wide, "fsdp", split_axis=2, concat_axis=1, tiled=True)
    q_grad = dp_scatter(wide[0], order_a)
    k_grad = dp_scatter(wide[1], order_b)
    v_grad = jnp.concatenate(
        [
            dp_scatter(wide[2][:, :half_d], order_a),
            dp_scatter(wide[2][:, half_d:], order_b),
        ],
        axis=1,
    )
    parts = [
        sum(dot(rows(g, r), w_heads[:, j], 1, 1) for j, g in enumerate(grads)) for r in range(n)
    ]
    grad_first = scatter_rot([parts[0]] + [p.astype(BF16) for p in parts[1:]])
    inverse_one = inverse_rms(x_own)
    normed_one = x_own * inverse_one
    scaled = grad_first * normed_one
    d_scale_attn = jnp.sum(scaled * gain_full[0], axis=0)
    gain_one = jnp.sum(scaled * (1.0 + scale_attn), axis=0)
    grad_input = (
        grad_after
        + rms_back(grad_first * gain_full[0] * (1.0 + scale_attn), normed_one, inverse_one)
    ).astype(BF16)

    grad_tk = (inv_t * (text_hat - normed_t * mean_t)).astype(BF16)
    text_pair = jnp.concatenate([grad_tk, dtv.astype(BF16)], axis=0).reshape(2, TEXT, own_d)
    pair_all = lax.all_gather(text_pair, "fsdp", axis=2, tiled=True)
    text_in = dot(pair_all[0], w_text[:, 0], 1, 1) + dot(pair_all[1], w_text[:, 1], 1, 1)
    text_in = lax.all_to_all(text_in.astype(BF16), "fsdp", split_axis=0, concat_axis=1, tiled=True)
    share = D // dpn
    outgoing = pair_all.reshape(2, TEXT, dpn, share).transpose(2, 0, 1, 3)
    pair_cols = dp_exchange(outgoing, order_a)
    halves = []
    for pieces in (text_a, text_b):
        total = 0.0
        for where, piece in pieces:
            for i, r in enumerate(where):
                total = total + jnp.einsum(
                    "jts,tk->jsk", pair_cols[r], piece[i], preferred_element_type=F32
                )
        halves.append(total)
    text_grad = jnp.concatenate(halves, axis=2)

    mods = jnp.stack([d_scale_attn, d_gate_attn, d_scale_ffn, d_gate_ffn])
    mods = pair_sum(dp_exchange(mods.reshape(4, dpn, share).transpose(1, 0, 2), order_a))
    times = time_embed(jnp.take(times_all, me ^ jnp.arange(dpn)))
    times = lax.dynamic_slice_in_dim(times, f * own_te, own_te, 1).astype(F32)
    ada_grad = lax.dot_general(
        mods.reshape(dpn, 4 * share), times, (((0,), (0,)), ((), ())),
        precision=lax.Precision.HIGHEST,
    ).reshape(4, share, own_te)
    two = scatter_rot(rot_blocks(jnp.stack([gain_one, gain_two]).reshape(2, n, own_d), 1))
    gate_row = jnp.pad(gate_total, (0, own_d - gate_total.shape[0]))[None]
    small = dp_total(
        jnp.concatenate([two, gain_q[:, :own_d], gain_k[:, :own_d], gain_text, gate_row], axis=0)
    )
    return (
        output[None],
        grad_input[None],
        text_in[None],
        ada_grad.transpose(2, 0, 1),
        text_grad.transpose(2, 0, 1),
        jnp.stack([q_grad, k_grad, v_grad]).transpose(2, 0, 1),
        out_grad.T,
        small[:5],
        small[5, : HEADS // n],
        jnp.stack([gate_grad, up_grad], axis=1),
        down_grad.T,
    )


def solution(mesh):
    return jax.shard_map(
        on_device,
        mesh=mesh,
        in_specs=(
            P("dp", "fsdp", None),
            P("dp", "fsdp", None),
            P("dp"),
            P("dp"),
            P("dp", None, "fsdp"),
            P("dp", "fsdp", None),
            P("fsdp", None, None),
            P("fsdp", None, None),
            P("fsdp", None, None),
            P("fsdp", None),
            P(None, "fsdp"),
            P("fsdp"),
            P(None, None, "fsdp"),
            P("fsdp", None),
        ),
        out_specs=(
            P("dp", "fsdp", None),
            P("dp", "fsdp", None),
            P("dp", "fsdp", None),
            P("fsdp", None, "dp"),
            P("fsdp", None, "dp"),
            P("fsdp", None, "dp"),
            P("fsdp", "dp"),
            P(None, "fsdp"),
            P("fsdp"),
            P("dp", None, "fsdp"),
            P("fsdp", "dp"),
        ),
        check_vma=False,
    )
```

```python
import functools
import math

import jax
import jax.numpy as jnp
from jax import lax
from jax.experimental import pallas as pl
from jax.experimental.pallas import tpu as pltpu
from jax.sharding import PartitionSpec as P

D = 1536
HEADS = 24
HD = 64
TW = 4096
TE = 1024
PATCHES = 1024
TEXT = 256
EPSILON = 1e-06
F32 = jnp.float32
BF16 = jnp.bfloat16
QC = 256


def dot(a, b, ca=1, cb=0):
    return lax.dot_general(a, b, (((ca,), (cb,)), ((), ())), preferred_element_type=F32)


def from_behind(value, step):
    n = lax.axis_size("fsdp")
    return lax.ppermute(value, "fsdp", [(i, (i + step) % n) for i in range(n)])


def gather_rot(value):
    return [value] + [from_behind(value, r) for r in range(1, lax.axis_size("fsdp"))]


def pair_sum(value):
    return functools.reduce(lambda a, b: a + b, gather_rot(value))


def row_sum(value):
    n = lax.axis_size("fsdp")
    rows = value.shape[-1] // n
    total = value
    for r in range(1, n):
        total = total + jnp.roll(from_behind(value, r), r * rows, axis=-1)
    return total


def scatter_rot(blocks):
    n = lax.axis_size("fsdp")
    total = blocks[0].astype(F32)
    for r in range(1, n):
        got = lax.ppermute(blocks[r], "fsdp", [(i, (i - r) % n) for i in range(n)])
        total = total + got.astype(F32)
    return total


def rot_blocks(value, axis):
    n, f = lax.axis_size("fsdp"), lax.axis_index("fsdp")
    return [lax.dynamic_index_in_dim(value, (f - r) % n, axis, keepdims=False) for r in range(n)]


def exchange_rot(value, axis):
    n, f = lax.axis_size("fsdp"), lax.axis_index("fsdp")
    out = []
    for r in range(n):
        send = lax.dynamic_index_in_dim(value, (f + r) % n, axis, keepdims=False)
        out.append(from_behind(send, r) if r else send)
    return out


def gather_natural(value):
    n, f = lax.axis_size("fsdp"), lax.axis_index("fsdp")
    blocks = jnp.stack(gather_rot(value))
    order = [lax.dynamic_index_in_dim(blocks, (f - g) % n, 0, keepdims=False) for g in range(n)]
    return jnp.concatenate(order, axis=-1)


def exchange(value):
    n, f = lax.axis_size("fsdp"), lax.axis_index("fsdp")
    sends = rot_blocks(value, 0)
    got = [sends[0]]
    for r in range(1, n):
        got.append(lax.ppermute(sends[r], "fsdp", [(i, (i - r) % n) for i in range(n)]))
    if n == 2:
        return [jnp.where(f == 0, got[0], got[1]), jnp.where(f == 0, got[1], got[0])]
    got = jnp.stack(got)
    return [lax.dynamic_index_in_dim(got, (g - f) % n, 0, keepdims=False) for g in range(n)]


def dp_bits():
    return int(lax.axis_size("dp")).bit_length() - 1


def dp_swap(value, bit):
    n = lax.axis_size("dp")
    return lax.ppermute(value, "dp", [(i, i ^ (1 << bit)) for i in range(n)])


def orders():
    bits = list(range(dp_bits()))
    return bits, bits[:2][::-1] + bits[2:], bits[2:3] + bits[:2][::-1] + bits[3:]


def split_bit(value, axis, bit):
    mine = (lax.axis_index("dp") >> bit) & 1
    keep = lax.dynamic_index_in_dim(value, mine, axis, keepdims=False)
    send = lax.dynamic_index_in_dim(value, 1 - mine, axis, keepdims=False)
    return keep, send


class Halving:
    def __init__(self, value, order, flip=0):
        nb = dp_bits()
        self.cur = value.reshape((2,) * nb + value.shape[1:])
        self.labels = list(range(nb))[::-1]
        self.order, self.flip = list(order), flip
        self.keep = self.got = None
        self.start()

    def start(self):
        if not self.order:
            return
        bit = self.order.pop(0)
        axis = self.labels.index(bit)
        mine = (lax.axis_index("dp") >> bit) & 1
        if bit == dp_bits() - 1:
            mine = mine ^ self.flip
        self.labels.remove(bit)
        self.keep = lax.dynamic_index_in_dim(self.cur, mine, axis, keepdims=False)
        send = lax.dynamic_index_in_dim(self.cur, 1 - mine, axis, keepdims=False)
        self.got = dp_swap(send, bit)

    def step(self):
        if self.got is None:
            return
        total = self.keep.astype(F32) + self.got.astype(F32)
        self.cur = total.astype(BF16) if self.order else total
        self.got = None
        self.start()


def advance(chains, value):
    live = [c for c in chains if c.got is not None]
    value, got = lax.optimization_barrier((value, [c.got for c in live]))
    for c, g in zip(live, got):
        c.got = g
        c.step()
    return value


def dp_exchange(value, order):
    nb = dp_bits()
    cur = value.reshape((2,) * nb + value.shape[1:])
    for bit in order:
        axis = nb - 1 - bit
        keep, send = split_bit(cur, axis, bit)
        cur = jnp.stack([keep, dp_swap(send, bit)], axis=axis)
    return cur.reshape(value.shape)


def dp_total(value):
    for bit in range(dp_bits()):
        value = value + dp_swap(value, bit)
    return value


def rope_block(value, cosine, sine, sign):
    width = value.shape[1]
    lane = lax.broadcasted_iota(jnp.int32, value.shape, 1)
    partner = jnp.where(
        lane % 32 < 16, pltpu.roll(value, width - 16, 1), pltpu.roll(value, 16, 1)
    )
    return value * cosine + sign * (partner * sine)


def masked(value, head):
    lane = lax.broadcasted_iota(jnp.int32, value.shape, 1)
    return jnp.where(lane // HD == head, value, jnp.zeros_like(value))


def attn_fwd_kernel(
    len_ref, qp_ref, kp_ref, vp_ref, iq_ref, ik_ref, gq_ref, gk_ref, cos_ref, sin_ref,
    tk_ref, tv_ref, gate_ref,
    q_ref, k_ref, v_ref, mixed_ref, so_ref, co_ref, ls_ref, lc_ref,
):
    tokens, width = qp_ref.shape
    heads = width // HD
    q = rope_block(qp_ref[...] * iq_ref[...] * gq_ref[...], cos_ref[...], sin_ref[...], 1.0)
    q_ref[...] = q.astype(BF16)
    k = rope_block(kp_ref[...] * ik_ref[...] * gk_ref[...], cos_ref[...], sin_ref[...], 1.0)
    k_ref[...] = k.astype(BF16)
    v_ref[...] = vp_ref[...].astype(BF16)
    length = len_ref[0]

    def one(keys, values, qm, limit):
        s = dot(qm, keys, 1, 1)
        if limit is not None:
            slot = lax.broadcasted_iota(jnp.int32, s.shape, 1)
            s = jnp.where(slot < limit, s, -1e30)
        peak = jnp.max(s, axis=1, keepdims=True)
        e = jnp.exp(s - peak)
        total = jnp.sum(e, axis=1, keepdims=True)
        o = dot(e.astype(BF16), values)
        return o * (1.0 / total), peak + jnp.log(total)

    lane = lax.broadcasted_iota(jnp.int32, (tokens, width), 1)
    qs = q_ref[...] * jnp.asarray(HD**-0.5, BF16)
    so = co = stats = jnp.zeros((tokens, width), F32)
    for h in range(heads):
        qm = masked(qs, h)
        o, lse = one(k_ref[...], v_ref[...], qm, None)
        so = jnp.where(lane // HD == h, o, so)
        stats = jnp.where(lane == h, lse, stats)
        o, lse = one(tk_ref[...], tv_ref[...], qm, length)
        co = jnp.where(lane // HD == h, o, co)
        stats = jnp.where(lane == heads + h, lse, stats)
    so_ref[...] = so
    co_ref[...] = co
    mixed_ref[...] = (so + gate_ref[...] * co).astype(BF16)
    stats = stats.T
    ls_ref[0] = stats[:heads]
    lc_ref[0] = stats[heads : 2 * heads]


def attn_bwd_kernel(
    len_ref, q_ref, k_ref, v_ref, tk_ref, tv_ref, g_ref, so_ref, co_ref, ls_ref, lc_ref,
    qp_ref, kp_ref, iq_ref, ik_ref, gq_ref, gk_ref, cos_ref, sin_ref, gate_ref,
    dq_ref, dk_ref, dv_ref, dtk_ref, dtv_ref, rq_ref, rk_ref, gainq_ref, gaink_ref, gateg_ref,
    gs_ref, gc_ref, ds_ref, dc_ref, kt_ref, tkt_ref, dqt_ref, dk_acc, dv_acc,
):
    tokens, width = q_ref.shape
    heads = width // HD
    scale = jnp.asarray(HD**-0.5, BF16)

    @pl.when(pl.program_id(0) == 0)
    def _():
        rq_ref[...] = jnp.zeros_like(rq_ref)
        rk_ref[...] = jnp.zeros_like(rk_ref)

    g = g_ref[...]
    gs_ref[...] = g.astype(BF16)
    gc_ref[...] = (g * gate_ref[...]).astype(BF16)
    prod_c = g * co_ref[...]
    gateg_ref[...] = jnp.sum(prod_c, axis=0, keepdims=True)
    prod_s = (g * so_ref[...]).T
    prod_c = (prod_c * gate_ref[...]).T
    for h in range(heads):
        ds_ref[h : h + 1, :] = jnp.sum(prod_s[h * HD : (h + 1) * HD], axis=0, keepdims=True)
        dc_ref[h : h + 1, :] = jnp.sum(prod_c[h * HD : (h + 1) * HD], axis=0, keepdims=True)
    kt_ref[...] = k_ref[...].astype(F32).T.astype(BF16)
    tkt_ref[...] = tk_ref[...].astype(F32).T.astype(BF16)
    dk_acc[...] = jnp.zeros_like(dk_acc)
    dv_acc[...] = jnp.zeros_like(dv_acc)
    dtk_ref[...] = jnp.zeros_like(dtk_ref)
    dtv_ref[...] = jnp.zeros_like(dtv_ref)
    length = len_ref[0]

    def one(keys, keys_t, values, qm, gm, lse, delta, head, limit):
        s = dot(keys, qm, 1, 1)
        p = jnp.exp(s - lse)
        if limit is not None:
            slot = lax.broadcasted_iota(jnp.int32, s.shape, 0)
            p = jnp.where(slot < limit, p, 0.0)
        dp = dot(values, gm, 1, 1)
        ds = (p * (dp - delta)).astype(BF16)
        dq = dot(keys_t[head * HD : (head + 1) * HD, :], ds)
        return dq, dot(ds, qm), dot(p.astype(BF16), gm)

    def chunk(c, carry):
        rows = pl.ds(pl.multiple_of(c * QC, QC), QC)
        qc = q_ref[rows, :] * scale
        for h in range(heads):
            qm = masked(qc, h)
            dq, dk, dv = one(
                k_ref[...], kt_ref, v_ref[...], qm, masked(gs_ref[rows, :], h),
                ls_ref[0, h : h + 1, rows], ds_ref[h : h + 1, rows], h, None,
            )
            dk_acc[...] += dk
            dv_acc[...] += dv
            dq2, dk, dv = one(
                tk_ref[...], tkt_ref, tv_ref[...], qm, masked(gc_ref[rows, :], h),
                lc_ref[0, h : h + 1, rows], dc_ref[h : h + 1, rows], h, length,
            )
            dtk_ref[...] += dk
            dtv_ref[...] += dv
            dqt_ref[h * HD : (h + 1) * HD, rows] = (dq + dq2) * HD**-0.5
        return carry

    lax.fori_loop(0, tokens // QC, chunk, 0)
    dq = rope_block(dqt_ref[...].T, cos_ref[...], sin_ref[...], -1.0)
    dq_ref[...] = dq
    prod = dq * (qp_ref[...] * iq_ref[...])
    gainq_ref[...] = jnp.sum(prod, axis=0, keepdims=True)
    rq_ref[...] += prod * gq_ref[...]
    dk = rope_block(dk_acc[...], cos_ref[...], sin_ref[...], -1.0)
    dk_ref[...] = dk
    prod = dk * (kp_ref[...] * ik_ref[...])
    gaink_ref[...] = jnp.sum(prod, axis=0, keepdims=True)
    rk_ref[...] += prod * gk_ref[...]
    dv_ref[...] = dv_acc[...].astype(BF16)


def specs(tokens, text, width, heads):
    col = pl.BlockSpec((tokens, width), lambda i: (0, i))
    tcol = pl.BlockSpec((text, width), lambda i: (0, i))
    stat = pl.BlockSpec((tokens, 1), lambda i: (0, 0))
    gain = pl.BlockSpec((1, width), lambda i: (0, i))
    table = pl.BlockSpec((tokens, width), lambda i: (0, 0))
    lse = pl.BlockSpec((1, heads, tokens), lambda i: (i, 0, 0))
    scalar = pl.BlockSpec(memory_space=pltpu.SMEM)
    return col, tcol, stat, gain, table, lse, scalar


def sds(shape, dtype=F32):
    return jax.ShapeDtypeStruct(shape, dtype)


def attn_forward(length, qp, kp, vp, iq, ik, gq, gk, cosine, sine, tk, tv, gate):
    tokens, columns = qp.shape
    text, width = tk.shape[0], cosine.shape[1]
    heads, blocks = width // HD, columns // width
    col, tcol, stat, gain, table, lse, scalar = specs(tokens, text, width, heads)
    return pl.pallas_call(
        attn_fwd_kernel,
        grid=(blocks,),
        in_specs=[scalar, col, col, col, stat, stat, gain, gain, table, table, tcol, tcol, gain],
        out_specs=[col, col, col, col, col, col, lse, lse],
        out_shape=[
            sds(qp.shape, BF16), sds(qp.shape, BF16), sds(qp.shape, BF16), sds(qp.shape, BF16),
            sds(qp.shape), sds(qp.shape),
            sds((blocks, heads, tokens)), sds((blocks, heads, tokens)),
        ],
    )(length, qp, kp, vp, iq, ik, gq, gk, cosine, sine, tk, tv, gate)


def attn_backward(length, q, k, v, tk, tv, g, so, co, ls, lc, qp, kp, iq, ik, gq, gk, cosine, sine, gate):
    tokens, columns = q.shape
    text, width = tk.shape[0], cosine.shape[1]
    heads, blocks = width // HD, columns // width
    col, tcol, stat, gain, table, lse, scalar = specs(tokens, text, width, heads)
    return pl.pallas_call(
        attn_bwd_kernel,
        grid=(blocks,),
        in_specs=[scalar, col, col, col, tcol, tcol, col, col, col, lse, lse,
                  col, col, stat, stat, gain, gain, table, table, gain],
        out_specs=[col, col, col, tcol, tcol, table, table, gain, gain, gain],
        out_shape=[
            sds(q.shape), sds(q.shape), sds(q.shape, BF16), sds(tk.shape), sds(tk.shape),
            sds((tokens, width)), sds((tokens, width)),
            sds((1, columns)), sds((1, columns)), sds((1, columns)),
        ],
        scratch_shapes=[
            pltpu.VMEM((tokens, width), BF16), pltpu.VMEM((tokens, width), BF16),
            pltpu.VMEM((heads, tokens), F32), pltpu.VMEM((heads, tokens), F32),
            pltpu.VMEM((width, tokens), BF16), pltpu.VMEM((width, text), BF16),
            pltpu.VMEM((width, tokens), F32),
            pltpu.VMEM((tokens, width), F32), pltpu.VMEM((tokens, width), F32),
        ],
    )(length, q, k, v, tk, tv, g, so, co, ls, lc, qp, kp, iq, ik, gq, gk, cosine, sine,
      gate)


def pick(rows, cols, step, part):
    i = lax.broadcasted_iota(jnp.int32, (rows, cols), 0)
    j = lax.broadcasted_iota(jnp.int32, (rows, cols), 1)
    hit = (j == step * i + part) if cols > rows else (i == step * j + part)
    return jnp.where(hit, 1.0, 0.0).astype(BF16)

def text_fwd_kernel(x_ref, w_ref, o_ref):
    @pl.when(pl.program_id(0) == 0)
    def _():
        o_ref[...] = jnp.zeros_like(o_ref)
    for b in range(w_ref.shape[0] // 128):
        rows = slice(b * 128, (b + 1) * 128)
        w = w_ref[rows].reshape(256, w_ref.shape[2])
        x = x_ref[:, rows]
        for j in range(2):
            spread = dot(x, pick(128, 256, 2, j)).astype(BF16)
            o_ref[j] += dot(spread, w)

def text_fwd(x, w):
    depth, _, cols = w.shape
    bk = 256
    return pl.pallas_call(
        text_fwd_kernel, grid=(depth // bk,),
        in_specs=[pl.BlockSpec((x.shape[0], bk), lambda i: (0, i)), pl.BlockSpec((bk, 2, cols), lambda i: (i, 0, 0))],
        out_specs=pl.BlockSpec((2, x.shape[0], cols), lambda i: (0, 0, 0)),
        out_shape=sds((2, x.shape[0], cols)),
    )(x, w)

def text_bwd_kernel(g_ref, w_ref, o_ref):
    for b in range(w_ref.shape[0] // 128):
        rows = slice(b * 128, (b + 1) * 128)
        w = w_ref[rows].reshape(256, w_ref.shape[2])
        total = 0.0
        for j in range(2):
            total = total + dot(g_ref[j], dot(pick(128, 256, 2, j), w).astype(BF16), 1, 1)
        o_ref[:, rows] = total.astype(BF16)

def text_bwd(g, w):
    depth, _, cols = w.shape
    bk = 256
    return pl.pallas_call(
        text_bwd_kernel, grid=(depth // bk,),
        in_specs=[pl.BlockSpec(g.shape, lambda i: (0, 0, 0)), pl.BlockSpec((bk, 2, cols), lambda i: (i, 0, 0))],
        out_specs=pl.BlockSpec((g.shape[1], bk), lambda i: (0, i)),
        out_shape=sds((g.shape[1], depth), BF16),
    )(g, w)

def ffn_kernel(
    s_ref, b_ref, w_ref, d_ref, wgo_ref, wuo_ref, wdo_ref, fo_ref, fp_ref, so_ref, sp_ref,
    st, bt, wg, wu, facc, sacc,
):
    step = pl.program_id(0)
    depth, _, cols = w_ref.shape
    own = fo_ref.shape[0]
    @pl.when(step == 0)
    def _():
        for c in range(depth // 256):
            part = slice(c * 256, (c + 1) * 256)
            st[part, :] = s_ref[:, part].astype(F32).T.astype(BF16)
            bt[part, :] = b_ref[:, part].astype(F32).T.astype(BF16)
        facc[...] = jnp.zeros_like(facc)
        sacc[...] = jnp.zeros_like(sacc)
    for c in range(depth // 128):
        part = slice(c * 128, (c + 1) * 128)
        w = w_ref[part].reshape(256, cols)
        wg[part, :] = dot(pick(128, 256, 2, 0), w).astype(BF16)
        wu[part, :] = dot(pick(128, 256, 2, 1), w).astype(BF16)
    s, b = s_ref[...], b_ref[...]
    gate = dot(s, wg[...])
    up = dot(s, wu[...])
    back = dot(b, d_ref[...], 1, 1)
    sig = jax.nn.sigmoid(gate)
    silu = gate * sig
    hidden = (silu * up).astype(BF16)
    g_gate = (back * up * (sig + silu * (1.0 - sig))).astype(BF16)
    g_up = (back * silu).astype(BF16)
    dp, rows, _ = wgo_ref.shape
    for out, left, right in ((wgo_ref, st, g_gate), (wuo_ref, st, g_up), (wdo_ref, bt, hidden)):
        out[...] = dot(left[...], right).astype(BF16).reshape(dp, rows, cols)
    facc[...] += dot(hidden, d_ref[...])
    sacc[...] += dot(g_gate, wg[...], 1, 1) + dot(g_up, wu[...], 1, 1)
    @pl.when(step == pl.num_programs(0) - 1)
    def _():
        fo_ref[...] = facc[:own]
        fp_ref[...] = facc[own:].astype(BF16)
        so_ref[...] = sacc[:own]
        sp_ref[...] = sacc[own:].astype(BF16)

def ffn(s, b, w, d, local, dp):
    tokens, depth = s.shape
    hid = d.shape[0]
    bc = min(256, hid)
    rest = max(tokens - local, 8)
    once = functools.partial(pl.BlockSpec, pipeline_mode=pl.Buffered(1))
    const = lambda i: (0, 0)
    return pl.pallas_call(
        ffn_kernel, grid=(hid // bc,),
        in_specs=[once((tokens, depth), const), once((tokens, depth), const),
                  pl.BlockSpec((depth, 2, bc), lambda i: (0, 0, i)), pl.BlockSpec((bc, depth), lambda i: (i, 0))],
        out_specs=[pl.BlockSpec((dp, depth // dp, bc), lambda i: (0, 0, i))] * 3 + [
                   once((local, depth), const), once((rest, depth), const), once((local, depth), const), once((rest, depth), const)],
        out_shape=[sds((dp, depth // dp, hid), BF16)] * 3 + [sds((local, depth)), sds((rest, depth), BF16), sds((local, depth)), sds((rest, depth), BF16)],
        scratch_shapes=[pltpu.VMEM((depth, tokens), BF16)] * 2 + [pltpu.VMEM((depth, bc), BF16)] * 2 + [pltpu.VMEM((tokens, depth), F32)] * 2,
        compiler_params=pltpu.CompilerParams(vmem_limit_bytes=62 << 20),
    )(s, b, w, d)


def time_embed(timesteps):
    half = TE // 2
    frequencies = jnp.exp(-math.log(10000.0) * jnp.arange(half, dtype=F32) / half)
    angles = timesteps.astype(F32)[:, None] * frequencies
    waves = jnp.concatenate([jnp.cos(angles), jnp.sin(angles)], axis=-1)
    return jax.nn.silu(waves).astype(BF16)


def rope_tables(positions, width):
    lane = jnp.arange(width)
    quarter = HD // 4
    frequencies = 10000.0 ** (-(lane % quarter).astype(F32) / quarter)
    place = jnp.where(lane % HD < HD // 2, positions[0][:, None], positions[1][:, None])
    angles = place.astype(F32) * frequencies
    return jnp.cos(angles), jnp.where(lane % 32 < 16, -1.0, 1.0) * jnp.sin(angles)


def inverse_rms(values):
    return lax.rsqrt(jnp.mean(values * values, axis=-1, keepdims=True) + EPSILON)


def rms_back(grad_hat, normed, inverse):
    return inverse * (grad_hat - normed * jnp.mean(grad_hat * normed, axis=-1, keepdims=True))


def pad_cols(value, width):
    extra = -value.shape[-1] % width
    return value if extra == 0 else jnp.pad(value, [(0, 0)] * (value.ndim - 1) + [(0, extra)])


def on_device(
    hidden_in, text_state, caption_lengths, timesteps, patch_positions, cotangent,
    w_ada, w_text, w_qkv, w_out, gains, cross_gate, w_gate_up, w_down,
):
    n, f = lax.axis_size("fsdp"), lax.axis_index("fsdp")
    dpn, me = lax.axis_size("dp"), lax.axis_index("dp")
    order_a, order_b, order_c = orders()
    own_d = D // n
    local = hidden_in.shape[1]
    width = 2 * HD
    share = D // dpn
    x_bf, dy_bf = hidden_in[0], cotangent[0]

    time_low = time_embed(timesteps)
    own_te = TE // n
    time_own = lax.dynamic_slice_in_dim(time_low[0], f * own_te, own_te, 0)
    modulation = pair_sum(
        jnp.einsum("k,kjd->jd", time_own, w_ada, preferred_element_type=F32)
    )
    scale_attn, gate_attn = modulation[0:1], jnp.tanh(modulation[1:2])
    scale_ffn, gate_ffn = modulation[2:3], jnp.tanh(modulation[3:4])

    x_all = jnp.concatenate(gather_rot(x_bf), axis=0)
    dy_all = jnp.concatenate(gather_rot(dy_bf), axis=0)
    places = jnp.concatenate(gather_rot(patch_positions[0]), axis=1)
    w_parts = exchange_rot(jnp.moveaxis(w_qkv, 1, 0).reshape(3, own_d, n, own_d), 2)
    w_heads = jnp.concatenate(w_parts, axis=1)
    text_cols = exchange(jnp.moveaxis(text_state[0].reshape(-1, n, TW // n), 1, 0))
    text_cols = jnp.concatenate(text_cols, axis=0)
    text_all = lax.all_gather(text_cols, "dp", axis=0, tiled=True)
    gain_full = lax.all_gather(gains, "fsdp", axis=1, tiled=True).astype(F32)
    gain_own = gains.astype(F32)
    times_all = timesteps
    for bit in range(dp_bits()):
        times_all = jnp.concatenate([times_all, dp_swap(times_all, bit)])

    x_f = x_all.astype(F32)
    inverse_all = inverse_rms(x_f)
    x_rot = jnp.concatenate(rot_blocks(x_all.reshape(-1, n, own_d), 1), axis=1).astype(F32)
    front = (gain_full[0] * (1.0 + scale_attn)).reshape(1, n, own_d)
    front = jnp.concatenate(rot_blocks(front, 1), axis=1)
    first_all = (x_rot * inverse_all * front).astype(BF16)
    q_pre, k_pre, v_pre = (dot(first_all, w_heads[j]) for j in range(3))
    squares = row_sum(jnp.stack([jnp.sum(q_pre * q_pre, -1), jnp.sum(k_pre * k_pre, -1)]))
    inverse = lax.rsqrt(squares / D + EPSILON)
    inv_q, inv_k = inverse[0][:, None], inverse[1][:, None]

    text_part = text_fwd(text_cols, w_text)
    text_pre = scatter_rot(rot_blocks(text_part.reshape(2, TEXT, n, own_d), 2))
    inv_t = lax.rsqrt(
        pair_sum(jnp.sum(text_pre[0] * text_pre[0], -1, keepdims=True)) / D + EPSILON
    )
    normed_t = text_pre[0] * inv_t
    tk = (normed_t * gain_own[4]).astype(BF16)
    tv = text_pre[1].astype(BF16)

    head_tanh = jnp.tanh(cross_gate.astype(F32))
    gate_row = pad_cols(jnp.repeat(head_tanh, HD)[None], width)
    cosine, sine = rope_tables(places, width)
    gq, gk = pad_cols(gain_own[2:3], width), pad_cols(gain_own[3:4], width)
    qp, kp, vp = (pad_cols(v, width) for v in (q_pre, k_pre, v_pre))
    tkp, tvp = pad_cols(tk, width), pad_cols(tv, width)
    q, k, v, mixed_p, so, co, ls, lc = attn_forward(
        caption_lengths, qp, kp, vp, inv_q, inv_k, gq, gk, cosine, sine, tkp, tvp, gate_row
    )
    mixed = mixed_p[:, :own_d]

    def rows(value, r):
        return value[r * local : (r + 1) * local]

    parts = [dot(rows(mixed, r), w_out) for r in range(n)]
    attn_branch = scatter_rot([parts[0]] + [p.astype(BF16) for p in parts[1:]])
    x_own = x_bf.astype(F32)
    after_attn = x_own + gate_attn * attn_branch
    inverse_two = inverse_rms(after_attn)
    normed_two = after_attn * inverse_two
    second = (normed_two * gain_full[1] * (1.0 + scale_ffn)).astype(BF16)

    second_all = jnp.concatenate(gather_rot(second), axis=0)
    branch_all = (gate_ffn * dy_all.astype(F32)).astype(BF16)
    d_gate, d_up, d_down, ffn_own, ffn_rest, back_own, back_rest = ffn(
        second_all, branch_all, w_gate_up, w_down, local, dpn
    )
    chains = [Halving(d_gate, order_a), Halving(d_up, order_b), Halving(d_down, order_c)]
    gate_chain, up_chain, down_chain = chains
    grad_second = scatter_rot([back_own] + [rows(back_rest, r) for r in range(n - 1)])
    ffn_branch = scatter_rot([ffn_own] + [rows(ffn_rest, r) for r in range(n - 1)])
    output = (after_attn + gate_ffn * ffn_branch).astype(BF16)
    dy = dy_bf.astype(F32)
    d_gate_ffn = jnp.sum(dy * ffn_branch, axis=0) * (1.0 - gate_ffn[0] * gate_ffn[0])

    scaled = grad_second * normed_two
    d_scale_ffn = jnp.sum(scaled * gain_full[1], axis=0)
    gain_two = jnp.sum(scaled * (1.0 + scale_ffn), axis=0)
    grad_after = dy + rms_back(
        grad_second * gain_full[1] * (1.0 + scale_ffn), normed_two, inverse_two
    )
    d_gate_attn = jnp.sum(grad_after * attn_branch, axis=0) * (1.0 - gate_attn[0] * gate_attn[0])
    grad_attn = (gate_attn * grad_after).astype(BF16)
    grad_attn_all = jnp.concatenate(gather_rot(grad_attn), axis=0)
    grad_mixed = dot(grad_attn_all, w_out, 1, 1)
    d_out = dot(grad_attn_all, mixed, 0, 0).astype(BF16)
    out_chain = Halving(d_out.reshape(dpn, share, own_d), order_c)
    chains.append(out_chain)
    dq, dk, dv, dtk, dtv, rq, rk, gain_q, gain_k, gate_g = attn_backward(
        caption_lengths, q, k, v, tkp, tvp, pad_cols(grad_mixed, width), so, co, ls, lc, qp, kp,
        inv_q, inv_k, gq, gk, cosine, sine, gate_row,
    )
    rq, rk, dtk = advance(chains, (rq, rk, dtk))
    dq, dk, dv, dtk, dtv = (v_[:, :own_d] for v_ in (dq, dk, dv, dtk, dtv))
    gate_total = jnp.sum(gate_g[0, :own_d].reshape(HEADS // n, HD), axis=1) * (
        1.0 - head_tanh * head_tanh
    )
    text_hat = dtk * gain_own[4]
    gain_text = jnp.sum(dtk * normed_t, axis=0, keepdims=True)
    means = row_sum(jnp.stack([jnp.sum(rq, -1), jnp.sum(rk, -1)])) / D
    mean_t = pair_sum(jnp.sum(text_hat * normed_t, -1, keepdims=True)) / D
    grad_q = (inv_q * (dq * gain_own[2] - q_pre * inv_q * means[0][:, None])).astype(BF16)
    grad_k = (inv_k * (dk * gain_own[3] - k_pre * inv_k * means[1][:, None])).astype(BF16)

    grads = (grad_q, grad_k, dv)
    wide = []
    for g in grads:
        blocks = [
            dot(g, first_all[:, r * own_d : (r + 1) * own_d], 0, 0).astype(BF16) for r in range(n)
        ]
        got = [blocks[0]]
        for r in range(1, n):
            got.append(lax.ppermute(blocks[r], "fsdp", [(i, (i - r) % n) for i in range(n)]))
        got = jnp.stack(got)
        if n != 2 or dpn == 1:
            got = jnp.stack(
                [lax.dynamic_index_in_dim(got, (g_ - f) % n, 0, keepdims=False) for g_ in range(n)]
            )
        wide.append(got.reshape(dpn, share, own_d))
    flip = f if n == 2 else 0
    qkv_chains = [
        Halving(w_, o, flip) for w_, o in zip(wide, (order_a, order_b, order_c))
    ]
    chains += qkv_chains

    grad_tk = (inv_t * (text_hat - normed_t * mean_t)).astype(BF16)
    text_pair = jnp.stack([grad_tk, dtv.astype(BF16)])
    pair_all = gather_natural(text_pair)
    text_in = text_bwd(pair_all, w_text)
    text_in = exchange(text_in.reshape(n, -1, TW // n))
    text_in = jnp.concatenate(text_in, axis=1)
    outgoing = pair_all.reshape(2, TEXT, dpn, share).transpose(2, 0, 1, 3)
    pair_cols = dp_exchange(outgoing, order_a)
    pair_cols = jnp.take(pair_cols, me ^ jnp.arange(dpn), axis=0)
    pair_cols = pair_cols.transpose(0, 2, 1, 3).reshape(dpn * TEXT, 2 * share)
    text_grad = dot(pair_cols, text_all, 0, 0).reshape(2, share, TW // n)

    parts = [
        sum(dot(rows(g, r), w_heads[j], 1, 1) for j, g in enumerate(grads)) for r in range(n)
    ]
    parts = [jnp.concatenate(rot_blocks(p.reshape(-1, n, own_d), 1), axis=1) for p in parts]
    grad_first = scatter_rot([parts[0]] + [p.astype(BF16) for p in parts[1:]])
    inverse_one = inverse_rms(x_own)
    normed_one = x_own * inverse_one
    scaled = grad_first * normed_one
    d_scale_attn = jnp.sum(scaled * gain_full[0], axis=0)
    gain_one = jnp.sum(scaled * (1.0 + scale_attn), axis=0)
    grad_input = (
        grad_after
        + rms_back(grad_first * gain_full[0] * (1.0 + scale_attn), normed_one, inverse_one)
    ).astype(BF16)

    mods = jnp.stack([d_scale_attn, d_gate_attn, d_scale_ffn, d_gate_ffn])
    mods = pair_sum(dp_exchange(mods.reshape(4, dpn, share).transpose(1, 0, 2), order_a))
    times = time_embed(times_all)
    times = lax.dynamic_slice_in_dim(times, f * own_te, own_te, 1).astype(F32)
    ada_grad = lax.dot_general(
        mods.reshape(dpn, 4 * share), times, (((0,), (0,)), ((), ())),
        precision=lax.Precision.HIGHEST,
    ).reshape(4, share, own_te)
    two = scatter_rot(rot_blocks(jnp.stack([gain_one, gain_two]).reshape(2, n, own_d), 1))
    gate_pad = jnp.pad(gate_total, (0, own_d - gate_total.shape[0]))[None]
    small = dp_total(
        jnp.concatenate([two, gain_q[:, :own_d], gain_k[:, :own_d], gain_text, gate_pad], axis=0)
    )
    while any(c.got is not None for c in chains):
        advance(chains, ())
    return (
        output[None],
        grad_input[None],
        text_in[None],
        ada_grad.transpose(2, 0, 1),
        text_grad.transpose(2, 0, 1),
        jnp.stack([c.cur for c in qkv_chains]).transpose(2, 0, 1),
        out_chain.cur.T,
        small[:5],
        small[5, : HEADS // n],
        jnp.stack([gate_chain.cur, up_chain.cur], axis=1),
        down_chain.cur.T,
    )


def solution(mesh):
    return jax.shard_map(
        on_device,
        mesh=mesh,
        in_specs=(
            P("dp", "fsdp", None),
            P("dp", "fsdp", None),
            P("dp"),
            P("dp"),
            P("dp", None, "fsdp"),
            P("dp", "fsdp", None),
            P("fsdp", None, None),
            P("fsdp", None, None),
            P("fsdp", None, None),
            P("fsdp", None),
            P(None, "fsdp"),
            P("fsdp"),
            P(None, None, "fsdp"),
            P("fsdp", None),
        ),
        out_specs=(
            P("dp", "fsdp", None),
            P("dp", "fsdp", None),
            P("dp", "fsdp", None),
            P("fsdp", None, "dp"),
            P("fsdp", None, "dp"),
            P("fsdp", None, "dp"),
            P("fsdp", "dp"),
            P(None, "fsdp"),
            P("fsdp"),
            P("dp", None, "fsdp"),
            P("fsdp", "dp"),
        ),
        check_vma=False,
    )
```

```python
import functools
import math

import jax
import jax.numpy as jnp
from jax import lax
from jax.experimental import pallas as pl
from jax.experimental.pallas import tpu as pltpu
from jax.sharding import PartitionSpec as P

D = 1536
HEADS = 24
HD = 64
TW = 4096
TE = 1024
PATCHES = 1024
TEXT = 256
EPSILON = 1e-06
F32 = jnp.float32
BF16 = jnp.bfloat16
QC = 256


def dot(a, b, ca=1, cb=0):
    return lax.dot_general(a, b, (((ca,), (cb,)), ((), ())), preferred_element_type=F32)


def from_behind(value, step):
    n = lax.axis_size("fsdp")
    return lax.ppermute(value, "fsdp", [(i, (i + step) % n) for i in range(n)])


def gather_rot(value):
    return [value] + [from_behind(value, r) for r in range(1, lax.axis_size("fsdp"))]


def pair_sum(value):
    return functools.reduce(lambda a, b: a + b, gather_rot(value))


def row_sum(value):
    n = lax.axis_size("fsdp")
    rows = value.shape[-1] // n
    total = value
    for r in range(1, n):
        total = total + jnp.roll(from_behind(value, r), r * rows, axis=-1)
    return total


def scatter_rot(blocks):
    n = lax.axis_size("fsdp")
    total = blocks[0].astype(F32)
    for r in range(1, n):
        got = lax.ppermute(blocks[r], "fsdp", [(i, (i - r) % n) for i in range(n)])
        total = total + got.astype(F32)
    return total


def block_of(value, index, axis):
    size = value.shape[axis] // lax.axis_size("fsdp")
    return lax.dynamic_slice_in_dim(value, index * size, size, axis)


def rot_blocks(value, axis):
    n, f = lax.axis_size("fsdp"), lax.axis_index("fsdp")
    return [block_of(value, (f - r) % n, axis) for r in range(n)]


def exchange_rot(value, axis):
    n, f = lax.axis_size("fsdp"), lax.axis_index("fsdp")
    out = [block_of(value, f, axis)]
    for r in range(1, n):
        out.append(from_behind(block_of(value, (f + r) % n, axis), r))
    return out


def natural(got):
    n, f = lax.axis_size("fsdp"), lax.axis_index("fsdp")
    if n == 2:
        return [jnp.where(f == 0, got[0], got[1]), jnp.where(f == 0, got[1], got[0])]
    got = jnp.stack(got)
    return [lax.dynamic_index_in_dim(got, (f - g) % n, 0, keepdims=False) for g in range(n)]


def dp_bits():
    return int(lax.axis_size("dp")).bit_length() - 1


def dp_swap(value, bit):
    n = lax.axis_size("dp")
    return lax.ppermute(value, "dp", [(i, i ^ (1 << bit)) for i in range(n)])


def orders(bits):
    return bits, bits[:2][::-1] + bits[2:], bits[2:3] + bits[:2][::-1] + bits[3:]


def relative(value):
    return jnp.take(value, lax.axis_index("dp") ^ jnp.arange(lax.axis_size("dp")), axis=0)


class Halving:
    def __init__(self, bits, order, whole=None, pair=None):
        self.labels, self.order = list(bits)[::-1], list(order)
        self.keep = self.got = None
        if pair is None:
            self.cur = whole
            self.start()
        else:
            bit = self.order.pop(0)
            self.labels.remove(bit)
            self.keep, self.got = pair[0], dp_swap(pair[1], bit)

    def start(self):
        if not self.order:
            return
        bit = self.order.pop(0)
        axis = self.labels.index(bit)
        cur = self.cur.reshape((2,) * len(self.labels) + self.cur.shape[1:])
        self.labels.remove(bit)
        self.keep, send = (
            lax.index_in_dim(cur, i, axis, keepdims=False).reshape((-1,) + self.cur.shape[1:])
            for i in range(2)
        )
        self.got = dp_swap(send, bit)

    def step(self):
        if self.got is None:
            return
        total = self.keep.astype(F32) + self.got.astype(F32)
        self.cur = total.astype(BF16)
        self.last = total
        self.got = None
        self.start()


def advance(chains, value):
    live = [c for c in chains if c.got is not None]
    value, got = lax.optimization_barrier((value, [c.got for c in live]))
    for c, g in zip(live, got):
        c.got = g
        c.step()
    return value


def dp_exchange(value, order):
    nb = dp_bits()
    cur = value.reshape((2,) * nb + value.shape[1:])
    for bit in order:
        axis = nb - 1 - bit
        keep, send = (lax.index_in_dim(cur, i, axis, keepdims=False) for i in range(2))
        cur = jnp.stack([keep, dp_swap(send, bit)], axis=axis)
    return cur.reshape(value.shape)


def dp_total(value):
    for bit in range(dp_bits()):
        value = value + dp_swap(value, bit)
    return value


def rope_block(value, cosine, sine, sign):
    width = value.shape[1]
    lane = lax.broadcasted_iota(jnp.int32, value.shape, 1)
    partner = jnp.where(
        lane % 32 < 16, pltpu.roll(value, width - 16, 1), pltpu.roll(value, 16, 1)
    )
    return value * cosine + sign * (partner * sine)


def column(ref, index, width):
    row = ref[index : index + 1, :] if isinstance(index, int) else ref[pl.ds(index, 1), :]
    return jnp.broadcast_to(row, (width, row.shape[1])).T


def masked(value, head):
    lane = lax.broadcasted_iota(jnp.int32, value.shape, 1)
    return jnp.where(lane // HD == head, value, jnp.zeros_like(value))


def attn_fwd_kernel(
    len_ref, pre_ref, inv_ref, gq_ref, gk_ref, cos_ref, sin_ref, tk_ref, tv_ref, gate_ref,
    q_ref, k_ref, v_ref, mixed_ref, so_ref, co_ref, ls_ref, lc_ref,
):
    _, tokens, width = pre_ref.shape
    heads = width // HD
    iq, ik = column(inv_ref, 0, width), column(inv_ref, 1, width)
    q = rope_block(pre_ref[0] * iq * gq_ref[...], cos_ref[...], sin_ref[...], 1.0)
    q_ref[...] = q.astype(BF16)
    k = rope_block(pre_ref[1] * ik * gk_ref[...], cos_ref[...], sin_ref[...], 1.0)
    k_ref[...] = k.astype(BF16)
    v_ref[...] = pre_ref[2].astype(BF16)
    length = len_ref[0]

    def one(keys, values, qm, limit):
        s = dot(qm, keys, 1, 1)
        if limit is not None:
            slot = lax.broadcasted_iota(jnp.int32, s.shape, 1)
            s = jnp.where(slot < limit, s, -1e30)
        peak = jnp.max(s, axis=1, keepdims=True)
        e = jnp.exp(s - peak)
        total = jnp.sum(e, axis=1, keepdims=True)
        o = dot(e.astype(BF16), values)
        return o * (1.0 / total), peak + jnp.log(total)

    lane = lax.broadcasted_iota(jnp.int32, (tokens, width), 1)
    qs = q_ref[...] * jnp.asarray(HD**-0.5, BF16)
    so = co = stats = jnp.zeros((tokens, width), F32)
    for h in range(heads):
        qm = masked(qs, h)
        o, lse = one(k_ref[...], v_ref[...], qm, None)
        so = jnp.where(lane // HD == h, o, so)
        stats = jnp.where(lane == h, lse, stats)
        o, lse = one(tk_ref[...], tv_ref[...], qm, length)
        co = jnp.where(lane // HD == h, o, co)
        stats = jnp.where(lane == heads + h, lse, stats)
    so_ref[...] = so
    co_ref[...] = co
    mixed_ref[...] = (so + gate_ref[...] * co).astype(BF16)
    stats = stats.T
    ls_ref[0] = stats[:heads]
    lc_ref[0] = stats[heads : 2 * heads]


def attn_bwd_kernel(
    len_ref, q_ref, k_ref, v_ref, tk_ref, tv_ref, g_ref, so_ref, co_ref, ls_ref, lc_ref,
    pre_ref, inv_ref, gq_ref, gk_ref, cos_ref, sin_ref, gate_ref,
    d_ref, dtk_ref, dtv_ref, rq_ref, rk_ref, gainq_ref, gaink_ref, gateg_ref,
    gs_ref, gc_ref, ds_ref, dc_ref, kt_ref, tkt_ref, dqt_ref, dk_acc, dv_acc,
):
    tokens, width = q_ref.shape
    heads = width // HD
    scale = jnp.asarray(HD**-0.5, BF16)

    @pl.when(pl.program_id(0) == 0)
    def _():
        rq_ref[...] = jnp.zeros_like(rq_ref)
        rk_ref[...] = jnp.zeros_like(rk_ref)

    g = g_ref[...]
    gs_ref[...] = g.astype(BF16)
    gc_ref[...] = (g * gate_ref[...]).astype(BF16)
    prod_c = g * co_ref[...]
    gateg_ref[...] = jnp.sum(prod_c, axis=0, keepdims=True)
    prod_s = (g * so_ref[...]).T
    prod_c = (prod_c * gate_ref[...]).T
    for h in range(heads):
        ds_ref[h : h + 1, :] = jnp.sum(prod_s[h * HD : (h + 1) * HD], axis=0, keepdims=True)
        dc_ref[h : h + 1, :] = jnp.sum(prod_c[h * HD : (h + 1) * HD], axis=0, keepdims=True)
    kt_ref[...] = k_ref[...].astype(F32).T.astype(BF16)
    tkt_ref[...] = tk_ref[...].astype(F32).T.astype(BF16)
    dk_acc[...] = jnp.zeros_like(dk_acc)
    dv_acc[...] = jnp.zeros_like(dv_acc)
    dtk_ref[...] = jnp.zeros_like(dtk_ref)
    dtv_ref[...] = jnp.zeros_like(dtv_ref)
    length = len_ref[0]

    def one(keys, keys_t, values, qm, gm, lse, delta, head, limit):
        s = dot(keys, qm, 1, 1)
        p = jnp.exp(s - lse)
        if limit is not None:
            slot = lax.broadcasted_iota(jnp.int32, s.shape, 0)
            p = jnp.where(slot < limit, p, 0.0)
        dp = dot(values, gm, 1, 1)
        ds = (p * (dp - delta)).astype(BF16)
        dq = dot(keys_t[head * HD : (head + 1) * HD, :], ds)
        return dq, dot(ds, qm), dot(p.astype(BF16), gm)

    def chunk(c, carry):
        rows = pl.ds(pl.multiple_of(c * QC, QC), QC)
        qc = q_ref[rows, :] * scale
        for h in range(heads):
            qm = masked(qc, h)
            dq, dk, dv = one(
                k_ref[...], kt_ref, v_ref[...], qm, masked(gs_ref[rows, :], h),
                ls_ref[0, h : h + 1, rows], ds_ref[h : h + 1, rows], h, None,
            )
            dk_acc[...] += dk
            dv_acc[...] += dv
            dq2, dk, dv = one(
                tk_ref[...], tkt_ref, tv_ref[...], qm, masked(gc_ref[rows, :], h),
                lc_ref[0, h : h + 1, rows], dc_ref[h : h + 1, rows], h, length,
            )
            dtk_ref[...] += dk
            dtv_ref[...] += dv
            dqt_ref[h * HD : (h + 1) * HD, rows] = (dq + dq2) * HD**-0.5
        return carry

    lax.fori_loop(0, tokens // QC, chunk, 0)
    dq = rope_block(dqt_ref[...].T, cos_ref[...], sin_ref[...], -1.0)
    d_ref[0] = dq
    prod = dq * (pre_ref[0] * column(inv_ref, 0, width))
    gainq_ref[...] = jnp.sum(prod, axis=0, keepdims=True)
    rq_ref[...] += prod * gq_ref[...]
    dk = rope_block(dk_acc[...], cos_ref[...], sin_ref[...], -1.0)
    d_ref[1] = dk
    prod = dk * (pre_ref[1] * column(inv_ref, 1, width))
    gaink_ref[...] = jnp.sum(prod, axis=0, keepdims=True)
    rk_ref[...] += prod * gk_ref[...]
    d_ref[2] = dv_acc[...]


def specs(tokens, text, width, heads):
    col = pl.BlockSpec((tokens, width), lambda i: (0, i))
    three = pl.BlockSpec((3, tokens, width), lambda i: (0, 0, i))
    tcol = pl.BlockSpec((text, width), lambda i: (0, i))
    stat = pl.BlockSpec((8, tokens), lambda i: (0, 0))
    gain = pl.BlockSpec((1, width), lambda i: (0, i))
    table = pl.BlockSpec((tokens, width), lambda i: (0, 0))
    lse = pl.BlockSpec((1, heads, tokens), lambda i: (i, 0, 0))
    scalar = pl.BlockSpec(memory_space=pltpu.SMEM)
    return col, three, tcol, stat, gain, table, lse, scalar


def sds(shape, dtype=F32):
    return jax.ShapeDtypeStruct(shape, dtype)


def attn_forward(length, pre, inv, gq, gk, cosine, sine, tk, tv, gate):
    _, tokens, columns = pre.shape
    text, width = tk.shape[0], cosine.shape[1]
    heads, blocks = width // HD, columns // width
    col, three, tcol, stat, gain, table, lse, scalar = specs(tokens, text, width, heads)
    flat = (tokens, columns)
    return pl.pallas_call(
        attn_fwd_kernel,
        grid=(blocks,),
        in_specs=[scalar, three, stat, gain, gain, table, table, tcol, tcol, gain],
        out_specs=[col, col, col, col, col, col, lse, lse],
        out_shape=[sds(flat, BF16)] * 4 + [sds(flat)] * 2 + [sds((blocks, heads, tokens))] * 2,
    )(length, pre, inv, gq, gk, cosine, sine, tk, tv, gate)


def attn_backward(length, q, k, v, tk, tv, g, so, co, ls, lc, pre, inv, gq, gk, cosine, sine, gate):
    tokens, columns = q.shape
    text, width = tk.shape[0], cosine.shape[1]
    heads, blocks = width // HD, columns // width
    col, three, tcol, stat, gain, table, lse, scalar = specs(tokens, text, width, heads)
    return pl.pallas_call(
        attn_bwd_kernel,
        grid=(blocks,),
        in_specs=[scalar, col, col, col, tcol, tcol, col, col, col, lse, lse,
                  three, stat, gain, gain, table, table, gain],
        out_specs=[three, tcol, tcol, table, table, gain, gain, gain],
        out_shape=[
            sds(pre.shape), sds(tk.shape), sds(tk.shape),
            sds((tokens, width)), sds((tokens, width)),
            sds((1, columns)), sds((1, columns)), sds((1, columns)),
        ],
        scratch_shapes=[
            pltpu.VMEM((tokens, width), BF16), pltpu.VMEM((tokens, width), BF16),
            pltpu.VMEM((heads, tokens), F32), pltpu.VMEM((heads, tokens), F32),
            pltpu.VMEM((width, tokens), BF16), pltpu.VMEM((width, text), BF16),
            pltpu.VMEM((width, tokens), F32),
            pltpu.VMEM((tokens, width), F32), pltpu.VMEM((tokens, width), F32),
        ],
    )(length, q, k, v, tk, tv, g, so, co, ls, lc, pre, inv, gq, gk, cosine, sine, gate)


def pick(rows, cols, step, part):
    i = lax.broadcasted_iota(jnp.int32, (rows, cols), 0)
    j = lax.broadcasted_iota(jnp.int32, (rows, cols), 1)
    hit = (j == step * i + part) if cols > rows else (i == step * j + part)
    return jnp.where(hit, 1.0, 0.0).astype(BF16)

def text_fwd_kernel(x_ref, w_ref, o_ref):
    @pl.when(pl.program_id(0) == 0)
    def _():
        o_ref[...] = jnp.zeros_like(o_ref)
    for b in range(w_ref.shape[0] // 128):
        rows = slice(b * 128, (b + 1) * 128)
        w = w_ref[rows].reshape(256, w_ref.shape[2])
        x = x_ref[:, rows]
        for j in range(2):
            spread = dot(x, pick(128, 256, 2, j)).astype(BF16)
            o_ref[j] += dot(spread, w)

def text_fwd(x, w):
    depth, _, cols = w.shape
    bk = 256
    return pl.pallas_call(
        text_fwd_kernel, grid=(depth // bk,),
        in_specs=[pl.BlockSpec((x.shape[0], bk), lambda i: (0, i)), pl.BlockSpec((bk, 2, cols), lambda i: (i, 0, 0))],
        out_specs=pl.BlockSpec((2, x.shape[0], cols), lambda i: (0, 0, 0)),
        out_shape=sds((2, x.shape[0], cols)),
    )(x, w)

def text_bwd_kernel(g_ref, w_ref, o_ref):
    for b in range(w_ref.shape[0] // 128):
        rows = slice(b * 128, (b + 1) * 128)
        w = w_ref[rows].reshape(256, w_ref.shape[2])
        total = 0.0
        for j in range(2):
            total = total + dot(g_ref[j], dot(pick(128, 256, 2, j), w).astype(BF16), 1, 1)
        o_ref[:, rows] = total.astype(BF16)

def text_bwd(g, w):
    depth, _, cols = w.shape
    bk = 256
    return pl.pallas_call(
        text_bwd_kernel, grid=(depth // bk,),
        in_specs=[pl.BlockSpec(g.shape, lambda i: (0, 0, 0)), pl.BlockSpec((bk, 2, cols), lambda i: (i, 0, 0))],
        out_specs=pl.BlockSpec((g.shape[1], bk), lambda i: (0, i)),
        out_shape=sds((g.shape[1], depth), BF16),
    )(g, w)

def put_relative(dst, src, me, count):
    rows = dst.shape[0] // count
    for p in range(count):
        start = pl.multiple_of((me ^ p) * rows, 16)
        dst[p * rows : (p + 1) * rows, :] = src[pl.ds(start, rows), :]


def put_halves(keep, send, value, count, bit):
    rows = value.shape[0] // count
    low = (1 << bit) - 1
    for p in range(count):
        place = (p & low) | (p >> (bit + 1) << bit)
        (send if p >> bit & 1 else keep)[place] = value[p * rows : (p + 1) * rows]


def ffn_kernel(
    bits, id_ref, s_ref, b_ref, w_ref, d_ref,
    gk_ref, gs_ref, uk_ref, us_ref, dk_ref, ds_ref, fo_ref, fp_ref, so_ref, sp_ref,
    st, bt, tmp, wg, wu, facc, sacc,
):
    step = pl.program_id(0)
    depth, _, cols = w_ref.shape
    own = fo_ref.shape[0]
    count = 2 * gk_ref.shape[0]

    @pl.when(step == 0)
    def _():
        for src, dst in ((s_ref, st), (b_ref, bt)):
            for c in range(depth // 256):
                part = slice(c * 256, (c + 1) * 256)
                tmp[part, :] = src[:, part].astype(F32).T.astype(BF16)
            put_relative(dst, tmp, id_ref[0], count)
        facc[...] = jnp.zeros_like(facc)
        sacc[...] = jnp.zeros_like(sacc)

    for c in range(depth // 128):
        part = slice(c * 128, (c + 1) * 128)
        w = w_ref[part].reshape(256, cols)
        wg[part, :] = dot(pick(128, 256, 2, 0), w).astype(BF16)
        wu[part, :] = dot(pick(128, 256, 2, 1), w).astype(BF16)
    s, b = s_ref[...], b_ref[...]
    gate = dot(s, wg[...])
    up = dot(s, wu[...])
    back = dot(b, d_ref[...], 1, 1)
    sig = jax.nn.sigmoid(gate)
    silu = gate * sig
    hidden = (silu * up).astype(BF16)
    g_gate = (back * up * (sig + silu * (1.0 - sig))).astype(BF16)
    g_up = (back * silu).astype(BF16)
    put_halves(gk_ref, gs_ref, dot(st[...], g_gate).astype(BF16), count, bits[0])
    put_halves(uk_ref, us_ref, dot(st[...], g_up).astype(BF16), count, bits[1])
    put_halves(dk_ref, ds_ref, dot(bt[...], hidden).astype(BF16), count, bits[2])
    facc[...] += dot(hidden, d_ref[...])
    sacc[...] += dot(g_gate, wg[...], 1, 1) + dot(g_up, wu[...], 1, 1)

    @pl.when(step == pl.num_programs(0) - 1)
    def _():
        fo_ref[...] = facc[:own]
        fp_ref[...] = facc[own:].astype(BF16)
        so_ref[...] = sacc[:own]
        sp_ref[...] = sacc[own:].astype(BF16)


def ffn(ids, s, b, w, d, local, dp, bits):
    tokens, depth = s.shape
    hid = d.shape[0]
    bc = min(256, hid)
    rest = tokens - local
    once = functools.partial(pl.BlockSpec, pipeline_mode=pl.Buffered(1))
    const = lambda i: (0, 0)
    half = pl.BlockSpec((dp // 2, depth // dp, bc), lambda i: (0, 0, i))
    return pl.pallas_call(
        functools.partial(ffn_kernel, bits),
        grid=(hid // bc,),
        in_specs=[
            pl.BlockSpec(memory_space=pltpu.SMEM),
            once((tokens, depth), const), once((tokens, depth), const),
            pl.BlockSpec((depth, 2, bc), lambda i: (0, 0, i)),
            pl.BlockSpec((bc, depth), lambda i: (i, 0)),
        ],
        out_specs=[half] * 6 + [
            once((local, depth), const), once((rest, depth), const),
            once((local, depth), const), once((rest, depth), const),
        ],
        out_shape=[sds((dp // 2, depth // dp, hid), BF16)] * 6 + [
            sds((local, depth)), sds((rest, depth), BF16),
            sds((local, depth)), sds((rest, depth), BF16),
        ],
        scratch_shapes=[
            pltpu.VMEM((depth, tokens), BF16), pltpu.VMEM((depth, tokens), BF16),
            pltpu.VMEM((depth, tokens), BF16),
            pltpu.VMEM((depth, bc), BF16), pltpu.VMEM((depth, bc), BF16),
            pltpu.VMEM((tokens, depth), F32), pltpu.VMEM((tokens, depth), F32),
        ],
        compiler_params=pltpu.CompilerParams(vmem_limit_bytes=62 << 20),
    )(ids, s, b, w, d)


def project_kernel(id_ref, xo_ref, xp_ref, front_ref, w_ref, got_ref, first_ref, pre_ref, sq_ref):
    j = pl.program_id(0)
    local, depth = xo_ref.shape
    own = got_ref.shape[2]
    f = id_ref[1]

    @pl.when(j == 0)
    def _():
        for i, ref in enumerate((xo_ref, xp_ref)):
            x = ref[...].astype(F32)
            inv = lax.rsqrt(jnp.sum(x * x, axis=1, keepdims=True) * (1.0 / depth) + EPSILON)
            first_ref[i * local : (i + 1) * local, :] = (x * inv * front_ref[...]).astype(BF16)
        sq_ref[...] = jnp.zeros_like(sq_ref)

    mine = pl.ds(pl.multiple_of(f * own, 128), own)
    other = pl.ds(pl.multiple_of((1 - f) * own, 128), own)
    out = dot(first_ref[:, mine], w_ref[0, :, mine]) + dot(first_ref[:, other], got_ref[0])
    pre_ref[0] = out
    square = out * out
    part = square[:, :128]
    for c in range(1, own // 128):
        part = part + square[:, c * 128 : (c + 1) * 128]
    sq_ref[pl.ds(j, 1), :] = jnp.sum(part.T, axis=0, keepdims=True)


def project(ids, xo, xp, front, w, got):
    local, depth = xo.shape
    own = got.shape[2]
    tokens = 2 * local
    const = lambda j: (0, 0)
    return pl.pallas_call(
        project_kernel,
        grid=(3,),
        in_specs=[
            pl.BlockSpec(memory_space=pltpu.SMEM),
            pl.BlockSpec((local, depth), const), pl.BlockSpec((local, depth), const),
            pl.BlockSpec((1, depth), const),
            pl.BlockSpec((1, own, depth), lambda j: (j, 0, 0)),
            pl.BlockSpec((1, own, own), lambda j: (j, 0, 0)),
        ],
        out_specs=[
            pl.BlockSpec((tokens, depth), const),
            pl.BlockSpec((1, tokens, own), lambda j: (j, 0, 0)),
            pl.BlockSpec((8, tokens), const),
        ],
        out_shape=[sds((tokens, depth), BF16), sds((3, tokens, own)), sds((8, tokens))],
    )(ids, xo, xp, front, w, got)


def project_back_kernel(
    bits, id_ref, d_ref, pre_ref, stat_ref, gain_ref, first_ref, w_ref, got_ref,
    qk_ref, qs_ref, kk_ref, ks_ref, vk_ref, vs_ref, own_ref, peer_ref, gt, tmp, acc,
):
    j = pl.program_id(0)
    tokens, own = d_ref.shape[1:]
    local = own_ref.shape[0]
    f = id_ref[1]
    count = 2 * qk_ref.shape[0]
    inv, mean = column(stat_ref, j, 128), column(stat_ref, j + 3, 128)
    grads = []
    for c in range(own // 128):
        part = slice(c * 128, (c + 1) * 128)
        g = inv * (d_ref[0, :, part] * gain_ref[0, :, part] - pre_ref[0, :, part] * inv * mean)
        tmp[part, :] = g.T.astype(BF16)
        grads.append(g.astype(BF16))
    g = jnp.concatenate(grads, axis=1)
    put_relative(gt, tmp, id_ref[0] % count, count)

    mine = pl.ds(pl.multiple_of(f * own, 128), own)
    other = pl.ds(pl.multiple_of((1 - f) * own, 128), own)
    wide = dot(gt[...], first_ref[...]).astype(BF16)
    refs = ((qk_ref, qs_ref), (kk_ref, ks_ref), (vk_ref, vs_ref))
    for i, (keep, send) in enumerate(refs):

        @pl.when(j == i)
        def _(i=i, keep=keep, send=send):
            put_halves(keep, send, wide, count, bits[i])

    @pl.when(j == 0)
    def _():
        acc[...] = jnp.zeros_like(acc)

    acc[:, mine] += dot(g, w_ref[0, :, mine], 1, 1)
    acc[:, other] += dot(g, got_ref[0], 1, 1)

    @pl.when(j == 2)
    def _():
        own_ref[...] = acc[:local]
        peer_ref[...] = acc[local:].astype(BF16)


def project_back(ids, d, pre, stats, gain, first, w, got, dp, bits):
    _, tokens, own = d.shape
    depth = first.shape[1]
    local = tokens // 2
    share = depth // dp
    const = lambda j: (0, 0)
    block = lambda j: (j, 0, 0)
    half = pl.BlockSpec((dp // 4, share, depth), lambda j: (0, 0, 0), pipeline_mode=pl.Buffered(1))
    return pl.pallas_call(
        functools.partial(project_back_kernel, bits),
        grid=(3,),
        in_specs=[
            pl.BlockSpec(memory_space=pltpu.SMEM),
            pl.BlockSpec((1, tokens, own), block), pl.BlockSpec((1, tokens, own), block),
            pl.BlockSpec((8, tokens), const),
            pl.BlockSpec((1, 1, own), block),
            pl.BlockSpec((tokens, depth), const, pipeline_mode=pl.Buffered(1)),
            pl.BlockSpec((1, own, depth), block), pl.BlockSpec((1, own, own), block),
        ],
        out_specs=[half] * 6 + [
            pl.BlockSpec((local, depth), const, pipeline_mode=pl.Buffered(1)),
            pl.BlockSpec((local, depth), const, pipeline_mode=pl.Buffered(1)),
        ],
        out_shape=[sds((dp // 4, share, depth), BF16)] * 6 + [
            sds((local, depth)), sds((local, depth), BF16),
        ],
        scratch_shapes=[
            pltpu.VMEM((own, tokens), BF16), pltpu.VMEM((own, tokens), BF16),
            pltpu.VMEM((tokens, depth), F32),
        ],
        compiler_params=pltpu.CompilerParams(vmem_limit_bytes=62 << 20),
    )(ids, d, pre, stats, gain, first, w, got)


def time_embed(timesteps):
    half = TE // 2
    frequencies = jnp.exp(-math.log(10000.0) * jnp.arange(half, dtype=F32) / half)
    angles = timesteps.astype(F32)[:, None] * frequencies
    waves = jnp.concatenate([jnp.cos(angles), jnp.sin(angles)], axis=-1)
    return jax.nn.silu(waves).astype(BF16)


def rope_tables(positions, width):
    lane = jnp.arange(width)
    quarter = HD // 4
    frequencies = 10000.0 ** (-(lane % quarter).astype(F32) / quarter)
    place = jnp.where(lane % HD < HD // 2, positions[0][:, None], positions[1][:, None])
    angles = place.astype(F32) * frequencies
    return jnp.cos(angles), jnp.where(lane % 32 < 16, -1.0, 1.0) * jnp.sin(angles)


def inverse_rms(values):
    return lax.rsqrt(jnp.mean(values * values, axis=-1, keepdims=True) + EPSILON)


def rms_back(grad_hat, normed, inverse):
    return inverse * (grad_hat - normed * jnp.mean(grad_hat * normed, axis=-1, keepdims=True))


def pad_cols(value, width):
    extra = -value.shape[-1] % width
    return value if extra == 0 else jnp.pad(value, [(0, 0)] * (value.ndim - 1) + [(0, extra)])


def on_device(
    hidden_in, text_state, caption_lengths, timesteps, patch_positions, cotangent,
    w_ada, w_text, w_qkv, w_out, gains, cross_gate, w_gate_up, w_down,
):
    n, f = lax.axis_size("fsdp"), lax.axis_index("fsdp")
    dpn, me = lax.axis_size("dp"), lax.axis_index("dp")
    bits = list(range(dp_bits()))
    order_a, order_b, order_c = orders(bits)
    low_bits = bits[:-1]
    own_d = D // n
    local = hidden_in.shape[1]
    tokens = n * local
    width = 2 * HD
    share = D // dpn
    paired = n == 2 and dpn >= 4
    ids = jnp.stack([me, f]).astype(jnp.int32)
    x_bf, dy_bf = hidden_in[0], cotangent[0]

    time_low = time_embed(timesteps)
    own_te = TE // n
    time_own = lax.dynamic_slice_in_dim(time_low[0], f * own_te, own_te, 0)
    modulation = pair_sum(
        jnp.einsum("k,kjd->jd", time_own, w_ada, preferred_element_type=F32)
    )
    scale_attn, gate_attn = modulation[0:1], jnp.tanh(modulation[1:2])
    scale_ffn, gate_ffn = modulation[2:3], jnp.tanh(modulation[3:4])

    w_flat = jnp.moveaxis(w_qkv, 1, 0)
    w_parts = exchange_rot(w_flat, 2)
    x_parts = gather_rot(x_bf)
    dy_all = jnp.concatenate(gather_rot(dy_bf), axis=0)
    places = jnp.concatenate(gather_rot(patch_positions[0]), axis=1)
    text_cols = jnp.concatenate(natural(exchange_rot(text_state[0], 1)), axis=0)
    text_all = lax.all_gather(text_cols, "dp", axis=0, tiled=True)
    gain_full = lax.all_gather(gains, "fsdp", axis=1, tiled=True).astype(F32)
    gain_own = gains.astype(F32)

    front = gain_full[0] * (1.0 + scale_attn)
    if paired:
        first_all, pre, squares = project(ids, *x_parts, front, w_flat, w_parts[1])
    else:
        w_heads = jnp.concatenate(natural(w_parts), axis=1)
        x_f = jnp.concatenate(x_parts, axis=0).astype(F32)
        first_all = (x_f * inverse_rms(x_f) * front).astype(BF16)
        pre = jnp.stack([dot(first_all, w_heads[j]) for j in range(3)])
        squares = jnp.pad(jnp.sum(pre[:2] * pre[:2], -1), ((0, 6), (0, 0)))
    inverse = lax.rsqrt(row_sum(squares) / D + EPSILON)

    text_part = text_fwd(text_cols, w_text)
    text_pre = scatter_rot(rot_blocks(text_part, 2))
    inv_t = lax.rsqrt(
        pair_sum(jnp.sum(text_pre[0] * text_pre[0], -1, keepdims=True)) / D + EPSILON
    )
    normed_t = text_pre[0] * inv_t
    tk = (normed_t * gain_own[4]).astype(BF16)
    tv = text_pre[1].astype(BF16)

    head_tanh = jnp.tanh(cross_gate.astype(F32))
    gate_row = pad_cols(jnp.repeat(head_tanh, HD)[None], width)
    cosine, sine = rope_tables(places, width)
    gq, gk = pad_cols(gain_own[2:3], width), pad_cols(gain_own[3:4], width)
    pre_p, tkp, tvp = pad_cols(pre, width), pad_cols(tk, width), pad_cols(tv, width)
    q, k, v, mixed_p, so, co, ls, lc = attn_forward(
        caption_lengths, pre_p, inverse, gq, gk, cosine, sine, tkp, tvp, gate_row
    )
    mixed = mixed_p[:, :own_d]

    def rows(value, r):
        return value[r * local : (r + 1) * local]

    parts = [dot(rows(mixed, r), w_out) for r in range(n)]
    attn_branch = scatter_rot([parts[0]] + [p.astype(BF16) for p in parts[1:]])
    x_own = x_bf.astype(F32)
    after_attn = x_own + gate_attn * attn_branch
    inverse_two = inverse_rms(after_attn)
    normed_two = after_attn * inverse_two
    second = (normed_two * gain_full[1] * (1.0 + scale_ffn)).astype(BF16)

    second_all = jnp.concatenate(gather_rot(second), axis=0)
    branch_all = (gate_ffn * dy_all.astype(F32)).astype(BF16)
    firsts = (order_a[0], order_b[0], order_c[0]) if bits else (0, 0, 0)
    *halves, ffn_own, ffn_rest, back_own, back_rest = ffn(
        ids, second_all, branch_all, w_gate_up, w_down, local, dpn, firsts
    )
    (ffn_own, ffn_rest, back_own, back_rest), text_all = lax.optimization_barrier(
        ((ffn_own, ffn_rest, back_own, back_rest), text_all)
    )
    chains = [
        Halving(bits, o, pair=halves[2 * i : 2 * i + 2])
        for i, o in enumerate((order_a, order_b, order_c))
    ]
    ffn_chains = list(chains)
    grad_second = scatter_rot([back_own] + [rows(back_rest, r) for r in range(n - 1)])
    ffn_branch = scatter_rot([ffn_own] + [rows(ffn_rest, r) for r in range(n - 1)])
    output = (after_attn + gate_ffn * ffn_branch).astype(BF16)
    dy = dy_bf.astype(F32)
    d_gate_ffn = jnp.sum(dy * ffn_branch, axis=0) * (1.0 - gate_ffn[0] * gate_ffn[0])

    scaled = grad_second * normed_two
    d_scale_ffn = jnp.sum(scaled * gain_full[1], axis=0)
    gain_two = jnp.sum(scaled * (1.0 + scale_ffn), axis=0)
    grad_after = dy + rms_back(
        grad_second * gain_full[1] * (1.0 + scale_ffn), normed_two, inverse_two
    )
    d_gate_attn = jnp.sum(grad_after * attn_branch, axis=0) * (1.0 - gate_attn[0] * gate_attn[0])
    grad_attn = (gate_attn * grad_after).astype(BF16)
    grad_attn_all = jnp.concatenate(gather_rot(grad_attn), axis=0)
    grad_mixed = dot(grad_attn_all, w_out, 1, 1)
    d, dtk, dtv, rq, rk, gain_q, gain_k, gate_g = attn_backward(
        caption_lengths, q, k, v, tkp, tvp, pad_cols(grad_mixed, width), so, co, ls, lc, pre_p,
        inverse, gq, gk, cosine, sine, gate_row,
    )
    rq, rk, dtk = advance(chains, (rq, rk, dtk))
    d_out = dot(grad_attn_all, mixed, 0, 0).astype(BF16)
    out_chain = Halving(bits, order_c, whole=relative(d_out.reshape(dpn, share, own_d)))
    d, dtk, dtv = d[:, :, :own_d], dtk[:, :own_d], dtv[:, :own_d]
    gate_total = jnp.sum(gate_g[0, :own_d].reshape(HEADS // n, HD), axis=1) * (
        1.0 - head_tanh * head_tanh
    )
    text_hat = dtk * gain_own[4]
    gain_text = jnp.sum(dtk * normed_t, axis=0, keepdims=True)
    means = row_sum(jnp.stack([jnp.sum(rq, -1), jnp.sum(rk, -1)])) / D
    mean_t = pair_sum(jnp.sum(text_hat * normed_t, -1, keepdims=True)) / D

    grad_tk = (inv_t * (text_hat - normed_t * mean_t)).astype(BF16)
    text_pair = jnp.stack([grad_tk, dtv.astype(BF16)])
    pair_all = jnp.concatenate(natural(gather_rot(text_pair)), axis=-1)
    outgoing = block_of(pair_all, f, 1).reshape(2, TEXT // n, dpn, share).transpose(2, 0, 1, 3)
    pair_cols = dp_exchange(relative(outgoing), order_a)

    ones, zeros = jnp.ones((1, tokens), F32), jnp.zeros((1, tokens), F32)
    if paired:
        stats = jnp.concatenate([inverse[:2], ones, means, zeros, zeros, zeros], axis=0)
        gain3 = jnp.stack([gain_own[2:3], gain_own[3:4], jnp.ones_like(gain_own[2:3])])
        low_orders = orders(low_bits)
        *halves, own_part, peer_part = project_back(
            ids, d, pre, stats, gain3, first_all, w_flat, w_parts[1], dpn,
            tuple(o[0] for o in low_orders),
        )
        qkv_chains = [
            Halving(low_bits, o, pair=halves[2 * i : 2 * i + 2]) for i, o in enumerate(low_orders)
        ]
        parts = [own_part, peer_part]
    else:
        inv, mean = inverse[:2, :, None], means[:, :, None]
        hat = d[:2] * gain_own[2:4][:, None] - pre[:2] * inv * mean
        grads = [(inv[0] * hat[0]).astype(BF16), (inv[1] * hat[1]).astype(BF16), d[2].astype(BF16)]
        wide = [dot(g, first_all, 0, 0).astype(BF16) for g in grads]
        wide = [jnp.concatenate(natural(exchange_rot(w_, 1)), axis=0) for w_ in wide]
        qkv_chains = [
            Halving(bits, o, whole=relative(w_.reshape(dpn, share, own_d)))
            for w_, o in zip(wide, (order_a, order_b, order_c))
        ]
        parts = [
            sum(dot(rows(g, r), w_heads[j], 1, 1) for j, g in enumerate(grads)) for r in range(n)
        ]
        parts = [parts[0]] + [p.astype(BF16) for p in parts[1:]]
    grad_first = scatter_rot(parts)

    text_in = text_bwd(pair_all, w_text)
    text_in = jnp.concatenate(natural(exchange_rot(text_in, 0)), axis=1)

    inverse_one = inverse_rms(x_own)
    normed_one = x_own * inverse_one
    scaled = grad_first * normed_one
    d_scale_attn = jnp.sum(scaled * gain_full[0], axis=0)
    gain_one = jnp.sum(scaled * (1.0 + scale_attn), axis=0)
    grad_input = (
        grad_after
        + rms_back(grad_first * gain_full[0] * (1.0 + scale_attn), normed_one, inverse_one)
    ).astype(BF16)

    mods = jnp.stack([d_scale_attn, d_gate_attn, d_scale_ffn, d_gate_ffn])
    mods = mods.reshape(4, dpn, share).transpose(1, 0, 2)
    stamp = jnp.full((dpn, 1, share), timesteps[0].astype(F32) / n)
    mods = pair_sum(dp_exchange(relative(jnp.concatenate([mods, stamp], axis=1)), order_a))
    times = time_embed(jnp.round(mods[:, 4, 0]))
    times = lax.dynamic_slice_in_dim(times, f * own_te, own_te, 1).astype(F32)
    ada_grad = lax.dot_general(
        mods[:, :4].reshape(dpn, 4 * share), times, (((0,), (0,)), ((), ())),
        precision=lax.Precision.HIGHEST,
    ).reshape(4, share, own_te)
    two = scatter_rot(rot_blocks(jnp.stack([gain_one, gain_two]), 1))
    gate_pad = jnp.pad(gate_total, (0, own_d - gate_total.shape[0]))[None]
    small = dp_total(
        jnp.concatenate([two, gain_q[:, :own_d], gain_k[:, :own_d], gain_text, gate_pad], axis=0)
    )

    pair_cols = jnp.concatenate(natural(gather_rot(pair_cols)), axis=2)
    pair_cols = relative(pair_cols).transpose(0, 2, 1, 3).reshape(dpn * TEXT, 2 * share)
    text_grad = dot(pair_cols, text_all, 0, 0).reshape(2, share, TW // n)

    chains += [out_chain] + qkv_chains
    while any(c.got is not None for c in chains):
        for c in chains:
            c.step()
    qkv_grad = [c.last[0] for c in qkv_chains]
    if paired:
        own_side = f == (me >> low_bits[-1] + 1)
        for i, c in enumerate(qkv_chains):
            mine, got = exchange_rot(c.cur[0], 1)
            keep, send = jnp.where(own_side, mine, got), jnp.where(own_side, got, mine)
            qkv_grad[i] = keep.astype(F32) + dp_swap(send, bits[-1]).astype(F32)
    return (
        output[None],
        grad_input[None],
        text_in[None],
        ada_grad.transpose(2, 0, 1),
        text_grad.transpose(2, 0, 1),
        jnp.stack(qkv_grad).transpose(2, 0, 1),
        out_chain.last[0].T,
        small[:5],
        small[5, : HEADS // n],
        jnp.stack([ffn_chains[0].last[0], ffn_chains[1].last[0]], axis=1),
        ffn_chains[2].last[0].T,
    )


def solution(mesh):
    return jax.shard_map(
        on_device,
        mesh=mesh,
        in_specs=(
            P("dp", "fsdp", None),
            P("dp", "fsdp", None),
            P("dp"),
            P("dp"),
            P("dp", None, "fsdp"),
            P("dp", "fsdp", None),
            P("fsdp", None, None),
            P("fsdp", None, None),
            P("fsdp", None, None),
            P("fsdp", None),
            P(None, "fsdp"),
            P("fsdp"),
            P(None, None, "fsdp"),
            P("fsdp", None),
        ),
        out_specs=(
            P("dp", "fsdp", None),
            P("dp", "fsdp", None),
            P("dp", "fsdp", None),
            P("fsdp", None, "dp"),
            P("fsdp", None, "dp"),
            P("fsdp", None, "dp"),
            P("fsdp", "dp"),
            P(None, "fsdp"),
            P("fsdp"),
            P("dp", None, "fsdp"),
            P("fsdp", "dp"),
        ),
        check_vma=False,
    )
```

```python
import functools
import math

import jax
import jax.numpy as jnp
from jax import lax
from jax.experimental import pallas as pl
from jax.experimental.pallas import tpu as pltpu
from jax.sharding import PartitionSpec as P

D = 1536
HEADS = 24
HD = 64
TW = 4096
TE = 1024
PATCHES = 1024
TEXT = 256
EPSILON = 1e-06
F32 = jnp.float32
BF16 = jnp.bfloat16
QC = 256


def dot(a, b, ca=1, cb=0):
    return lax.dot_general(a, b, (((ca,), (cb,)), ((), ())), preferred_element_type=F32)


def from_behind(value, step):
    n = lax.axis_size("fsdp")
    return lax.ppermute(value, "fsdp", [(i, (i + step) % n) for i in range(n)])


def gather_rot(value):
    return [value] + [from_behind(value, r) for r in range(1, lax.axis_size("fsdp"))]


def pair_sum(value):
    return functools.reduce(lambda a, b: a + b, gather_rot(value))


def row_sum(value):
    n = lax.axis_size("fsdp")
    rows = value.shape[-1] // n
    total = value
    for r in range(1, n):
        total = total + jnp.roll(from_behind(value, r), r * rows, axis=-1)
    return total


def scatter_rot(blocks):
    n = lax.axis_size("fsdp")
    total = blocks[0].astype(F32)
    for r in range(1, n):
        got = lax.ppermute(blocks[r], "fsdp", [(i, (i - r) % n) for i in range(n)])
        total = total + got.astype(F32)
    return total


def block_of(value, index, axis):
    size = value.shape[axis] // lax.axis_size("fsdp")
    return lax.dynamic_slice_in_dim(value, index * size, size, axis)


def rot_blocks(value, axis):
    n, f = lax.axis_size("fsdp"), lax.axis_index("fsdp")
    return [block_of(value, (f - r) % n, axis) for r in range(n)]


def exchange_rot(value, axis):
    n, f = lax.axis_size("fsdp"), lax.axis_index("fsdp")
    out = [block_of(value, f, axis)]
    for r in range(1, n):
        out.append(from_behind(block_of(value, (f + r) % n, axis), r))
    return out


def natural(got):
    n, f = lax.axis_size("fsdp"), lax.axis_index("fsdp")
    if n == 2:
        return [jnp.where(f == 0, got[0], got[1]), jnp.where(f == 0, got[1], got[0])]
    got = jnp.stack(got)
    return [lax.dynamic_index_in_dim(got, (f - g) % n, 0, keepdims=False) for g in range(n)]


def dp_bits():
    return int(lax.axis_size("dp")).bit_length() - 1


def swapped(p):
    return (p & ~3) | ((p & 1) << 1) | ((p >> 1) & 1)


def turned(p, f):
    return p if dp_bits() < 3 else jnp.where(f % 2 == 0, p, swapped(p))


def dp_swap(value, bit):
    n, dpn = lax.axis_size("fsdp"), lax.axis_size("dp")
    pairs = []
    for i in range(dpn):
        for f in range(n):
            flip = 1 << bit if dp_bits() < 3 or f % 2 == 0 else swapped(1 << bit)
            pairs.append((i * n + f, (i ^ flip) * n + f))
    return lax.ppermute(value, ("dp", "fsdp"), pairs)


def relative(value):
    places = turned(jnp.arange(lax.axis_size("dp")), lax.axis_index("fsdp"))
    return jnp.take(value, lax.axis_index("dp") ^ places, axis=0)


def absolute(value):
    places = lax.axis_index("dp") ^ jnp.arange(lax.axis_size("dp"))
    return jnp.take(value, turned(places, lax.axis_index("fsdp")), axis=0)


class Halving:
    def __init__(self, bits, order, pair):
        self.labels, self.order = list(bits)[::-1], list(order)
        bit = self.order.pop(0)
        self.labels.remove(bit)
        self.keep, self.got = pair[0], dp_swap(pair[1], bit)

    def step(self):
        if self.got is None:
            return

        def add(keep, got):
            return keep.astype(F32) + got.astype(F32)

        if not self.order:
            self.last = add(self.keep, self.got)
            self.got = None
            return
        bit = self.order.pop(0)
        axis = self.labels.index(bit)
        tail = self.keep.shape[1:]
        parts = [v.reshape((2,) * len(self.labels) + tail) for v in (self.keep, self.got)]
        self.labels.remove(bit)
        self.keep, send = (
            add(*(lax.index_in_dim(v, i, axis, keepdims=False) for v in parts))
            .astype(BF16)
            .reshape((-1,) + tail)
            for i in range(2)
        )
        self.got = dp_swap(send, bit)


class Exchange:
    def __init__(self, value):
        self.bits, self.shape = list(range(dp_bits())), value.shape
        self.cur = value.reshape((2,) * dp_bits() + value.shape[1:])
        self.keep = self.got = None
        self.start()

    def start(self):
        if self.bits:
            self.bit = self.bits.pop(0)
            self.axis = dp_bits() - 1 - self.bit
            self.keep, send = (
                lax.index_in_dim(self.cur, i, self.axis, keepdims=False) for i in range(2)
            )
            self.got = dp_swap(send, self.bit)

    def step(self):
        if self.got is not None:
            self.cur = jnp.stack([self.keep, self.got], axis=self.axis)
            self.got = None
            self.start()


class Gather:
    def __init__(self, value):
        self.bits, self.cur = list(range(dp_bits())), value[None]
        self.got = None
        self.start()

    def start(self):
        if self.bits:
            self.got = dp_swap(self.cur, self.bits.pop(0))

    def step(self):
        if self.got is not None:
            self.cur = jnp.concatenate([self.cur, self.got], axis=0)
            self.got = None
            self.start()


def advance(chains, value):
    live = [c for c in chains if c.got is not None]
    value, got = lax.optimization_barrier((value, [c.got for c in live]))
    for c, g in zip(live, got):
        c.got = g
        c.step()
    return value


def rope_block(value, cosine, sine, sign):
    width = value.shape[1]
    lane = lax.broadcasted_iota(jnp.int32, value.shape, 1)
    partner = jnp.where(
        lane % 32 < 16, pltpu.roll(value, width - 16, 1), pltpu.roll(value, 16, 1)
    )
    return value * cosine + sign * (partner * sine)


def column(ref, index, width):
    row = ref[index : index + 1, :] if isinstance(index, int) else ref[pl.ds(index, 1), :]
    return jnp.broadcast_to(row, (width, row.shape[1])).T


def masked(value, head):
    lane = lax.broadcasted_iota(jnp.int32, value.shape, 1)
    return jnp.where(lane // HD == head, value, jnp.zeros_like(value))


def attn_fwd_kernel(
    len_ref, pre_ref, inv_ref, gq_ref, gk_ref, cos_ref, sin_ref, tk_ref, tv_ref, gate_ref,
    q_ref, k_ref, v_ref, mixed_ref, so_ref, co_ref, ls_ref, lc_ref,
):
    _, tokens, width = pre_ref.shape
    heads = width // HD
    iq, ik = column(inv_ref, 0, width), column(inv_ref, 1, width)
    q = rope_block(pre_ref[0] * iq * gq_ref[...], cos_ref[...], sin_ref[...], 1.0)
    q_ref[...] = q.astype(BF16)
    k = rope_block(pre_ref[1] * ik * gk_ref[...], cos_ref[...], sin_ref[...], 1.0)
    k_ref[...] = k.astype(BF16)
    v_ref[...] = pre_ref[2].astype(BF16)
    length = len_ref[0]

    def one(keys, values, qm, limit):
        s = dot(qm, keys, 1, 1)
        if limit is not None:
            slot = lax.broadcasted_iota(jnp.int32, s.shape, 1)
            s = jnp.where(slot < limit, s, -1e30)
        peak = jnp.max(s, axis=1, keepdims=True)
        e = jnp.exp(s - peak)
        total = jnp.sum(e, axis=1, keepdims=True)
        o = dot(e.astype(BF16), values)
        return o * (1.0 / total), peak + jnp.log(total)

    lane = lax.broadcasted_iota(jnp.int32, (tokens, width), 1)
    qs = q_ref[...] * jnp.asarray(HD**-0.5, BF16)
    so = co = stats = jnp.zeros((tokens, width), F32)
    for h in range(heads):
        qm = masked(qs, h)
        o, lse = one(k_ref[...], v_ref[...], qm, None)
        so = jnp.where(lane // HD == h, o, so)
        stats = jnp.where(lane == h, lse, stats)
        o, lse = one(tk_ref[...], tv_ref[...], qm, length)
        co = jnp.where(lane // HD == h, o, co)
        stats = jnp.where(lane == heads + h, lse, stats)
    so_ref[...] = so
    co_ref[...] = co
    mixed_ref[...] = (so + gate_ref[...] * co).astype(BF16)
    stats = stats.T
    ls_ref[0] = stats[:heads]
    lc_ref[0] = stats[heads : 2 * heads]


def attn_bwd_kernel(
    len_ref, q_ref, k_ref, v_ref, tk_ref, tv_ref, g_ref, so_ref, co_ref, ls_ref, lc_ref,
    pre_ref, inv_ref, gq_ref, gk_ref, cos_ref, sin_ref, gate_ref,
    d_ref, dtk_ref, dtv_ref, stat_ref, gainq_ref, gaink_ref, gateg_ref,
    gs_ref, gc_ref, ds_ref, dc_ref, kt_ref, tkt_ref, dqt_ref, dk_acc, dv_acc, rq_ref, rk_ref,
):
    tokens, width = q_ref.shape
    heads = width // HD
    scale = jnp.asarray(HD**-0.5, BF16)

    @pl.when(pl.program_id(0) == 0)
    def _():
        rq_ref[...] = jnp.zeros_like(rq_ref)
        rk_ref[...] = jnp.zeros_like(rk_ref)

    g = g_ref[...]
    gs_ref[...] = g.astype(BF16)
    gc_ref[...] = (g * gate_ref[...]).astype(BF16)
    prod_c = g * co_ref[...]
    gateg_ref[...] = jnp.sum(prod_c, axis=0, keepdims=True)
    prod_s = (g * so_ref[...]).T
    prod_c = (prod_c * gate_ref[...]).T
    for h in range(heads):
        ds_ref[h : h + 1, :] = jnp.sum(prod_s[h * HD : (h + 1) * HD], axis=0, keepdims=True)
        dc_ref[h : h + 1, :] = jnp.sum(prod_c[h * HD : (h + 1) * HD], axis=0, keepdims=True)
    kt_ref[...] = k_ref[...].astype(F32).T.astype(BF16)
    tkt_ref[...] = tk_ref[...].astype(F32).T.astype(BF16)
    dk_acc[...] = jnp.zeros_like(dk_acc)
    dv_acc[...] = jnp.zeros_like(dv_acc)
    dtk_ref[...] = jnp.zeros_like(dtk_ref)
    dtv_ref[...] = jnp.zeros_like(dtv_ref)
    length = len_ref[0]

    def one(keys, keys_t, values, qm, gm, lse, delta, head, limit):
        s = dot(keys, qm, 1, 1)
        p = jnp.exp(s - lse)
        if limit is not None:
            slot = lax.broadcasted_iota(jnp.int32, s.shape, 0)
            p = jnp.where(slot < limit, p, 0.0)
        dp = dot(values, gm, 1, 1)
        ds = (p * (dp - delta)).astype(BF16)
        dq = dot(keys_t[head * HD : (head + 1) * HD, :], ds)
        return dq, dot(ds, qm), dot(p.astype(BF16), gm)

    def chunk(c, carry):
        rows = pl.ds(pl.multiple_of(c * QC, QC), QC)
        qc = q_ref[rows, :] * scale
        for h in range(heads):
            qm = masked(qc, h)
            dq, dk, dv = one(
                k_ref[...], kt_ref, v_ref[...], qm, masked(gs_ref[rows, :], h),
                ls_ref[0, h : h + 1, rows], ds_ref[h : h + 1, rows], h, None,
            )
            dk_acc[...] += dk
            dv_acc[...] += dv
            dq2, dk, dv = one(
                tk_ref[...], tkt_ref, tv_ref[...], qm, masked(gc_ref[rows, :], h),
                lc_ref[0, h : h + 1, rows], dc_ref[h : h + 1, rows], h, length,
            )
            dtk_ref[...] += dk
            dtv_ref[...] += dv
            dqt_ref[h * HD : (h + 1) * HD, rows] = (dq + dq2) * HD**-0.5
        return carry

    lax.fori_loop(0, tokens // QC, chunk, 0)
    dq = rope_block(dqt_ref[...].T, cos_ref[...], sin_ref[...], -1.0)
    d_ref[0] = dq
    prod = dq * (pre_ref[0] * column(inv_ref, 0, width))
    gainq_ref[...] = jnp.sum(prod, axis=0, keepdims=True)
    rq_ref[...] += prod * gq_ref[...]
    dk = rope_block(dk_acc[...], cos_ref[...], sin_ref[...], -1.0)
    d_ref[1] = dk
    prod = dk * (pre_ref[1] * column(inv_ref, 1, width))
    gaink_ref[...] = jnp.sum(prod, axis=0, keepdims=True)
    rk_ref[...] += prod * gk_ref[...]
    d_ref[2] = dv_acc[...]

    @pl.when(pl.program_id(0) == pl.num_programs(0) - 1)
    def _():
        stat_ref[...] = jnp.zeros_like(stat_ref)
        for i, ref in enumerate((rq_ref, rk_ref)):
            stat_ref[i : i + 1, :] = jnp.sum(ref[...].T, axis=0, keepdims=True)


def specs(tokens, text, width, heads, at=0):
    col = pl.BlockSpec((tokens, width), lambda i: (0, i + at))
    three = pl.BlockSpec((3, tokens, width), lambda i: (0, 0, i + at))
    tcol = pl.BlockSpec((text, width), lambda i: (0, i + at))
    stat = pl.BlockSpec((8, tokens), lambda i: (0, 0))
    gain = pl.BlockSpec((1, width), lambda i: (0, i + at))
    table = pl.BlockSpec((tokens, width), lambda i: (0, 0))
    lse = pl.BlockSpec((1, heads, tokens), lambda i: (i + at, 0, 0))
    scalar = pl.BlockSpec(memory_space=pltpu.SMEM)
    return col, three, tcol, stat, gain, table, lse, scalar


def sds(shape, dtype=F32):
    return jax.ShapeDtypeStruct(shape, dtype)


def attn_forward(length, pre, inv, gq, gk, cosine, sine, tk, tv, gate):
    _, tokens, columns = pre.shape
    text, width = tk.shape[0], cosine.shape[1]
    heads, blocks = width // HD, columns // width
    col, three, tcol, stat, gain, table, lse, scalar = specs(tokens, text, width, heads)
    flat = (tokens, columns)
    return pl.pallas_call(
        attn_fwd_kernel,
        grid=(blocks,),
        in_specs=[scalar, three, stat, gain, gain, table, table, tcol, tcol, gain],
        out_specs=[col, col, col, col, col, col, lse, lse],
        out_shape=[sds(flat, BF16)] * 4 + [sds(flat)] * 2 + [sds((blocks, heads, tokens))] * 2,
    )(length, pre, inv, gq, gk, cosine, sine, tk, tv, gate)


def attn_backward(at, blocks, length, q, k, v, tk, tv, g, so, co, ls, lc, pre, inv, gq, gk, cosine, sine, gate):
    tokens = q.shape[0]
    text, width = tk.shape[0], cosine.shape[1]
    heads, columns = width // HD, blocks * width
    col, three, tcol, stat, gain, table, lse, scalar = specs(tokens, text, width, heads, at)
    _, three_o, tcol_o, _, gain_o, _, _, _ = specs(tokens, text, width, heads)
    return pl.pallas_call(
        attn_bwd_kernel,
        grid=(blocks,),
        in_specs=[scalar, col, col, col, tcol, tcol, col, col, col, lse, lse,
                  three, stat, gain, gain, table, table, gain],
        out_specs=[three_o, tcol_o, tcol_o, stat, gain_o, gain_o, gain_o],
        out_shape=[
            sds((3, tokens, columns)), sds((text, columns)), sds((text, columns)),
            sds((8, tokens)), sds((1, columns)), sds((1, columns)), sds((1, columns)),
        ],
        scratch_shapes=[
            pltpu.VMEM((tokens, width), BF16), pltpu.VMEM((tokens, width), BF16),
            pltpu.VMEM((heads, tokens), F32), pltpu.VMEM((heads, tokens), F32),
            pltpu.VMEM((width, tokens), BF16), pltpu.VMEM((width, text), BF16),
            pltpu.VMEM((width, tokens), F32),
            pltpu.VMEM((tokens, width), F32), pltpu.VMEM((tokens, width), F32),
            pltpu.VMEM((tokens, width), F32), pltpu.VMEM((tokens, width), F32),
        ],
    )(length, q, k, v, tk, tv, g, so, co, ls, lc, pre, inv, gq, gk, cosine, sine, gate)


def pick(rows, cols, step, part):
    i = lax.broadcasted_iota(jnp.int32, (rows, cols), 0)
    j = lax.broadcasted_iota(jnp.int32, (rows, cols), 1)
    hit = (j == step * i + part) if cols > rows else (i == step * j + part)
    return jnp.where(hit, 1.0, 0.0).astype(BF16)

def text_fwd_kernel(x_ref, w_ref, o_ref):
    @pl.when(pl.program_id(0) == 0)
    def _():
        o_ref[...] = jnp.zeros_like(o_ref)
    for b in range(w_ref.shape[0] // 128):
        rows = slice(b * 128, (b + 1) * 128)
        w = w_ref[rows].reshape(256, w_ref.shape[2])
        x = x_ref[:, rows]
        for j in range(2):
            spread = dot(x, pick(128, 256, 2, j)).astype(BF16)
            o_ref[j] += dot(spread, w)

def text_fwd(x, w):
    depth, _, cols = w.shape
    bk = 256
    return pl.pallas_call(
        text_fwd_kernel, grid=(depth // bk,),
        in_specs=[pl.BlockSpec((x.shape[0], bk), lambda i: (0, i)), pl.BlockSpec((bk, 2, cols), lambda i: (i, 0, 0))],
        out_specs=pl.BlockSpec((2, x.shape[0], cols), lambda i: (0, 0, 0)),
        out_shape=sds((2, x.shape[0], cols)),
    )(x, w)

def text_bwd_kernel(g_ref, w_ref, o_ref):
    for b in range(w_ref.shape[0] // 128):
        rows = slice(b * 128, (b + 1) * 128)
        w = w_ref[rows].reshape(256, w_ref.shape[2])
        total = 0.0
        for j in range(2):
            total = total + dot(g_ref[j], dot(pick(128, 256, 2, j), w).astype(BF16), 1, 1)
        o_ref[:, rows] = total.astype(BF16)

def text_bwd(g, w):
    depth, _, cols = w.shape
    bk = 256
    return pl.pallas_call(
        text_bwd_kernel, grid=(depth // bk,),
        in_specs=[pl.BlockSpec(g.shape, lambda i: (0, 0, 0)), pl.BlockSpec((bk, 2, cols), lambda i: (i, 0, 0))],
        out_specs=pl.BlockSpec((g.shape[1], bk), lambda i: (0, i)),
        out_shape=sds((g.shape[1], depth), BF16),
    )(g, w)

def put_relative(dst, src, me, f, count):
    rows = dst.shape[0] // count
    for p in range(count):
        start = pl.multiple_of((me ^ turned(p, f)) * rows, 16)
        dst[p * rows : (p + 1) * rows, :] = src[pl.ds(start, rows), :]


def put_halves(keep, send, value, count, bit, slot=None):
    rows = value.shape[0] // count
    low = (1 << bit) - 1
    for p in range(count):
        place = (p & low) | (p >> (bit + 1) << bit)
        where = place if slot is None else (place, slot)
        (send if p >> bit & 1 else keep)[where] = value[p * rows : (p + 1) * rows]


def ffn_kernel(
    bits, id_ref, s_ref, b_ref, w_ref, d_ref,
    wk_ref, ws_ref, dk_ref, ds_ref, fo_ref, fp_ref, so_ref, sp_ref,
    st, bt, tmp, wg, wu, facc, sacc,
):
    step = pl.program_id(0)
    depth, _, cols = w_ref.shape
    own = fo_ref.shape[0]
    count = 2 * dk_ref.shape[0]

    @pl.when(step == 0)
    def _():
        for src, dst in ((s_ref, st), (b_ref, bt)):
            for c in range(depth // 256):
                part = slice(c * 256, (c + 1) * 256)
                tmp[part, :] = src[:, part].astype(F32).T.astype(BF16)
            put_relative(dst, tmp, id_ref[0], id_ref[1], count)
        facc[...] = jnp.zeros_like(facc)
        sacc[...] = jnp.zeros_like(sacc)

    for c in range(depth // 128):
        part = slice(c * 128, (c + 1) * 128)
        w = w_ref[part].reshape(256, cols)
        wg[part, :] = dot(pick(128, 256, 2, 0), w).astype(BF16)
        wu[part, :] = dot(pick(128, 256, 2, 1), w).astype(BF16)
    s, b = s_ref[...], b_ref[...]
    gate = dot(s, wg[...])
    up = dot(s, wu[...])
    back = dot(b, d_ref[...], 1, 1)
    sig = jax.nn.sigmoid(gate)
    silu = gate * sig
    hidden = (silu * up).astype(BF16)
    g_gate = (back * up * (sig + silu * (1.0 - sig))).astype(BF16)
    g_up = (back * silu).astype(BF16)
    put_halves(wk_ref, ws_ref, dot(st[...], g_gate).astype(BF16), count, bits[0], 0)
    put_halves(wk_ref, ws_ref, dot(st[...], g_up).astype(BF16), count, bits[0], 1)
    put_halves(dk_ref, ds_ref, dot(bt[...], hidden).astype(BF16), count, bits[1])
    facc[...] += dot(hidden, d_ref[...])
    sacc[...] += dot(g_gate, wg[...], 1, 1) + dot(g_up, wu[...], 1, 1)

    @pl.when(step == pl.num_programs(0) - 1)
    def _():
        fo_ref[...] = facc[:own]
        fp_ref[...] = facc[own:].astype(BF16)
        so_ref[...] = sacc[:own]
        sp_ref[...] = sacc[own:].astype(BF16)


def ffn(ids, s, b, w, d, local, dp, bits):
    tokens, depth = s.shape
    hid = d.shape[0]
    bc = min(256, hid)
    rest = tokens - local
    once = functools.partial(pl.BlockSpec, pipeline_mode=pl.Buffered(1))
    const = lambda i: (0, 0)
    share = depth // dp
    half = pl.BlockSpec((dp // 2, share, bc), lambda i: (0, 0, i))
    halves = pl.BlockSpec((dp // 2, 2, share, bc), lambda i: (0, 0, 0, i))
    return pl.pallas_call(
        functools.partial(ffn_kernel, bits),
        grid=(hid // bc,),
        in_specs=[
            pl.BlockSpec(memory_space=pltpu.SMEM),
            once((tokens, depth), const), once((tokens, depth), const),
            pl.BlockSpec((depth, 2, bc), lambda i: (0, 0, i)),
            pl.BlockSpec((bc, depth), lambda i: (i, 0)),
        ],
        out_specs=[halves] * 2 + [half] * 2 + [
            once((local, depth), const), once((rest, depth), const),
            once((local, depth), const), once((rest, depth), const),
        ],
        out_shape=[sds((dp // 2, 2, share, hid), BF16)] * 2 + [sds((dp // 2, share, hid), BF16)] * 2 + [
            sds((local, depth)), sds((rest, depth), BF16),
            sds((local, depth)), sds((rest, depth), BF16),
        ],
        scratch_shapes=[
            pltpu.VMEM((depth, tokens), BF16), pltpu.VMEM((depth, tokens), BF16),
            pltpu.VMEM((depth, tokens), BF16),
            pltpu.VMEM((depth, bc), BF16), pltpu.VMEM((depth, bc), BF16),
            pltpu.VMEM((tokens, depth), F32), pltpu.VMEM((tokens, depth), F32),
        ],
        compiler_params=pltpu.CompilerParams(vmem_limit_bytes=62 << 20),
    )(ids, s, b, w, d)


def project_kernel(id_ref, xo_ref, xp_ref, front_ref, w_ref, got_ref, first_ref, pre_ref, sq_ref):
    j = pl.program_id(0)
    local, depth = xo_ref.shape
    own = got_ref.shape[2]
    f = id_ref[1]

    @pl.when(j == 0)
    def _():
        for i, ref in enumerate((xo_ref, xp_ref)):
            x = ref[...].astype(F32)
            inv = lax.rsqrt(jnp.sum(x * x, axis=1, keepdims=True) * (1.0 / depth) + EPSILON)
            first_ref[i * local : (i + 1) * local, :] = (x * inv * front_ref[...]).astype(BF16)
        sq_ref[...] = jnp.zeros_like(sq_ref)

    mine = pl.ds(pl.multiple_of(f * own, 128), own)
    other = pl.ds(pl.multiple_of((1 - f) * own, 128), own)
    out = dot(first_ref[:, mine], w_ref[0, :, mine]) + dot(first_ref[:, other], got_ref[0])
    pre_ref[0] = out
    square = out * out
    part = square[:, :128]
    for c in range(1, own // 128):
        part = part + square[:, c * 128 : (c + 1) * 128]
    sq_ref[pl.ds(j, 1), :] = jnp.sum(part.T, axis=0, keepdims=True)


def project(ids, xo, xp, front, w, got):
    local, depth = xo.shape
    own = got.shape[2]
    tokens = 2 * local
    const = lambda j: (0, 0)
    return pl.pallas_call(
        project_kernel,
        grid=(3,),
        in_specs=[
            pl.BlockSpec(memory_space=pltpu.SMEM),
            pl.BlockSpec((local, depth), const), pl.BlockSpec((local, depth), const),
            pl.BlockSpec((1, depth), const),
            pl.BlockSpec((1, own, depth), lambda j: (j, 0, 0)),
            pl.BlockSpec((1, own, own), lambda j: (j, 0, 0)),
        ],
        out_specs=[
            pl.BlockSpec((tokens, depth), const),
            pl.BlockSpec((1, tokens, own), lambda j: (j, 0, 0)),
            pl.BlockSpec((8, tokens), const),
        ],
        out_shape=[sds((tokens, depth), BF16), sds((3, tokens, own)), sds((8, tokens))],
    )(ids, xo, xp, front, w, got)


def project_back_kernel(
    id_ref, da_ref, db_ref, pre_ref, stat_ref, gain_ref, first_ref, w_ref, got_ref,
    keep_ref, send_ref, own_ref, peer_ref, gt, tmp, acc,
):
    j = pl.program_id(0)
    tokens, own = pre_ref.shape[1:]
    cut = da_ref.shape[2]
    local = own_ref.shape[0]
    f = id_ref[1]
    count = 2 * keep_ref.shape[0]
    inv, mean = column(stat_ref, j, 128), column(stat_ref, j + 3, 128)
    grads = []
    for c in range(own // 128):
        part = slice(c * 128, (c + 1) * 128)
        here = slice(c * 128 - cut, (c + 1) * 128 - cut) if c * 128 >= cut else part
        d = (db_ref if c * 128 >= cut else da_ref)[0, :, here]
        g = inv * (d * gain_ref[0, :, part] - pre_ref[0, :, part] * inv * mean)
        tmp[part, :] = g.T.astype(BF16)
        grads.append(g.astype(BF16))
    g = jnp.concatenate(grads, axis=1)
    put_relative(gt, tmp, id_ref[0] % count, f, count)
    put_halves(keep_ref, send_ref, dot(gt[...], first_ref[...]).astype(BF16), count, 0, j)

    @pl.when(j == 0)
    def _():
        acc[...] = jnp.zeros_like(acc)

    mine = pl.ds(pl.multiple_of(f * own, 128), own)
    other = pl.ds(pl.multiple_of((1 - f) * own, 128), own)
    acc[:, mine] += dot(g, w_ref[0, :, mine], 1, 1)
    acc[:, other] += dot(g, got_ref[0], 1, 1)

    @pl.when(j == 2)
    def _():
        own_ref[...] = acc[:local]
        peer_ref[...] = acc[local:].astype(BF16)


def project_back(ids, da, db, pre, stats, gain, first, w, got, dp):
    _, tokens, own = pre.shape
    depth = first.shape[1]
    local = tokens // 2
    share = depth // dp
    const = lambda j: (0, 0)
    block = lambda j: (j, 0, 0)
    once = functools.partial(pl.BlockSpec, pipeline_mode=pl.Buffered(1))
    half = once((dp // 4, 3, share, depth), lambda j: (0, 0, 0, 0))
    return pl.pallas_call(
        project_back_kernel,
        grid=(3,),
        in_specs=[
            pl.BlockSpec(memory_space=pltpu.SMEM),
            pl.BlockSpec((1,) + da.shape[1:], block), pl.BlockSpec((1,) + db.shape[1:], block),
            pl.BlockSpec((1, tokens, own), block),
            pl.BlockSpec((8, tokens), const),
            pl.BlockSpec((1, 1, own), block),
            once((tokens, depth), const),
            pl.BlockSpec((1, own, depth), block), pl.BlockSpec((1, own, own), block),
        ],
        out_specs=[half, half, once((local, depth), const), once((local, depth), const)],
        out_shape=[sds((dp // 4, 3, share, depth), BF16)] * 2 + [
            sds((local, depth)), sds((local, depth), BF16),
        ],
        scratch_shapes=[
            pltpu.VMEM((own, tokens), BF16), pltpu.VMEM((own, tokens), BF16),
            pltpu.VMEM((tokens, depth), F32),
        ],
        compiler_params=pltpu.CompilerParams(vmem_limit_bytes=62 << 20),
    )(ids, da, db, pre, stats, gain, first, w, got)


def out_back_kernel(id_ref, *refs):
    n = len(refs) - 8
    blocks, (w_ref, mixed_ref, g_ref, keep_ref, send_ref, all_ref, gt, tmp) = refs[:n], refs[n:]
    local = blocks[0].shape[0]
    for r, ref in enumerate(blocks):
        all_ref[r * local : (r + 1) * local, :] = ref[...]
    grad = all_ref[...]
    g_ref[...] = dot(grad, w_ref[...], 1, 1)
    for c in range(grad.shape[1] // 256):
        part = slice(c * 256, (c + 1) * 256)
        tmp[part, :] = grad[:, part].astype(F32).T.astype(BF16)
    count = 2 * keep_ref.shape[0]
    put_relative(gt, tmp, id_ref[0], id_ref[1], count)
    put_halves(keep_ref, send_ref, dot(gt[...], mixed_ref[...]).astype(BF16), count, 0)


def out_back(ids, blocks, w, mixed, dp):
    tokens, own = mixed.shape
    depth = w.shape[1]
    vmem = pl.BlockSpec(memory_space=pltpu.VMEM)
    half = sds((dp // 2, depth // dp, own), BF16)
    return pl.pallas_call(
        out_back_kernel,
        in_specs=[pl.BlockSpec(memory_space=pltpu.SMEM)] + [vmem] * (len(blocks) + 2),
        out_specs=[vmem] * 3,
        out_shape=[sds((tokens, own)), half, half],
        scratch_shapes=[
            pltpu.VMEM((tokens, depth), BF16),
            pltpu.VMEM((depth, tokens), BF16), pltpu.VMEM((depth, tokens), BF16),
        ],
    )(ids, *blocks, w, mixed)


def time_embed(timesteps):
    half = TE // 2
    frequencies = jnp.exp(-math.log(10000.0) * jnp.arange(half, dtype=F32) / half)
    angles = timesteps.astype(F32)[:, None] * frequencies
    waves = jnp.concatenate([jnp.cos(angles), jnp.sin(angles)], axis=-1)
    return jax.nn.silu(waves).astype(BF16)


def rope_tables(positions, width):
    lane = jnp.arange(width)
    quarter = HD // 4
    frequencies = 10000.0 ** (-(lane % quarter).astype(F32) / quarter)
    place = jnp.where(lane % HD < HD // 2, positions[0][:, None], positions[1][:, None])
    angles = place.astype(F32) * frequencies
    return jnp.cos(angles), jnp.where(lane % 32 < 16, -1.0, 1.0) * jnp.sin(angles)


def inverse_rms(values):
    return lax.rsqrt(jnp.mean(values * values, axis=-1, keepdims=True) + EPSILON)


def rms_back(grad_hat, normed, inverse):
    return inverse * (grad_hat - normed * jnp.mean(grad_hat * normed, axis=-1, keepdims=True))


def pad_cols(value, width):
    extra = -value.shape[-1] % width
    return value if extra == 0 else jnp.pad(value, [(0, 0)] * (value.ndim - 1) + [(0, extra)])


def on_device(
    hidden_in, text_state, caption_lengths, timesteps, patch_positions, cotangent,
    w_ada, w_text, w_qkv, w_out, gains, cross_gate, w_gate_up, w_down,
):
    n, f = lax.axis_size("fsdp"), lax.axis_index("fsdp")
    dpn, me = lax.axis_size("dp"), lax.axis_index("dp")
    bits = list(range(dp_bits()))
    low_bits = bits[:-1]
    late = bits[2:] + bits[:2]
    own_d = D // n
    local = hidden_in.shape[1]
    tokens = n * local
    width = 2 * HD
    share = D // dpn
    paired = n == 2 and dpn >= 4
    ids = jnp.stack([me, f]).astype(jnp.int32)
    x_bf, dy_bf = hidden_in[0], cotangent[0]

    time_low = time_embed(timesteps)
    own_te = TE // n
    time_own = lax.dynamic_slice_in_dim(time_low[0], f * own_te, own_te, 0)
    modulation = pair_sum(
        jnp.einsum("k,kjd->jd", time_own, w_ada, preferred_element_type=F32)
    )
    scale_attn, gate_attn = modulation[0:1], jnp.tanh(modulation[1:2])
    scale_ffn, gate_ffn = modulation[2:3], jnp.tanh(modulation[3:4])

    w_flat = jnp.moveaxis(w_qkv, 1, 0)
    w_parts = exchange_rot(w_flat, 2)
    x_parts = gather_rot(x_bf)
    dy_all = jnp.concatenate(gather_rot(dy_bf), axis=0)
    places = jnp.concatenate(gather_rot(patch_positions[0]), axis=1)
    text_cols = jnp.concatenate(natural(exchange_rot(text_state[0], 1)), axis=0)
    text_all = lax.all_gather(text_cols, "dp", axis=0, tiled=True)
    gain_full = lax.all_gather(gains, "fsdp", axis=1, tiled=True).astype(F32)
    gain_own = gains.astype(F32)

    front = gain_full[0] * (1.0 + scale_attn)
    if paired:
        first_all, pre, squares = project(ids, *x_parts, front, w_flat, w_parts[1])
    else:
        w_heads = jnp.concatenate(natural(w_parts), axis=1)
        x_f = jnp.concatenate(x_parts, axis=0).astype(F32)
        first_all = (x_f * inverse_rms(x_f) * front).astype(BF16)
        pre = jnp.stack([dot(first_all, w_heads[j]) for j in range(3)])
        squares = jnp.pad(jnp.sum(pre[:2] * pre[:2], -1), ((0, 6), (0, 0)))
    inverse = lax.rsqrt(row_sum(squares) / D + EPSILON)

    text_part = text_fwd(text_cols, w_text)
    text_pre = scatter_rot(rot_blocks(text_part, 2))
    inv_t = lax.rsqrt(
        pair_sum(jnp.sum(text_pre[0] * text_pre[0], -1, keepdims=True)) / D + EPSILON
    )
    normed_t = text_pre[0] * inv_t
    tk = (normed_t * gain_own[4]).astype(BF16)
    tv = text_pre[1].astype(BF16)

    head_tanh = jnp.tanh(cross_gate.astype(F32))
    gate_row = pad_cols(jnp.repeat(head_tanh, HD)[None], width)
    cosine, sine = rope_tables(places, width)
    gq, gk = pad_cols(gain_own[2:3], width), pad_cols(gain_own[3:4], width)
    pre_p, tkp, tvp = pad_cols(pre, width), pad_cols(tk, width), pad_cols(tv, width)
    q, k, v, mixed_p, so, co, ls, lc = attn_forward(
        caption_lengths, pre_p, inverse, gq, gk, cosine, sine, tkp, tvp, gate_row
    )
    mixed = mixed_p[:, :own_d]

    def rows(value, r):
        return value[r * local : (r + 1) * local]

    parts = [dot(rows(mixed, r), w_out) for r in range(n)]
    attn_branch = scatter_rot([parts[0]] + [p.astype(BF16) for p in parts[1:]])
    x_own = x_bf.astype(F32)
    after_attn = x_own + gate_attn * attn_branch
    inverse_two = inverse_rms(after_attn)
    normed_two = after_attn * inverse_two
    second = (normed_two * gain_full[1] * (1.0 + scale_ffn)).astype(BF16)

    second_all = jnp.concatenate(gather_rot(second), axis=0)
    branch_all = (gate_ffn * dy_all.astype(F32)).astype(BF16)
    wide_keep, wide_send, down_keep, down_send, ffn_own, ffn_rest, back_own, back_rest = ffn(
        ids, second_all, branch_all, w_gate_up, w_down, local, dpn, (bits[0], late[0])
    )
    (ffn_own, ffn_rest, back_own, back_rest), text_all = lax.optimization_barrier(
        ((ffn_own, ffn_rest, back_own, back_rest), text_all)
    )
    wide_chain = Halving(bits, bits, (wide_keep, wide_send))
    down_chain = Halving(bits, late, (down_keep, down_send))
    grad_second = scatter_rot([back_own] + [rows(back_rest, r) for r in range(n - 1)])
    ffn_branch = scatter_rot([ffn_own] + [rows(ffn_rest, r) for r in range(n - 1)])
    output = (after_attn + gate_ffn * ffn_branch).astype(BF16)
    dy = dy_bf.astype(F32)
    d_gate_ffn = jnp.sum(dy * ffn_branch, axis=0) * (1.0 - gate_ffn[0] * gate_ffn[0])

    scaled = grad_second * normed_two
    d_scale_ffn = jnp.sum(scaled * gain_full[1], axis=0)
    gain_two = jnp.sum(scaled * (1.0 + scale_ffn), axis=0)
    grad_after = dy + rms_back(
        grad_second * gain_full[1] * (1.0 + scale_ffn), normed_two, inverse_two
    )
    d_gate_attn = jnp.sum(grad_after * attn_branch, axis=0) * (1.0 - gate_attn[0] * gate_attn[0])
    grad_attn = (gate_attn * grad_after).astype(BF16)
    grad_mixed, *halves = out_back(ids, gather_rot(grad_attn), w_out, mixed, dpn)
    out_chain = Halving(bits, bits, halves)
    blocks = pre_p.shape[2] // width
    cut = max(1, 2 * blocks // 3)
    grad_mixed = pad_cols(grad_mixed, width)
    inputs = (so, co, ls, lc, pre_p, inverse, gq, gk, cosine, sine, gate_row)
    part_a = attn_backward(0, cut, caption_lengths, q, k, v, tkp, tvp, grad_mixed, *inputs)
    part_a, grad_mixed = lax.optimization_barrier((part_a, grad_mixed))
    grad_mixed = advance([wide_chain, down_chain], grad_mixed)
    part_b = attn_backward(
        cut, blocks - cut, caption_lengths, q, k, v, tkp, tvp, grad_mixed, *inputs
    )
    dtk, dtv, gain_q, gain_k, gate_g = (
        jnp.concatenate([part_a[i], part_b[i]], axis=1)[:, :own_d] for i in (1, 2, 4, 5, 6)
    )
    means = row_sum(part_a[3] + part_b[3])[:2] / D
    gate_total = jnp.sum(gate_g[0].reshape(HEADS // n, HD), axis=1) * (
        1.0 - head_tanh * head_tanh
    )
    text_hat = dtk * gain_own[4]
    gain_text = jnp.sum(dtk * normed_t, axis=0, keepdims=True)
    mean_t = pair_sum(jnp.sum(text_hat * normed_t, -1, keepdims=True)) / D

    grad_tk = (inv_t * (text_hat - normed_t * mean_t)).astype(BF16)
    text_pair = jnp.stack([grad_tk, dtv.astype(BF16)])
    pair_all = jnp.concatenate(natural(gather_rot(text_pair)), axis=-1)
    outgoing = block_of(pair_all, f, 1).reshape(2, TEXT // n, dpn, share).transpose(2, 0, 1, 3)
    pair_chain = Exchange(relative(outgoing))

    ones, zeros = jnp.ones((1, tokens), F32), jnp.zeros((1, tokens), F32)
    if paired:
        stats = jnp.concatenate([inverse[:2], ones, means, zeros, zeros, zeros], axis=0)
        gain3 = jnp.stack([gain_own[2:3], gain_own[3:4], jnp.ones_like(gain_own[2:3])])
        *halves, own_part, peer_part = project_back(
            ids, part_a[0], part_b[0], pre, stats, gain3, first_all, w_flat, w_parts[1], dpn
        )
        qkv_chain = Halving(low_bits, low_bits, halves)
        parts = [own_part, peer_part]
    else:
        d = jnp.concatenate([part_a[0], part_b[0]], axis=2)[:, :, :own_d]
        inv, mean = inverse[:2, :, None], means[:, :, None]
        hat = d[:2] * gain_own[2:4][:, None] - pre[:2] * inv * mean
        grads = [(inv[0] * hat[0]).astype(BF16), (inv[1] * hat[1]).astype(BF16), d[2].astype(BF16)]
        wide = [dot(g, first_all, 0, 0).astype(BF16) for g in grads]
        wide = [jnp.concatenate(natural(exchange_rot(w_, 1)), axis=0) for w_ in wide]
        wide = relative(jnp.stack([w_.reshape(dpn, share, own_d) for w_ in wide], axis=1))
        wide = wide.reshape((dpn // 2, 2) + wide.shape[1:])
        qkv_chain = Halving(bits, bits, (wide[:, 0], wide[:, 1]))
        parts = [
            sum(dot(rows(g, r), w_heads[j], 1, 1) for j, g in enumerate(grads)) for r in range(n)
        ]
        parts = [parts[0]] + [p.astype(BF16) for p in parts[1:]]
    chains = [wide_chain, down_chain, out_chain]
    parts = advance([wide_chain, down_chain, out_chain, pair_chain], parts)
    grad_first = scatter_rot(parts)

    text_in = text_bwd(pair_all, w_text)
    text_in = advance([out_chain, pair_chain], text_in)
    text_in = jnp.concatenate(natural(exchange_rot(text_in, 0)), axis=1)

    inverse_one = inverse_rms(x_own)
    normed_one = x_own * inverse_one
    scaled = grad_first * normed_one
    d_scale_attn = jnp.sum(scaled * gain_full[0], axis=0)
    gain_one = jnp.sum(scaled * (1.0 + scale_attn), axis=0)
    grad_input = (
        grad_after
        + rms_back(grad_first * gain_full[0] * (1.0 + scale_attn), normed_one, inverse_one)
    ).astype(BF16)

    grad_input = advance([wide_chain, down_chain, qkv_chain], grad_input)

    sums = [d_scale_attn, d_gate_attn, d_scale_ffn, d_gate_ffn, gain_one, gain_two]
    sums = pair_sum(jnp.stack(sums))
    stamp = jnp.full((1, D), timesteps[0].astype(F32))
    gate_pad = jnp.pad(gate_total, (0, own_d - gate_total.shape[0]))[None]
    small = jnp.concatenate([block_of(sums[4:], f, 1), gain_q, gain_k, gain_text, gate_pad], axis=0)
    small_chain = Gather(
        jnp.concatenate([sums[:4], stamp, jnp.pad(small, ((0, 0), (0, D - own_d)))], axis=0)
    )

    def rest(chain):
        while chain.got is not None:
            chain.step()

    advance([pair_chain, out_chain, small_chain], ())
    rest(pair_chain)
    pair_cols = absolute(pair_chain.cur.reshape(pair_chain.shape))
    pair_cols = jnp.concatenate(natural(gather_rot(pair_cols)), axis=2)
    pair_cols = pair_cols.transpose(0, 2, 1, 3).reshape(dpn * TEXT, 2 * share)
    text_grad = dot(pair_cols, text_all, 0, 0).reshape(2, share, TW // n)
    text_grad = advance([qkv_chain, small_chain, wide_chain, down_chain], text_grad)
    for chain in (small_chain, qkv_chain, out_chain, wide_chain, down_chain):
        rest(chain)
    total = jnp.sum(small_chain.cur[:, 5:, :own_d], axis=0)
    mods = lax.dynamic_slice_in_dim(small_chain.cur[:, :4], me * share, share, 2)
    times = time_embed(small_chain.cur[:, 4, 0])
    times = lax.dynamic_slice_in_dim(times, f * own_te, own_te, 1).astype(F32)
    ada_grad = lax.dot_general(
        mods.reshape(dpn, 4 * share), times, (((0,), (0,)), ((), ())),
        precision=lax.Precision.HIGHEST,
    ).reshape(4, share, own_te)
    qkv_grad = qkv_chain.last[0]
    if paired:
        own_side = f == (me >> low_bits[-1] + 1)
        mine, got = exchange_rot(qkv_grad.astype(BF16), 2)
        keep, send = jnp.where(own_side, mine, got), jnp.where(own_side, got, mine)
        qkv_grad = keep.astype(F32) + dp_swap(send, bits[-1]).astype(F32)
    return (
        output[None],
        grad_input[None],
        text_in[None],
        ada_grad.transpose(2, 0, 1),
        text_grad.transpose(2, 0, 1),
        qkv_grad.transpose(2, 0, 1),
        out_chain.last[0].T,
        total[:5],
        total[5, : HEADS // n],
        wide_chain.last[0].transpose(1, 0, 2),
        down_chain.last[0].T,
    )


def solution(mesh):
    return jax.shard_map(
        on_device,
        mesh=mesh,
        in_specs=(
            P("dp", "fsdp", None),
            P("dp", "fsdp", None),
            P("dp"),
            P("dp"),
            P("dp", None, "fsdp"),
            P("dp", "fsdp", None),
            P("fsdp", None, None),
            P("fsdp", None, None),
            P("fsdp", None, None),
            P("fsdp", None),
            P(None, "fsdp"),
            P("fsdp"),
            P(None, None, "fsdp"),
            P("fsdp", None),
        ),
        out_specs=(
            P("dp", "fsdp", None),
            P("dp", "fsdp", None),
            P("dp", "fsdp", None),
            P("fsdp", None, "dp"),
            P("fsdp", None, "dp"),
            P("fsdp", None, "dp"),
            P("fsdp", "dp"),
            P(None, "fsdp"),
            P("fsdp"),
            P("dp", None, "fsdp"),
            P("fsdp", "dp"),
        ),
        check_vma=False,
    )
```

```python
import functools
import math

import jax
import jax.numpy as jnp
from jax import lax
from jax.experimental import pallas as pl
from jax.experimental.pallas import tpu as pltpu
from jax.sharding import PartitionSpec as P

D = 1536
HEADS = 24
HD = 64
TW = 4096
TE = 1024
PATCHES = 1024
TEXT = 256
EPSILON = 1e-06
F32 = jnp.float32
BF16 = jnp.bfloat16
QC = 256


def dot(a, b, ca=1, cb=0):
    return lax.dot_general(a, b, (((ca,), (cb,)), ((), ())), preferred_element_type=F32)


def from_behind(value, step):
    n = lax.axis_size("fsdp")
    return lax.ppermute(value, "fsdp", [(i, (i + step) % n) for i in range(n)])


def gather_rot(value):
    return [value] + [from_behind(value, r) for r in range(1, lax.axis_size("fsdp"))]


def pair_sum(value):
    return functools.reduce(lambda a, b: a + b, gather_rot(value))


def row_sum(value):
    n = lax.axis_size("fsdp")
    rows = value.shape[-1] // n
    total = value
    for r in range(1, n):
        total = total + jnp.roll(from_behind(value, r), r * rows, axis=-1)
    return total


def scatter_rot(blocks):
    n = lax.axis_size("fsdp")
    total = blocks[0].astype(F32)
    for r in range(1, n):
        got = lax.ppermute(blocks[r], "fsdp", [(i, (i - r) % n) for i in range(n)])
        total = total + got.astype(F32)
    return total


def block_of(value, index, axis):
    size = value.shape[axis] // lax.axis_size("fsdp")
    return lax.dynamic_slice_in_dim(value, index * size, size, axis)


def rot_blocks(value, axis):
    n, f = lax.axis_size("fsdp"), lax.axis_index("fsdp")
    return [block_of(value, (f - r) % n, axis) for r in range(n)]


def exchange_rot(value, axis):
    n, f = lax.axis_size("fsdp"), lax.axis_index("fsdp")
    out = [block_of(value, f, axis)]
    for r in range(1, n):
        out.append(from_behind(block_of(value, (f + r) % n, axis), r))
    return out


def natural(got):
    n, f = lax.axis_size("fsdp"), lax.axis_index("fsdp")
    if n == 2:
        return [jnp.where(f == 0, got[0], got[1]), jnp.where(f == 0, got[1], got[0])]
    got = jnp.stack(got)
    return [lax.dynamic_index_in_dim(got, (f - g) % n, 0, keepdims=False) for g in range(n)]


def dp_bits():
    return int(lax.axis_size("dp")).bit_length() - 1


def swapped(p):
    return (p & ~3) | ((p & 1) << 1) | ((p >> 1) & 1)


def turned(p, f):
    return p if dp_bits() < 3 else jnp.where(f % 2 == 0, p, swapped(p))


def dp_swap(value, bit):
    n, dpn = lax.axis_size("fsdp"), lax.axis_size("dp")
    pairs = []
    for i in range(dpn):
        for f in range(n):
            flip = 1 << bit if dp_bits() < 3 or f % 2 == 0 else swapped(1 << bit)
            pairs.append((i * n + f, (i ^ flip) * n + f))
    return lax.ppermute(value, ("dp", "fsdp"), pairs)


def relative(value):
    places = turned(jnp.arange(lax.axis_size("dp")), lax.axis_index("fsdp"))
    return jnp.take(value, lax.axis_index("dp") ^ places, axis=0)


def absolute(value):
    places = lax.axis_index("dp") ^ jnp.arange(lax.axis_size("dp"))
    return jnp.take(value, turned(places, lax.axis_index("fsdp")), axis=0)


class Halving:
    def __init__(self, order, keep, send):
        self.order = list(order)
        self.keep, self.got = keep, dp_swap(send, self.order.pop(0))

    def step(self):
        if self.got is None:
            return

        def add(part):
            return self.keep[part].astype(F32) + self.got[part].astype(F32)

        if not self.order:
            self.last = add(slice(None))
            self.got = None
            return
        half = self.keep.shape[0] // 2
        send = add(slice(half, None)).astype(BF16)
        self.keep = add(slice(half)).astype(BF16)
        self.got = dp_swap(send, self.order.pop(0))


def place_of(p, order):
    return sum((p >> bit & 1) << i for i, bit in enumerate(reversed(order)))


class Exchange:
    def __init__(self, value):
        self.bits, self.shape = list(range(dp_bits())), value.shape
        self.cur = value.reshape((2,) * dp_bits() + value.shape[1:])
        self.keep = self.got = None
        self.start()

    def start(self):
        if self.bits:
            self.bit = self.bits.pop(0)
            self.axis = dp_bits() - 1 - self.bit
            self.keep, send = (
                lax.index_in_dim(self.cur, i, self.axis, keepdims=False) for i in range(2)
            )
            self.got = dp_swap(send, self.bit)

    def step(self):
        if self.got is not None:
            self.cur = jnp.stack([self.keep, self.got], axis=self.axis)
            self.got = None
            self.start()


class Small:
    def __init__(self, parts, total):
        self.bits, self.shape, self.total = list(range(dp_bits())), parts.shape, total
        self.cur = parts.reshape((2,) * dp_bits() + parts.shape[1:])
        self.got = None
        self.start()

    def start(self):
        if self.bits:
            self.bit = self.bits.pop(0)
            self.axis = dp_bits() - 1 - self.bit
            self.keep, send = (
                lax.index_in_dim(self.cur, i, self.axis, keepdims=False) for i in range(2)
            )
            flat = jnp.concatenate([send.reshape(-1, 128), self.total], axis=0)
            self.got = dp_swap(flat, self.bit)

    def step(self):
        if self.got is not None:
            rows = self.keep.size // 128
            self.total = self.total + self.got[rows:]
            got = self.got[:rows].reshape(self.keep.shape)
            self.cur = jnp.stack([self.keep, got], axis=self.axis)
            self.got = None
            self.start()


def advance(chains, value):
    live = [c for c in chains if c.got is not None]
    value, got = lax.optimization_barrier((value, [c.got for c in live]))
    for c, g in zip(live, got):
        c.got = g
        c.step()
    return value


def rope_block(value, cosine, sine, sign):
    width = value.shape[1]
    lane = lax.broadcasted_iota(jnp.int32, value.shape, 1)
    partner = jnp.where(
        lane % 32 < 16, pltpu.roll(value, width - 16, 1), pltpu.roll(value, 16, 1)
    )
    return value * cosine + sign * (partner * sine)


def column(ref, index, width):
    row = ref[index : index + 1, :] if isinstance(index, int) else ref[pl.ds(index, 1), :]
    return jnp.broadcast_to(row, (width, row.shape[1])).T


def masked(value, head):
    lane = lax.broadcasted_iota(jnp.int32, value.shape, 1)
    return jnp.where(lane // HD == head, value, jnp.zeros_like(value))


def attn_fwd_kernel(
    len_ref, pre_ref, inv_ref, gq_ref, gk_ref, cos_ref, sin_ref, tk_ref, tv_ref, gate_ref,
    q_ref, k_ref, v_ref, mixed_ref, so_ref, co_ref, ls_ref, lc_ref,
):
    _, tokens, width = pre_ref.shape
    heads = width // HD
    iq, ik = column(inv_ref, 0, width), column(inv_ref, 1, width)
    q = rope_block(pre_ref[0] * iq * gq_ref[...], cos_ref[...], sin_ref[...], 1.0)
    q_ref[...] = q.astype(BF16)
    k = rope_block(pre_ref[1] * ik * gk_ref[...], cos_ref[...], sin_ref[...], 1.0)
    k_ref[...] = k.astype(BF16)
    v_ref[...] = pre_ref[2].astype(BF16)
    length = len_ref[0]

    def one(keys, values, qm, limit):
        s = dot(qm, keys, 1, 1)
        if limit is not None:
            slot = lax.broadcasted_iota(jnp.int32, s.shape, 1)
            s = jnp.where(slot < limit, s, -1e30)
        peak = jnp.max(s, axis=1, keepdims=True)
        e = jnp.exp(s - peak)
        total = jnp.sum(e, axis=1, keepdims=True)
        o = dot(e.astype(BF16), values)
        return o * (1.0 / total), peak + jnp.log(total)

    lane = lax.broadcasted_iota(jnp.int32, (tokens, width), 1)
    qs = q_ref[...] * jnp.asarray(HD**-0.5, BF16)
    so = co = stats = jnp.zeros((tokens, width), F32)
    for h in range(heads):
        qm = masked(qs, h)
        o, lse = one(k_ref[...], v_ref[...], qm, None)
        so = jnp.where(lane // HD == h, o, so)
        stats = jnp.where(lane == h, lse, stats)
        o, lse = one(tk_ref[...], tv_ref[...], qm, length)
        co = jnp.where(lane // HD == h, o, co)
        stats = jnp.where(lane == heads + h, lse, stats)
    so_ref[...] = so
    co_ref[...] = co
    mixed_ref[...] = (so + gate_ref[...] * co).astype(BF16)
    stats = stats.T
    ls_ref[0] = stats[:heads]
    lc_ref[0] = stats[heads : 2 * heads]


def attn_bwd_kernel(
    len_ref, q_ref, k_ref, v_ref, tk_ref, tv_ref, g_ref, so_ref, co_ref, ls_ref, lc_ref,
    pre_ref, inv_ref, gq_ref, gk_ref, cos_ref, sin_ref, gate_ref,
    d_ref, dtk_ref, dtv_ref, stat_ref, gainq_ref, gaink_ref, gateg_ref,
    gs_ref, gc_ref, ds_ref, dc_ref, kt_ref, tkt_ref, dqt_ref, dk_acc, dv_acc, rq_ref, rk_ref,
):
    tokens, width = q_ref.shape
    heads = width // HD
    scale = jnp.asarray(HD**-0.5, BF16)

    @pl.when(pl.program_id(0) == 0)
    def _():
        rq_ref[...] = jnp.zeros_like(rq_ref)
        rk_ref[...] = jnp.zeros_like(rk_ref)

    g = g_ref[...]
    gs_ref[...] = g.astype(BF16)
    gc_ref[...] = (g * gate_ref[...]).astype(BF16)
    prod_c = g * co_ref[...]
    gateg_ref[...] = jnp.sum(prod_c, axis=0, keepdims=True)
    prod_s = (g * so_ref[...]).T
    prod_c = (prod_c * gate_ref[...]).T
    for h in range(heads):
        ds_ref[h : h + 1, :] = jnp.sum(prod_s[h * HD : (h + 1) * HD], axis=0, keepdims=True)
        dc_ref[h : h + 1, :] = jnp.sum(prod_c[h * HD : (h + 1) * HD], axis=0, keepdims=True)
    kt_ref[...] = k_ref[...].astype(F32).T.astype(BF16)
    tkt_ref[...] = tk_ref[...].astype(F32).T.astype(BF16)
    dk_acc[...] = jnp.zeros_like(dk_acc)
    dv_acc[...] = jnp.zeros_like(dv_acc)
    dtk_ref[...] = jnp.zeros_like(dtk_ref)
    dtv_ref[...] = jnp.zeros_like(dtv_ref)
    length = len_ref[0]

    def one(keys, keys_t, values, qm, gm, lse, delta, head, limit):
        s = dot(keys, qm, 1, 1)
        p = jnp.exp(s - lse)
        if limit is not None:
            slot = lax.broadcasted_iota(jnp.int32, s.shape, 0)
            p = jnp.where(slot < limit, p, 0.0)
        dp = dot(values, gm, 1, 1)
        ds = (p * (dp - delta)).astype(BF16)
        dq = dot(keys_t[head * HD : (head + 1) * HD, :], ds)
        return dq, dot(ds, qm), dot(p.astype(BF16), gm)

    def chunk(c, carry):
        rows = pl.ds(pl.multiple_of(c * QC, QC), QC)
        qc = q_ref[rows, :] * scale
        for h in range(heads):
            qm = masked(qc, h)
            dq, dk, dv = one(
                k_ref[...], kt_ref, v_ref[...], qm, masked(gs_ref[rows, :], h),
                ls_ref[0, h : h + 1, rows], ds_ref[h : h + 1, rows], h, None,
            )
            dk_acc[...] += dk
            dv_acc[...] += dv
            dq2, dk, dv = one(
                tk_ref[...], tkt_ref, tv_ref[...], qm, masked(gc_ref[rows, :], h),
                lc_ref[0, h : h + 1, rows], dc_ref[h : h + 1, rows], h, length,
            )
            dtk_ref[...] += dk
            dtv_ref[...] += dv
            dqt_ref[h * HD : (h + 1) * HD, rows] = (dq + dq2) * HD**-0.5
        return carry

    lax.fori_loop(0, tokens // QC, chunk, 0)
    dq = rope_block(dqt_ref[...].T, cos_ref[...], sin_ref[...], -1.0)
    d_ref[0] = dq
    prod = dq * (pre_ref[0] * column(inv_ref, 0, width))
    gainq_ref[...] = jnp.sum(prod, axis=0, keepdims=True)
    rq_ref[...] += prod * gq_ref[...]
    dk = rope_block(dk_acc[...], cos_ref[...], sin_ref[...], -1.0)
    d_ref[1] = dk
    prod = dk * (pre_ref[1] * column(inv_ref, 1, width))
    gaink_ref[...] = jnp.sum(prod, axis=0, keepdims=True)
    rk_ref[...] += prod * gk_ref[...]
    d_ref[2] = dv_acc[...]

    @pl.when(pl.program_id(0) == pl.num_programs(0) - 1)
    def _():
        stat_ref[...] = jnp.zeros_like(stat_ref)
        for i, ref in enumerate((rq_ref, rk_ref)):
            stat_ref[i : i + 1, :] = jnp.sum(ref[...].T, axis=0, keepdims=True)


def specs(tokens, text, width, heads, at=0):
    col = pl.BlockSpec((tokens, width), lambda i: (0, i + at))
    three = pl.BlockSpec((3, tokens, width), lambda i: (0, 0, i + at))
    tcol = pl.BlockSpec((text, width), lambda i: (0, i + at))
    stat = pl.BlockSpec((8, tokens), lambda i: (0, 0))
    gain = pl.BlockSpec((1, width), lambda i: (0, i + at))
    table = pl.BlockSpec((tokens, width), lambda i: (0, 0))
    lse = pl.BlockSpec((1, heads, tokens), lambda i: (i + at, 0, 0))
    scalar = pl.BlockSpec(memory_space=pltpu.SMEM)
    return col, three, tcol, stat, gain, table, lse, scalar


def sds(shape, dtype=F32):
    return jax.ShapeDtypeStruct(shape, dtype)


def attn_forward(length, pre, inv, gq, gk, cosine, sine, tk, tv, gate):
    _, tokens, columns = pre.shape
    text, width = tk.shape[0], cosine.shape[1]
    heads, blocks = width // HD, columns // width
    col, three, tcol, stat, gain, table, lse, scalar = specs(tokens, text, width, heads)
    flat = (tokens, columns)
    return pl.pallas_call(
        attn_fwd_kernel,
        grid=(blocks,),
        in_specs=[scalar, three, stat, gain, gain, table, table, tcol, tcol, gain],
        out_specs=[col, col, col, col, col, col, lse, lse],
        out_shape=[sds(flat, BF16)] * 4 + [sds(flat)] * 2 + [sds((blocks, heads, tokens))] * 2,
    )(length, pre, inv, gq, gk, cosine, sine, tk, tv, gate)


def attn_backward(at, blocks, length, q, k, v, tk, tv, g, so, co, ls, lc, pre, inv, gq, gk, cosine, sine, gate):
    tokens = q.shape[0]
    text, width = tk.shape[0], cosine.shape[1]
    heads, columns = width // HD, blocks * width
    col, three, tcol, stat, gain, table, lse, scalar = specs(tokens, text, width, heads, at)
    _, three_o, tcol_o, _, gain_o, _, _, _ = specs(tokens, text, width, heads)
    return pl.pallas_call(
        attn_bwd_kernel,
        grid=(blocks,),
        in_specs=[scalar, col, col, col, tcol, tcol, col, col, col, lse, lse,
                  three, stat, gain, gain, table, table, gain],
        out_specs=[three_o, tcol_o, tcol_o, stat, gain_o, gain_o, gain_o],
        out_shape=[
            sds((3, tokens, columns)), sds((text, columns)), sds((text, columns)),
            sds((8, tokens)), sds((1, columns)), sds((1, columns)), sds((1, columns)),
        ],
        scratch_shapes=[
            pltpu.VMEM((tokens, width), BF16), pltpu.VMEM((tokens, width), BF16),
            pltpu.VMEM((heads, tokens), F32), pltpu.VMEM((heads, tokens), F32),
            pltpu.VMEM((width, tokens), BF16), pltpu.VMEM((width, text), BF16),
            pltpu.VMEM((width, tokens), F32),
            pltpu.VMEM((tokens, width), F32), pltpu.VMEM((tokens, width), F32),
            pltpu.VMEM((tokens, width), F32), pltpu.VMEM((tokens, width), F32),
        ],
    )(length, q, k, v, tk, tv, g, so, co, ls, lc, pre, inv, gq, gk, cosine, sine, gate)


def pick(rows, cols, step, part):
    i = lax.broadcasted_iota(jnp.int32, (rows, cols), 0)
    j = lax.broadcasted_iota(jnp.int32, (rows, cols), 1)
    hit = (j == step * i + part) if cols > rows else (i == step * j + part)
    return jnp.where(hit, 1.0, 0.0).astype(BF16)

def text_fwd_kernel(x_ref, w_ref, o_ref):
    @pl.when(pl.program_id(0) == 0)
    def _():
        o_ref[...] = jnp.zeros_like(o_ref)
    for b in range(w_ref.shape[0] // 128):
        rows = slice(b * 128, (b + 1) * 128)
        w = w_ref[rows].reshape(256, w_ref.shape[2])
        x = x_ref[:, rows]
        for j in range(2):
            spread = dot(x, pick(128, 256, 2, j)).astype(BF16)
            o_ref[j] += dot(spread, w)

def text_fwd(x, w):
    depth, _, cols = w.shape
    bk = 256
    return pl.pallas_call(
        text_fwd_kernel, grid=(depth // bk,),
        in_specs=[pl.BlockSpec((x.shape[0], bk), lambda i: (0, i)), pl.BlockSpec((bk, 2, cols), lambda i: (i, 0, 0))],
        out_specs=pl.BlockSpec((2, x.shape[0], cols), lambda i: (0, 0, 0)),
        out_shape=sds((2, x.shape[0], cols)),
    )(x, w)

def text_bwd_kernel(g_ref, w_ref, o_ref):
    for b in range(w_ref.shape[0] // 128):
        rows = slice(b * 128, (b + 1) * 128)
        w = w_ref[rows].reshape(256, w_ref.shape[2])
        total = 0.0
        for j in range(2):
            total = total + dot(g_ref[j], dot(pick(128, 256, 2, j), w).astype(BF16), 1, 1)
        o_ref[:, rows] = total.astype(BF16)

def text_bwd(g, w):
    depth, _, cols = w.shape
    bk = 256
    return pl.pallas_call(
        text_bwd_kernel, grid=(depth // bk,),
        in_specs=[pl.BlockSpec(g.shape, lambda i: (0, 0, 0)), pl.BlockSpec((bk, 2, cols), lambda i: (i, 0, 0))],
        out_specs=pl.BlockSpec((g.shape[1], bk), lambda i: (0, i)),
        out_shape=sds((g.shape[1], depth), BF16),
    )(g, w)

def put_relative(dst, src, me, f, count):
    rows = dst.shape[0] // count
    for p in range(count):
        start = pl.multiple_of((me ^ turned(p, f)) * rows, 16)
        dst[p * rows : (p + 1) * rows, :] = src[pl.ds(start, rows), :]


def put_halves(keep, send, value, count, order, slot=None):
    rows = value.shape[0] // count
    for p in range(count):
        place = place_of(p, order[1:])
        where = place if slot is None else (place, slot)
        (send if p >> order[0] & 1 else keep)[where] = value[p * rows : (p + 1) * rows]


def ffn_kernel(
    orders, id_ref, s_ref, b_ref, w_ref, d_ref,
    wk_ref, ws_ref, dk_ref, ds_ref, fo_ref, fp_ref, so_ref, sp_ref,
    st, bt, tmp, wg, wu, facc, sacc,
):
    step = pl.program_id(0)
    depth, _, cols = w_ref.shape
    own = fo_ref.shape[0]
    count = 2 * dk_ref.shape[0]

    @pl.when(step == 0)
    def _():
        for src, dst in ((s_ref, st), (b_ref, bt)):
            for c in range(depth // 256):
                part = slice(c * 256, (c + 1) * 256)
                tmp[part, :] = src[:, part].astype(F32).T.astype(BF16)
            put_relative(dst, tmp, id_ref[0], id_ref[1], count)
        facc[...] = jnp.zeros_like(facc)
        sacc[...] = jnp.zeros_like(sacc)

    for c in range(depth // 128):
        part = slice(c * 128, (c + 1) * 128)
        w = w_ref[part].reshape(256, cols)
        wg[part, :] = dot(pick(128, 256, 2, 0), w).astype(BF16)
        wu[part, :] = dot(pick(128, 256, 2, 1), w).astype(BF16)
    s, b = s_ref[...], b_ref[...]
    gate = dot(s, wg[...])
    up = dot(s, wu[...])
    back = dot(b, d_ref[...], 1, 1)
    sig = jax.nn.sigmoid(gate)
    silu = gate * sig
    hidden = (silu * up).astype(BF16)
    g_gate = (back * up * (sig + silu * (1.0 - sig))).astype(BF16)
    g_up = (back * silu).astype(BF16)
    put_halves(wk_ref, ws_ref, dot(st[...], g_gate).astype(BF16), count, orders[0], 0)
    put_halves(wk_ref, ws_ref, dot(st[...], g_up).astype(BF16), count, orders[0], 1)
    put_halves(dk_ref, ds_ref, dot(bt[...], hidden).astype(BF16), count, orders[1])
    facc[...] += dot(hidden, d_ref[...])
    sacc[...] += dot(g_gate, wg[...], 1, 1) + dot(g_up, wu[...], 1, 1)

    @pl.when(step == pl.num_programs(0) - 1)
    def _():
        fo_ref[...] = facc[:own]
        fp_ref[...] = facc[own:].astype(BF16)
        so_ref[...] = sacc[:own]
        sp_ref[...] = sacc[own:].astype(BF16)


def ffn(ids, s, b, w, d, local, dp, orders):
    tokens, depth = s.shape
    hid = d.shape[0]
    bc = min(256, hid)
    rest = tokens - local
    once = functools.partial(pl.BlockSpec, pipeline_mode=pl.Buffered(1))
    const = lambda i: (0, 0)
    share = depth // dp
    half = pl.BlockSpec((dp // 2, share, bc), lambda i: (0, 0, i))
    halves = pl.BlockSpec((dp // 2, 2, share, bc), lambda i: (0, 0, 0, i))
    return pl.pallas_call(
        functools.partial(ffn_kernel, orders),
        grid=(hid // bc,),
        in_specs=[
            pl.BlockSpec(memory_space=pltpu.SMEM),
            once((tokens, depth), const), once((tokens, depth), const),
            pl.BlockSpec((depth, 2, bc), lambda i: (0, 0, i)),
            pl.BlockSpec((bc, depth), lambda i: (i, 0)),
        ],
        out_specs=[halves] * 2 + [half] * 2 + [
            once((local, depth), const), once((rest, depth), const),
            once((local, depth), const), once((rest, depth), const),
        ],
        out_shape=[sds((dp // 2, 2, share, hid), BF16)] * 2 + [sds((dp // 2, share, hid), BF16)] * 2 + [
            sds((local, depth)), sds((rest, depth), BF16),
            sds((local, depth)), sds((rest, depth), BF16),
        ],
        scratch_shapes=[
            pltpu.VMEM((depth, tokens), BF16), pltpu.VMEM((depth, tokens), BF16),
            pltpu.VMEM((depth, tokens), BF16),
            pltpu.VMEM((depth, bc), BF16), pltpu.VMEM((depth, bc), BF16),
            pltpu.VMEM((tokens, depth), F32), pltpu.VMEM((tokens, depth), F32),
        ],
        compiler_params=pltpu.CompilerParams(vmem_limit_bytes=62 << 20),
    )(ids, s, b, w, d)


def project_kernel(id_ref, xo_ref, xp_ref, front_ref, w_ref, got_ref, first_ref, pre_ref, sq_ref):
    j = pl.program_id(0)
    local, depth = xo_ref.shape
    own = got_ref.shape[2]
    f = id_ref[1]

    @pl.when(j == 0)
    def _():
        for i, ref in enumerate((xo_ref, xp_ref)):
            x = ref[...].astype(F32)
            inv = lax.rsqrt(jnp.sum(x * x, axis=1, keepdims=True) * (1.0 / depth) + EPSILON)
            first_ref[i * local : (i + 1) * local, :] = (x * inv * front_ref[...]).astype(BF16)
        sq_ref[...] = jnp.zeros_like(sq_ref)

    mine = pl.ds(pl.multiple_of(f * own, 128), own)
    other = pl.ds(pl.multiple_of((1 - f) * own, 128), own)
    out = dot(first_ref[:, mine], w_ref[0, :, mine]) + dot(first_ref[:, other], got_ref[0])
    pre_ref[0] = out
    square = out * out
    part = square[:, :128]
    for c in range(1, own // 128):
        part = part + square[:, c * 128 : (c + 1) * 128]
    sq_ref[pl.ds(j, 1), :] = jnp.sum(part.T, axis=0, keepdims=True)


def project(ids, xo, xp, front, w, got):
    local, depth = xo.shape
    own = got.shape[2]
    tokens = 2 * local
    const = lambda j: (0, 0)
    return pl.pallas_call(
        project_kernel,
        grid=(3,),
        in_specs=[
            pl.BlockSpec(memory_space=pltpu.SMEM),
            pl.BlockSpec((local, depth), const), pl.BlockSpec((local, depth), const),
            pl.BlockSpec((1, depth), const),
            pl.BlockSpec((1, own, depth), lambda j: (j, 0, 0)),
            pl.BlockSpec((1, own, own), lambda j: (j, 0, 0)),
        ],
        out_specs=[
            pl.BlockSpec((tokens, depth), const),
            pl.BlockSpec((1, tokens, own), lambda j: (j, 0, 0)),
            pl.BlockSpec((8, tokens), const),
        ],
        out_shape=[sds((tokens, depth), BF16), sds((3, tokens, own)), sds((8, tokens))],
    )(ids, xo, xp, front, w, got)


def project_grad_kernel(
    orders, id_ref, da_ref, db_ref, pre_ref, stat_ref, gain_ref, first_ref,
    keep_ref, send_ref, vkeep_ref, vsend_ref, g_ref, gt, tmp,
):
    order, late = orders
    j = pl.program_id(0)
    own = pre_ref.shape[2]
    cut = da_ref.shape[2]
    count = 2 * keep_ref.shape[0]
    inv, mean = column(stat_ref, j, 128), column(stat_ref, j + 3, 128)
    for c in range(own // 128):
        part = slice(c * 128, (c + 1) * 128)
        here = slice(c * 128 - cut, (c + 1) * 128 - cut) if c * 128 >= cut else part
        d = (db_ref if c * 128 >= cut else da_ref)[0, :, here]
        g = inv * (d * gain_ref[0, :, part] - pre_ref[0, :, part] * inv * mean)
        tmp[part, :] = g.T.astype(BF16)
        g_ref[0, :, part] = g.astype(BF16)
    put_relative(gt, tmp, id_ref[0] % count, id_ref[1], count)
    wide = dot(gt[...], first_ref[...]).astype(BF16)

    @pl.when(j < 2)
    def _():
        put_halves(keep_ref, send_ref, wide, count, order, j)

    @pl.when(j == 2)
    def _():
        put_halves(vkeep_ref, vsend_ref, wide, count, late)


def project_grad(ids, da, db, pre, stats, gain, first, dp, orders):
    _, tokens, own = pre.shape
    depth = first.shape[1]
    share = depth // dp
    const = lambda j: (0, 0)
    block = lambda j: (j, 0, 0)
    once = functools.partial(pl.BlockSpec, pipeline_mode=pl.Buffered(1))
    half = once((dp // 4, 2, share, depth), lambda j: (0, 0, 0, 0))
    vhalf = once((dp // 4, share, depth), lambda j: (0, 0, 0))
    return pl.pallas_call(
        functools.partial(project_grad_kernel, orders),
        grid=(3,),
        in_specs=[
            pl.BlockSpec(memory_space=pltpu.SMEM),
            pl.BlockSpec((1,) + da.shape[1:], block), pl.BlockSpec((1,) + db.shape[1:], block),
            pl.BlockSpec((1, tokens, own), block),
            pl.BlockSpec((8, tokens), const),
            pl.BlockSpec((1, 1, own), block),
            once((tokens, depth), const),
        ],
        out_specs=[half, half, vhalf, vhalf, pl.BlockSpec((1, tokens, own), block)],
        out_shape=[sds((dp // 4, 2, share, depth), BF16)] * 2
        + [sds((dp // 4, share, depth), BF16)] * 2
        + [sds((3, tokens, own), BF16)],
        scratch_shapes=[pltpu.VMEM((own, tokens), BF16), pltpu.VMEM((own, tokens), BF16)],
    )(ids, da, db, pre, stats, gain, first)


def project_back_kernel(id_ref, g_ref, w_ref, got_ref, own_ref, peer_ref, acc):
    j = pl.program_id(0)
    own = g_ref.shape[2]
    local = own_ref.shape[0]
    f = id_ref[1]
    mine = pl.ds(pl.multiple_of(f * own, 128), own)
    other = pl.ds(pl.multiple_of((1 - f) * own, 128), own)

    @pl.when(j == 0)
    def _():
        acc[...] = jnp.zeros_like(acc)

    acc[:, mine] += dot(g_ref[0], w_ref[0, :, mine], 1, 1)
    acc[:, other] += dot(g_ref[0], got_ref[0], 1, 1)

    @pl.when(j == 2)
    def _():
        own_ref[...] = acc[:local]
        peer_ref[...] = acc[local:].astype(BF16)


def project_back(ids, g, w, got):
    _, tokens, own = g.shape
    depth = w.shape[2]
    local = tokens // 2
    const = lambda j: (0, 0)
    block = lambda j: (j, 0, 0)
    once = functools.partial(pl.BlockSpec, pipeline_mode=pl.Buffered(1))
    return pl.pallas_call(
        project_back_kernel,
        grid=(3,),
        in_specs=[
            pl.BlockSpec(memory_space=pltpu.SMEM),
            pl.BlockSpec((1, tokens, own), block),
            pl.BlockSpec((1, own, depth), block), pl.BlockSpec((1, own, own), block),
        ],
        out_specs=[once((local, depth), const), once((local, depth), const)],
        out_shape=[sds((local, depth)), sds((local, depth), BF16)],
        scratch_shapes=[pltpu.VMEM((tokens, depth), F32)],
    )(ids, g, w, got)


def out_back_kernel(order, id_ref, *refs):
    n = len(refs) - 8
    blocks, (w_ref, mixed_ref, g_ref, keep_ref, send_ref, all_ref, gt, tmp) = refs[:n], refs[n:]
    local = blocks[0].shape[0]
    for r, ref in enumerate(blocks):
        all_ref[r * local : (r + 1) * local, :] = ref[...]
    grad = all_ref[...]
    g_ref[...] = dot(grad, w_ref[...], 1, 1)
    for c in range(grad.shape[1] // 256):
        part = slice(c * 256, (c + 1) * 256)
        tmp[part, :] = grad[:, part].astype(F32).T.astype(BF16)
    count = 2 * keep_ref.shape[0]
    put_relative(gt, tmp, id_ref[0], id_ref[1], count)
    put_halves(keep_ref, send_ref, dot(gt[...], mixed_ref[...]).astype(BF16), count, order)


def out_back(ids, blocks, w, mixed, dp, order):
    tokens, own = mixed.shape
    depth = w.shape[1]
    vmem = pl.BlockSpec(memory_space=pltpu.VMEM)
    half = sds((dp // 2, depth // dp, own), BF16)
    return pl.pallas_call(
        functools.partial(out_back_kernel, order),
        in_specs=[pl.BlockSpec(memory_space=pltpu.SMEM)] + [vmem] * (len(blocks) + 2),
        out_specs=[vmem] * 3,
        out_shape=[sds((tokens, own)), half, half],
        scratch_shapes=[
            pltpu.VMEM((tokens, depth), BF16),
            pltpu.VMEM((depth, tokens), BF16), pltpu.VMEM((depth, tokens), BF16),
        ],
    )(ids, *blocks, w, mixed)


def time_embed(timesteps):
    half = TE // 2
    frequencies = jnp.exp(-math.log(10000.0) * jnp.arange(half, dtype=F32) / half)
    angles = timesteps.astype(F32)[:, None] * frequencies
    waves = jnp.concatenate([jnp.cos(angles), jnp.sin(angles)], axis=-1)
    return jax.nn.silu(waves).astype(BF16)


def rope_tables(positions, width):
    lane = jnp.arange(width)
    quarter = HD // 4
    frequencies = 10000.0 ** (-(lane % quarter).astype(F32) / quarter)
    place = jnp.where(lane % HD < HD // 2, positions[0][:, None], positions[1][:, None])
    angles = place.astype(F32) * frequencies
    return jnp.cos(angles), jnp.where(lane % 32 < 16, -1.0, 1.0) * jnp.sin(angles)


def inverse_rms(values):
    return lax.rsqrt(jnp.mean(values * values, axis=-1, keepdims=True) + EPSILON)


def rms_back(grad_hat, normed, inverse):
    return inverse * (grad_hat - normed * jnp.mean(grad_hat * normed, axis=-1, keepdims=True))


def pad_cols(value, width):
    extra = -value.shape[-1] % width
    return value if extra == 0 else jnp.pad(value, [(0, 0)] * (value.ndim - 1) + [(0, extra)])


def on_device(
    hidden_in, text_state, caption_lengths, timesteps, patch_positions, cotangent,
    w_ada, w_text, w_qkv, w_out, gains, cross_gate, w_gate_up, w_down,
):
    n, f = lax.axis_size("fsdp"), lax.axis_index("fsdp")
    dpn, me = lax.axis_size("dp"), lax.axis_index("dp")
    bits = list(range(dp_bits()))
    low_bits = bits[:-1]
    late = bits[2:3] + bits[:2] + bits[3:]
    own_d = D // n
    local = hidden_in.shape[1]
    tokens = n * local
    width = 2 * HD
    share = D // dpn
    paired = n == 2 and dpn >= 4
    ids = jnp.stack([me, f]).astype(jnp.int32)
    x_bf, dy_bf = hidden_in[0], cotangent[0]

    time_low = time_embed(timesteps)
    own_te = TE // n
    time_own = lax.dynamic_slice_in_dim(time_low[0], f * own_te, own_te, 0)
    modulation = pair_sum(
        jnp.einsum("k,kjd->jd", time_own, w_ada, preferred_element_type=F32)
    )
    scale_attn, gate_attn = modulation[0:1], jnp.tanh(modulation[1:2])
    scale_ffn, gate_ffn = modulation[2:3], jnp.tanh(modulation[3:4])

    w_flat = jnp.moveaxis(w_qkv, 1, 0)
    w_parts = exchange_rot(w_flat, 2)
    x_parts = gather_rot(x_bf)
    dy_all = jnp.concatenate(gather_rot(dy_bf), axis=0)
    places = jnp.concatenate(gather_rot(patch_positions[0]), axis=1)
    text_cols = jnp.concatenate(natural(exchange_rot(text_state[0], 1)), axis=0)
    text_all = lax.all_gather(text_cols, "dp", axis=0, tiled=True)
    gain_full = lax.all_gather(gains, "fsdp", axis=1, tiled=True).astype(F32)
    gain_own = gains.astype(F32)

    front = gain_full[0] * (1.0 + scale_attn)
    if paired:
        first_all, pre, squares = project(ids, *x_parts, front, w_flat, w_parts[1])
    else:
        w_heads = jnp.concatenate(natural(w_parts), axis=1)
        x_f = jnp.concatenate(x_parts, axis=0).astype(F32)
        first_all = (x_f * inverse_rms(x_f) * front).astype(BF16)
        pre = jnp.stack([dot(first_all, w_heads[j]) for j in range(3)])
        squares = jnp.pad(jnp.sum(pre[:2] * pre[:2], -1), ((0, 6), (0, 0)))
    inverse = lax.rsqrt(row_sum(squares) / D + EPSILON)

    text_part = text_fwd(text_cols, w_text)
    text_pre = scatter_rot(rot_blocks(text_part, 2))
    inv_t = lax.rsqrt(
        pair_sum(jnp.sum(text_pre[0] * text_pre[0], -1, keepdims=True)) / D + EPSILON
    )
    normed_t = text_pre[0] * inv_t
    tk = (normed_t * gain_own[4]).astype(BF16)
    tv = text_pre[1].astype(BF16)

    head_tanh = jnp.tanh(cross_gate.astype(F32))
    gate_row = pad_cols(jnp.repeat(head_tanh, HD)[None], width)
    cosine, sine = rope_tables(places, width)
    gq, gk = pad_cols(gain_own[2:3], width), pad_cols(gain_own[3:4], width)
    pre_p, tkp, tvp = pad_cols(pre, width), pad_cols(tk, width), pad_cols(tv, width)
    q, k, v, mixed_p, so, co, ls, lc = attn_forward(
        caption_lengths, pre_p, inverse, gq, gk, cosine, sine, tkp, tvp, gate_row
    )
    mixed = mixed_p[:, :own_d]

    def rows(value, r):
        return value[r * local : (r + 1) * local]

    parts = [dot(rows(mixed, r), w_out) for r in range(n)]
    attn_branch = scatter_rot([parts[0]] + [p.astype(BF16) for p in parts[1:]])
    x_own = x_bf.astype(F32)
    after_attn = x_own + gate_attn * attn_branch
    inverse_two = inverse_rms(after_attn)
    normed_two = after_attn * inverse_two
    second = (normed_two * gain_full[1] * (1.0 + scale_ffn)).astype(BF16)

    second_all = jnp.concatenate(gather_rot(second), axis=0)
    branch_all = (gate_ffn * dy_all.astype(F32)).astype(BF16)
    wide_keep, wide_send, down_keep, down_send, ffn_own, ffn_rest, back_own, back_rest = ffn(
        ids, second_all, branch_all, w_gate_up, w_down, local, dpn, (bits, late)
    )
    (ffn_own, ffn_rest, back_own, back_rest), text_all = lax.optimization_barrier(
        ((ffn_own, ffn_rest, back_own, back_rest), text_all)
    )
    wide_chain = Halving(bits, wide_keep, wide_send)
    down_chain = Halving(late, down_keep, down_send)
    grad_second = scatter_rot([back_own] + [rows(back_rest, r) for r in range(n - 1)])
    ffn_branch = scatter_rot([ffn_own] + [rows(ffn_rest, r) for r in range(n - 1)])
    output = (after_attn + gate_ffn * ffn_branch).astype(BF16)
    dy = dy_bf.astype(F32)
    d_gate_ffn = jnp.sum(dy * ffn_branch, axis=0) * (1.0 - gate_ffn[0] * gate_ffn[0])

    scaled = grad_second * normed_two
    d_scale_ffn = jnp.sum(scaled * gain_full[1], axis=0)
    gain_two = jnp.sum(scaled * (1.0 + scale_ffn), axis=0)
    grad_after = dy + rms_back(
        grad_second * gain_full[1] * (1.0 + scale_ffn), normed_two, inverse_two
    )
    d_gate_attn = jnp.sum(grad_after * attn_branch, axis=0) * (1.0 - gate_attn[0] * gate_attn[0])
    grad_attn = (gate_attn * grad_after).astype(BF16)
    grad_mixed, *halves = out_back(ids, gather_rot(grad_attn), w_out, mixed, dpn, bits)
    out_chain = Halving(bits, *halves)
    blocks = pre_p.shape[2] // width
    cut = max(1, 2 * blocks // 3)
    grad_mixed = pad_cols(grad_mixed, width)
    inputs = (so, co, ls, lc, pre_p, inverse, gq, gk, cosine, sine, gate_row)
    part_a = attn_backward(0, cut, caption_lengths, q, k, v, tkp, tvp, grad_mixed, *inputs)
    part_a, grad_mixed = lax.optimization_barrier((part_a, grad_mixed))
    grad_mixed = advance([wide_chain, down_chain], grad_mixed)
    part_b = attn_backward(
        cut, blocks - cut, caption_lengths, q, k, v, tkp, tvp, grad_mixed, *inputs
    )
    dtk, dtv, gain_q, gain_k, gate_g = (
        jnp.concatenate([part_a[i], part_b[i]], axis=1)[:, :own_d] for i in (1, 2, 4, 5, 6)
    )
    means = row_sum(part_a[3] + part_b[3])[:2] / D
    gate_total = jnp.sum(gate_g[0].reshape(HEADS // n, HD), axis=1) * (
        1.0 - head_tanh * head_tanh
    )
    text_hat = dtk * gain_own[4]
    gain_text = jnp.sum(dtk * normed_t, axis=0, keepdims=True)
    mean_t = pair_sum(jnp.sum(text_hat * normed_t, -1, keepdims=True)) / D

    grad_tk = (inv_t * (text_hat - normed_t * mean_t)).astype(BF16)
    text_pair = jnp.stack([grad_tk, dtv.astype(BF16)])
    pair_all = jnp.concatenate(natural(gather_rot(text_pair)), axis=-1)
    outgoing = block_of(pair_all, f, 1).reshape(2, TEXT // n, dpn, share).transpose(2, 0, 1, 3)
    pair_chain = Exchange(relative(outgoing))

    ones, zeros = jnp.ones((1, tokens), F32), jnp.zeros((1, tokens), F32)
    if paired:
        stats = jnp.concatenate([inverse[:2], ones, means, zeros, zeros, zeros], axis=0)
        gain3 = jnp.stack([gain_own[2:3], gain_own[3:4], jnp.ones_like(gain_own[2:3])])
        *halves, grads = project_grad(
            ids, part_a[0], part_b[0], pre, stats, gain3, first_all, dpn,
            (low_bits, low_bits[2:] + low_bits[:2]),
        )
        qkv_chains = [
            Halving(low_bits, *halves[:2]), Halving(low_bits[2:] + low_bits[:2], *halves[2:]),
        ]
        grads = advance([wide_chain, down_chain, out_chain, pair_chain], grads)
        parts = project_back(ids, grads, w_flat, w_parts[1])
    else:
        d = jnp.concatenate([part_a[0], part_b[0]], axis=2)[:, :, :own_d]
        inv, mean = inverse[:2, :, None], means[:, :, None]
        hat = d[:2] * gain_own[2:4][:, None] - pre[:2] * inv * mean
        grads = [(inv[0] * hat[0]).astype(BF16), (inv[1] * hat[1]).astype(BF16), d[2].astype(BF16)]
        wide = [dot(g, first_all, 0, 0).astype(BF16) for g in grads]
        wide = [jnp.concatenate(natural(exchange_rot(w_, 1)), axis=0) for w_ in wide]
        wide = relative(jnp.stack([w_.reshape(dpn, share, own_d) for w_ in wide], axis=1))
        wide = jnp.stack([wide[p] for p in sorted(range(dpn), key=lambda p: place_of(p, bits))])
        qkv_chains = [Halving(bits, wide[: dpn // 2], wide[dpn // 2 :])]
        parts = [
            sum(dot(rows(g, r), w_heads[j], 1, 1) for j, g in enumerate(grads)) for r in range(n)
        ]
        parts = [parts[0]] + [p.astype(BF16) for p in parts[1:]]
    parts = advance([out_chain, pair_chain], parts)
    grad_first = scatter_rot(parts)

    text_in = text_bwd(pair_all, w_text)
    text_in = advance([wide_chain, down_chain, *qkv_chains, out_chain, pair_chain], text_in)
    text_in = jnp.concatenate(natural(exchange_rot(text_in, 0)), axis=1)

    inverse_one = inverse_rms(x_own)
    normed_one = x_own * inverse_one
    scaled = grad_first * normed_one
    d_scale_attn = jnp.sum(scaled * gain_full[0], axis=0)
    gain_one = jnp.sum(scaled * (1.0 + scale_attn), axis=0)
    grad_input = (
        grad_after
        + rms_back(grad_first * gain_full[0] * (1.0 + scale_attn), normed_one, inverse_one)
    ).astype(BF16)


    sums = [d_scale_attn, d_gate_attn, d_scale_ffn, d_gate_ffn, gain_one, gain_two]
    sums = pair_sum(jnp.stack(sums))
    stamp = jnp.full((1, D), timesteps[0].astype(F32))
    gate_pad = jnp.pad(gate_total, (0, own_d - gate_total.shape[0]))[None]
    small = jnp.concatenate([block_of(sums[4:], f, 1), gain_q, gain_k, gain_text, gate_pad], axis=0)
    mods = jnp.concatenate([sums[:4], stamp], axis=0).reshape(5, dpn, share).transpose(1, 0, 2)
    mods = jnp.pad(mods, ((0, 0), (0, 3), (0, -share % 128)))
    small_chain = Small(relative(mods), small.reshape(-1, 128))

    def rest(chain):
        while chain.got is not None:
            chain.step()

    grad_input = advance([*qkv_chains, small_chain, pair_chain], grad_input)
    rest(pair_chain)
    pair_cols = absolute(pair_chain.cur.reshape(pair_chain.shape))
    pair_cols = jnp.concatenate(natural(gather_rot(pair_cols)), axis=2)
    pair_cols = pair_cols.transpose(0, 2, 1, 3).reshape(dpn * TEXT, 2 * share)
    text_grad = dot(pair_cols, text_all, 0, 0).reshape(2, share, TW // n)
    for chain in (*qkv_chains, small_chain, out_chain, wide_chain, down_chain):
        rest(chain)
    total = small_chain.total.reshape(6, own_d)
    mods = small_chain.cur.reshape(small_chain.shape)
    times = time_embed(mods[:, 4, 0])
    times = lax.dynamic_slice_in_dim(times, f * own_te, own_te, 1).astype(F32)
    ada_grad = lax.dot_general(
        mods[:, :4, :share].reshape(dpn, 4 * share), times, (((0,), (0,)), ((), ())),
        precision=lax.Precision.HIGHEST,
    ).reshape(4, share, own_te)
    qkv_grad = qkv_chains[0].last[0]
    if paired:
        qkv_grad = jnp.concatenate([qkv_grad, qkv_chains[1].last])
        own_side = f == (me >> low_bits[-1] + 1)
        mine, got = exchange_rot(qkv_grad.astype(BF16), 2)
        keep, send = jnp.where(own_side, mine, got), jnp.where(own_side, got, mine)
        qkv_grad = keep.astype(F32) + dp_swap(send, bits[-1]).astype(F32)
    return (
        output[None],
        grad_input[None],
        text_in[None],
        ada_grad.transpose(2, 0, 1),
        text_grad.transpose(2, 0, 1),
        qkv_grad.transpose(2, 0, 1),
        out_chain.last[0].T,
        total[:5],
        total[5, : HEADS // n],
        wide_chain.last[0].transpose(1, 0, 2),
        down_chain.last[0].T,
    )


def solution(mesh):
    return jax.shard_map(
        on_device,
        mesh=mesh,
        in_specs=(
            P("dp", "fsdp", None),
            P("dp", "fsdp", None),
            P("dp"),
            P("dp"),
            P("dp", None, "fsdp"),
            P("dp", "fsdp", None),
            P("fsdp", None, None),
            P("fsdp", None, None),
            P("fsdp", None, None),
            P("fsdp", None),
            P(None, "fsdp"),
            P("fsdp"),
            P(None, None, "fsdp"),
            P("fsdp", None),
        ),
        out_specs=(
            P("dp", "fsdp", None),
            P("dp", "fsdp", None),
            P("dp", "fsdp", None),
            P("fsdp", None, "dp"),
            P("fsdp", None, "dp"),
            P("fsdp", None, "dp"),
            P("fsdp", "dp"),
            P(None, "fsdp"),
            P("fsdp"),
            P("dp", None, "fsdp"),
            P("fsdp", "dp"),
        ),
        check_vma=False,
    )
```

```python
import functools
import math

import jax
import jax.numpy as jnp
from jax import lax
from jax.experimental import pallas as pl
from jax.experimental.pallas import tpu as pltpu
from jax.sharding import PartitionSpec as P

D = 1536
HEADS = 24
HD = 64
TW = 4096
TE = 1024
PATCHES = 1024
TEXT = 256
EPSILON = 1e-06
F32 = jnp.float32
BF16 = jnp.bfloat16
QC = 256


def dot(a, b, ca=1, cb=0):
    return lax.dot_general(a, b, (((ca,), (cb,)), ((), ())), preferred_element_type=F32)


def from_behind(value, step):
    n = lax.axis_size("fsdp")
    return lax.ppermute(value, "fsdp", [(i, (i + step) % n) for i in range(n)])


def gather_rot(value):
    return [value] + [from_behind(value, r) for r in range(1, lax.axis_size("fsdp"))]


def pair_sum(value):
    return functools.reduce(lambda a, b: a + b, gather_rot(value))


def row_sum(value):
    n = lax.axis_size("fsdp")
    rows = value.shape[-1] // n
    total = value
    for r in range(1, n):
        total = total + jnp.roll(from_behind(value, r), r * rows, axis=-1)
    return total


def scatter_rot(blocks):
    n = lax.axis_size("fsdp")
    total = blocks[0].astype(F32)
    for r in range(1, n):
        got = lax.ppermute(blocks[r], "fsdp", [(i, (i - r) % n) for i in range(n)])
        total = total + got.astype(F32)
    return total


def block_of(value, index, axis):
    size = value.shape[axis] // lax.axis_size("fsdp")
    return lax.dynamic_slice_in_dim(value, index * size, size, axis)


def rot_blocks(value, axis):
    n, f = lax.axis_size("fsdp"), lax.axis_index("fsdp")
    return [block_of(value, (f - r) % n, axis) for r in range(n)]


def exchange_rot(value, axis):
    n, f = lax.axis_size("fsdp"), lax.axis_index("fsdp")
    out = [block_of(value, f, axis)]
    for r in range(1, n):
        out.append(from_behind(block_of(value, (f + r) % n, axis), r))
    return out


def natural(got):
    n, f = lax.axis_size("fsdp"), lax.axis_index("fsdp")
    if n == 2:
        return [jnp.where(f == 0, got[0], got[1]), jnp.where(f == 0, got[1], got[0])]
    got = jnp.stack(got)
    return [lax.dynamic_index_in_dim(got, (f - g) % n, 0, keepdims=False) for g in range(n)]


def dp_bits():
    return int(lax.axis_size("dp")).bit_length() - 1


def swapped(p):
    return (p & ~3) | ((p & 1) << 1) | ((p >> 1) & 1)


def turned(p, f):
    return p if dp_bits() < 3 else jnp.where(f % 2 == 0, p, swapped(p))


def dp_swap(value, bit):
    n, dpn = lax.axis_size("fsdp"), lax.axis_size("dp")
    pairs = []
    for i in range(dpn):
        for f in range(n):
            flip = 1 << bit if dp_bits() < 3 or f % 2 == 0 else swapped(1 << bit)
            pairs.append((i * n + f, (i ^ flip) * n + f))
    return lax.ppermute(value, ("dp", "fsdp"), pairs)


def relative(value):
    places = turned(jnp.arange(lax.axis_size("dp")), lax.axis_index("fsdp"))
    return jnp.take(value, lax.axis_index("dp") ^ places, axis=0)


def absolute(value):
    places = lax.axis_index("dp") ^ jnp.arange(lax.axis_size("dp"))
    return jnp.take(value, turned(places, lax.axis_index("fsdp")), axis=0)


class Halving:
    def __init__(self, order, keep, send):
        self.order = list(order)
        self.keep, self.got = keep, dp_swap(send, self.order.pop(0))

    def step(self):
        if self.got is None:
            return

        def add(part):
            return self.keep[part].astype(F32) + self.got[part].astype(F32)

        if not self.order:
            self.last = add(slice(None))
            self.got = None
            return
        half = self.keep.shape[0] // 2
        send = add(slice(half, None)).astype(BF16)
        self.keep = add(slice(half)).astype(BF16)
        self.got = dp_swap(send, self.order.pop(0))


def place_of(p, order):
    return sum((p >> bit & 1) << i for i, bit in enumerate(reversed(order)))


class Exchange:
    def __init__(self, value):
        self.bits, self.shape = list(range(dp_bits())), value.shape
        self.cur = value.reshape((2,) * dp_bits() + value.shape[1:])
        self.keep = self.got = None
        self.start()

    def start(self):
        if self.bits:
            self.bit = self.bits.pop(0)
            self.axis = dp_bits() - 1 - self.bit
            self.keep, send = (
                lax.index_in_dim(self.cur, i, self.axis, keepdims=False) for i in range(2)
            )
            self.got = dp_swap(send, self.bit)

    def step(self):
        if self.got is not None:
            self.cur = jnp.stack([self.keep, self.got], axis=self.axis)
            self.got = None
            self.start()


class Small:
    def __init__(self, parts, total):
        self.bits, self.shape, self.total = list(range(dp_bits())), parts.shape, total
        self.cur = parts.reshape((2,) * dp_bits() + parts.shape[1:])
        self.got = None
        self.start()

    def start(self):
        if self.bits:
            self.bit = self.bits.pop(0)
            self.axis = dp_bits() - 1 - self.bit
            self.keep, send = (
                lax.index_in_dim(self.cur, i, self.axis, keepdims=False) for i in range(2)
            )
            flat = jnp.concatenate([send.reshape(-1, 128), self.total], axis=0)
            self.got = dp_swap(flat, self.bit)

    def step(self):
        if self.got is not None:
            rows = self.keep.size // 128
            self.total = self.total + self.got[rows:]
            got = self.got[:rows].reshape(self.keep.shape)
            self.cur = jnp.stack([self.keep, got], axis=self.axis)
            self.got = None
            self.start()


def advance(chains, value):
    live = [c for c in chains if c.got is not None]
    value, got = lax.optimization_barrier((value, [c.got for c in live]))
    for c, g in zip(live, got):
        c.got = g
        c.step()
    return value


def rope_block(value, cosine, sine, sign):
    width = value.shape[1]
    lane = lax.broadcasted_iota(jnp.int32, value.shape, 1)
    partner = jnp.where(
        lane % 32 < 16, pltpu.roll(value, width - 16, 1), pltpu.roll(value, 16, 1)
    )
    return value * cosine + sign * (partner * sine)


def column(ref, index, width):
    row = ref[index : index + 1, :] if isinstance(index, int) else ref[pl.ds(index, 1), :]
    return jnp.broadcast_to(row, (width, row.shape[1])).T


def masked(value, head):
    lane = lax.broadcasted_iota(jnp.int32, value.shape, 1)
    return jnp.where(lane // HD == head, value, jnp.zeros_like(value))


def attn_fwd_kernel(
    len_ref, pre_ref, inv_ref, gq_ref, gk_ref, cos_ref, sin_ref, tk_ref, tv_ref, gate_ref,
    q_ref, k_ref, v_ref, mixed_ref, so_ref, co_ref, ls_ref, lc_ref,
):
    _, tokens, width = pre_ref.shape
    heads = width // HD
    iq, ik = column(inv_ref, 0, width), column(inv_ref, 1, width)
    q = rope_block(pre_ref[0] * iq * gq_ref[...], cos_ref[...], sin_ref[...], 1.0)
    q_ref[...] = q.astype(BF16)
    k = rope_block(pre_ref[1] * ik * gk_ref[...], cos_ref[...], sin_ref[...], 1.0)
    k_ref[...] = k.astype(BF16)
    v_ref[...] = pre_ref[2].astype(BF16)
    length = len_ref[0]

    def one(keys, values, qm, limit):
        s = dot(qm, keys, 1, 1)
        if limit is not None:
            slot = lax.broadcasted_iota(jnp.int32, s.shape, 1)
            s = jnp.where(slot < limit, s, -1e30)
        peak = jnp.max(s, axis=1, keepdims=True)
        e = jnp.exp(s - peak)
        total = jnp.sum(e, axis=1, keepdims=True)
        o = dot(e.astype(BF16), values)
        return o * (1.0 / total), peak + jnp.log(total)

    lane = lax.broadcasted_iota(jnp.int32, (tokens, width), 1)
    qs = q_ref[...] * jnp.asarray(HD**-0.5, BF16)
    so = co = stats = jnp.zeros((tokens, width), F32)
    for h in range(heads):
        qm = masked(qs, h)
        o, lse = one(k_ref[...], v_ref[...], qm, None)
        so = jnp.where(lane // HD == h, o, so)
        stats = jnp.where(lane == h, lse, stats)
        o, lse = one(tk_ref[...], tv_ref[...], qm, length)
        co = jnp.where(lane // HD == h, o, co)
        stats = jnp.where(lane == heads + h, lse, stats)
    so_ref[...] = so
    co_ref[...] = co
    mixed_ref[...] = (so + gate_ref[...] * co).astype(BF16)
    stats = stats.T
    ls_ref[0] = stats[:heads]
    lc_ref[0] = stats[heads : 2 * heads]


def attn_bwd_kernel(
    len_ref, q_ref, k_ref, v_ref, tk_ref, tv_ref, g_ref, so_ref, co_ref, ls_ref, lc_ref,
    pre_ref, inv_ref, gq_ref, gk_ref, cos_ref, sin_ref, gate_ref,
    d_ref, dtk_ref, dtv_ref, stat_ref, gainq_ref, gaink_ref, gateg_ref,
    gs_ref, gc_ref, ds_ref, dc_ref, kt_ref, tkt_ref, dqt_ref, dk_acc, dv_acc, rq_ref, rk_ref,
):
    tokens, width = q_ref.shape
    heads = width // HD
    scale = jnp.asarray(HD**-0.5, BF16)

    @pl.when(pl.program_id(0) == 0)
    def _():
        rq_ref[...] = jnp.zeros_like(rq_ref)
        rk_ref[...] = jnp.zeros_like(rk_ref)

    g = g_ref[...]
    gs_ref[...] = g.astype(BF16)
    gc_ref[...] = (g * gate_ref[...]).astype(BF16)
    prod_c = g * co_ref[...]
    gateg_ref[...] = jnp.sum(prod_c, axis=0, keepdims=True)
    prod_s = (g * so_ref[...]).T
    prod_c = (prod_c * gate_ref[...]).T
    for h in range(heads):
        ds_ref[h : h + 1, :] = jnp.sum(prod_s[h * HD : (h + 1) * HD], axis=0, keepdims=True)
        dc_ref[h : h + 1, :] = jnp.sum(prod_c[h * HD : (h + 1) * HD], axis=0, keepdims=True)
    kt_ref[...] = k_ref[...].astype(F32).T.astype(BF16)
    tkt_ref[...] = tk_ref[...].astype(F32).T.astype(BF16)
    dk_acc[...] = jnp.zeros_like(dk_acc)
    dv_acc[...] = jnp.zeros_like(dv_acc)
    dtk_ref[...] = jnp.zeros_like(dtk_ref)
    dtv_ref[...] = jnp.zeros_like(dtv_ref)
    length = len_ref[0]

    def one(keys, keys_t, values, qm, gm, lse, delta, head, limit):
        s = dot(keys, qm, 1, 1)
        p = jnp.exp(s - lse)
        if limit is not None:
            slot = lax.broadcasted_iota(jnp.int32, s.shape, 0)
            p = jnp.where(slot < limit, p, 0.0)
        dp = dot(values, gm, 1, 1)
        ds = (p * (dp - delta)).astype(BF16)
        dq = dot(keys_t[head * HD : (head + 1) * HD, :], ds)
        return dq, dot(ds, qm), dot(p.astype(BF16), gm)

    def chunk(c, carry):
        rows = pl.ds(pl.multiple_of(c * QC, QC), QC)
        qc = q_ref[rows, :] * scale
        for h in range(heads):
            qm = masked(qc, h)
            dq, dk, dv = one(
                k_ref[...], kt_ref, v_ref[...], qm, masked(gs_ref[rows, :], h),
                ls_ref[0, h : h + 1, rows], ds_ref[h : h + 1, rows], h, None,
            )
            dk_acc[...] += dk
            dv_acc[...] += dv
            dq2, dk, dv = one(
                tk_ref[...], tkt_ref, tv_ref[...], qm, masked(gc_ref[rows, :], h),
                lc_ref[0, h : h + 1, rows], dc_ref[h : h + 1, rows], h, length,
            )
            dtk_ref[...] += dk
            dtv_ref[...] += dv
            dqt_ref[h * HD : (h + 1) * HD, rows] = (dq + dq2) * HD**-0.5
        return carry

    lax.fori_loop(0, tokens // QC, chunk, 0)
    dq = rope_block(dqt_ref[...].T, cos_ref[...], sin_ref[...], -1.0)
    d_ref[0] = dq
    prod = dq * (pre_ref[0] * column(inv_ref, 0, width))
    gainq_ref[...] = jnp.sum(prod, axis=0, keepdims=True)
    rq_ref[...] += prod * gq_ref[...]
    dk = rope_block(dk_acc[...], cos_ref[...], sin_ref[...], -1.0)
    d_ref[1] = dk
    prod = dk * (pre_ref[1] * column(inv_ref, 1, width))
    gaink_ref[...] = jnp.sum(prod, axis=0, keepdims=True)
    rk_ref[...] += prod * gk_ref[...]
    d_ref[2] = dv_acc[...]

    @pl.when(pl.program_id(0) == pl.num_programs(0) - 1)
    def _():
        stat_ref[...] = jnp.zeros_like(stat_ref)
        for i, ref in enumerate((rq_ref, rk_ref)):
            stat_ref[i : i + 1, :] = jnp.sum(ref[...].T, axis=0, keepdims=True)


def specs(tokens, text, width, heads, at=0):
    col = pl.BlockSpec((tokens, width), lambda i: (0, i + at))
    three = pl.BlockSpec((3, tokens, width), lambda i: (0, 0, i + at))
    tcol = pl.BlockSpec((text, width), lambda i: (0, i + at))
    stat = pl.BlockSpec((8, tokens), lambda i: (0, 0))
    gain = pl.BlockSpec((1, width), lambda i: (0, i + at))
    table = pl.BlockSpec((tokens, width), lambda i: (0, 0))
    lse = pl.BlockSpec((1, heads, tokens), lambda i: (i + at, 0, 0))
    scalar = pl.BlockSpec(memory_space=pltpu.SMEM)
    return col, three, tcol, stat, gain, table, lse, scalar


def sds(shape, dtype=F32):
    return jax.ShapeDtypeStruct(shape, dtype)


def attn_forward(length, pre, inv, gq, gk, cosine, sine, tk, tv, gate):
    _, tokens, columns = pre.shape
    text, width = tk.shape[0], cosine.shape[1]
    heads, blocks = width // HD, columns // width
    col, three, tcol, stat, gain, table, lse, scalar = specs(tokens, text, width, heads)
    flat = (tokens, columns)
    return pl.pallas_call(
        attn_fwd_kernel,
        grid=(blocks,),
        in_specs=[scalar, three, stat, gain, gain, table, table, tcol, tcol, gain],
        out_specs=[col, col, col, col, col, col, lse, lse],
        out_shape=[sds(flat, BF16)] * 4 + [sds(flat)] * 2 + [sds((blocks, heads, tokens))] * 2,
    )(length, pre, inv, gq, gk, cosine, sine, tk, tv, gate)


def attn_backward(at, blocks, length, q, k, v, tk, tv, g, so, co, ls, lc, pre, inv, gq, gk, cosine, sine, gate):
    tokens = q.shape[0]
    text, width = tk.shape[0], cosine.shape[1]
    heads, columns = width // HD, blocks * width
    col, three, tcol, stat, gain, table, lse, scalar = specs(tokens, text, width, heads, at)
    _, three_o, tcol_o, _, gain_o, _, _, _ = specs(tokens, text, width, heads)
    return pl.pallas_call(
        attn_bwd_kernel,
        grid=(blocks,),
        in_specs=[scalar, col, col, col, tcol, tcol, col, col, col, lse, lse,
                  three, stat, gain, gain, table, table, gain],
        out_specs=[three_o, tcol_o, tcol_o, stat, gain_o, gain_o, gain_o],
        out_shape=[
            sds((3, tokens, columns)), sds((text, columns)), sds((text, columns)),
            sds((8, tokens)), sds((1, columns)), sds((1, columns)), sds((1, columns)),
        ],
        scratch_shapes=[
            pltpu.VMEM((tokens, width), BF16), pltpu.VMEM((tokens, width), BF16),
            pltpu.VMEM((heads, tokens), F32), pltpu.VMEM((heads, tokens), F32),
            pltpu.VMEM((width, tokens), BF16), pltpu.VMEM((width, text), BF16),
            pltpu.VMEM((width, tokens), F32),
            pltpu.VMEM((tokens, width), F32), pltpu.VMEM((tokens, width), F32),
            pltpu.VMEM((tokens, width), F32), pltpu.VMEM((tokens, width), F32),
        ],
    )(length, q, k, v, tk, tv, g, so, co, ls, lc, pre, inv, gq, gk, cosine, sine, gate)


def pick(rows, cols, step, part):
    i = lax.broadcasted_iota(jnp.int32, (rows, cols), 0)
    j = lax.broadcasted_iota(jnp.int32, (rows, cols), 1)
    hit = (j == step * i + part) if cols > rows else (i == step * j + part)
    return jnp.where(hit, 1.0, 0.0).astype(BF16)

def text_fwd_kernel(x_ref, w_ref, o_ref):
    @pl.when(pl.program_id(0) == 0)
    def _():
        o_ref[...] = jnp.zeros_like(o_ref)
    for b in range(w_ref.shape[0] // 128):
        rows = slice(b * 128, (b + 1) * 128)
        w = w_ref[rows].reshape(256, w_ref.shape[2])
        x = x_ref[:, rows]
        for j in range(2):
            spread = dot(x, pick(128, 256, 2, j)).astype(BF16)
            o_ref[j] += dot(spread, w)

def text_fwd(x, w):
    depth, _, cols = w.shape
    bk = 256
    return pl.pallas_call(
        text_fwd_kernel, grid=(depth // bk,),
        in_specs=[pl.BlockSpec((x.shape[0], bk), lambda i: (0, i)), pl.BlockSpec((bk, 2, cols), lambda i: (i, 0, 0))],
        out_specs=pl.BlockSpec((2, x.shape[0], cols), lambda i: (0, 0, 0)),
        out_shape=sds((2, x.shape[0], cols)),
    )(x, w)

def text_bwd_kernel(g_ref, w_ref, o_ref):
    for b in range(w_ref.shape[0] // 128):
        rows = slice(b * 128, (b + 1) * 128)
        w = w_ref[rows].reshape(256, w_ref.shape[2])
        total = 0.0
        for j in range(2):
            total = total + dot(g_ref[j], dot(pick(128, 256, 2, j), w).astype(BF16), 1, 1)
        o_ref[:, rows] = total.astype(BF16)

def text_bwd(g, w):
    depth, _, cols = w.shape
    bk = 256
    return pl.pallas_call(
        text_bwd_kernel, grid=(depth // bk,),
        in_specs=[pl.BlockSpec(g.shape, lambda i: (0, 0, 0)), pl.BlockSpec((bk, 2, cols), lambda i: (i, 0, 0))],
        out_specs=pl.BlockSpec((g.shape[1], bk), lambda i: (0, i)),
        out_shape=sds((g.shape[1], depth), BF16),
    )(g, w)

def put_relative(dst, src, me, f, count):
    rows = dst.shape[0] // count
    for p in range(count):
        start = pl.multiple_of((me ^ turned(p, f)) * rows, 16)
        dst[p * rows : (p + 1) * rows, :] = src[pl.ds(start, rows), :]


def put_halves(keep, send, value, count, order, slot=None):
    rows = value.shape[0] // count
    for p in range(count):
        place = place_of(p, order[1:])
        where = place if slot is None else (place, slot)
        (send if p >> order[0] & 1 else keep)[where] = value[p * rows : (p + 1) * rows]


def ffn_kernel(
    orders, id_ref, s_ref, b_ref, w_ref, d_ref,
    wk_ref, ws_ref, dk_ref, ds_ref, fo_ref, fp_ref, so_ref, sp_ref,
    st, bt, tmp, wg, wu, facc, sacc,
):
    step = pl.program_id(0)
    depth, _, cols = w_ref.shape
    own = fo_ref.shape[0]
    count = 2 * dk_ref.shape[0]

    @pl.when(step == 0)
    def _():
        for src, dst in ((s_ref, st), (b_ref, bt)):
            for c in range(depth // 256):
                part = slice(c * 256, (c + 1) * 256)
                tmp[part, :] = src[:, part].astype(F32).T.astype(BF16)
            put_relative(dst, tmp, id_ref[0], id_ref[1], count)
        facc[...] = jnp.zeros_like(facc)
        sacc[...] = jnp.zeros_like(sacc)

    for c in range(depth // 128):
        part = slice(c * 128, (c + 1) * 128)
        w = w_ref[part].reshape(256, cols)
        wg[part, :] = dot(pick(128, 256, 2, 0), w).astype(BF16)
        wu[part, :] = dot(pick(128, 256, 2, 1), w).astype(BF16)
    s, b = s_ref[...], b_ref[...]
    gate = dot(s, wg[...])
    up = dot(s, wu[...])
    back = dot(b, d_ref[...], 1, 1)
    sig = jax.nn.sigmoid(gate)
    silu = gate * sig
    hidden = (silu * up).astype(BF16)
    g_gate = (back * up * (sig + silu * (1.0 - sig))).astype(BF16)
    g_up = (back * silu).astype(BF16)
    put_halves(wk_ref, ws_ref, dot(st[...], g_gate).astype(BF16), count, orders[0], 0)
    put_halves(wk_ref, ws_ref, dot(st[...], g_up).astype(BF16), count, orders[0], 1)
    put_halves(dk_ref, ds_ref, dot(bt[...], hidden).astype(BF16), count, orders[1])
    facc[...] += dot(hidden, d_ref[...])
    sacc[...] += dot(g_gate, wg[...], 1, 1) + dot(g_up, wu[...], 1, 1)

    @pl.when(step == pl.num_programs(0) - 1)
    def _():
        fo_ref[...] = facc[:own]
        fp_ref[...] = facc[own:].astype(BF16)
        so_ref[...] = sacc[:own]
        sp_ref[...] = sacc[own:].astype(BF16)


def ffn(ids, s, b, w, d, local, dp, orders):
    tokens, depth = s.shape
    hid = d.shape[0]
    bc = min(256, hid)
    rest = tokens - local
    once = functools.partial(pl.BlockSpec, pipeline_mode=pl.Buffered(1))
    const = lambda i: (0, 0)
    share = depth // dp
    half = pl.BlockSpec((dp // 2, share, bc), lambda i: (0, 0, i))
    halves = pl.BlockSpec((dp // 2, 2, share, bc), lambda i: (0, 0, 0, i))
    return pl.pallas_call(
        functools.partial(ffn_kernel, orders),
        grid=(hid // bc,),
        in_specs=[
            pl.BlockSpec(memory_space=pltpu.SMEM),
            once((tokens, depth), const), once((tokens, depth), const),
            pl.BlockSpec((depth, 2, bc), lambda i: (0, 0, i)),
            pl.BlockSpec((bc, depth), lambda i: (i, 0)),
        ],
        out_specs=[halves] * 2 + [half] * 2 + [
            once((local, depth), const), once((rest, depth), const),
            once((local, depth), const), once((rest, depth), const),
        ],
        out_shape=[sds((dp // 2, 2, share, hid), BF16)] * 2 + [sds((dp // 2, share, hid), BF16)] * 2 + [
            sds((local, depth)), sds((rest, depth), BF16),
            sds((local, depth)), sds((rest, depth), BF16),
        ],
        scratch_shapes=[
            pltpu.VMEM((depth, tokens), BF16), pltpu.VMEM((depth, tokens), BF16),
            pltpu.VMEM((depth, tokens), BF16),
            pltpu.VMEM((depth, bc), BF16), pltpu.VMEM((depth, bc), BF16),
            pltpu.VMEM((tokens, depth), F32), pltpu.VMEM((tokens, depth), F32),
        ],
        compiler_params=pltpu.CompilerParams(vmem_limit_bytes=62 << 20),
    )(ids, s, b, w, d)


def project_kernel(id_ref, xo_ref, xp_ref, front_ref, w_ref, got_ref, first_ref, pre_ref, sq_ref):
    j = pl.program_id(0)
    local, depth = xo_ref.shape
    own = got_ref.shape[2]
    f = id_ref[1]

    @pl.when(j == 0)
    def _():
        for i, ref in enumerate((xo_ref, xp_ref)):
            x = ref[...].astype(F32)
            inv = lax.rsqrt(jnp.sum(x * x, axis=1, keepdims=True) * (1.0 / depth) + EPSILON)
            first_ref[i * local : (i + 1) * local, :] = (x * inv * front_ref[...]).astype(BF16)
        sq_ref[...] = jnp.zeros_like(sq_ref)

    mine = pl.ds(pl.multiple_of(f * own, 128), own)
    other = pl.ds(pl.multiple_of((1 - f) * own, 128), own)
    out = dot(first_ref[:, mine], w_ref[0, :, mine]) + dot(first_ref[:, other], got_ref[0])
    pre_ref[0] = out
    square = out * out
    part = square[:, :128]
    for c in range(1, own // 128):
        part = part + square[:, c * 128 : (c + 1) * 128]
    sq_ref[pl.ds(j, 1), :] = jnp.sum(part.T, axis=0, keepdims=True)


def project(ids, xo, xp, front, w, got):
    local, depth = xo.shape
    own = got.shape[2]
    tokens = 2 * local
    const = lambda j: (0, 0)
    return pl.pallas_call(
        project_kernel,
        grid=(3,),
        in_specs=[
            pl.BlockSpec(memory_space=pltpu.SMEM),
            pl.BlockSpec((local, depth), const), pl.BlockSpec((local, depth), const),
            pl.BlockSpec((1, depth), const),
            pl.BlockSpec((1, own, depth), lambda j: (j, 0, 0)),
            pl.BlockSpec((1, own, own), lambda j: (j, 0, 0)),
        ],
        out_specs=[
            pl.BlockSpec((tokens, depth), const),
            pl.BlockSpec((1, tokens, own), lambda j: (j, 0, 0)),
            pl.BlockSpec((8, tokens), const),
        ],
        out_shape=[sds((tokens, depth), BF16), sds((3, tokens, own)), sds((8, tokens))],
    )(ids, xo, xp, front, w, got)


def project_grad_kernel(
    orders, id_ref, da_ref, db_ref, pre_ref, stat_ref, gain_ref, first_ref, okeep_ref, osend_ref,
    keep_ref, send_ref, vkeep_ref, vsend_ref, g_ref, gt, tmp,
):
    order, late = orders
    j = pl.program_id(0)
    own = pre_ref.shape[2]
    cut = da_ref.shape[2]
    count = 2 * keep_ref.shape[0]
    inv, mean = column(stat_ref, j, 128), column(stat_ref, j + 3, 128)
    for c in range(own // 128):
        part = slice(c * 128, (c + 1) * 128)
        here = slice(c * 128 - cut, (c + 1) * 128 - cut) if c * 128 >= cut else part
        d = (db_ref if c * 128 >= cut else da_ref)[0, :, here]
        g = inv * (d * gain_ref[0, :, part] - pre_ref[0, :, part] * inv * mean)
        tmp[part, :] = g.T.astype(BF16)
        g_ref[0, :, part] = g.astype(BF16)
    put_relative(gt, tmp, id_ref[0] % count, id_ref[1], count)
    wide = dot(gt[...], first_ref[...]).astype(BF16)

    depth = first_ref.shape[1]

    @pl.when(j < 2)
    def _():
        put_halves(keep_ref.at[..., :depth], send_ref.at[..., :depth], wide, count, order, j)
        for src, dst in ((okeep_ref, keep_ref), (osend_ref, send_ref)):
            for p in range(dst.shape[0]):
                dst[p, j, :, depth:] = src[2 * p + j]

    @pl.when(j == 2)
    def _():
        put_halves(vkeep_ref, vsend_ref, wide, count, late)


def project_grad(ids, da, db, pre, stats, gain, first, okeep, osend, dp, orders):
    _, tokens, own = pre.shape
    depth = first.shape[1]
    share = depth // dp
    const = lambda j: (0, 0)
    block = lambda j: (j, 0, 0)
    once = functools.partial(pl.BlockSpec, pipeline_mode=pl.Buffered(1))
    half = once((dp // 4, 2, share, depth + own), lambda j: (0, 0, 0, 0))
    whole = once(okeep.shape, lambda j: (0, 0, 0))
    vhalf = once((dp // 4, share, depth), lambda j: (0, 0, 0))
    return pl.pallas_call(
        functools.partial(project_grad_kernel, orders),
        grid=(3,),
        in_specs=[
            pl.BlockSpec(memory_space=pltpu.SMEM),
            pl.BlockSpec((1,) + da.shape[1:], block), pl.BlockSpec((1,) + db.shape[1:], block),
            pl.BlockSpec((1, tokens, own), block),
            pl.BlockSpec((8, tokens), const),
            pl.BlockSpec((1, 1, own), block),
            once((tokens, depth), const), whole, whole,
        ],
        out_specs=[half, half, vhalf, vhalf, pl.BlockSpec((1, tokens, own), block)],
        out_shape=[sds((dp // 4, 2, share, depth + own), BF16)] * 2
        + [sds((dp // 4, share, depth), BF16)] * 2
        + [sds((3, tokens, own), BF16)],
        scratch_shapes=[pltpu.VMEM((own, tokens), BF16), pltpu.VMEM((own, tokens), BF16)],
    )(ids, da, db, pre, stats, gain, first, okeep, osend)


def project_back_kernel(id_ref, g_ref, w_ref, got_ref, own_ref, peer_ref, acc):
    j = pl.program_id(0)
    own = g_ref.shape[2]
    local = own_ref.shape[0]
    f = id_ref[1]
    mine = pl.ds(pl.multiple_of(f * own, 128), own)
    other = pl.ds(pl.multiple_of((1 - f) * own, 128), own)

    @pl.when(j == 0)
    def _():
        acc[...] = jnp.zeros_like(acc)

    acc[:, mine] += dot(g_ref[0], w_ref[0, :, mine], 1, 1)
    acc[:, other] += dot(g_ref[0], got_ref[0], 1, 1)

    @pl.when(j == 2)
    def _():
        own_ref[...] = acc[:local]
        peer_ref[...] = acc[local:].astype(BF16)


def project_back(ids, g, w, got):
    _, tokens, own = g.shape
    depth = w.shape[2]
    local = tokens // 2
    const = lambda j: (0, 0)
    block = lambda j: (j, 0, 0)
    once = functools.partial(pl.BlockSpec, pipeline_mode=pl.Buffered(1))
    return pl.pallas_call(
        project_back_kernel,
        grid=(3,),
        in_specs=[
            pl.BlockSpec(memory_space=pltpu.SMEM),
            pl.BlockSpec((1, tokens, own), block),
            pl.BlockSpec((1, own, depth), block), pl.BlockSpec((1, own, own), block),
        ],
        out_specs=[once((local, depth), const), once((local, depth), const)],
        out_shape=[sds((local, depth)), sds((local, depth), BF16)],
        scratch_shapes=[pltpu.VMEM((tokens, depth), F32)],
    )(ids, g, w, got)


def out_back_kernel(order, id_ref, *refs):
    n = len(refs) - 8
    blocks, (w_ref, mixed_ref, g_ref, keep_ref, send_ref, all_ref, gt, tmp) = refs[:n], refs[n:]
    local = blocks[0].shape[0]
    for r, ref in enumerate(blocks):
        all_ref[r * local : (r + 1) * local, :] = ref[...]
    grad = all_ref[...]
    g_ref[...] = dot(grad, w_ref[...], 1, 1)
    for c in range(grad.shape[1] // 256):
        part = slice(c * 256, (c + 1) * 256)
        tmp[part, :] = grad[:, part].astype(F32).T.astype(BF16)
    count = 2 * keep_ref.shape[0]
    put_relative(gt, tmp, id_ref[0], id_ref[1], count)
    put_halves(keep_ref, send_ref, dot(gt[...], mixed_ref[...]).astype(BF16), count, order)


def out_back(ids, blocks, w, mixed, dp, order):
    tokens, own = mixed.shape
    depth = w.shape[1]
    vmem = pl.BlockSpec(memory_space=pltpu.VMEM)
    half = sds((dp // 2, depth // dp, own), BF16)
    return pl.pallas_call(
        functools.partial(out_back_kernel, order),
        in_specs=[pl.BlockSpec(memory_space=pltpu.SMEM)] + [vmem] * (len(blocks) + 2),
        out_specs=[vmem] * 3,
        out_shape=[sds((tokens, own)), half, half],
        scratch_shapes=[
            pltpu.VMEM((tokens, depth), BF16),
            pltpu.VMEM((depth, tokens), BF16), pltpu.VMEM((depth, tokens), BF16),
        ],
    )(ids, *blocks, w, mixed)


def time_embed(timesteps):
    half = TE // 2
    frequencies = jnp.exp(-math.log(10000.0) * jnp.arange(half, dtype=F32) / half)
    angles = timesteps.astype(F32)[:, None] * frequencies
    waves = jnp.concatenate([jnp.cos(angles), jnp.sin(angles)], axis=-1)
    return jax.nn.silu(waves).astype(BF16)


def rope_tables(positions, width):
    lane = jnp.arange(width)
    quarter = HD // 4
    frequencies = 10000.0 ** (-(lane % quarter).astype(F32) / quarter)
    place = jnp.where(lane % HD < HD // 2, positions[0][:, None], positions[1][:, None])
    angles = place.astype(F32) * frequencies
    return jnp.cos(angles), jnp.where(lane % 32 < 16, -1.0, 1.0) * jnp.sin(angles)


def inverse_rms(values):
    return lax.rsqrt(jnp.mean(values * values, axis=-1, keepdims=True) + EPSILON)


def rms_back(grad_hat, normed, inverse):
    return inverse * (grad_hat - normed * jnp.mean(grad_hat * normed, axis=-1, keepdims=True))


def pad_cols(value, width):
    extra = -value.shape[-1] % width
    return value if extra == 0 else jnp.pad(value, [(0, 0)] * (value.ndim - 1) + [(0, extra)])


def on_device(
    hidden_in, text_state, caption_lengths, timesteps, patch_positions, cotangent,
    w_ada, w_text, w_qkv, w_out, gains, cross_gate, w_gate_up, w_down,
):
    n, f = lax.axis_size("fsdp"), lax.axis_index("fsdp")
    dpn, me = lax.axis_size("dp"), lax.axis_index("dp")
    bits = list(range(dp_bits()))
    low_bits = bits[:-1]
    late = bits[2:] + bits[:2]
    own_d = D // n
    local = hidden_in.shape[1]
    tokens = n * local
    width = 2 * HD
    share = D // dpn
    paired = n == 2 and dpn >= 4
    ids = jnp.stack([me, f]).astype(jnp.int32)
    x_bf, dy_bf = hidden_in[0], cotangent[0]

    time_low = time_embed(timesteps)
    own_te = TE // n
    time_own = lax.dynamic_slice_in_dim(time_low[0], f * own_te, own_te, 0)
    modulation = pair_sum(
        jnp.einsum("k,kjd->jd", time_own, w_ada, preferred_element_type=F32)
    )
    scale_attn, gate_attn = modulation[0:1], jnp.tanh(modulation[1:2])
    scale_ffn, gate_ffn = modulation[2:3], jnp.tanh(modulation[3:4])

    w_flat = jnp.moveaxis(w_qkv, 1, 0)
    w_parts = exchange_rot(w_flat, 2)
    x_parts = gather_rot(x_bf)
    dy_all = jnp.concatenate(gather_rot(dy_bf), axis=0)
    places = jnp.concatenate(gather_rot(patch_positions[0]), axis=1)
    text_cols = jnp.concatenate(natural(exchange_rot(text_state[0], 1)), axis=0)
    text_all = lax.all_gather(text_cols, "dp", axis=0, tiled=True)
    gain_full = lax.all_gather(gains, "fsdp", axis=1, tiled=True).astype(F32)
    gain_own = gains.astype(F32)

    front = gain_full[0] * (1.0 + scale_attn)
    if paired:
        first_all, pre, squares = project(ids, *x_parts, front, w_flat, w_parts[1])
    else:
        w_heads = jnp.concatenate(natural(w_parts), axis=1)
        x_f = jnp.concatenate(x_parts, axis=0).astype(F32)
        first_all = (x_f * inverse_rms(x_f) * front).astype(BF16)
        pre = jnp.stack([dot(first_all, w_heads[j]) for j in range(3)])
        squares = jnp.pad(jnp.sum(pre[:2] * pre[:2], -1), ((0, 6), (0, 0)))
    inverse = lax.rsqrt(row_sum(squares) / D + EPSILON)

    text_part = text_fwd(text_cols, w_text)
    text_pre = scatter_rot(rot_blocks(text_part, 2))
    inv_t = lax.rsqrt(
        pair_sum(jnp.sum(text_pre[0] * text_pre[0], -1, keepdims=True)) / D + EPSILON
    )
    normed_t = text_pre[0] * inv_t
    tk = (normed_t * gain_own[4]).astype(BF16)
    tv = text_pre[1].astype(BF16)

    head_tanh = jnp.tanh(cross_gate.astype(F32))
    gate_row = pad_cols(jnp.repeat(head_tanh, HD)[None], width)
    cosine, sine = rope_tables(places, width)
    gq, gk = pad_cols(gain_own[2:3], width), pad_cols(gain_own[3:4], width)
    pre_p, tkp, tvp = pad_cols(pre, width), pad_cols(tk, width), pad_cols(tv, width)
    q, k, v, mixed_p, so, co, ls, lc = attn_forward(
        caption_lengths, pre_p, inverse, gq, gk, cosine, sine, tkp, tvp, gate_row
    )
    mixed = mixed_p[:, :own_d]

    def rows(value, r):
        return value[r * local : (r + 1) * local]

    parts = [dot(rows(mixed, r), w_out) for r in range(n)]
    attn_branch = scatter_rot([parts[0]] + [p.astype(BF16) for p in parts[1:]])
    x_own = x_bf.astype(F32)
    after_attn = x_own + gate_attn * attn_branch
    inverse_two = inverse_rms(after_attn)
    normed_two = after_attn * inverse_two
    second = (normed_two * gain_full[1] * (1.0 + scale_ffn)).astype(BF16)

    second_all = jnp.concatenate(gather_rot(second), axis=0)
    branch_all = (gate_ffn * dy_all.astype(F32)).astype(BF16)
    wide_keep, wide_send, down_keep, down_send, ffn_own, ffn_rest, back_own, back_rest = ffn(
        ids, second_all, branch_all, w_gate_up, w_down, local, dpn, (bits, late)
    )
    (ffn_own, ffn_rest, back_own, back_rest), text_all = lax.optimization_barrier(
        ((ffn_own, ffn_rest, back_own, back_rest), text_all)
    )
    wide_chain = Halving(bits, wide_keep, wide_send)
    down_chain = Halving(late, down_keep, down_send)
    grad_second = scatter_rot([back_own] + [rows(back_rest, r) for r in range(n - 1)])
    ffn_branch = scatter_rot([ffn_own] + [rows(ffn_rest, r) for r in range(n - 1)])
    output = (after_attn + gate_ffn * ffn_branch).astype(BF16)
    dy = dy_bf.astype(F32)
    d_gate_ffn = jnp.sum(dy * ffn_branch, axis=0) * (1.0 - gate_ffn[0] * gate_ffn[0])

    scaled = grad_second * normed_two
    d_scale_ffn = jnp.sum(scaled * gain_full[1], axis=0)
    gain_two = jnp.sum(scaled * (1.0 + scale_ffn), axis=0)
    grad_after = dy + rms_back(
        grad_second * gain_full[1] * (1.0 + scale_ffn), normed_two, inverse_two
    )
    d_gate_attn = jnp.sum(grad_after * attn_branch, axis=0) * (1.0 - gate_attn[0] * gate_attn[0])
    grad_attn = (gate_attn * grad_after).astype(BF16)
    grad_mixed, *out_halves = out_back(ids, gather_rot(grad_attn), w_out, mixed, dpn, bits)
    blocks = pre_p.shape[2] // width
    cut = max(1, 2 * blocks // 3)
    grad_mixed = pad_cols(grad_mixed, width)
    inputs = (so, co, ls, lc, pre_p, inverse, gq, gk, cosine, sine, gate_row)
    part_a = attn_backward(0, cut, caption_lengths, q, k, v, tkp, tvp, grad_mixed, *inputs)
    part_a, grad_mixed = lax.optimization_barrier((part_a, grad_mixed))
    grad_mixed = advance([wide_chain, down_chain], grad_mixed)
    part_b = attn_backward(
        cut, blocks - cut, caption_lengths, q, k, v, tkp, tvp, grad_mixed, *inputs
    )
    means = row_sum(part_a[3] + part_b[3])[:2] / D

    ones, zeros = jnp.ones((1, tokens), F32), jnp.zeros((1, tokens), F32)
    if paired:
        stats = jnp.concatenate([inverse[:2], ones, means, zeros, zeros, zeros], axis=0)
        gain3 = jnp.stack([gain_own[2:3], gain_own[3:4], jnp.ones_like(gain_own[2:3])])
        low_late = low_bits[2:] + low_bits[:2]
        keep, send, v_keep, v_send, grads = project_grad(
            ids, part_a[0], part_b[0], pre, stats, gain3, first_all, *out_halves, dpn,
            (low_bits, low_late),
        )
        part_a, part_b, grads = advance([wide_chain], (part_a[1:], part_b[1:], grads))
        qkv_chains = [Halving(low_bits, keep, send), Halving(low_late, v_keep, v_send)]
        parts = project_back(ids, grads, w_flat, w_parts[1])
    else:
        d = jnp.concatenate([part_a[0], part_b[0]], axis=2)[:, :, :own_d]
        part_a, part_b = part_a[1:], part_b[1:]
        inv, mean = inverse[:2, :, None], means[:, :, None]
        hat = d[:2] * gain_own[2:4][:, None] - pre[:2] * inv * mean
        grads = [(inv[0] * hat[0]).astype(BF16), (inv[1] * hat[1]).astype(BF16), d[2].astype(BF16)]
        wide = [dot(g, first_all, 0, 0).astype(BF16) for g in grads]
        wide = [jnp.concatenate(natural(exchange_rot(w_, 1)), axis=0) for w_ in wide]
        wide = relative(jnp.stack([w_.reshape(dpn, share, own_d) for w_ in wide], axis=1))
        wide = jnp.stack([wide[p] for p in sorted(range(dpn), key=lambda p: place_of(p, bits))])
        qkv_chains = [
            Halving(bits, wide[: dpn // 2], wide[dpn // 2 :]), Halving(bits, *out_halves),
        ]
        parts = [
            sum(dot(rows(g, r), w_heads[j], 1, 1) for j, g in enumerate(grads)) for r in range(n)
        ]
        parts = [parts[0]] + [p.astype(BF16) for p in parts[1:]]
    grad_first = scatter_rot(parts)

    dtk, dtv, gain_q, gain_k, gate_g = (
        jnp.concatenate([part_a[i], part_b[i]], axis=1)[:, :own_d] for i in (0, 1, 3, 4, 5)
    )
    gate_total = jnp.sum(gate_g[0].reshape(HEADS // n, HD), axis=1) * (
        1.0 - head_tanh * head_tanh
    )
    text_hat = dtk * gain_own[4]
    gain_text = jnp.sum(dtk * normed_t, axis=0, keepdims=True)
    mean_t = pair_sum(jnp.sum(text_hat * normed_t, -1, keepdims=True)) / D
    grad_tk = (inv_t * (text_hat - normed_t * mean_t)).astype(BF16)
    text_pair = jnp.stack([grad_tk, dtv.astype(BF16)])
    pair_all = jnp.concatenate(natural(gather_rot(text_pair)), axis=-1)
    outgoing = block_of(pair_all, f, 1).reshape(2, TEXT // n, dpn, share).transpose(2, 0, 1, 3)
    pair_chain = Exchange(relative(outgoing))
    text_in = text_bwd(pair_all, w_text)
    text_in, grad_first = advance(
        [*qkv_chains, wide_chain, pair_chain], (text_in, grad_first)
    )
    text_in = jnp.concatenate(natural(exchange_rot(text_in, 0)), axis=1)

    inverse_one = inverse_rms(x_own)
    normed_one = x_own * inverse_one
    scaled = grad_first * normed_one
    d_scale_attn = jnp.sum(scaled * gain_full[0], axis=0)
    gain_one = jnp.sum(scaled * (1.0 + scale_attn), axis=0)
    grad_input = (
        grad_after
        + rms_back(grad_first * gain_full[0] * (1.0 + scale_attn), normed_one, inverse_one)
    ).astype(BF16)


    sums = [d_scale_attn, d_gate_attn, d_scale_ffn, d_gate_ffn, gain_one, gain_two]
    sums = pair_sum(jnp.stack(sums))
    stamp = jnp.full((1, D), timesteps[0].astype(F32))
    gate_pad = jnp.pad(gate_total, (0, own_d - gate_total.shape[0]))[None]
    small = jnp.concatenate([block_of(sums[4:], f, 1), gain_q, gain_k, gain_text, gate_pad], axis=0)
    mods = jnp.concatenate([sums[:4], stamp], axis=0).reshape(5, dpn, share).transpose(1, 0, 2)
    mods = jnp.pad(mods, ((0, 0), (0, 3), (0, -share % 128)))
    small_chain = Small(relative(mods), small.reshape(-1, 128))

    grad_input = advance([*qkv_chains, small_chain, pair_chain, down_chain], grad_input)
    advance([small_chain, pair_chain], ())
    advance([*qkv_chains, small_chain, pair_chain, down_chain], ())
    if paired:
        last, v_last = (c.last[0].astype(BF16) for c in qkv_chains)
        own_side = f == (me >> low_bits[-1] + 1)
        side = jnp.concatenate([last[:, :, :D], v_last[None]])
        mine, got = exchange_rot(side, 2)
        keep = jnp.concatenate([jnp.where(own_side, mine, got), last[:1, :, D:]])
        send = jnp.concatenate([jnp.where(own_side, got, mine), last[1:, :, D:]])
        final_chain = Halving(bits[-1:], keep, send)
    else:
        final_chain = qkv_chains[0]
    pair_cols = absolute(pair_chain.cur.reshape(pair_chain.shape))
    pair_cols = jnp.concatenate(natural(gather_rot(pair_cols)), axis=2)
    pair_cols = pair_cols.transpose(0, 2, 1, 3).reshape(dpn * TEXT, 2 * share)
    text_grad = dot(pair_cols, text_all, 0, 0).reshape(2, share, TW // n)

    def rest(chain):
        while chain.got is not None:
            chain.step()

    for chain in (pair_chain, small_chain, wide_chain, down_chain, *qkv_chains, final_chain):
        rest(chain)
    if paired:
        qkv_grad, out_grad = final_chain.last[:3], final_chain.last[3]
    else:
        qkv_grad, out_grad = qkv_chains[0].last[0], qkv_chains[1].last[0]
    total = small_chain.total.reshape(6, own_d)
    mods = small_chain.cur.reshape(small_chain.shape)
    times = time_embed(mods[:, 4, 0])
    times = lax.dynamic_slice_in_dim(times, f * own_te, own_te, 1).astype(F32)
    ada_grad = lax.dot_general(
        mods[:, :4, :share].reshape(dpn, 4 * share), times, (((0,), (0,)), ((), ())),
        precision=lax.Precision.HIGHEST,
    ).reshape(4, share, own_te)
    return (
        output[None],
        grad_input[None],
        text_in[None],
        ada_grad.transpose(2, 0, 1),
        text_grad.transpose(2, 0, 1),
        qkv_grad.transpose(2, 0, 1),
        out_grad.T,
        total[:5],
        total[5, : HEADS // n],
        wide_chain.last[0].transpose(1, 0, 2),
        down_chain.last[0].T,
    )


def solution(mesh):
    return jax.shard_map(
        on_device,
        mesh=mesh,
        in_specs=(
            P("dp", "fsdp", None),
            P("dp", "fsdp", None),
            P("dp"),
            P("dp"),
            P("dp", None, "fsdp"),
            P("dp", "fsdp", None),
            P("fsdp", None, None),
            P("fsdp", None, None),
            P("fsdp", None, None),
            P("fsdp", None),
            P(None, "fsdp"),
            P("fsdp"),
            P(None, None, "fsdp"),
            P("fsdp", None),
        ),
        out_specs=(
            P("dp", "fsdp", None),
            P("dp", "fsdp", None),
            P("dp", "fsdp", None),
            P("fsdp", None, "dp"),
            P("fsdp", None, "dp"),
            P("fsdp", None, "dp"),
            P("fsdp", "dp"),
            P(None, "fsdp"),
            P("fsdp"),
            P("dp", None, "fsdp"),
            P("fsdp", "dp"),
        ),
        check_vma=False,
    )
```

```python
import functools
import math

import jax
import jax.numpy as jnp
from jax import lax
from jax.experimental import pallas as pl
from jax.experimental.pallas import tpu as pltpu
from jax.sharding import PartitionSpec as P

D = 1536
HEADS = 24
HD = 64
TW = 4096
TE = 1024
PATCHES = 1024
TEXT = 256
EPSILON = 1e-06
F32 = jnp.float32
BF16 = jnp.bfloat16
QC = 256


def dot(a, b, ca=1, cb=0):
    return lax.dot_general(a, b, (((ca,), (cb,)), ((), ())), preferred_element_type=F32)


def from_behind(value, step):
    n = lax.axis_size("fsdp")
    return lax.ppermute(value, "fsdp", [(i, (i + step) % n) for i in range(n)])


def gather_rot(value):
    return [value] + [from_behind(value, r) for r in range(1, lax.axis_size("fsdp"))]


def pair_sum(value):
    return functools.reduce(lambda a, b: a + b, gather_rot(value))


def row_sum(value):
    n = lax.axis_size("fsdp")
    rows = value.shape[-1] // n
    total = value
    for r in range(1, n):
        total = total + jnp.roll(from_behind(value, r), r * rows, axis=-1)
    return total


def scatter_rot(blocks):
    n = lax.axis_size("fsdp")
    total = blocks[0].astype(F32)
    for r in range(1, n):
        got = lax.ppermute(blocks[r], "fsdp", [(i, (i - r) % n) for i in range(n)])
        total = total + got.astype(F32)
    return total


def block_of(value, index, axis):
    size = value.shape[axis] // lax.axis_size("fsdp")
    return lax.dynamic_slice_in_dim(value, index * size, size, axis)


def rot_blocks(value, axis):
    n, f = lax.axis_size("fsdp"), lax.axis_index("fsdp")
    return [block_of(value, (f - r) % n, axis) for r in range(n)]


def exchange_rot(value, axis):
    n, f = lax.axis_size("fsdp"), lax.axis_index("fsdp")
    out = [block_of(value, f, axis)]
    for r in range(1, n):
        out.append(from_behind(block_of(value, (f + r) % n, axis), r))
    return out


def natural(got):
    n, f = lax.axis_size("fsdp"), lax.axis_index("fsdp")
    if n == 2:
        return [jnp.where(f == 0, got[0], got[1]), jnp.where(f == 0, got[1], got[0])]
    got = jnp.stack(got)
    return [lax.dynamic_index_in_dim(got, (f - g) % n, 0, keepdims=False) for g in range(n)]


def dp_bits():
    return int(lax.axis_size("dp")).bit_length() - 1


def swapped(p):
    return (p & ~3) | ((p & 1) << 1) | ((p >> 1) & 1)


def turned(p, f):
    return p if dp_bits() < 3 else jnp.where(f % 2 == 0, p, swapped(p))


def dp_swap(value, bit):
    n, dpn = lax.axis_size("fsdp"), lax.axis_size("dp")
    pairs = []
    for i in range(dpn):
        for f in range(n):
            flip = 1 << bit if dp_bits() < 3 or f % 2 == 0 else swapped(1 << bit)
            pairs.append((i * n + f, (i ^ flip) * n + f))
    return lax.ppermute(value, ("dp", "fsdp"), pairs)


def relative(value):
    places = turned(jnp.arange(lax.axis_size("dp")), lax.axis_index("fsdp"))
    return jnp.take(value, lax.axis_index("dp") ^ places, axis=0)


class Halving:
    def __init__(self, order, keep, send):
        self.order = list(order)
        self.keep, self.got = keep, dp_swap(send, self.order.pop(0))

    def step(self):
        if self.got is None:
            return

        def add(part):
            return self.keep[part].astype(F32) + self.got[part].astype(F32)

        if not self.order:
            self.last = add(slice(None))
            self.got = None
            return
        half = self.keep.shape[0] // 2
        send = add(slice(half, None)).astype(BF16)
        self.keep = add(slice(half)).astype(BF16)
        self.got = dp_swap(send, self.order.pop(0))


def place_of(p, order):
    return sum((p >> bit & 1) << i for i, bit in enumerate(reversed(order)))


def swap_all_kernel(text_ref, mod_ref, small_ref, text_out, mod_out, small_out, sends, gets, own):
    dpn, me = lax.axis_size("dp"), lax.axis_index("dp")
    copies = []
    for r in range(1, dpn):
        peer = me ^ r
        moves = (
            (text_ref.at[peer], text_out.at[me]),
            (mod_ref.at[peer], mod_out.at[me]),
            (small_ref, small_out.at[me]),
        )
        for i, (src, dst) in enumerate(moves):
            copies.append(
                pltpu.make_async_remote_copy(
                    src_ref=src, dst_ref=dst, send_sem=sends.at[i, r], recv_sem=gets.at[i, r],
                    device_id={"dp": peer}, device_id_type=pl.DeviceIdType.MESH,
                )
            )
            copies[-1].start()
    local = (
        pltpu.make_async_copy(text_ref.at[me], text_out.at[me], own.at[0]),
        pltpu.make_async_copy(mod_ref.at[me], mod_out.at[me], own.at[1]),
        pltpu.make_async_copy(small_ref, small_out.at[me], own.at[2]),
    )
    for copy in local:
        copy.start()
    for copy in (*local, *copies):
        copy.wait()


def swap_all(text, mods, small):
    vmem = pl.BlockSpec(memory_space=pltpu.VMEM)
    count = text.shape[0]
    return pl.pallas_call(
        swap_all_kernel,
        in_specs=[vmem] * 3,
        out_specs=[vmem] * 3,
        out_shape=[
            jax.ShapeDtypeStruct(text.shape, text.dtype),
            jax.ShapeDtypeStruct(mods.shape, mods.dtype),
            jax.ShapeDtypeStruct((count,) + small.shape, small.dtype),
        ],
        scratch_shapes=[
            pltpu.SemaphoreType.DMA((3, count)), pltpu.SemaphoreType.DMA((3, count)),
            pltpu.SemaphoreType.DMA((3,)),
        ],
        compiler_params=pltpu.CompilerParams(has_side_effects=True),
    )(text, mods, small)


def advance(chains, value):
    live = [c for c in chains if c.got is not None]
    value, got = lax.optimization_barrier((value, [c.got for c in live]))
    for c, g in zip(live, got):
        c.got = g
        c.step()
    return value


def rope_block(value, cosine, sine, sign):
    width = value.shape[1]
    lane = lax.broadcasted_iota(jnp.int32, value.shape, 1)
    partner = jnp.where(
        lane % 32 < 16, pltpu.roll(value, width - 16, 1), pltpu.roll(value, 16, 1)
    )
    return value * cosine + sign * (partner * sine)


def column(ref, index, width):
    row = ref[index : index + 1, :] if isinstance(index, int) else ref[pl.ds(index, 1), :]
    return jnp.broadcast_to(row, (width, row.shape[1])).T


def masked(value, head):
    lane = lax.broadcasted_iota(jnp.int32, value.shape, 1)
    return jnp.where(lane // HD == head, value, jnp.zeros_like(value))


def attn_fwd_kernel(
    len_ref, pre_ref, inv_ref, gq_ref, gk_ref, cos_ref, sin_ref, tk_ref, tv_ref, gate_ref,
    q_ref, k_ref, v_ref, mixed_ref, so_ref, co_ref, ls_ref, lc_ref,
):
    _, tokens, width = pre_ref.shape
    heads = width // HD
    iq, ik = column(inv_ref, 0, width), column(inv_ref, 1, width)
    q = rope_block(pre_ref[0] * iq * gq_ref[...], cos_ref[...], sin_ref[...], 1.0)
    q_ref[...] = q.astype(BF16)
    k = rope_block(pre_ref[1] * ik * gk_ref[...], cos_ref[...], sin_ref[...], 1.0)
    k_ref[...] = k.astype(BF16)
    v_ref[...] = pre_ref[2].astype(BF16)
    length = len_ref[0]

    def one(keys, values, qm, limit):
        s = dot(qm, keys, 1, 1)
        if limit is not None:
            slot = lax.broadcasted_iota(jnp.int32, s.shape, 1)
            s = jnp.where(slot < limit, s, -1e30)
        peak = jnp.max(s, axis=1, keepdims=True)
        e = jnp.exp(s - peak)
        total = jnp.sum(e, axis=1, keepdims=True)
        o = dot(e.astype(BF16), values)
        return o * (1.0 / total), peak + jnp.log(total)

    lane = lax.broadcasted_iota(jnp.int32, (tokens, width), 1)
    qs = q_ref[...] * jnp.asarray(HD**-0.5, BF16)
    so = co = stats = jnp.zeros((tokens, width), F32)
    for h in range(heads):
        qm = masked(qs, h)
        o, lse = one(k_ref[...], v_ref[...], qm, None)
        so = jnp.where(lane // HD == h, o, so)
        stats = jnp.where(lane == h, lse, stats)
        o, lse = one(tk_ref[...], tv_ref[...], qm, length)
        co = jnp.where(lane // HD == h, o, co)
        stats = jnp.where(lane == heads + h, lse, stats)
    so_ref[...] = so
    co_ref[...] = co
    mixed_ref[...] = (so + gate_ref[...] * co).astype(BF16)
    stats = stats.T
    ls_ref[0] = stats[:heads]
    lc_ref[0] = stats[heads : 2 * heads]


def attn_bwd_kernel(
    len_ref, q_ref, k_ref, v_ref, tk_ref, tv_ref, g_ref, so_ref, co_ref, ls_ref, lc_ref,
    pre_ref, inv_ref, gq_ref, gk_ref, cos_ref, sin_ref, gate_ref,
    d_ref, dtk_ref, dtv_ref, stat_ref, gainq_ref, gaink_ref, gateg_ref,
    gs_ref, gc_ref, ds_ref, dc_ref, kt_ref, tkt_ref, dqt_ref, dk_acc, dv_acc, rq_ref, rk_ref,
):
    tokens, width = q_ref.shape
    heads = width // HD
    scale = jnp.asarray(HD**-0.5, BF16)

    @pl.when(pl.program_id(0) == 0)
    def _():
        rq_ref[...] = jnp.zeros_like(rq_ref)
        rk_ref[...] = jnp.zeros_like(rk_ref)

    g = g_ref[...]
    gs_ref[...] = g.astype(BF16)
    gc_ref[...] = (g * gate_ref[...]).astype(BF16)
    prod_c = g * co_ref[...]
    gateg_ref[...] = jnp.sum(prod_c, axis=0, keepdims=True)
    prod_s = (g * so_ref[...]).T
    prod_c = (prod_c * gate_ref[...]).T
    for h in range(heads):
        ds_ref[h : h + 1, :] = jnp.sum(prod_s[h * HD : (h + 1) * HD], axis=0, keepdims=True)
        dc_ref[h : h + 1, :] = jnp.sum(prod_c[h * HD : (h + 1) * HD], axis=0, keepdims=True)
    kt_ref[...] = k_ref[...].astype(F32).T.astype(BF16)
    tkt_ref[...] = tk_ref[...].astype(F32).T.astype(BF16)
    dk_acc[...] = jnp.zeros_like(dk_acc)
    dv_acc[...] = jnp.zeros_like(dv_acc)
    dtk_ref[...] = jnp.zeros_like(dtk_ref)
    dtv_ref[...] = jnp.zeros_like(dtv_ref)
    length = len_ref[0]

    def one(keys, keys_t, values, qm, gm, lse, delta, head, limit):
        s = dot(keys, qm, 1, 1)
        p = jnp.exp(s - lse)
        if limit is not None:
            slot = lax.broadcasted_iota(jnp.int32, s.shape, 0)
            p = jnp.where(slot < limit, p, 0.0)
        dp = dot(values, gm, 1, 1)
        ds = (p * (dp - delta)).astype(BF16)
        dq = dot(keys_t[head * HD : (head + 1) * HD, :], ds)
        return dq, dot(ds, qm), dot(p.astype(BF16), gm)

    def chunk(c, carry):
        rows = pl.ds(pl.multiple_of(c * QC, QC), QC)
        qc = q_ref[rows, :] * scale
        for h in range(heads):
            qm = masked(qc, h)
            dq, dk, dv = one(
                k_ref[...], kt_ref, v_ref[...], qm, masked(gs_ref[rows, :], h),
                ls_ref[0, h : h + 1, rows], ds_ref[h : h + 1, rows], h, None,
            )
            dk_acc[...] += dk
            dv_acc[...] += dv
            dq2, dk, dv = one(
                tk_ref[...], tkt_ref, tv_ref[...], qm, masked(gc_ref[rows, :], h),
                lc_ref[0, h : h + 1, rows], dc_ref[h : h + 1, rows], h, length,
            )
            dtk_ref[...] += dk
            dtv_ref[...] += dv
            dqt_ref[h * HD : (h + 1) * HD, rows] = (dq + dq2) * HD**-0.5
        return carry

    lax.fori_loop(0, tokens // QC, chunk, 0)
    dq = rope_block(dqt_ref[...].T, cos_ref[...], sin_ref[...], -1.0)
    d_ref[0] = dq
    prod = dq * (pre_ref[0] * column(inv_ref, 0, width))
    gainq_ref[...] = jnp.sum(prod, axis=0, keepdims=True)
    rq_ref[...] += prod * gq_ref[...]
    dk = rope_block(dk_acc[...], cos_ref[...], sin_ref[...], -1.0)
    d_ref[1] = dk
    prod = dk * (pre_ref[1] * column(inv_ref, 1, width))
    gaink_ref[...] = jnp.sum(prod, axis=0, keepdims=True)
    rk_ref[...] += prod * gk_ref[...]
    d_ref[2] = dv_acc[...]

    @pl.when(pl.program_id(0) == pl.num_programs(0) - 1)
    def _():
        stat_ref[...] = jnp.zeros_like(stat_ref)
        for i, ref in enumerate((rq_ref, rk_ref)):
            stat_ref[i : i + 1, :] = jnp.sum(ref[...].T, axis=0, keepdims=True)


def specs(tokens, text, width, heads, at=0):
    col = pl.BlockSpec((tokens, width), lambda i: (0, i + at))
    three = pl.BlockSpec((3, tokens, width), lambda i: (0, 0, i + at))
    tcol = pl.BlockSpec((text, width), lambda i: (0, i + at))
    stat = pl.BlockSpec((8, tokens), lambda i: (0, 0))
    gain = pl.BlockSpec((1, width), lambda i: (0, i + at))
    table = pl.BlockSpec((tokens, width), lambda i: (0, 0))
    lse = pl.BlockSpec((1, heads, tokens), lambda i: (i + at, 0, 0))
    scalar = pl.BlockSpec(memory_space=pltpu.SMEM)
    return col, three, tcol, stat, gain, table, lse, scalar


def sds(shape, dtype=F32):
    return jax.ShapeDtypeStruct(shape, dtype)


def attn_forward(length, pre, inv, gq, gk, cosine, sine, tk, tv, gate):
    _, tokens, columns = pre.shape
    text, width = tk.shape[0], cosine.shape[1]
    heads, blocks = width // HD, columns // width
    col, three, tcol, stat, gain, table, lse, scalar = specs(tokens, text, width, heads)
    flat = (tokens, columns)
    return pl.pallas_call(
        attn_fwd_kernel,
        grid=(blocks,),
        in_specs=[scalar, three, stat, gain, gain, table, table, tcol, tcol, gain],
        out_specs=[col, col, col, col, col, col, lse, lse],
        out_shape=[sds(flat, BF16)] * 4 + [sds(flat)] * 2 + [sds((blocks, heads, tokens))] * 2,
    )(length, pre, inv, gq, gk, cosine, sine, tk, tv, gate)


def attn_backward(at, blocks, length, q, k, v, tk, tv, g, so, co, ls, lc, pre, inv, gq, gk, cosine, sine, gate):
    tokens = q.shape[0]
    text, width = tk.shape[0], cosine.shape[1]
    heads, columns = width // HD, blocks * width
    col, three, tcol, stat, gain, table, lse, scalar = specs(tokens, text, width, heads, at)
    _, three_o, tcol_o, _, gain_o, _, _, _ = specs(tokens, text, width, heads)
    return pl.pallas_call(
        attn_bwd_kernel,
        grid=(blocks,),
        in_specs=[scalar, col, col, col, tcol, tcol, col, col, col, lse, lse,
                  three, stat, gain, gain, table, table, gain],
        out_specs=[three_o, tcol_o, tcol_o, stat, gain_o, gain_o, gain_o],
        out_shape=[
            sds((3, tokens, columns)), sds((text, columns)), sds((text, columns)),
            sds((8, tokens)), sds((1, columns)), sds((1, columns)), sds((1, columns)),
        ],
        scratch_shapes=[
            pltpu.VMEM((tokens, width), BF16), pltpu.VMEM((tokens, width), BF16),
            pltpu.VMEM((heads, tokens), F32), pltpu.VMEM((heads, tokens), F32),
            pltpu.VMEM((width, tokens), BF16), pltpu.VMEM((width, text), BF16),
            pltpu.VMEM((width, tokens), F32),
            pltpu.VMEM((tokens, width), F32), pltpu.VMEM((tokens, width), F32),
            pltpu.VMEM((tokens, width), F32), pltpu.VMEM((tokens, width), F32),
        ],
    )(length, q, k, v, tk, tv, g, so, co, ls, lc, pre, inv, gq, gk, cosine, sine, gate)


def pick(rows, cols, step, part):
    i = lax.broadcasted_iota(jnp.int32, (rows, cols), 0)
    j = lax.broadcasted_iota(jnp.int32, (rows, cols), 1)
    hit = (j == step * i + part) if cols > rows else (i == step * j + part)
    return jnp.where(hit, 1.0, 0.0).astype(BF16)

def text_fwd_kernel(x_ref, w_ref, o_ref):
    @pl.when(pl.program_id(0) == 0)
    def _():
        o_ref[...] = jnp.zeros_like(o_ref)
    for b in range(w_ref.shape[0] // 128):
        rows = slice(b * 128, (b + 1) * 128)
        w = w_ref[rows].reshape(256, w_ref.shape[2])
        x = x_ref[:, rows]
        for j in range(2):
            spread = dot(x, pick(128, 256, 2, j)).astype(BF16)
            o_ref[j] += dot(spread, w)

def text_fwd(x, w):
    depth, _, cols = w.shape
    bk = 256
    return pl.pallas_call(
        text_fwd_kernel, grid=(depth // bk,),
        in_specs=[pl.BlockSpec((x.shape[0], bk), lambda i: (0, i)), pl.BlockSpec((bk, 2, cols), lambda i: (i, 0, 0))],
        out_specs=pl.BlockSpec((2, x.shape[0], cols), lambda i: (0, 0, 0)),
        out_shape=sds((2, x.shape[0], cols)),
    )(x, w)

def text_bwd_kernel(g_ref, w_ref, o_ref):
    for b in range(w_ref.shape[0] // 128):
        rows = slice(b * 128, (b + 1) * 128)
        w = w_ref[rows].reshape(256, w_ref.shape[2])
        total = 0.0
        for j in range(2):
            total = total + dot(g_ref[j], dot(pick(128, 256, 2, j), w).astype(BF16), 1, 1)
        o_ref[:, rows] = total.astype(BF16)

def text_bwd(g, w):
    depth, _, cols = w.shape
    bk = 256
    return pl.pallas_call(
        text_bwd_kernel, grid=(depth // bk,),
        in_specs=[pl.BlockSpec(g.shape, lambda i: (0, 0, 0)), pl.BlockSpec((bk, 2, cols), lambda i: (i, 0, 0))],
        out_specs=pl.BlockSpec((g.shape[1], bk), lambda i: (0, i)),
        out_shape=sds((g.shape[1], depth), BF16),
    )(g, w)

def put_relative(dst, src, me, f, count):
    rows = dst.shape[0] // count
    for p in range(count):
        start = pl.multiple_of((me ^ turned(p, f)) * rows, 16)
        dst[p * rows : (p + 1) * rows, :] = src[pl.ds(start, rows), :]


def put_halves(keep, send, value, count, order, slot=None):
    rows = value.shape[0] // count
    for p in range(count):
        place = place_of(p, order[1:])
        where = place if slot is None else (place, slot)
        (send if p >> order[0] & 1 else keep)[where] = value[p * rows : (p + 1) * rows]


def ffn_kernel(
    orders, id_ref, s_ref, b_ref, w_ref, d_ref,
    wk_ref, ws_ref, dk_ref, ds_ref, fo_ref, fp_ref, so_ref, sp_ref,
    st, bt, tmp, wg, wu, facc, sacc,
):
    step = pl.program_id(0)
    depth, _, cols = w_ref.shape
    own = fo_ref.shape[0]
    count = 2 * dk_ref.shape[0]

    @pl.when(step == 0)
    def _():
        for src, dst in ((s_ref, st), (b_ref, bt)):
            for c in range(depth // 256):
                part = slice(c * 256, (c + 1) * 256)
                tmp[part, :] = src[:, part].astype(F32).T.astype(BF16)
            put_relative(dst, tmp, id_ref[0], id_ref[1], count)
        facc[...] = jnp.zeros_like(facc)
        sacc[...] = jnp.zeros_like(sacc)

    for c in range(depth // 128):
        part = slice(c * 128, (c + 1) * 128)
        w = w_ref[part].reshape(256, cols)
        wg[part, :] = dot(pick(128, 256, 2, 0), w).astype(BF16)
        wu[part, :] = dot(pick(128, 256, 2, 1), w).astype(BF16)
    s, b = s_ref[...], b_ref[...]
    gate = dot(s, wg[...])
    up = dot(s, wu[...])
    back = dot(b, d_ref[...], 1, 1)
    sig = jax.nn.sigmoid(gate)
    silu = gate * sig
    hidden = (silu * up).astype(BF16)
    g_gate = (back * up * (sig + silu * (1.0 - sig))).astype(BF16)
    g_up = (back * silu).astype(BF16)
    put_halves(wk_ref, ws_ref, dot(st[...], g_gate).astype(BF16), count, orders[0], 0)
    put_halves(wk_ref, ws_ref, dot(st[...], g_up).astype(BF16), count, orders[0], 1)
    put_halves(dk_ref, ds_ref, dot(bt[...], hidden).astype(BF16), count, orders[1])
    facc[...] += dot(hidden, d_ref[...])
    sacc[...] += dot(g_gate, wg[...], 1, 1) + dot(g_up, wu[...], 1, 1)

    @pl.when(step == pl.num_programs(0) - 1)
    def _():
        fo_ref[...] = facc[:own]
        fp_ref[...] = facc[own:].astype(BF16)
        so_ref[...] = sacc[:own]
        sp_ref[...] = sacc[own:].astype(BF16)


def ffn(ids, s, b, w, d, local, dp, orders):
    tokens, depth = s.shape
    hid = d.shape[0]
    bc = min(256, hid)
    rest = tokens - local
    once = functools.partial(pl.BlockSpec, pipeline_mode=pl.Buffered(1))
    const = lambda i: (0, 0)
    share = depth // dp
    half = pl.BlockSpec((dp // 2, share, bc), lambda i: (0, 0, i))
    halves = pl.BlockSpec((dp // 2, 2, share, bc), lambda i: (0, 0, 0, i))
    return pl.pallas_call(
        functools.partial(ffn_kernel, orders),
        grid=(hid // bc,),
        in_specs=[
            pl.BlockSpec(memory_space=pltpu.SMEM),
            once((tokens, depth), const), once((tokens, depth), const),
            pl.BlockSpec((depth, 2, bc), lambda i: (0, 0, i)),
            pl.BlockSpec((bc, depth), lambda i: (i, 0)),
        ],
        out_specs=[halves] * 2 + [half] * 2 + [
            once((local, depth), const), once((rest, depth), const),
            once((local, depth), const), once((rest, depth), const),
        ],
        out_shape=[sds((dp // 2, 2, share, hid), BF16)] * 2 + [sds((dp // 2, share, hid), BF16)] * 2 + [
            sds((local, depth)), sds((rest, depth), BF16),
            sds((local, depth)), sds((rest, depth), BF16),
        ],
        scratch_shapes=[
            pltpu.VMEM((depth, tokens), BF16), pltpu.VMEM((depth, tokens), BF16),
            pltpu.VMEM((depth, tokens), BF16),
            pltpu.VMEM((depth, bc), BF16), pltpu.VMEM((depth, bc), BF16),
            pltpu.VMEM((tokens, depth), F32), pltpu.VMEM((tokens, depth), F32),
        ],
        compiler_params=pltpu.CompilerParams(vmem_limit_bytes=62 << 20),
    )(ids, s, b, w, d)


def project_kernel(id_ref, xo_ref, xp_ref, front_ref, w_ref, got_ref, first_ref, pre_ref, sq_ref):
    j = pl.program_id(0)
    local, depth = xo_ref.shape
    own = got_ref.shape[2]
    f = id_ref[1]

    @pl.when(j == 0)
    def _():
        for i, ref in enumerate((xo_ref, xp_ref)):
            x = ref[...].astype(F32)
            inv = lax.rsqrt(jnp.sum(x * x, axis=1, keepdims=True) * (1.0 / depth) + EPSILON)
            first_ref[i * local : (i + 1) * local, :] = (x * inv * front_ref[...]).astype(BF16)
        sq_ref[...] = jnp.zeros_like(sq_ref)

    mine = pl.ds(pl.multiple_of(f * own, 128), own)
    other = pl.ds(pl.multiple_of((1 - f) * own, 128), own)
    out = dot(first_ref[:, mine], w_ref[0, :, mine]) + dot(first_ref[:, other], got_ref[0])
    pre_ref[0] = out
    square = out * out
    part = square[:, :128]
    for c in range(1, own // 128):
        part = part + square[:, c * 128 : (c + 1) * 128]
    sq_ref[pl.ds(j, 1), :] = jnp.sum(part.T, axis=0, keepdims=True)


def project(ids, xo, xp, front, w, got):
    local, depth = xo.shape
    own = got.shape[2]
    tokens = 2 * local
    const = lambda j: (0, 0)
    return pl.pallas_call(
        project_kernel,
        grid=(3,),
        in_specs=[
            pl.BlockSpec(memory_space=pltpu.SMEM),
            pl.BlockSpec((local, depth), const), pl.BlockSpec((local, depth), const),
            pl.BlockSpec((1, depth), const),
            pl.BlockSpec((1, own, depth), lambda j: (j, 0, 0)),
            pl.BlockSpec((1, own, own), lambda j: (j, 0, 0)),
        ],
        out_specs=[
            pl.BlockSpec((tokens, depth), const),
            pl.BlockSpec((1, tokens, own), lambda j: (j, 0, 0)),
            pl.BlockSpec((8, tokens), const),
        ],
        out_shape=[sds((tokens, depth), BF16), sds((3, tokens, own)), sds((8, tokens))],
    )(ids, xo, xp, front, w, got)


def project_grad_kernel(
    order, id_ref, da_ref, db_ref, pre_ref, stat_ref, gain_ref, first_ref,
    keep_ref, send_ref, g_ref, gt, tmp,
):
    j = pl.program_id(0)
    own = pre_ref.shape[2]
    cut = da_ref.shape[2]
    count = 2 * keep_ref.shape[0]
    inv, mean = column(stat_ref, j, 128), column(stat_ref, j + 3, 128)
    for c in range(own // 128):
        part = slice(c * 128, (c + 1) * 128)
        here = slice(c * 128 - cut, (c + 1) * 128 - cut) if c * 128 >= cut else part
        d = (db_ref if c * 128 >= cut else da_ref)[0, :, here]
        g = inv * (d * gain_ref[0, :, part] - pre_ref[0, :, part] * inv * mean)
        tmp[part, :] = g.T.astype(BF16)
        g_ref[0, :, part] = g.astype(BF16)
    put_relative(gt, tmp, id_ref[0] % count, id_ref[1], count)
    put_halves(keep_ref, send_ref, dot(gt[...], first_ref[...]).astype(BF16), count, order, j)


def project_grad(ids, da, db, pre, stats, gain, first, dp, order):
    _, tokens, own = pre.shape
    depth = first.shape[1]
    share = depth // dp
    const = lambda j: (0, 0)
    block = lambda j: (j, 0, 0)
    once = functools.partial(pl.BlockSpec, pipeline_mode=pl.Buffered(1))
    half = once((dp // 4, 3, share, depth), lambda j: (0, 0, 0, 0))
    return pl.pallas_call(
        functools.partial(project_grad_kernel, order),
        grid=(3,),
        in_specs=[
            pl.BlockSpec(memory_space=pltpu.SMEM),
            pl.BlockSpec((1,) + da.shape[1:], block), pl.BlockSpec((1,) + db.shape[1:], block),
            pl.BlockSpec((1, tokens, own), block),
            pl.BlockSpec((8, tokens), const),
            pl.BlockSpec((1, 1, own), block),
            once((tokens, depth), const),
        ],
        out_specs=[half, half, pl.BlockSpec((1, tokens, own), block)],
        out_shape=[sds((dp // 4, 3, share, depth), BF16)] * 2
        + [sds((3, tokens, own), BF16)],
        scratch_shapes=[pltpu.VMEM((own, tokens), BF16), pltpu.VMEM((own, tokens), BF16)],
    )(ids, da, db, pre, stats, gain, first)


def project_back_kernel(id_ref, g_ref, w_ref, got_ref, own_ref, peer_ref, acc):
    j = pl.program_id(0)
    own = g_ref.shape[2]
    local = own_ref.shape[0]
    f = id_ref[1]
    mine = pl.ds(pl.multiple_of(f * own, 128), own)
    other = pl.ds(pl.multiple_of((1 - f) * own, 128), own)

    @pl.when(j == 0)
    def _():
        acc[...] = jnp.zeros_like(acc)

    acc[:, mine] += dot(g_ref[0], w_ref[0, :, mine], 1, 1)
    acc[:, other] += dot(g_ref[0], got_ref[0], 1, 1)

    @pl.when(j == 2)
    def _():
        own_ref[...] = acc[:local]
        peer_ref[...] = acc[local:].astype(BF16)


def project_back(ids, g, w, got):
    _, tokens, own = g.shape
    depth = w.shape[2]
    local = tokens // 2
    const = lambda j: (0, 0)
    block = lambda j: (j, 0, 0)
    once = functools.partial(pl.BlockSpec, pipeline_mode=pl.Buffered(1))
    return pl.pallas_call(
        project_back_kernel,
        grid=(3,),
        in_specs=[
            pl.BlockSpec(memory_space=pltpu.SMEM),
            pl.BlockSpec((1, tokens, own), block),
            pl.BlockSpec((1, own, depth), block), pl.BlockSpec((1, own, own), block),
        ],
        out_specs=[once((local, depth), const), once((local, depth), const)],
        out_shape=[sds((local, depth)), sds((local, depth), BF16)],
        scratch_shapes=[pltpu.VMEM((tokens, depth), F32)],
    )(ids, g, w, got)


def out_back_kernel(order, id_ref, *refs):
    n = len(refs) - 8
    blocks, (w_ref, mixed_ref, g_ref, keep_ref, send_ref, all_ref, gt, tmp) = refs[:n], refs[n:]
    local = blocks[0].shape[0]
    for r, ref in enumerate(blocks):
        all_ref[r * local : (r + 1) * local, :] = ref[...]
    grad = all_ref[...]
    g_ref[...] = dot(grad, w_ref[...], 1, 1)
    for c in range(grad.shape[1] // 256):
        part = slice(c * 256, (c + 1) * 256)
        tmp[part, :] = grad[:, part].astype(F32).T.astype(BF16)
    count = 2 * keep_ref.shape[0]
    put_relative(gt, tmp, id_ref[0], id_ref[1], count)
    put_halves(keep_ref, send_ref, dot(gt[...], mixed_ref[...]).astype(BF16), count, order)


def out_back(ids, blocks, w, mixed, dp, order):
    tokens, own = mixed.shape
    depth = w.shape[1]
    vmem = pl.BlockSpec(memory_space=pltpu.VMEM)
    half = sds((dp // 2, depth // dp, own), BF16)
    return pl.pallas_call(
        functools.partial(out_back_kernel, order),
        in_specs=[pl.BlockSpec(memory_space=pltpu.SMEM)] + [vmem] * (len(blocks) + 2),
        out_specs=[vmem] * 3,
        out_shape=[sds((tokens, own)), half, half],
        scratch_shapes=[
            pltpu.VMEM((tokens, depth), BF16),
            pltpu.VMEM((depth, tokens), BF16), pltpu.VMEM((depth, tokens), BF16),
        ],
    )(ids, *blocks, w, mixed)


def time_embed(timesteps):
    half = TE // 2
    frequencies = jnp.exp(-math.log(10000.0) * jnp.arange(half, dtype=F32) / half)
    angles = timesteps.astype(F32)[:, None] * frequencies
    waves = jnp.concatenate([jnp.cos(angles), jnp.sin(angles)], axis=-1)
    return jax.nn.silu(waves).astype(BF16)


def rope_tables(positions, width):
    lane = jnp.arange(width)
    quarter = HD // 4
    frequencies = 10000.0 ** (-(lane % quarter).astype(F32) / quarter)
    place = jnp.where(lane % HD < HD // 2, positions[0][:, None], positions[1][:, None])
    angles = place.astype(F32) * frequencies
    return jnp.cos(angles), jnp.where(lane % 32 < 16, -1.0, 1.0) * jnp.sin(angles)


def inverse_rms(values):
    return lax.rsqrt(jnp.mean(values * values, axis=-1, keepdims=True) + EPSILON)


def rms_back(grad_hat, normed, inverse):
    return inverse * (grad_hat - normed * jnp.mean(grad_hat * normed, axis=-1, keepdims=True))


def pad_cols(value, width):
    extra = -value.shape[-1] % width
    return value if extra == 0 else jnp.pad(value, [(0, 0)] * (value.ndim - 1) + [(0, extra)])


def on_device(
    hidden_in, text_state, caption_lengths, timesteps, patch_positions, cotangent,
    w_ada, w_text, w_qkv, w_out, gains, cross_gate, w_gate_up, w_down,
):
    n, f = lax.axis_size("fsdp"), lax.axis_index("fsdp")
    dpn, me = lax.axis_size("dp"), lax.axis_index("dp")
    bits = list(range(dp_bits()))
    low_bits = bits[:-1]
    late = bits[2:] + bits[:2]
    own_d = D // n
    local = hidden_in.shape[1]
    tokens = n * local
    width = 2 * HD
    share = D // dpn
    paired = n == 2 and dpn >= 4
    ids = jnp.stack([me, f]).astype(jnp.int32)
    x_bf, dy_bf = hidden_in[0], cotangent[0]

    time_low = time_embed(timesteps)
    own_te = TE // n
    time_own = lax.dynamic_slice_in_dim(time_low[0], f * own_te, own_te, 0)
    modulation = pair_sum(
        jnp.einsum("k,kjd->jd", time_own, w_ada, preferred_element_type=F32)
    )
    scale_attn, gate_attn = modulation[0:1], jnp.tanh(modulation[1:2])
    scale_ffn, gate_ffn = modulation[2:3], jnp.tanh(modulation[3:4])

    w_flat = jnp.moveaxis(w_qkv, 1, 0)
    w_parts = exchange_rot(w_flat, 2)
    x_parts = gather_rot(x_bf)
    dy_all = jnp.concatenate(gather_rot(dy_bf), axis=0)
    places = jnp.concatenate(gather_rot(patch_positions[0]), axis=1)
    text_cols = jnp.concatenate(natural(exchange_rot(text_state[0], 1)), axis=0)
    text_all = lax.all_gather(text_cols, "dp", axis=0, tiled=True)
    gain_full = lax.all_gather(gains, "fsdp", axis=1, tiled=True).astype(F32)
    gain_own = gains.astype(F32)

    front = gain_full[0] * (1.0 + scale_attn)
    if paired:
        first_all, pre, squares = project(ids, *x_parts, front, w_flat, w_parts[1])
    else:
        w_heads = jnp.concatenate(natural(w_parts), axis=1)
        x_f = jnp.concatenate(x_parts, axis=0).astype(F32)
        first_all = (x_f * inverse_rms(x_f) * front).astype(BF16)
        pre = jnp.stack([dot(first_all, w_heads[j]) for j in range(3)])
        squares = jnp.pad(jnp.sum(pre[:2] * pre[:2], -1), ((0, 6), (0, 0)))
    inverse = lax.rsqrt(row_sum(squares) / D + EPSILON)

    text_part = text_fwd(text_cols, w_text)
    text_pre = scatter_rot(rot_blocks(text_part, 2))
    inv_t = lax.rsqrt(
        pair_sum(jnp.sum(text_pre[0] * text_pre[0], -1, keepdims=True)) / D + EPSILON
    )
    normed_t = text_pre[0] * inv_t
    tk = (normed_t * gain_own[4]).astype(BF16)
    tv = text_pre[1].astype(BF16)

    head_tanh = jnp.tanh(cross_gate.astype(F32))
    gate_row = pad_cols(jnp.repeat(head_tanh, HD)[None], width)
    cosine, sine = rope_tables(places, width)
    gq, gk = pad_cols(gain_own[2:3], width), pad_cols(gain_own[3:4], width)
    pre_p, tkp, tvp = pad_cols(pre, width), pad_cols(tk, width), pad_cols(tv, width)
    q, k, v, mixed_p, so, co, ls, lc = attn_forward(
        caption_lengths, pre_p, inverse, gq, gk, cosine, sine, tkp, tvp, gate_row
    )
    mixed = mixed_p[:, :own_d]

    def rows(value, r):
        return value[r * local : (r + 1) * local]

    parts = [dot(rows(mixed, r), w_out) for r in range(n)]
    attn_branch = scatter_rot([parts[0]] + [p.astype(BF16) for p in parts[1:]])
    x_own = x_bf.astype(F32)
    after_attn = x_own + gate_attn * attn_branch
    inverse_two = inverse_rms(after_attn)
    normed_two = after_attn * inverse_two
    second = (normed_two * gain_full[1] * (1.0 + scale_ffn)).astype(BF16)

    second_all = jnp.concatenate(gather_rot(second), axis=0)
    branch_all = (gate_ffn * dy_all.astype(F32)).astype(BF16)
    wide_keep, wide_send, down_keep, down_send, ffn_own, ffn_rest, back_own, back_rest = ffn(
        ids, second_all, branch_all, w_gate_up, w_down, local, dpn, (bits, late)
    )
    (ffn_own, ffn_rest, back_own, back_rest), text_all = lax.optimization_barrier(
        ((ffn_own, ffn_rest, back_own, back_rest), text_all)
    )
    wide_chain = Halving(bits, wide_keep, wide_send)
    down_chain = Halving(late, down_keep, down_send)
    grad_second = scatter_rot([back_own] + [rows(back_rest, r) for r in range(n - 1)])
    ffn_branch = scatter_rot([ffn_own] + [rows(ffn_rest, r) for r in range(n - 1)])
    output = (after_attn + gate_ffn * ffn_branch).astype(BF16)
    dy = dy_bf.astype(F32)
    d_gate_ffn = jnp.sum(dy * ffn_branch, axis=0) * (1.0 - gate_ffn[0] * gate_ffn[0])

    scaled = grad_second * normed_two
    d_scale_ffn = jnp.sum(scaled * gain_full[1], axis=0)
    gain_two = jnp.sum(scaled * (1.0 + scale_ffn), axis=0)
    grad_after = dy + rms_back(
        grad_second * gain_full[1] * (1.0 + scale_ffn), normed_two, inverse_two
    )
    d_gate_attn = jnp.sum(grad_after * attn_branch, axis=0) * (1.0 - gate_attn[0] * gate_attn[0])
    grad_attn = (gate_attn * grad_after).astype(BF16)
    grad_mixed, *out_halves = out_back(ids, gather_rot(grad_attn), w_out, mixed, dpn, bits)
    out_chain = Halving(bits, *out_halves)
    blocks = pre_p.shape[2] // width
    cut = max(1, 2 * blocks // 3)
    grad_mixed = pad_cols(grad_mixed, width)
    inputs = (so, co, ls, lc, pre_p, inverse, gq, gk, cosine, sine, gate_row)
    part_a = attn_backward(0, cut, caption_lengths, q, k, v, tkp, tvp, grad_mixed, *inputs)
    part_a, grad_mixed = lax.optimization_barrier((part_a, grad_mixed))
    grad_mixed = advance([wide_chain, down_chain], grad_mixed)
    part_b = attn_backward(
        cut, blocks - cut, caption_lengths, q, k, v, tkp, tvp, grad_mixed, *inputs
    )
    means = row_sum(part_a[3] + part_b[3])[:2] / D

    ones, zeros = jnp.ones((1, tokens), F32), jnp.zeros((1, tokens), F32)
    if paired:
        stats = jnp.concatenate([inverse[:2], ones, means, zeros, zeros, zeros], axis=0)
        gain3 = jnp.stack([gain_own[2:3], gain_own[3:4], jnp.ones_like(gain_own[2:3])])
        keep, send, grads = project_grad(
            ids, part_a[0], part_b[0], pre, stats, gain3, first_all, dpn, low_bits
        )
        part_a, part_b, grads = advance([wide_chain, out_chain], (part_a[1:], part_b[1:], grads))
        qkv_chain = Halving(low_bits, keep, send)
        parts = project_back(ids, grads, w_flat, w_parts[1])
    else:
        d = jnp.concatenate([part_a[0], part_b[0]], axis=2)[:, :, :own_d]
        part_a, part_b = part_a[1:], part_b[1:]
        inv, mean = inverse[:2, :, None], means[:, :, None]
        hat = d[:2] * gain_own[2:4][:, None] - pre[:2] * inv * mean
        grads = [(inv[0] * hat[0]).astype(BF16), (inv[1] * hat[1]).astype(BF16), d[2].astype(BF16)]
        wide = [dot(g, first_all, 0, 0).astype(BF16) for g in grads]
        wide = [jnp.concatenate(natural(exchange_rot(w_, 1)), axis=0) for w_ in wide]
        wide = relative(jnp.stack([w_.reshape(dpn, share, own_d) for w_ in wide], axis=1))
        wide = jnp.stack([wide[p] for p in sorted(range(dpn), key=lambda p: place_of(p, bits))])
        qkv_chain = Halving(bits, wide[: dpn // 2], wide[dpn // 2 :])
        parts = [
            sum(dot(rows(g, r), w_heads[j], 1, 1) for j, g in enumerate(grads)) for r in range(n)
        ]
        parts = [parts[0]] + [p.astype(BF16) for p in parts[1:]]
    grad_first = scatter_rot(parts)

    dtk, dtv, gain_q, gain_k, gate_g = (
        jnp.concatenate([part_a[i], part_b[i]], axis=1)[:, :own_d] for i in (0, 1, 3, 4, 5)
    )
    gate_total = jnp.sum(gate_g[0].reshape(HEADS // n, HD), axis=1) * (
        1.0 - head_tanh * head_tanh
    )
    text_hat = dtk * gain_own[4]
    gain_text = jnp.sum(dtk * normed_t, axis=0, keepdims=True)
    mean_t = pair_sum(jnp.sum(text_hat * normed_t, -1, keepdims=True)) / D
    grad_tk = (inv_t * (text_hat - normed_t * mean_t)).astype(BF16)
    text_pair = jnp.stack([grad_tk, dtv.astype(BF16)])
    pair_all = jnp.concatenate(natural(gather_rot(text_pair)), axis=-1)
    pair_all = advance([qkv_chain, out_chain], pair_all)
    text_in = text_bwd(pair_all, w_text)
    text_in = jnp.concatenate(natural(exchange_rot(text_in, 0)), axis=1)

    inverse_one = inverse_rms(x_own)
    normed_one = x_own * inverse_one
    scaled = grad_first * normed_one
    d_scale_attn = jnp.sum(scaled * gain_full[0], axis=0)
    gain_one = jnp.sum(scaled * (1.0 + scale_attn), axis=0)
    grad_input = (
        grad_after
        + rms_back(grad_first * gain_full[0] * (1.0 + scale_attn), normed_one, inverse_one)
    ).astype(BF16)


    sums = [d_scale_attn, d_gate_attn, d_scale_ffn, d_gate_ffn, gain_one, gain_two]
    sums = pair_sum(jnp.stack(sums))
    stamp = jnp.full((1, D), timesteps[0].astype(F32))
    gate_pad = jnp.pad(gate_total, (0, own_d - gate_total.shape[0]))[None]
    small = jnp.concatenate([block_of(sums[4:], f, 1), gain_q, gain_k, gain_text, gate_pad], axis=0)
    mods = jnp.concatenate([sums[:4], stamp], axis=0).reshape(5, dpn, share).transpose(1, 0, 2)
    mods = jnp.pad(mods, ((0, 0), (0, 3), (0, -share % 128)))
    small = jnp.pad(small.reshape(-1, 128), ((0, -small.size // 128 % 8), (0, 0)))
    outgoing = block_of(pair_all, f, 1).reshape(2, TEXT // n, dpn, share).transpose(2, 0, 1, 3)
    mods = advance([wide_chain, down_chain, qkv_chain, out_chain], mods)
    pair_cols, mods, small = swap_all(outgoing, mods, small)
    pair_cols = jnp.concatenate(natural(gather_rot(pair_cols)), axis=2)
    pair_cols = pair_cols.transpose(0, 2, 1, 3).reshape(dpn * TEXT, 2 * share)
    text_grad = dot(pair_cols, text_all, 0, 0).reshape(2, share, TW // n)
    total = jnp.sum(small, axis=0)[: 6 * own_d // 128].reshape(6, own_d)
    times = time_embed(mods[:, 4, 0])
    times = lax.dynamic_slice_in_dim(times, f * own_te, own_te, 1).astype(F32)
    ada_grad = lax.dot_general(
        mods[:, :4, :share].reshape(dpn, 4 * share), times, (((0,), (0,)), ((), ())),
        precision=lax.Precision.HIGHEST,
    ).reshape(4, share, own_te)

    text_grad = advance([qkv_chain, down_chain], text_grad)
    if paired:
        own_side = f == (me >> low_bits[-1] + 1)
        mine, got = exchange_rot(qkv_chain.last[0].astype(BF16), 2)
        qkv_chain = Halving(
            bits[-1:], jnp.where(own_side, mine, got)[None], jnp.where(own_side, got, mine)[None]
        )
    for chain in (out_chain, down_chain, wide_chain, qkv_chain):
        while chain.got is not None:
            chain.step()
    return (
        output[None],
        grad_input[None],
        text_in[None],
        ada_grad.transpose(2, 0, 1),
        text_grad.transpose(2, 0, 1),
        qkv_chain.last[0].transpose(2, 0, 1),
        out_chain.last[0].T,
        total[:5],
        total[5, : HEADS // n],
        wide_chain.last[0].transpose(1, 0, 2),
        down_chain.last[0].T,
    )


def solution(mesh):
    return jax.shard_map(
        on_device,
        mesh=mesh,
        in_specs=(
            P("dp", "fsdp", None),
            P("dp", "fsdp", None),
            P("dp"),
            P("dp"),
            P("dp", None, "fsdp"),
            P("dp", "fsdp", None),
            P("fsdp", None, None),
            P("fsdp", None, None),
            P("fsdp", None, None),
            P("fsdp", None),
            P(None, "fsdp"),
            P("fsdp"),
            P(None, None, "fsdp"),
            P("fsdp", None),
        ),
        out_specs=(
            P("dp", "fsdp", None),
            P("dp", "fsdp", None),
            P("dp", "fsdp", None),
            P("fsdp", None, "dp"),
            P("fsdp", None, "dp"),
            P("fsdp", None, "dp"),
            P("fsdp", "dp"),
            P(None, "fsdp"),
            P("fsdp"),
            P("dp", None, "fsdp"),
            P("fsdp", "dp"),
        ),
        check_vma=False,
    )
```

```python
import functools
import math

import jax
import jax.numpy as jnp
from jax import lax
from jax.experimental import pallas as pl
from jax.experimental.pallas import tpu as pltpu
from jax.sharding import PartitionSpec as P

D = 1536
HEADS = 24
HD = 64
TW = 4096
TE = 1024
PATCHES = 1024
TEXT = 256
EPSILON = 1e-06
F32 = jnp.float32
BF16 = jnp.bfloat16
QC = 256


def dot(a, b, ca=1, cb=0):
    return lax.dot_general(a, b, (((ca,), (cb,)), ((), ())), preferred_element_type=F32)


def from_behind(value, step):
    n = lax.axis_size("fsdp")
    return lax.ppermute(value, "fsdp", [(i, (i + step) % n) for i in range(n)])


def gather_rot(value):
    return [value] + [from_behind(value, r) for r in range(1, lax.axis_size("fsdp"))]


def pair_sum(value):
    return functools.reduce(lambda a, b: a + b, gather_rot(value))


def row_sum(value):
    n = lax.axis_size("fsdp")
    rows = value.shape[-1] // n
    total = value
    for r in range(1, n):
        total = total + jnp.roll(from_behind(value, r), r * rows, axis=-1)
    return total


def scatter_rot(blocks):
    n = lax.axis_size("fsdp")
    total = blocks[0].astype(F32)
    for r in range(1, n):
        got = lax.ppermute(blocks[r], "fsdp", [(i, (i - r) % n) for i in range(n)])
        total = total + got.astype(F32)
    return total


def block_of(value, index, axis):
    size = value.shape[axis] // lax.axis_size("fsdp")
    return lax.dynamic_slice_in_dim(value, index * size, size, axis)


def rot_blocks(value, axis):
    n, f = lax.axis_size("fsdp"), lax.axis_index("fsdp")
    return [block_of(value, (f - r) % n, axis) for r in range(n)]


def exchange_rot(value, axis):
    n, f = lax.axis_size("fsdp"), lax.axis_index("fsdp")
    out = [block_of(value, f, axis)]
    for r in range(1, n):
        out.append(from_behind(block_of(value, (f + r) % n, axis), r))
    return out


def natural(got):
    n, f = lax.axis_size("fsdp"), lax.axis_index("fsdp")
    if n == 2:
        return [jnp.where(f == 0, got[0], got[1]), jnp.where(f == 0, got[1], got[0])]
    got = jnp.stack(got)
    return [lax.dynamic_index_in_dim(got, (f - g) % n, 0, keepdims=False) for g in range(n)]


def dp_bits():
    return int(lax.axis_size("dp")).bit_length() - 1


def swapped(p):
    return (p & ~3) | ((p & 1) << 1) | ((p >> 1) & 1)


def turned(p, f):
    return p if dp_bits() < 3 else jnp.where(f % 2 == 0, p, swapped(p))


def dp_swap(value, bit):
    n, dpn = lax.axis_size("fsdp"), lax.axis_size("dp")
    pairs = []
    for i in range(dpn):
        for f in range(n):
            flip = 1 << bit if dp_bits() < 3 or f % 2 == 0 else swapped(1 << bit)
            pairs.append((i * n + f, (i ^ flip) * n + f))
    return lax.ppermute(value, ("dp", "fsdp"), pairs)


def relative(value):
    places = turned(jnp.arange(lax.axis_size("dp")), lax.axis_index("fsdp"))
    return jnp.take(value, lax.axis_index("dp") ^ places, axis=0)


class Halving:
    def __init__(self, order, keep, send):
        self.order = list(order)
        self.keep, self.got = keep, dp_swap(send, self.order.pop(0))

    def step(self):
        if self.got is None:
            return

        def add(part):
            return self.keep[part].astype(F32) + self.got[part].astype(F32)

        if not self.order:
            self.last = add(slice(None))
            self.got = None
            return
        half = self.keep.shape[0] // 2
        send = add(slice(half, None)).astype(BF16)
        self.keep = add(slice(half)).astype(BF16)
        self.got = dp_swap(send, self.order.pop(0))


def place_of(p, order):
    return sum((p >> bit & 1) << i for i, bit in enumerate(reversed(order)))


SUMS = 3


def swap_all_kernel(text_ref, mod_ref, text_out, mod_out, sum_out, part, sends, gets, own):
    dpn, me = lax.axis_size("dp"), lax.axis_index("dp")

    def to_all(kind, source, target):
        copies = []
        for r in range(1, dpn):
            peer = me ^ r
            copies.append(
                pltpu.make_async_remote_copy(
                    src_ref=source(peer), dst_ref=target,
                    send_sem=sends.at[kind, r], recv_sem=gets.at[kind, r],
                    device_id={"dp": peer}, device_id_type=pl.DeviceIdType.MESH,
                )
            )
            copies[-1].start()
        return copies

    mods = to_all(0, lambda peer: mod_ref.at[peer], mod_out.at[me])
    texts = to_all(1, lambda peer: text_ref.at[peer], text_out.at[me])
    local = (
        pltpu.make_async_copy(text_ref.at[me], text_out.at[me], own.at[0]),
        pltpu.make_async_copy(mod_ref.at[me], mod_out.at[me], own.at[1]),
    )
    for copy in local:
        copy.start()
    for copy in (*local, *mods):
        copy.wait()
    part[...] = jnp.sum(mod_out[...], axis=0)
    sums = to_all(2, lambda peer: part, sum_out.at[me])
    mine = pltpu.make_async_copy(part, sum_out.at[me], own.at[2])
    mine.start()
    for copy in (mine, *sums, *texts):
        copy.wait()


def swap_all(text, mods):
    vmem = pl.BlockSpec(memory_space=pltpu.VMEM)
    count = text.shape[0]
    return pl.pallas_call(
        swap_all_kernel,
        in_specs=[vmem] * 2,
        out_specs=[vmem] * 3,
        out_shape=[
            jax.ShapeDtypeStruct(v.shape, v.dtype) for v in (text, mods, mods)
        ],
        scratch_shapes=[
            pltpu.VMEM(mods.shape[1:], mods.dtype),
            pltpu.SemaphoreType.DMA((3, count)), pltpu.SemaphoreType.DMA((3, count)),
            pltpu.SemaphoreType.DMA((3,)),
        ],
        compiler_params=pltpu.CompilerParams(has_side_effects=True),
    )(text, mods)


def advance(chains, value):
    live = [c for c in chains if c.got is not None]
    value, got = lax.optimization_barrier((value, [c.got for c in live]))
    for c, g in zip(live, got):
        c.got = g
        c.step()
    return value


def rope_block(value, cosine, sine, sign):
    width = value.shape[1]
    lane = lax.broadcasted_iota(jnp.int32, value.shape, 1)
    partner = jnp.where(
        lane % 32 < 16, pltpu.roll(value, width - 16, 1), pltpu.roll(value, 16, 1)
    )
    return value * cosine + sign * (partner * sine)


def column(ref, index, width):
    row = ref[index : index + 1, :] if isinstance(index, int) else ref[pl.ds(index, 1), :]
    return jnp.broadcast_to(row, (width, row.shape[1])).T


def masked(value, head):
    lane = lax.broadcasted_iota(jnp.int32, value.shape, 1)
    return jnp.where(lane // HD == head, value, jnp.zeros_like(value))


def attn_fwd_kernel(
    len_ref, pre_ref, inv_ref, gq_ref, gk_ref, cos_ref, sin_ref, tk_ref, tv_ref, gate_ref,
    q_ref, k_ref, v_ref, mixed_ref, so_ref, co_ref, ls_ref, lc_ref,
):
    _, tokens, width = pre_ref.shape
    heads = width // HD
    iq, ik = column(inv_ref, 0, width), column(inv_ref, 1, width)
    q = rope_block(pre_ref[0] * iq * gq_ref[...], cos_ref[...], sin_ref[...], 1.0)
    q_ref[...] = q.astype(BF16)
    k = rope_block(pre_ref[1] * ik * gk_ref[...], cos_ref[...], sin_ref[...], 1.0)
    k_ref[...] = k.astype(BF16)
    v_ref[...] = pre_ref[2].astype(BF16)
    length = len_ref[0]

    def one(keys, values, qm, limit):
        s = dot(qm, keys, 1, 1)
        if limit is not None:
            slot = lax.broadcasted_iota(jnp.int32, s.shape, 1)
            s = jnp.where(slot < limit, s, -1e30)
        peak = jnp.max(s, axis=1, keepdims=True)
        e = jnp.exp(s - peak)
        total = jnp.sum(e, axis=1, keepdims=True)
        o = dot(e.astype(BF16), values)
        return o * (1.0 / total), peak + jnp.log(total)

    lane = lax.broadcasted_iota(jnp.int32, (tokens, width), 1)
    qs = q_ref[...] * jnp.asarray(HD**-0.5, BF16)
    so = co = stats = jnp.zeros((tokens, width), F32)
    for h in range(heads):
        qm = masked(qs, h)
        o, lse = one(k_ref[...], v_ref[...], qm, None)
        so = jnp.where(lane // HD == h, o, so)
        stats = jnp.where(lane == h, lse, stats)
        o, lse = one(tk_ref[...], tv_ref[...], qm, length)
        co = jnp.where(lane // HD == h, o, co)
        stats = jnp.where(lane == heads + h, lse, stats)
    so_ref[...] = so
    co_ref[...] = co
    mixed_ref[...] = (so + gate_ref[...] * co).astype(BF16)
    stats = stats.T
    ls_ref[0] = stats[:heads]
    lc_ref[0] = stats[heads : 2 * heads]


def attn_bwd_kernel(
    len_ref, q_ref, k_ref, v_ref, tk_ref, tv_ref, g_ref, so_ref, co_ref, ls_ref, lc_ref,
    pre_ref, inv_ref, gq_ref, gk_ref, cos_ref, sin_ref, gate_ref,
    d_ref, dtk_ref, dtv_ref, stat_ref, gainq_ref, gaink_ref, gateg_ref,
    gs_ref, gc_ref, ds_ref, dc_ref, kt_ref, tkt_ref, dqt_ref, dk_acc, dv_acc, rq_ref, rk_ref,
):
    tokens, width = q_ref.shape
    heads = width // HD
    scale = jnp.asarray(HD**-0.5, BF16)

    @pl.when(pl.program_id(0) == 0)
    def _():
        rq_ref[...] = jnp.zeros_like(rq_ref)
        rk_ref[...] = jnp.zeros_like(rk_ref)

    g = g_ref[...]
    gs_ref[...] = g.astype(BF16)
    gc_ref[...] = (g * gate_ref[...]).astype(BF16)
    prod_c = g * co_ref[...]
    gateg_ref[...] = jnp.sum(prod_c, axis=0, keepdims=True)
    prod_s = (g * so_ref[...]).T
    prod_c = (prod_c * gate_ref[...]).T
    for h in range(heads):
        ds_ref[h : h + 1, :] = jnp.sum(prod_s[h * HD : (h + 1) * HD], axis=0, keepdims=True)
        dc_ref[h : h + 1, :] = jnp.sum(prod_c[h * HD : (h + 1) * HD], axis=0, keepdims=True)
    kt_ref[...] = k_ref[...].astype(F32).T.astype(BF16)
    tkt_ref[...] = tk_ref[...].astype(F32).T.astype(BF16)
    dk_acc[...] = jnp.zeros_like(dk_acc)
    dv_acc[...] = jnp.zeros_like(dv_acc)
    dtk_ref[...] = jnp.zeros_like(dtk_ref)
    dtv_ref[...] = jnp.zeros_like(dtv_ref)
    length = len_ref[0]

    def one(keys, keys_t, values, qm, gm, lse, delta, head, limit):
        s = dot(keys, qm, 1, 1)
        p = jnp.exp(s - lse)
        if limit is not None:
            slot = lax.broadcasted_iota(jnp.int32, s.shape, 0)
            p = jnp.where(slot < limit, p, 0.0)
        dp = dot(values, gm, 1, 1)
        ds = (p * (dp - delta)).astype(BF16)
        dq = dot(keys_t[head * HD : (head + 1) * HD, :], ds)
        return dq, dot(ds, qm), dot(p.astype(BF16), gm)

    def chunk(c, carry):
        rows = pl.ds(pl.multiple_of(c * QC, QC), QC)
        qc = q_ref[rows, :] * scale
        for h in range(heads):
            qm = masked(qc, h)
            dq, dk, dv = one(
                k_ref[...], kt_ref, v_ref[...], qm, masked(gs_ref[rows, :], h),
                ls_ref[0, h : h + 1, rows], ds_ref[h : h + 1, rows], h, None,
            )
            dk_acc[...] += dk
            dv_acc[...] += dv
            dq2, dk, dv = one(
                tk_ref[...], tkt_ref, tv_ref[...], qm, masked(gc_ref[rows, :], h),
                lc_ref[0, h : h + 1, rows], dc_ref[h : h + 1, rows], h, length,
            )
            dtk_ref[...] += dk
            dtv_ref[...] += dv
            dqt_ref[h * HD : (h + 1) * HD, rows] = (dq + dq2) * HD**-0.5
        return carry

    lax.fori_loop(0, tokens // QC, chunk, 0)
    dq = rope_block(dqt_ref[...].T, cos_ref[...], sin_ref[...], -1.0)
    d_ref[0] = dq
    prod = dq * (pre_ref[0] * column(inv_ref, 0, width))
    gainq_ref[...] = jnp.sum(prod, axis=0, keepdims=True)
    rq_ref[...] += prod * gq_ref[...]
    dk = rope_block(dk_acc[...], cos_ref[...], sin_ref[...], -1.0)
    d_ref[1] = dk
    prod = dk * (pre_ref[1] * column(inv_ref, 1, width))
    gaink_ref[...] = jnp.sum(prod, axis=0, keepdims=True)
    rk_ref[...] += prod * gk_ref[...]
    d_ref[2] = dv_acc[...]

    @pl.when(pl.program_id(0) == pl.num_programs(0) - 1)
    def _():
        stat_ref[...] = jnp.zeros_like(stat_ref)
        for i, ref in enumerate((rq_ref, rk_ref)):
            stat_ref[i : i + 1, :] = jnp.sum(ref[...].T, axis=0, keepdims=True)


def specs(tokens, text, width, heads, at=0):
    col = pl.BlockSpec((tokens, width), lambda i: (0, i + at))
    three = pl.BlockSpec((3, tokens, width), lambda i: (0, 0, i + at))
    tcol = pl.BlockSpec((text, width), lambda i: (0, i + at))
    stat = pl.BlockSpec((8, tokens), lambda i: (0, 0))
    gain = pl.BlockSpec((1, width), lambda i: (0, i + at))
    table = pl.BlockSpec((tokens, width), lambda i: (0, 0))
    lse = pl.BlockSpec((1, heads, tokens), lambda i: (i + at, 0, 0))
    scalar = pl.BlockSpec(memory_space=pltpu.SMEM)
    return col, three, tcol, stat, gain, table, lse, scalar


def sds(shape, dtype=F32):
    return jax.ShapeDtypeStruct(shape, dtype)


def attn_forward(length, pre, inv, gq, gk, cosine, sine, tk, tv, gate):
    _, tokens, columns = pre.shape
    text, width = tk.shape[0], cosine.shape[1]
    heads, blocks = width // HD, columns // width
    col, three, tcol, stat, gain, table, lse, scalar = specs(tokens, text, width, heads)
    flat = (tokens, columns)
    return pl.pallas_call(
        attn_fwd_kernel,
        grid=(blocks,),
        in_specs=[scalar, three, stat, gain, gain, table, table, tcol, tcol, gain],
        out_specs=[col, col, col, col, col, col, lse, lse],
        out_shape=[sds(flat, BF16)] * 4 + [sds(flat)] * 2 + [sds((blocks, heads, tokens))] * 2,
    )(length, pre, inv, gq, gk, cosine, sine, tk, tv, gate)


def attn_backward(at, blocks, length, q, k, v, tk, tv, g, so, co, ls, lc, pre, inv, gq, gk, cosine, sine, gate):
    tokens = q.shape[0]
    text, width = tk.shape[0], cosine.shape[1]
    heads, columns = width // HD, blocks * width
    col, three, tcol, stat, gain, table, lse, scalar = specs(tokens, text, width, heads, at)
    _, three_o, tcol_o, _, gain_o, _, _, _ = specs(tokens, text, width, heads)
    return pl.pallas_call(
        attn_bwd_kernel,
        grid=(blocks,),
        in_specs=[scalar, col, col, col, tcol, tcol, col, col, col, lse, lse,
                  three, stat, gain, gain, table, table, gain],
        out_specs=[three_o, tcol_o, tcol_o, stat, gain_o, gain_o, gain_o],
        out_shape=[
            sds((3, tokens, columns)), sds((text, columns)), sds((text, columns)),
            sds((8, tokens)), sds((1, columns)), sds((1, columns)), sds((1, columns)),
        ],
        scratch_shapes=[
            pltpu.VMEM((tokens, width), BF16), pltpu.VMEM((tokens, width), BF16),
            pltpu.VMEM((heads, tokens), F32), pltpu.VMEM((heads, tokens), F32),
            pltpu.VMEM((width, tokens), BF16), pltpu.VMEM((width, text), BF16),
            pltpu.VMEM((width, tokens), F32),
            pltpu.VMEM((tokens, width), F32), pltpu.VMEM((tokens, width), F32),
            pltpu.VMEM((tokens, width), F32), pltpu.VMEM((tokens, width), F32),
        ],
    )(length, q, k, v, tk, tv, g, so, co, ls, lc, pre, inv, gq, gk, cosine, sine, gate)


def pick(rows, cols, step, part):
    i = lax.broadcasted_iota(jnp.int32, (rows, cols), 0)
    j = lax.broadcasted_iota(jnp.int32, (rows, cols), 1)
    hit = (j == step * i + part) if cols > rows else (i == step * j + part)
    return jnp.where(hit, 1.0, 0.0).astype(BF16)

def text_fwd_kernel(x_ref, w_ref, o_ref):
    @pl.when(pl.program_id(0) == 0)
    def _():
        o_ref[...] = jnp.zeros_like(o_ref)
    for b in range(w_ref.shape[0] // 128):
        rows = slice(b * 128, (b + 1) * 128)
        w = w_ref[rows].reshape(256, w_ref.shape[2])
        x = x_ref[:, rows]
        for j in range(2):
            spread = dot(x, pick(128, 256, 2, j)).astype(BF16)
            o_ref[j] += dot(spread, w)

def text_fwd(x, w):
    depth, _, cols = w.shape
    bk = 256
    return pl.pallas_call(
        text_fwd_kernel, grid=(depth // bk,),
        in_specs=[pl.BlockSpec((x.shape[0], bk), lambda i: (0, i)), pl.BlockSpec((bk, 2, cols), lambda i: (i, 0, 0))],
        out_specs=pl.BlockSpec((2, x.shape[0], cols), lambda i: (0, 0, 0)),
        out_shape=sds((2, x.shape[0], cols)),
    )(x, w)

def text_bwd_kernel(g_ref, w_ref, o_ref):
    for b in range(w_ref.shape[0] // 128):
        rows = slice(b * 128, (b + 1) * 128)
        w = w_ref[rows].reshape(256, w_ref.shape[2])
        total = 0.0
        for j in range(2):
            total = total + dot(g_ref[j], dot(pick(128, 256, 2, j), w).astype(BF16), 1, 1)
        o_ref[:, rows] = total.astype(BF16)

def text_bwd(g, w):
    depth, _, cols = w.shape
    bk = 256
    return pl.pallas_call(
        text_bwd_kernel, grid=(depth // bk,),
        in_specs=[pl.BlockSpec(g.shape, lambda i: (0, 0, 0)), pl.BlockSpec((bk, 2, cols), lambda i: (i, 0, 0))],
        out_specs=pl.BlockSpec((g.shape[1], bk), lambda i: (0, i)),
        out_shape=sds((g.shape[1], depth), BF16),
    )(g, w)

def put_relative(dst, src, me, f, count):
    rows = dst.shape[0] // count
    for p in range(count):
        start = pl.multiple_of((me ^ turned(p, f)) * rows, 16)
        dst[p * rows : (p + 1) * rows, :] = src[pl.ds(start, rows), :]


def put_halves(keep, send, value, count, order, slot=None):
    rows = value.shape[0] // count
    for p in range(count):
        place = place_of(p, order[1:])
        where = place if slot is None else (place, slot)
        (send if p >> order[0] & 1 else keep)[where] = value[p * rows : (p + 1) * rows]


def ffn_kernel(
    orders, id_ref, s_ref, b_ref, w_ref, d_ref,
    wk_ref, ws_ref, dk_ref, ds_ref, fo_ref, fp_ref, so_ref, sp_ref,
    st, bt, tmp, wg, wu, facc, sacc,
):
    step = pl.program_id(0)
    depth, _, cols = w_ref.shape
    own = fo_ref.shape[0]
    count = 2 * dk_ref.shape[0]

    @pl.when(step == 0)
    def _():
        for src, dst in ((s_ref, st), (b_ref, bt)):
            for c in range(depth // 256):
                part = slice(c * 256, (c + 1) * 256)
                tmp[part, :] = src[:, part].astype(F32).T.astype(BF16)
            put_relative(dst, tmp, id_ref[0], id_ref[1], count)
        facc[...] = jnp.zeros_like(facc)
        sacc[...] = jnp.zeros_like(sacc)

    for c in range(depth // 128):
        part = slice(c * 128, (c + 1) * 128)
        w = w_ref[part].reshape(256, cols)
        wg[part, :] = dot(pick(128, 256, 2, 0), w).astype(BF16)
        wu[part, :] = dot(pick(128, 256, 2, 1), w).astype(BF16)
    s, b = s_ref[...], b_ref[...]
    gate = dot(s, wg[...])
    up = dot(s, wu[...])
    back = dot(b, d_ref[...], 1, 1)
    sig = jax.nn.sigmoid(gate)
    silu = gate * sig
    hidden = (silu * up).astype(BF16)
    g_gate = (back * up * (sig + silu * (1.0 - sig))).astype(BF16)
    g_up = (back * silu).astype(BF16)
    put_halves(wk_ref, ws_ref, dot(st[...], g_gate).astype(BF16), count, orders[0], 0)
    put_halves(wk_ref, ws_ref, dot(st[...], g_up).astype(BF16), count, orders[0], 1)
    put_halves(dk_ref, ds_ref, dot(bt[...], hidden).astype(BF16), count, orders[1])
    facc[...] += dot(hidden, d_ref[...])
    sacc[...] += dot(g_gate, wg[...], 1, 1) + dot(g_up, wu[...], 1, 1)

    @pl.when(step == pl.num_programs(0) - 1)
    def _():
        fo_ref[...] = facc[:own]
        fp_ref[...] = facc[own:].astype(BF16)
        so_ref[...] = sacc[:own]
        sp_ref[...] = sacc[own:].astype(BF16)


def ffn(ids, s, b, w, d, local, dp, orders):
    tokens, depth = s.shape
    hid = d.shape[0]
    bc = min(256, hid)
    rest = tokens - local
    once = functools.partial(pl.BlockSpec, pipeline_mode=pl.Buffered(1))
    const = lambda i: (0, 0)
    share = depth // dp
    half = pl.BlockSpec((dp // 2, share, bc), lambda i: (0, 0, i))
    halves = pl.BlockSpec((dp // 2, 2, share, bc), lambda i: (0, 0, 0, i))
    return pl.pallas_call(
        functools.partial(ffn_kernel, orders),
        grid=(hid // bc,),
        in_specs=[
            pl.BlockSpec(memory_space=pltpu.SMEM),
            once((tokens, depth), const), once((tokens, depth), const),
            pl.BlockSpec((depth, 2, bc), lambda i: (0, 0, i)),
            pl.BlockSpec((bc, depth), lambda i: (i, 0)),
        ],
        out_specs=[halves] * 2 + [half] * 2 + [
            once((local, depth), const), once((rest, depth), const),
            once((local, depth), const), once((rest, depth), const),
        ],
        out_shape=[sds((dp // 2, 2, share, hid), BF16)] * 2 + [sds((dp // 2, share, hid), BF16)] * 2 + [
            sds((local, depth)), sds((rest, depth), BF16),
            sds((local, depth)), sds((rest, depth), BF16),
        ],
        scratch_shapes=[
            pltpu.VMEM((depth, tokens), BF16), pltpu.VMEM((depth, tokens), BF16),
            pltpu.VMEM((depth, tokens), BF16),
            pltpu.VMEM((depth, bc), BF16), pltpu.VMEM((depth, bc), BF16),
            pltpu.VMEM((tokens, depth), F32), pltpu.VMEM((tokens, depth), F32),
        ],
        compiler_params=pltpu.CompilerParams(vmem_limit_bytes=62 << 20),
    )(ids, s, b, w, d)


def project_kernel(id_ref, xo_ref, xp_ref, front_ref, w_ref, got_ref, first_ref, pre_ref, sq_ref):
    j = pl.program_id(0)
    local, depth = xo_ref.shape
    own = got_ref.shape[2]
    f = id_ref[1]

    @pl.when(j == 0)
    def _():
        for i, ref in enumerate((xo_ref, xp_ref)):
            x = ref[...].astype(F32)
            inv = lax.rsqrt(jnp.sum(x * x, axis=1, keepdims=True) * (1.0 / depth) + EPSILON)
            first_ref[i * local : (i + 1) * local, :] = (x * inv * front_ref[...]).astype(BF16)
        sq_ref[...] = jnp.zeros_like(sq_ref)

    mine = pl.ds(pl.multiple_of(f * own, 128), own)
    other = pl.ds(pl.multiple_of((1 - f) * own, 128), own)
    out = dot(first_ref[:, mine], w_ref[0, :, mine]) + dot(first_ref[:, other], got_ref[0])
    pre_ref[0] = out
    square = out * out
    part = square[:, :128]
    for c in range(1, own // 128):
        part = part + square[:, c * 128 : (c + 1) * 128]
    sq_ref[pl.ds(j, 1), :] = jnp.sum(part.T, axis=0, keepdims=True)


def project(ids, xo, xp, front, w, got):
    local, depth = xo.shape
    own = got.shape[2]
    tokens = 2 * local
    const = lambda j: (0, 0)
    return pl.pallas_call(
        project_kernel,
        grid=(3,),
        in_specs=[
            pl.BlockSpec(memory_space=pltpu.SMEM),
            pl.BlockSpec((local, depth), const), pl.BlockSpec((local, depth), const),
            pl.BlockSpec((1, depth), const),
            pl.BlockSpec((1, own, depth), lambda j: (j, 0, 0)),
            pl.BlockSpec((1, own, own), lambda j: (j, 0, 0)),
        ],
        out_specs=[
            pl.BlockSpec((tokens, depth), const),
            pl.BlockSpec((1, tokens, own), lambda j: (j, 0, 0)),
            pl.BlockSpec((8, tokens), const),
        ],
        out_shape=[sds((tokens, depth), BF16), sds((3, tokens, own)), sds((8, tokens))],
    )(ids, xo, xp, front, w, got)


def project_grad_kernel(
    order, id_ref, da_ref, db_ref, pre_ref, stat_ref, gain_ref, first_ref,
    keep_ref, send_ref, g_ref, gt, tmp,
):
    j = pl.program_id(0)
    own = pre_ref.shape[2]
    cut = da_ref.shape[2]
    count = 2 * keep_ref.shape[0]
    inv, mean = column(stat_ref, j, 128), column(stat_ref, j + 3, 128)
    for c in range(own // 128):
        part = slice(c * 128, (c + 1) * 128)
        here = slice(c * 128 - cut, (c + 1) * 128 - cut) if c * 128 >= cut else part
        d = (db_ref if c * 128 >= cut else da_ref)[0, :, here]
        g = inv * (d * gain_ref[0, :, part] - pre_ref[0, :, part] * inv * mean)
        tmp[part, :] = g.T.astype(BF16)
        g_ref[0, :, part] = g.astype(BF16)
    put_relative(gt, tmp, id_ref[0] % count, id_ref[1], count)
    put_halves(keep_ref, send_ref, dot(gt[...], first_ref[...]).astype(BF16), count, order, j)


def project_grad(ids, da, db, pre, stats, gain, first, dp, order):
    _, tokens, own = pre.shape
    depth = first.shape[1]
    share = depth // dp
    const = lambda j: (0, 0)
    block = lambda j: (j, 0, 0)
    once = functools.partial(pl.BlockSpec, pipeline_mode=pl.Buffered(1))
    half = once((dp // 4, 3, share, depth), lambda j: (0, 0, 0, 0))
    return pl.pallas_call(
        functools.partial(project_grad_kernel, order),
        grid=(3,),
        in_specs=[
            pl.BlockSpec(memory_space=pltpu.SMEM),
            pl.BlockSpec((1,) + da.shape[1:], block), pl.BlockSpec((1,) + db.shape[1:], block),
            pl.BlockSpec((1, tokens, own), block),
            pl.BlockSpec((8, tokens), const),
            pl.BlockSpec((1, 1, own), block),
            once((tokens, depth), const),
        ],
        out_specs=[half, half, pl.BlockSpec((1, tokens, own), block)],
        out_shape=[sds((dp // 4, 3, share, depth), BF16)] * 2
        + [sds((3, tokens, own), BF16)],
        scratch_shapes=[pltpu.VMEM((own, tokens), BF16), pltpu.VMEM((own, tokens), BF16)],
    )(ids, da, db, pre, stats, gain, first)


def project_back_kernel(id_ref, g_ref, w_ref, got_ref, own_ref, peer_ref, acc):
    j = pl.program_id(0)
    own = g_ref.shape[2]
    local = own_ref.shape[0]
    f = id_ref[1]
    mine = pl.ds(pl.multiple_of(f * own, 128), own)
    other = pl.ds(pl.multiple_of((1 - f) * own, 128), own)

    @pl.when(j == 0)
    def _():
        acc[...] = jnp.zeros_like(acc)

    acc[:, mine] += dot(g_ref[0], w_ref[0, :, mine], 1, 1)
    acc[:, other] += dot(g_ref[0], got_ref[0], 1, 1)

    @pl.when(j == 2)
    def _():
        own_ref[...] = acc[:local]
        peer_ref[...] = acc[local:].astype(BF16)


def project_back(ids, g, w, got):
    _, tokens, own = g.shape
    depth = w.shape[2]
    local = tokens // 2
    const = lambda j: (0, 0)
    block = lambda j: (j, 0, 0)
    once = functools.partial(pl.BlockSpec, pipeline_mode=pl.Buffered(1))
    return pl.pallas_call(
        project_back_kernel,
        grid=(3,),
        in_specs=[
            pl.BlockSpec(memory_space=pltpu.SMEM),
            pl.BlockSpec((1, tokens, own), block),
            pl.BlockSpec((1, own, depth), block), pl.BlockSpec((1, own, own), block),
        ],
        out_specs=[once((local, depth), const), once((local, depth), const)],
        out_shape=[sds((local, depth)), sds((local, depth), BF16)],
        scratch_shapes=[pltpu.VMEM((tokens, depth), F32)],
    )(ids, g, w, got)


def out_back_kernel(order, id_ref, *refs):
    n = len(refs) - 8
    blocks, (w_ref, mixed_ref, g_ref, keep_ref, send_ref, all_ref, gt, tmp) = refs[:n], refs[n:]
    local = blocks[0].shape[0]
    for r, ref in enumerate(blocks):
        all_ref[r * local : (r + 1) * local, :] = ref[...]
    grad = all_ref[...]
    g_ref[...] = dot(grad, w_ref[...], 1, 1)
    for c in range(grad.shape[1] // 256):
        part = slice(c * 256, (c + 1) * 256)
        tmp[part, :] = grad[:, part].astype(F32).T.astype(BF16)
    count = 2 * keep_ref.shape[0]
    put_relative(gt, tmp, id_ref[0], id_ref[1], count)
    put_halves(keep_ref, send_ref, dot(gt[...], mixed_ref[...]).astype(BF16), count, order)


def out_back(ids, blocks, w, mixed, dp, order):
    tokens, own = mixed.shape
    depth = w.shape[1]
    vmem = pl.BlockSpec(memory_space=pltpu.VMEM)
    half = sds((dp // 2, depth // dp, own), BF16)
    return pl.pallas_call(
        functools.partial(out_back_kernel, order),
        in_specs=[pl.BlockSpec(memory_space=pltpu.SMEM)] + [vmem] * (len(blocks) + 2),
        out_specs=[vmem] * 3,
        out_shape=[sds((tokens, own)), half, half],
        scratch_shapes=[
            pltpu.VMEM((tokens, depth), BF16),
            pltpu.VMEM((depth, tokens), BF16), pltpu.VMEM((depth, tokens), BF16),
        ],
    )(ids, *blocks, w, mixed)


def time_embed(timesteps):
    half = TE // 2
    frequencies = jnp.exp(-math.log(10000.0) * jnp.arange(half, dtype=F32) / half)
    angles = timesteps.astype(F32)[:, None] * frequencies
    waves = jnp.concatenate([jnp.cos(angles), jnp.sin(angles)], axis=-1)
    return jax.nn.silu(waves).astype(BF16)


def rope_tables(positions, width):
    lane = jnp.arange(width)
    quarter = HD // 4
    frequencies = 10000.0 ** (-(lane % quarter).astype(F32) / quarter)
    place = jnp.where(lane % HD < HD // 2, positions[0][:, None], positions[1][:, None])
    angles = place.astype(F32) * frequencies
    return jnp.cos(angles), jnp.where(lane % 32 < 16, -1.0, 1.0) * jnp.sin(angles)


def inverse_rms(values):
    return lax.rsqrt(jnp.mean(values * values, axis=-1, keepdims=True) + EPSILON)


def rms_back(grad_hat, normed, inverse):
    return inverse * (grad_hat - normed * jnp.mean(grad_hat * normed, axis=-1, keepdims=True))


def pad_cols(value, width):
    extra = -value.shape[-1] % width
    return value if extra == 0 else jnp.pad(value, [(0, 0)] * (value.ndim - 1) + [(0, extra)])


def on_device(
    hidden_in, text_state, caption_lengths, timesteps, patch_positions, cotangent,
    w_ada, w_text, w_qkv, w_out, gains, cross_gate, w_gate_up, w_down,
):
    n, f = lax.axis_size("fsdp"), lax.axis_index("fsdp")
    dpn, me = lax.axis_size("dp"), lax.axis_index("dp")
    bits = list(range(dp_bits()))
    low_bits = bits[:-1]
    late = bits[2:] + bits[:2]
    own_d = D // n
    local = hidden_in.shape[1]
    tokens = n * local
    width = 2 * HD
    share = D // dpn
    paired = n == 2 and dpn >= 4
    ids = jnp.stack([me, f]).astype(jnp.int32)
    x_bf, dy_bf = hidden_in[0], cotangent[0]

    time_low = time_embed(timesteps)
    own_te = TE // n
    time_own = lax.dynamic_slice_in_dim(time_low[0], f * own_te, own_te, 0)
    modulation = pair_sum(
        jnp.einsum("k,kjd->jd", time_own, w_ada, preferred_element_type=F32)
    )
    scale_attn, gate_attn = modulation[0:1], jnp.tanh(modulation[1:2])
    scale_ffn, gate_ffn = modulation[2:3], jnp.tanh(modulation[3:4])

    w_flat = jnp.moveaxis(w_qkv, 1, 0)
    w_parts = exchange_rot(w_flat, 2)
    x_parts = gather_rot(x_bf)
    dy_all = jnp.concatenate(gather_rot(dy_bf), axis=0)
    places = jnp.concatenate(gather_rot(patch_positions[0]), axis=1)
    text_cols = jnp.concatenate(natural(exchange_rot(text_state[0], 1)), axis=0)
    text_all = lax.all_gather(text_cols, "dp", axis=0, tiled=True)
    gain_full = lax.all_gather(gains, "fsdp", axis=1, tiled=True).astype(F32)
    gain_own = gains.astype(F32)

    front = gain_full[0] * (1.0 + scale_attn)
    if paired:
        first_all, pre, squares = project(ids, *x_parts, front, w_flat, w_parts[1])
    else:
        w_heads = jnp.concatenate(natural(w_parts), axis=1)
        x_f = jnp.concatenate(x_parts, axis=0).astype(F32)
        first_all = (x_f * inverse_rms(x_f) * front).astype(BF16)
        pre = jnp.stack([dot(first_all, w_heads[j]) for j in range(3)])
        squares = jnp.pad(jnp.sum(pre[:2] * pre[:2], -1), ((0, 6), (0, 0)))
    inverse = lax.rsqrt(row_sum(squares) / D + EPSILON)

    text_part = text_fwd(text_cols, w_text)
    text_pre = scatter_rot(rot_blocks(text_part, 2))
    inv_t = lax.rsqrt(
        pair_sum(jnp.sum(text_pre[0] * text_pre[0], -1, keepdims=True)) / D + EPSILON
    )
    normed_t = text_pre[0] * inv_t
    tk = (normed_t * gain_own[4]).astype(BF16)
    tv = text_pre[1].astype(BF16)

    head_tanh = jnp.tanh(cross_gate.astype(F32))
    gate_row = pad_cols(jnp.repeat(head_tanh, HD)[None], width)
    cosine, sine = rope_tables(places, width)
    gq, gk = pad_cols(gain_own[2:3], width), pad_cols(gain_own[3:4], width)
    pre_p, tkp, tvp = pad_cols(pre, width), pad_cols(tk, width), pad_cols(tv, width)
    q, k, v, mixed_p, so, co, ls, lc = attn_forward(
        caption_lengths, pre_p, inverse, gq, gk, cosine, sine, tkp, tvp, gate_row
    )
    mixed = mixed_p[:, :own_d]

    def rows(value, r):
        return value[r * local : (r + 1) * local]

    parts = [dot(rows(mixed, r), w_out) for r in range(n)]
    attn_branch = scatter_rot([parts[0]] + [p.astype(BF16) for p in parts[1:]])
    x_own = x_bf.astype(F32)
    after_attn = x_own + gate_attn * attn_branch
    inverse_two = inverse_rms(after_attn)
    normed_two = after_attn * inverse_two
    second = (normed_two * gain_full[1] * (1.0 + scale_ffn)).astype(BF16)

    second_all = jnp.concatenate(gather_rot(second), axis=0)
    branch_all = (gate_ffn * dy_all.astype(F32)).astype(BF16)
    wide_keep, wide_send, down_keep, down_send, ffn_own, ffn_rest, back_own, back_rest = ffn(
        ids, second_all, branch_all, w_gate_up, w_down, local, dpn, (bits, late)
    )
    (ffn_own, ffn_rest, back_own, back_rest), text_all = lax.optimization_barrier(
        ((ffn_own, ffn_rest, back_own, back_rest), text_all)
    )
    wide_chain = Halving(bits, wide_keep, wide_send)
    down_chain = Halving(late, down_keep, down_send)
    grad_second = scatter_rot([back_own] + [rows(back_rest, r) for r in range(n - 1)])
    ffn_branch = scatter_rot([ffn_own] + [rows(ffn_rest, r) for r in range(n - 1)])
    output = (after_attn + gate_ffn * ffn_branch).astype(BF16)
    dy = dy_bf.astype(F32)
    d_gate_ffn = jnp.sum(dy * ffn_branch, axis=0) * (1.0 - gate_ffn[0] * gate_ffn[0])

    scaled = grad_second * normed_two
    d_scale_ffn = jnp.sum(scaled * gain_full[1], axis=0)
    gain_two = jnp.sum(scaled * (1.0 + scale_ffn), axis=0)
    grad_after = dy + rms_back(
        grad_second * gain_full[1] * (1.0 + scale_ffn), normed_two, inverse_two
    )
    d_gate_attn = jnp.sum(grad_after * attn_branch, axis=0) * (1.0 - gate_attn[0] * gate_attn[0])
    grad_attn = (gate_attn * grad_after).astype(BF16)
    grad_mixed, *out_halves = out_back(ids, gather_rot(grad_attn), w_out, mixed, dpn, bits)
    out_chain = Halving(bits, *out_halves)
    blocks = pre_p.shape[2] // width
    cut = max(1, 2 * blocks // 3)
    grad_mixed = pad_cols(grad_mixed, width)
    inputs = (so, co, ls, lc, pre_p, inverse, gq, gk, cosine, sine, gate_row)
    part_a = attn_backward(0, cut, caption_lengths, q, k, v, tkp, tvp, grad_mixed, *inputs)
    part_a, grad_mixed = lax.optimization_barrier((part_a, grad_mixed))
    grad_mixed = advance([wide_chain, down_chain], grad_mixed)
    part_b = attn_backward(
        cut, blocks - cut, caption_lengths, q, k, v, tkp, tvp, grad_mixed, *inputs
    )
    means = row_sum(part_a[3] + part_b[3])[:2] / D

    ones, zeros = jnp.ones((1, tokens), F32), jnp.zeros((1, tokens), F32)
    if paired:
        stats = jnp.concatenate([inverse[:2], ones, means, zeros, zeros, zeros], axis=0)
        gain3 = jnp.stack([gain_own[2:3], gain_own[3:4], jnp.ones_like(gain_own[2:3])])
        keep, send, grads = project_grad(
            ids, part_a[0], part_b[0], pre, stats, gain3, first_all, dpn, low_bits
        )
        part_a, part_b, grads = advance([wide_chain, out_chain], (part_a[1:], part_b[1:], grads))
        qkv_chain = Halving(low_bits, keep, send)
        parts = project_back(ids, grads, w_flat, w_parts[1])
    else:
        d = jnp.concatenate([part_a[0], part_b[0]], axis=2)[:, :, :own_d]
        part_a, part_b = part_a[1:], part_b[1:]
        inv, mean = inverse[:2, :, None], means[:, :, None]
        hat = d[:2] * gain_own[2:4][:, None] - pre[:2] * inv * mean
        grads = [(inv[0] * hat[0]).astype(BF16), (inv[1] * hat[1]).astype(BF16), d[2].astype(BF16)]
        wide = [dot(g, first_all, 0, 0).astype(BF16) for g in grads]
        wide = [jnp.concatenate(natural(exchange_rot(w_, 1)), axis=0) for w_ in wide]
        wide = relative(jnp.stack([w_.reshape(dpn, share, own_d) for w_ in wide], axis=1))
        wide = jnp.stack([wide[p] for p in sorted(range(dpn), key=lambda p: place_of(p, bits))])
        qkv_chain = Halving(bits, wide[: dpn // 2], wide[dpn // 2 :])
        parts = [
            sum(dot(rows(g, r), w_heads[j], 1, 1) for j, g in enumerate(grads)) for r in range(n)
        ]
        parts = [parts[0]] + [p.astype(BF16) for p in parts[1:]]
    grad_first = scatter_rot(parts)

    dtk, dtv, gain_q, gain_k, gate_g = (
        jnp.concatenate([part_a[i], part_b[i]], axis=1)[:, :own_d] for i in (0, 1, 3, 4, 5)
    )
    gate_total = jnp.sum(gate_g[0].reshape(HEADS // n, HD), axis=1) * (
        1.0 - head_tanh * head_tanh
    )
    text_hat = dtk * gain_own[4]
    gain_text = jnp.sum(dtk * normed_t, axis=0, keepdims=True)
    mean_t = pair_sum(jnp.sum(text_hat * normed_t, -1, keepdims=True)) / D
    grad_tk = (inv_t * (text_hat - normed_t * mean_t)).astype(BF16)
    text_pair = jnp.stack([grad_tk, dtv.astype(BF16)])
    pair_all = jnp.concatenate(natural(gather_rot(text_pair)), axis=-1)
    pair_all = advance([qkv_chain], pair_all)
    text_in = text_bwd(pair_all, w_text)
    text_in, grad_first = advance([qkv_chain], (text_in, grad_first))
    text_in = jnp.concatenate(natural(exchange_rot(text_in, 0)), axis=1)

    inverse_one = inverse_rms(x_own)
    normed_one = x_own * inverse_one
    scaled = grad_first * normed_one
    d_scale_attn = jnp.sum(scaled * gain_full[0], axis=0)
    gain_one = jnp.sum(scaled * (1.0 + scale_attn), axis=0)
    grad_input = (
        grad_after
        + rms_back(grad_first * gain_full[0] * (1.0 + scale_attn), normed_one, inverse_one)
    ).astype(BF16)


    sums = [d_scale_attn, d_gate_attn, d_scale_ffn, d_gate_ffn, gain_one, gain_two]
    sums = pair_sum(jnp.stack(sums))
    stamp = jnp.full((1, D), timesteps[0].astype(F32))
    gate_pad = jnp.pad(gate_total, (0, own_d - gate_total.shape[0]))[None]
    small = jnp.concatenate([block_of(sums[4:], f, 1), gain_q, gain_k, gain_text, gate_pad], axis=0)
    small = jnp.pad(small.reshape(-1), (0, dpn * SUMS * 128 - small.size))
    mods = jnp.concatenate([sums[:4], stamp], axis=0).reshape(5, dpn, share).transpose(1, 0, 2)
    mods = jnp.pad(mods, ((0, 0), (0, 0), (0, -share % 128)))
    mods = jnp.concatenate([mods, small.reshape(dpn, SUMS, 128)], axis=1)
    outgoing = block_of(pair_all.transpose(0, 2, 1), f, 2)
    outgoing = outgoing.reshape(2, dpn, share, TEXT // n).transpose(1, 0, 2, 3)
    mods = advance([wide_chain, down_chain, out_chain], mods)
    pair_cols, mods, small = swap_all(outgoing, mods)
    chains = [out_chain, down_chain] if paired else [qkv_chain, out_chain, down_chain]
    if paired:
        qkv_got = qkv_chain.got
        (pair_cols, mods, small), qkv_chain.got = lax.optimization_barrier(
            ((pair_cols, mods, small), qkv_got)
        )
        qkv_chain.step()
        own_side = f == (me >> low_bits[-1] + 1)
        mine, got = exchange_rot(qkv_chain.last[0].astype(BF16), 2)
        got, wide_chain.keep = lax.optimization_barrier((got, wide_chain.keep))
        qkv_chain = Halving(
            bits[-1:], jnp.where(own_side, mine, got)[None], jnp.where(own_side, got, mine)[None]
        )
    pair_cols = advance(chains, pair_cols)
    pair_cols = jnp.concatenate(natural(gather_rot(pair_cols)), axis=3)
    pair_cols = pair_cols.transpose(1, 2, 0, 3).reshape(2 * share, dpn * TEXT)
    text_grad = dot(pair_cols, text_all).reshape(2, share, TW // n)
    total = small[:, 5 : 5 + SUMS].reshape(-1)[: 6 * own_d].reshape(6, own_d)
    times = time_embed(mods[:, 4, 0])
    times = lax.dynamic_slice_in_dim(times, f * own_te, own_te, 1).astype(F32)
    ada_grad = lax.dot_general(
        mods[:, :4, :share].reshape(dpn, 4 * share), times, (((0,), (0,)), ((), ())),
        precision=lax.Precision.HIGHEST,
    ).reshape(4, share, own_te)

    for chain in (out_chain, down_chain, wide_chain, qkv_chain):
        while chain.got is not None:
            chain.step()
    return (
        output[None],
        grad_input[None],
        text_in[None],
        ada_grad.transpose(2, 0, 1),
        text_grad.transpose(2, 0, 1),
        qkv_chain.last[0].transpose(2, 0, 1),
        out_chain.last[0].T,
        total[:5],
        total[5, : HEADS // n],
        wide_chain.last[0].transpose(1, 0, 2),
        down_chain.last[0].T,
    )


def solution(mesh):
    return jax.shard_map(
        on_device,
        mesh=mesh,
        in_specs=(
            P("dp", "fsdp", None),
            P("dp", "fsdp", None),
            P("dp"),
            P("dp"),
            P("dp", None, "fsdp"),
            P("dp", "fsdp", None),
            P("fsdp", None, None),
            P("fsdp", None, None),
            P("fsdp", None, None),
            P("fsdp", None),
            P(None, "fsdp"),
            P("fsdp"),
            P(None, None, "fsdp"),
            P("fsdp", None),
        ),
        out_specs=(
            P("dp", "fsdp", None),
            P("dp", "fsdp", None),
            P("dp", "fsdp", None),
            P("fsdp", None, "dp"),
            P("fsdp", None, "dp"),
            P("fsdp", None, "dp"),
            P("fsdp", "dp"),
            P(None, "fsdp"),
            P("fsdp"),
            P("dp", None, "fsdp"),
            P("fsdp", "dp"),
        ),
        check_vma=False,
    )
```

```python
import functools
import math

import jax
import jax.numpy as jnp
from jax import lax
from jax.experimental import pallas as pl
from jax.experimental.pallas import tpu as pltpu
from jax.sharding import PartitionSpec as P

D = 1536
HEADS = 24
HD = 64
TW = 4096
TE = 1024
PATCHES = 1024
TEXT = 256
EPSILON = 1e-06
F32 = jnp.float32
BF16 = jnp.bfloat16
QC = 256


def dot(a, b, ca=1, cb=0):
    return lax.dot_general(a, b, (((ca,), (cb,)), ((), ())), preferred_element_type=F32)


def from_behind(value, step):
    n = lax.axis_size("fsdp")
    return lax.ppermute(value, "fsdp", [(i, (i + step) % n) for i in range(n)])


def gather_rot(value):
    return [value] + [from_behind(value, r) for r in range(1, lax.axis_size("fsdp"))]


def pair_sum(value):
    return functools.reduce(lambda a, b: a + b, gather_rot(value))


def row_sum(value):
    n = lax.axis_size("fsdp")
    rows = value.shape[-1] // n
    total = value
    for r in range(1, n):
        total = total + jnp.roll(from_behind(value, r), r * rows, axis=-1)
    return total


def scatter_rot(blocks):
    n = lax.axis_size("fsdp")
    total = blocks[0].astype(F32)
    for r in range(1, n):
        got = lax.ppermute(blocks[r], "fsdp", [(i, (i - r) % n) for i in range(n)])
        total = total + got.astype(F32)
    return total


def block_of(value, index, axis):
    size = value.shape[axis] // lax.axis_size("fsdp")
    return lax.dynamic_slice_in_dim(value, index * size, size, axis)


def rot_blocks(value, axis):
    n, f = lax.axis_size("fsdp"), lax.axis_index("fsdp")
    return [block_of(value, (f - r) % n, axis) for r in range(n)]


def exchange_rot(value, axis):
    n, f = lax.axis_size("fsdp"), lax.axis_index("fsdp")
    out = [block_of(value, f, axis)]
    for r in range(1, n):
        out.append(from_behind(block_of(value, (f + r) % n, axis), r))
    return out


def natural(got):
    n, f = lax.axis_size("fsdp"), lax.axis_index("fsdp")
    if n == 2:
        return [jnp.where(f == 0, got[0], got[1]), jnp.where(f == 0, got[1], got[0])]
    got = jnp.stack(got)
    return [lax.dynamic_index_in_dim(got, (f - g) % n, 0, keepdims=False) for g in range(n)]


def dp_bits():
    return int(lax.axis_size("dp")).bit_length() - 1


def swapped(p):
    return (p & ~3) | ((p & 1) << 1) | ((p >> 1) & 1)


def turned(p, f):
    return p if dp_bits() < 3 else jnp.where(f % 2 == 0, p, swapped(p))


def dp_swap(value, bit):
    n, dpn = lax.axis_size("fsdp"), lax.axis_size("dp")
    pairs = []
    for i in range(dpn):
        for f in range(n):
            flip = 1 << bit if dp_bits() < 3 or f % 2 == 0 else swapped(1 << bit)
            pairs.append((i * n + f, (i ^ flip) * n + f))
    return lax.ppermute(value, ("dp", "fsdp"), pairs)


def relative(value):
    places = turned(jnp.arange(lax.axis_size("dp")), lax.axis_index("fsdp"))
    return jnp.take(value, lax.axis_index("dp") ^ places, axis=0)


class Halving:
    def __init__(self, order, keep, send):
        self.order = list(order)
        self.keep, self.got = keep, dp_swap(send, self.order.pop(0))

    def step(self):
        if self.got is None:
            return

        def add(part):
            return self.keep[part].astype(F32) + self.got[part].astype(F32)

        if not self.order:
            self.last = add(slice(None))
            self.got = None
            return
        half = self.keep.shape[0] // 2
        send = add(slice(half, None)).astype(BF16)
        self.keep = add(slice(half)).astype(BF16)
        self.got = dp_swap(send, self.order.pop(0))


def place_of(p, order):
    return sum((p >> bit & 1) << i for i, bit in enumerate(reversed(order)))


SUMS = 3


def swap_all_kernel(text_ref, mod_ref, text_out, mod_out, sum_out, part, sends, gets, own):
    dpn, me = lax.axis_size("dp"), lax.axis_index("dp")

    def to_all(kind, source, target):
        copies = []
        for r in range(1, dpn):
            peer = me ^ r
            copies.append(
                pltpu.make_async_remote_copy(
                    src_ref=source(peer), dst_ref=target,
                    send_sem=sends.at[kind, r], recv_sem=gets.at[kind, r],
                    device_id={"dp": peer}, device_id_type=pl.DeviceIdType.MESH,
                )
            )
            copies[-1].start()
        return copies

    mods = to_all(0, lambda peer: mod_ref.at[peer], mod_out.at[me])
    texts = to_all(1, lambda peer: text_ref.at[peer], text_out.at[me])
    local = (
        pltpu.make_async_copy(text_ref.at[me], text_out.at[me], own.at[0]),
        pltpu.make_async_copy(mod_ref.at[me], mod_out.at[me], own.at[1]),
    )
    for copy in local:
        copy.start()
    for copy in (*local, *mods):
        copy.wait()
    part[...] = jnp.sum(mod_out[...], axis=0)
    sums = to_all(2, lambda peer: part, sum_out.at[me])
    mine = pltpu.make_async_copy(part, sum_out.at[me], own.at[2])
    mine.start()
    for copy in (mine, *sums, *texts):
        copy.wait()


def swap_all(text, mods):
    vmem = pl.BlockSpec(memory_space=pltpu.VMEM)
    count = text.shape[0]
    return pl.pallas_call(
        swap_all_kernel,
        in_specs=[vmem] * 2,
        out_specs=[vmem] * 3,
        out_shape=[
            jax.ShapeDtypeStruct(v.shape, v.dtype) for v in (text, mods, mods)
        ],
        scratch_shapes=[
            pltpu.VMEM(mods.shape[1:], mods.dtype),
            pltpu.SemaphoreType.DMA((3, count)), pltpu.SemaphoreType.DMA((3, count)),
            pltpu.SemaphoreType.DMA((3,)),
        ],
        compiler_params=pltpu.CompilerParams(has_side_effects=True),
    )(text, mods)


def advance(chains, value):
    live = [c for c in chains if c.got is not None]
    value, got = lax.optimization_barrier((value, [c.got for c in live]))
    for c, g in zip(live, got):
        c.got = g
        c.step()
    return value


def rope_block(value, cosine, sine, sign):
    width = value.shape[1]
    lane = lax.broadcasted_iota(jnp.int32, value.shape, 1)
    partner = jnp.where(
        lane % 32 < 16, pltpu.roll(value, width - 16, 1), pltpu.roll(value, 16, 1)
    )
    return value * cosine + sign * (partner * sine)


def column(ref, index, width):
    row = ref[index : index + 1, :] if isinstance(index, int) else ref[pl.ds(index, 1), :]
    return jnp.broadcast_to(row, (width, row.shape[1])).T


def masked(value, head):
    lane = lax.broadcasted_iota(jnp.int32, value.shape, 1)
    return jnp.where(lane // HD == head, value, jnp.zeros_like(value))


def attn_fwd_kernel(
    len_ref, pre_ref, inv_ref, gq_ref, gk_ref, cos_ref, sin_ref, tk_ref, tv_ref, gate_ref,
    q_ref, k_ref, v_ref, mixed_ref, so_ref, co_ref, ls_ref, lc_ref,
):
    _, tokens, width = pre_ref.shape
    heads = width // HD
    iq, ik = column(inv_ref, 0, width), column(inv_ref, 1, width)
    q = rope_block(pre_ref[0] * iq * gq_ref[...], cos_ref[...], sin_ref[...], 1.0)
    q_ref[...] = q.astype(BF16)
    k = rope_block(pre_ref[1] * ik * gk_ref[...], cos_ref[...], sin_ref[...], 1.0)
    k_ref[...] = k.astype(BF16)
    v_ref[...] = pre_ref[2].astype(BF16)
    length = len_ref[0]

    def one(keys, values, qm, limit):
        s = dot(qm, keys, 1, 1)
        if limit is not None:
            slot = lax.broadcasted_iota(jnp.int32, s.shape, 1)
            s = jnp.where(slot < limit, s, -1e30)
        peak = jnp.max(s, axis=1, keepdims=True)
        e = jnp.exp(s - peak)
        total = jnp.sum(e, axis=1, keepdims=True)
        o = dot(e.astype(BF16), values)
        return o * (1.0 / total), peak + jnp.log(total)

    lane = lax.broadcasted_iota(jnp.int32, (tokens, width), 1)
    qs = q_ref[...] * jnp.asarray(HD**-0.5, BF16)
    so = co = stats = jnp.zeros((tokens, width), F32)
    for h in range(heads):
        qm = masked(qs, h)
        o, lse = one(k_ref[...], v_ref[...], qm, None)
        so = jnp.where(lane // HD == h, o, so)
        stats = jnp.where(lane == h, lse, stats)
        o, lse = one(tk_ref[...], tv_ref[...], qm, length)
        co = jnp.where(lane // HD == h, o, co)
        stats = jnp.where(lane == heads + h, lse, stats)
    so_ref[...] = so
    co_ref[...] = co
    mixed_ref[...] = (so + gate_ref[...] * co).astype(BF16)
    stats = stats.T
    ls_ref[0] = stats[:heads]
    lc_ref[0] = stats[heads : 2 * heads]


def attn_bwd_kernel(
    len_ref, q_ref, k_ref, v_ref, tk_ref, tv_ref, g_ref, so_ref, co_ref, ls_ref, lc_ref,
    pre_ref, inv_ref, gq_ref, gk_ref, cos_ref, sin_ref, gate_ref,
    d_ref, dtk_ref, dtv_ref, stat_ref, gainq_ref, gaink_ref, gateg_ref,
    gs_ref, gc_ref, ds_ref, dc_ref, kt_ref, tkt_ref, dqt_ref, dk_acc, dv_acc, rq_ref, rk_ref,
):
    tokens, width = q_ref.shape
    heads = width // HD
    scale = jnp.asarray(HD**-0.5, BF16)

    @pl.when(pl.program_id(0) == 0)
    def _():
        rq_ref[...] = jnp.zeros_like(rq_ref)
        rk_ref[...] = jnp.zeros_like(rk_ref)

    g = g_ref[...]
    gs_ref[...] = g.astype(BF16)
    gc_ref[...] = (g * gate_ref[...]).astype(BF16)
    prod_c = g * co_ref[...]
    gateg_ref[...] = jnp.sum(prod_c, axis=0, keepdims=True)
    prod_s = (g * so_ref[...]).T
    prod_c = (prod_c * gate_ref[...]).T
    for h in range(heads):
        ds_ref[h : h + 1, :] = jnp.sum(prod_s[h * HD : (h + 1) * HD], axis=0, keepdims=True)
        dc_ref[h : h + 1, :] = jnp.sum(prod_c[h * HD : (h + 1) * HD], axis=0, keepdims=True)
    kt_ref[...] = k_ref[...].astype(F32).T.astype(BF16)
    tkt_ref[...] = tk_ref[...].astype(F32).T.astype(BF16)
    dk_acc[...] = jnp.zeros_like(dk_acc)
    dv_acc[...] = jnp.zeros_like(dv_acc)
    dtk_ref[...] = jnp.zeros_like(dtk_ref)
    dtv_ref[...] = jnp.zeros_like(dtv_ref)
    length = len_ref[0]

    def one(keys, keys_t, values, qm, gm, lse, delta, head, limit):
        s = dot(keys, qm, 1, 1)
        p = jnp.exp(s - lse)
        if limit is not None:
            slot = lax.broadcasted_iota(jnp.int32, s.shape, 0)
            p = jnp.where(slot < limit, p, 0.0)
        dp = dot(values, gm, 1, 1)
        ds = (p * (dp - delta)).astype(BF16)
        dq = dot(keys_t[head * HD : (head + 1) * HD, :], ds)
        return dq, dot(ds, qm), dot(p.astype(BF16), gm)

    def chunk(c, carry):
        rows = pl.ds(pl.multiple_of(c * QC, QC), QC)
        qc = q_ref[rows, :] * scale
        for h in range(heads):
            qm = masked(qc, h)
            dq, dk, dv = one(
                k_ref[...], kt_ref, v_ref[...], qm, masked(gs_ref[rows, :], h),
                ls_ref[0, h : h + 1, rows], ds_ref[h : h + 1, rows], h, None,
            )
            dk_acc[...] += dk
            dv_acc[...] += dv
            dq2, dk, dv = one(
                tk_ref[...], tkt_ref, tv_ref[...], qm, masked(gc_ref[rows, :], h),
                lc_ref[0, h : h + 1, rows], dc_ref[h : h + 1, rows], h, length,
            )
            dtk_ref[...] += dk
            dtv_ref[...] += dv
            dqt_ref[h * HD : (h + 1) * HD, rows] = (dq + dq2) * HD**-0.5
        return carry

    lax.fori_loop(0, tokens // QC, chunk, 0)
    dq = rope_block(dqt_ref[...].T, cos_ref[...], sin_ref[...], -1.0)
    d_ref[0] = dq
    prod = dq * (pre_ref[0] * column(inv_ref, 0, width))
    gainq_ref[...] = jnp.sum(prod, axis=0, keepdims=True)
    rq_ref[...] += prod * gq_ref[...]
    dk = rope_block(dk_acc[...], cos_ref[...], sin_ref[...], -1.0)
    d_ref[1] = dk
    prod = dk * (pre_ref[1] * column(inv_ref, 1, width))
    gaink_ref[...] = jnp.sum(prod, axis=0, keepdims=True)
    rk_ref[...] += prod * gk_ref[...]
    d_ref[2] = dv_acc[...]

    @pl.when(pl.program_id(0) == pl.num_programs(0) - 1)
    def _():
        stat_ref[...] = jnp.zeros_like(stat_ref)
        for i, ref in enumerate((rq_ref, rk_ref)):
            stat_ref[i : i + 1, :] = jnp.sum(ref[...].T, axis=0, keepdims=True)


def specs(tokens, text, width, heads, at=0):
    col = pl.BlockSpec((tokens, width), lambda i: (0, i + at))
    three = pl.BlockSpec((3, tokens, width), lambda i: (0, 0, i + at))
    tcol = pl.BlockSpec((text, width), lambda i: (0, i + at))
    stat = pl.BlockSpec((8, tokens), lambda i: (0, 0))
    gain = pl.BlockSpec((1, width), lambda i: (0, i + at))
    table = pl.BlockSpec((tokens, width), lambda i: (0, 0))
    lse = pl.BlockSpec((1, heads, tokens), lambda i: (i + at, 0, 0))
    scalar = pl.BlockSpec(memory_space=pltpu.SMEM)
    return col, three, tcol, stat, gain, table, lse, scalar


def sds(shape, dtype=F32):
    return jax.ShapeDtypeStruct(shape, dtype)


def attn_forward(length, pre, inv, gq, gk, cosine, sine, tk, tv, gate):
    _, tokens, columns = pre.shape
    text, width = tk.shape[0], cosine.shape[1]
    heads, blocks = width // HD, columns // width
    col, three, tcol, stat, gain, table, lse, scalar = specs(tokens, text, width, heads)
    flat = (tokens, columns)
    return pl.pallas_call(
        attn_fwd_kernel,
        grid=(blocks,),
        in_specs=[scalar, three, stat, gain, gain, table, table, tcol, tcol, gain],
        out_specs=[col, col, col, col, col, col, lse, lse],
        out_shape=[sds(flat, BF16)] * 4 + [sds(flat)] * 2 + [sds((blocks, heads, tokens))] * 2,
    )(length, pre, inv, gq, gk, cosine, sine, tk, tv, gate)


def attn_backward(at, blocks, length, q, k, v, tk, tv, g, so, co, ls, lc, pre, inv, gq, gk, cosine, sine, gate):
    tokens = q.shape[0]
    text, width = tk.shape[0], cosine.shape[1]
    heads, columns = width // HD, blocks * width
    col, three, tcol, stat, gain, table, lse, scalar = specs(tokens, text, width, heads, at)
    _, three_o, tcol_o, _, gain_o, _, _, _ = specs(tokens, text, width, heads)
    return pl.pallas_call(
        attn_bwd_kernel,
        grid=(blocks,),
        in_specs=[scalar, col, col, col, tcol, tcol, col, col, col, lse, lse,
                  three, stat, gain, gain, table, table, gain],
        out_specs=[three_o, tcol_o, tcol_o, stat, gain_o, gain_o, gain_o],
        out_shape=[
            sds((3, tokens, columns)), sds((text, columns)), sds((text, columns)),
            sds((8, tokens)), sds((1, columns)), sds((1, columns)), sds((1, columns)),
        ],
        scratch_shapes=[
            pltpu.VMEM((tokens, width), BF16), pltpu.VMEM((tokens, width), BF16),
            pltpu.VMEM((heads, tokens), F32), pltpu.VMEM((heads, tokens), F32),
            pltpu.VMEM((width, tokens), BF16), pltpu.VMEM((width, text), BF16),
            pltpu.VMEM((width, tokens), F32),
            pltpu.VMEM((tokens, width), F32), pltpu.VMEM((tokens, width), F32),
            pltpu.VMEM((tokens, width), F32), pltpu.VMEM((tokens, width), F32),
        ],
    )(length, q, k, v, tk, tv, g, so, co, ls, lc, pre, inv, gq, gk, cosine, sine, gate)


def pick(rows, cols, step, part):
    i = lax.broadcasted_iota(jnp.int32, (rows, cols), 0)
    j = lax.broadcasted_iota(jnp.int32, (rows, cols), 1)
    hit = (j == step * i + part) if cols > rows else (i == step * j + part)
    return jnp.where(hit, 1.0, 0.0).astype(BF16)

def text_fwd_kernel(x_ref, w_ref, o_ref):
    @pl.when(pl.program_id(0) == 0)
    def _():
        o_ref[...] = jnp.zeros_like(o_ref)
    for b in range(w_ref.shape[0] // 128):
        rows = slice(b * 128, (b + 1) * 128)
        w = w_ref[rows].reshape(256, w_ref.shape[2])
        x = x_ref[:, rows]
        for j in range(2):
            spread = dot(x, pick(128, 256, 2, j)).astype(BF16)
            o_ref[j] += dot(spread, w)

def text_fwd(x, w):
    depth, _, cols = w.shape
    bk = 256
    return pl.pallas_call(
        text_fwd_kernel, grid=(depth // bk,),
        in_specs=[pl.BlockSpec((x.shape[0], bk), lambda i: (0, i)), pl.BlockSpec((bk, 2, cols), lambda i: (i, 0, 0))],
        out_specs=pl.BlockSpec((2, x.shape[0], cols), lambda i: (0, 0, 0)),
        out_shape=sds((2, x.shape[0], cols)),
    )(x, w)

def text_bwd_kernel(g_ref, w_ref, o_ref):
    for b in range(w_ref.shape[0] // 128):
        rows = slice(b * 128, (b + 1) * 128)
        w = w_ref[rows].reshape(256, w_ref.shape[2])
        total = 0.0
        for j in range(2):
            total = total + dot(g_ref[j], dot(pick(128, 256, 2, j), w).astype(BF16), 1, 1)
        o_ref[:, rows] = total.astype(BF16)

def text_bwd(g, w):
    depth, _, cols = w.shape
    bk = 256
    return pl.pallas_call(
        text_bwd_kernel, grid=(depth // bk,),
        in_specs=[pl.BlockSpec(g.shape, lambda i: (0, 0, 0)), pl.BlockSpec((bk, 2, cols), lambda i: (i, 0, 0))],
        out_specs=pl.BlockSpec((g.shape[1], bk), lambda i: (0, i)),
        out_shape=sds((g.shape[1], depth), BF16),
    )(g, w)

def put_relative(dst, src, me, f, count):
    rows = dst.shape[0] // count
    for p in range(count):
        start = pl.multiple_of((me ^ turned(p, f)) * rows, 16)
        dst[p * rows : (p + 1) * rows, :] = src[pl.ds(start, rows), :]


def put_halves(keep, send, value, count, order, slot=None):
    rows = value.shape[0] // count
    for p in range(count):
        place = place_of(p, order[1:])
        where = place if slot is None else (place, slot)
        (send if p >> order[0] & 1 else keep)[where] = value[p * rows : (p + 1) * rows]


def ffn_kernel(
    orders, id_ref, s_ref, b_ref, w_ref, d_ref,
    wk_ref, ws_ref, dk_ref, ds_ref, fo_ref, fp_ref, so_ref, sp_ref,
    st, bt, tmp, wg, wu, facc, sacc,
):
    step = pl.program_id(0)
    depth, _, cols = w_ref.shape
    own = fo_ref.shape[0]
    count = 2 * dk_ref.shape[0]

    @pl.when(step == 0)
    def _():
        for src, dst in ((s_ref, st), (b_ref, bt)):
            for c in range(depth // 256):
                part = slice(c * 256, (c + 1) * 256)
                tmp[part, :] = src[:, part].astype(F32).T.astype(BF16)
            put_relative(dst, tmp, id_ref[0], id_ref[1], count)
        facc[...] = jnp.zeros_like(facc)
        sacc[...] = jnp.zeros_like(sacc)

    for c in range(depth // 128):
        part = slice(c * 128, (c + 1) * 128)
        w = w_ref[part].reshape(256, cols)
        wg[part, :] = dot(pick(128, 256, 2, 0), w).astype(BF16)
        wu[part, :] = dot(pick(128, 256, 2, 1), w).astype(BF16)
    s, b = s_ref[...], b_ref[...]
    gate = dot(s, wg[...])
    up = dot(s, wu[...])
    back = dot(b, d_ref[...], 1, 1)
    sig = jax.nn.sigmoid(gate)
    silu = gate * sig
    hidden = (silu * up).astype(BF16)
    g_gate = (back * up * (sig + silu * (1.0 - sig))).astype(BF16)
    g_up = (back * silu).astype(BF16)
    put_halves(wk_ref, ws_ref, dot(st[...], g_gate).astype(BF16), count, orders[0], 0)
    put_halves(wk_ref, ws_ref, dot(st[...], g_up).astype(BF16), count, orders[0], 1)
    put_halves(dk_ref, ds_ref, dot(bt[...], hidden).astype(BF16), count, orders[1])
    facc[...] += dot(hidden, d_ref[...])
    sacc[...] += dot(g_gate, wg[...], 1, 1) + dot(g_up, wu[...], 1, 1)

    @pl.when(step == pl.num_programs(0) - 1)
    def _():
        fo_ref[...] = facc[:own]
        fp_ref[...] = facc[own:].astype(BF16)
        so_ref[...] = sacc[:own]
        sp_ref[...] = sacc[own:].astype(BF16)


def ffn(ids, s, b, w, d, local, dp, orders):
    tokens, depth = s.shape
    hid = d.shape[0]
    bc = min(256, hid)
    rest = tokens - local
    once = functools.partial(pl.BlockSpec, pipeline_mode=pl.Buffered(1))
    const = lambda i: (0, 0)
    share = depth // dp
    half = pl.BlockSpec((dp // 2, share, bc), lambda i: (0, 0, i))
    halves = pl.BlockSpec((dp // 2, 2, share, bc), lambda i: (0, 0, 0, i))
    return pl.pallas_call(
        functools.partial(ffn_kernel, orders),
        grid=(hid // bc,),
        in_specs=[
            pl.BlockSpec(memory_space=pltpu.SMEM),
            once((tokens, depth), const), once((tokens, depth), const),
            pl.BlockSpec((depth, 2, bc), lambda i: (0, 0, i)),
            pl.BlockSpec((bc, depth), lambda i: (i, 0)),
        ],
        out_specs=[halves] * 2 + [half] * 2 + [
            once((local, depth), const), once((rest, depth), const),
            once((local, depth), const), once((rest, depth), const),
        ],
        out_shape=[sds((dp // 2, 2, share, hid), BF16)] * 2 + [sds((dp // 2, share, hid), BF16)] * 2 + [
            sds((local, depth)), sds((rest, depth), BF16),
            sds((local, depth)), sds((rest, depth), BF16),
        ],
        scratch_shapes=[
            pltpu.VMEM((depth, tokens), BF16), pltpu.VMEM((depth, tokens), BF16),
            pltpu.VMEM((depth, tokens), BF16),
            pltpu.VMEM((depth, bc), BF16), pltpu.VMEM((depth, bc), BF16),
            pltpu.VMEM((tokens, depth), F32), pltpu.VMEM((tokens, depth), F32),
        ],
        compiler_params=pltpu.CompilerParams(vmem_limit_bytes=62 << 20),
    )(ids, s, b, w, d)


def project_kernel(id_ref, xo_ref, xp_ref, front_ref, w_ref, got_ref, first_ref, pre_ref, sq_ref):
    j = pl.program_id(0)
    local, depth = xo_ref.shape
    own = got_ref.shape[2]
    f = id_ref[1]

    @pl.when(j == 0)
    def _():
        for i, ref in enumerate((xo_ref, xp_ref)):
            x = ref[...].astype(F32)
            inv = lax.rsqrt(jnp.sum(x * x, axis=1, keepdims=True) * (1.0 / depth) + EPSILON)
            first_ref[i * local : (i + 1) * local, :] = (x * inv * front_ref[...]).astype(BF16)
        sq_ref[...] = jnp.zeros_like(sq_ref)

    mine = pl.ds(pl.multiple_of(f * own, 128), own)
    other = pl.ds(pl.multiple_of((1 - f) * own, 128), own)
    out = dot(first_ref[:, mine], w_ref[0, :, mine]) + dot(first_ref[:, other], got_ref[0])
    pre_ref[0] = out
    square = out * out
    part = square[:, :128]
    for c in range(1, own // 128):
        part = part + square[:, c * 128 : (c + 1) * 128]
    sq_ref[pl.ds(j, 1), :] = jnp.sum(part.T, axis=0, keepdims=True)


def project(ids, xo, xp, front, w, got):
    local, depth = xo.shape
    own = got.shape[2]
    tokens = 2 * local
    const = lambda j: (0, 0)
    return pl.pallas_call(
        project_kernel,
        grid=(3,),
        in_specs=[
            pl.BlockSpec(memory_space=pltpu.SMEM),
            pl.BlockSpec((local, depth), const), pl.BlockSpec((local, depth), const),
            pl.BlockSpec((1, depth), const),
            pl.BlockSpec((1, own, depth), lambda j: (j, 0, 0)),
            pl.BlockSpec((1, own, own), lambda j: (j, 0, 0)),
        ],
        out_specs=[
            pl.BlockSpec((tokens, depth), const),
            pl.BlockSpec((1, tokens, own), lambda j: (j, 0, 0)),
            pl.BlockSpec((8, tokens), const),
        ],
        out_shape=[sds((tokens, depth), BF16), sds((3, tokens, own)), sds((8, tokens))],
    )(ids, xo, xp, front, w, got)


def project_grad_kernel(
    order, id_ref, da_ref, db_ref, pre_ref, stat_ref, gain_ref, first_ref,
    keep_ref, send_ref, g_ref, gt, tmp,
):
    j = pl.program_id(0)
    own = pre_ref.shape[2]
    cut = da_ref.shape[2]
    count = 2 * keep_ref.shape[0]
    inv, mean = column(stat_ref, j, 128), column(stat_ref, j + 3, 128)
    for c in range(own // 128):
        part = slice(c * 128, (c + 1) * 128)
        here = slice(c * 128 - cut, (c + 1) * 128 - cut) if c * 128 >= cut else part
        d = (db_ref if c * 128 >= cut else da_ref)[0, :, here]
        g = inv * (d * gain_ref[0, :, part] - pre_ref[0, :, part] * inv * mean)
        tmp[part, :] = g.T.astype(BF16)
        g_ref[0, :, part] = g.astype(BF16)
    put_relative(gt, tmp, id_ref[0] % count, id_ref[1], count)
    put_halves(keep_ref, send_ref, dot(gt[...], first_ref[...]).astype(BF16), count, order, j)


def project_grad(ids, da, db, pre, stats, gain, first, dp, order):
    _, tokens, own = pre.shape
    depth = first.shape[1]
    share = depth // dp
    const = lambda j: (0, 0)
    block = lambda j: (j, 0, 0)
    once = functools.partial(pl.BlockSpec, pipeline_mode=pl.Buffered(1))
    half = once((dp // 4, 3, share, depth), lambda j: (0, 0, 0, 0))
    return pl.pallas_call(
        functools.partial(project_grad_kernel, order),
        grid=(3,),
        in_specs=[
            pl.BlockSpec(memory_space=pltpu.SMEM),
            pl.BlockSpec((1,) + da.shape[1:], block), pl.BlockSpec((1,) + db.shape[1:], block),
            pl.BlockSpec((1, tokens, own), block),
            pl.BlockSpec((8, tokens), const),
            pl.BlockSpec((1, 1, own), block),
            once((tokens, depth), const),
        ],
        out_specs=[half, half, pl.BlockSpec((1, tokens, own), block)],
        out_shape=[sds((dp // 4, 3, share, depth), BF16)] * 2
        + [sds((3, tokens, own), BF16)],
        scratch_shapes=[pltpu.VMEM((own, tokens), BF16), pltpu.VMEM((own, tokens), BF16)],
    )(ids, da, db, pre, stats, gain, first)


def project_back_kernel(id_ref, g_ref, w_ref, got_ref, own_ref, peer_ref, acc):
    j = pl.program_id(0)
    own = g_ref.shape[2]
    local = own_ref.shape[0]
    f = id_ref[1]
    mine = pl.ds(pl.multiple_of(f * own, 128), own)
    other = pl.ds(pl.multiple_of((1 - f) * own, 128), own)

    @pl.when(j == 0)
    def _():
        acc[...] = jnp.zeros_like(acc)

    acc[:, mine] += dot(g_ref[0], w_ref[0, :, mine], 1, 1)
    acc[:, other] += dot(g_ref[0], got_ref[0], 1, 1)

    @pl.when(j == 2)
    def _():
        own_ref[...] = acc[:local]
        peer_ref[...] = acc[local:].astype(BF16)


def project_back(ids, g, w, got):
    _, tokens, own = g.shape
    depth = w.shape[2]
    local = tokens // 2
    const = lambda j: (0, 0)
    block = lambda j: (j, 0, 0)
    once = functools.partial(pl.BlockSpec, pipeline_mode=pl.Buffered(1))
    return pl.pallas_call(
        project_back_kernel,
        grid=(3,),
        in_specs=[
            pl.BlockSpec(memory_space=pltpu.SMEM),
            pl.BlockSpec((1, tokens, own), block),
            pl.BlockSpec((1, own, depth), block), pl.BlockSpec((1, own, own), block),
        ],
        out_specs=[once((local, depth), const), once((local, depth), const)],
        out_shape=[sds((local, depth)), sds((local, depth), BF16)],
        scratch_shapes=[pltpu.VMEM((tokens, depth), F32)],
    )(ids, g, w, got)


def out_back_kernel(order, id_ref, *refs):
    n = len(refs) - 8
    blocks, (w_ref, mixed_ref, g_ref, keep_ref, send_ref, all_ref, gt, tmp) = refs[:n], refs[n:]
    local = blocks[0].shape[0]
    for r, ref in enumerate(blocks):
        all_ref[r * local : (r + 1) * local, :] = ref[...]
    grad = all_ref[...]
    g_ref[...] = dot(grad, w_ref[...], 1, 1)
    for c in range(grad.shape[1] // 256):
        part = slice(c * 256, (c + 1) * 256)
        tmp[part, :] = grad[:, part].astype(F32).T.astype(BF16)
    count = 2 * keep_ref.shape[0]
    put_relative(gt, tmp, id_ref[0], id_ref[1], count)
    put_halves(keep_ref, send_ref, dot(gt[...], mixed_ref[...]).astype(BF16), count, order)


def out_back(ids, blocks, w, mixed, dp, order):
    tokens, own = mixed.shape
    depth = w.shape[1]
    vmem = pl.BlockSpec(memory_space=pltpu.VMEM)
    half = sds((dp // 2, depth // dp, own), BF16)
    return pl.pallas_call(
        functools.partial(out_back_kernel, order),
        in_specs=[pl.BlockSpec(memory_space=pltpu.SMEM)] + [vmem] * (len(blocks) + 2),
        out_specs=[vmem] * 3,
        out_shape=[sds((tokens, own)), half, half],
        scratch_shapes=[
            pltpu.VMEM((tokens, depth), BF16),
            pltpu.VMEM((depth, tokens), BF16), pltpu.VMEM((depth, tokens), BF16),
        ],
    )(ids, *blocks, w, mixed)


def time_embed(timesteps):
    half = TE // 2
    frequencies = jnp.exp(-math.log(10000.0) * jnp.arange(half, dtype=F32) / half)
    angles = timesteps.astype(F32)[:, None] * frequencies
    waves = jnp.concatenate([jnp.cos(angles), jnp.sin(angles)], axis=-1)
    return jax.nn.silu(waves).astype(BF16)


def rope_tables(positions, width):
    lane = jnp.arange(width)
    quarter = HD // 4
    frequencies = 10000.0 ** (-(lane % quarter).astype(F32) / quarter)
    place = jnp.where(lane % HD < HD // 2, positions[0][:, None], positions[1][:, None])
    angles = place.astype(F32) * frequencies
    return jnp.cos(angles), jnp.where(lane % 32 < 16, -1.0, 1.0) * jnp.sin(angles)


def inverse_rms(values):
    return lax.rsqrt(jnp.mean(values * values, axis=-1, keepdims=True) + EPSILON)


def rms_back(grad_hat, normed, inverse):
    return inverse * (grad_hat - normed * jnp.mean(grad_hat * normed, axis=-1, keepdims=True))


def pad_cols(value, width):
    extra = -value.shape[-1] % width
    return value if extra == 0 else jnp.pad(value, [(0, 0)] * (value.ndim - 1) + [(0, extra)])


def on_device(
    hidden_in, text_state, caption_lengths, timesteps, patch_positions, cotangent,
    w_ada, w_text, w_qkv, w_out, gains, cross_gate, w_gate_up, w_down,
):
    n, f = lax.axis_size("fsdp"), lax.axis_index("fsdp")
    dpn, me = lax.axis_size("dp"), lax.axis_index("dp")
    bits = list(range(dp_bits()))
    low_bits = bits[:-1]
    late = bits[2:3] + bits[:2] + bits[3:]
    own_d = D // n
    local = hidden_in.shape[1]
    tokens = n * local
    width = 2 * HD
    share = D // dpn
    paired = n == 2 and dpn >= 4
    ids = jnp.stack([me, f]).astype(jnp.int32)
    x_bf, dy_bf = hidden_in[0], cotangent[0]

    time_low = time_embed(timesteps)
    own_te = TE // n
    time_own = lax.dynamic_slice_in_dim(time_low[0], f * own_te, own_te, 0)
    modulation = pair_sum(
        jnp.einsum("k,kjd->jd", time_own, w_ada, preferred_element_type=F32)
    )
    scale_attn, gate_attn = modulation[0:1], jnp.tanh(modulation[1:2])
    scale_ffn, gate_ffn = modulation[2:3], jnp.tanh(modulation[3:4])

    w_flat = jnp.moveaxis(w_qkv, 1, 0)
    w_parts = exchange_rot(w_flat, 2)
    x_parts = gather_rot(x_bf)
    dy_all = jnp.concatenate(gather_rot(dy_bf), axis=0)
    places = jnp.concatenate(gather_rot(patch_positions[0]), axis=1)
    text_cols = jnp.concatenate(natural(exchange_rot(text_state[0], 1)), axis=0)
    text_all = lax.all_gather(text_cols, "dp", axis=0, tiled=True)
    gain_full = lax.all_gather(gains, "fsdp", axis=1, tiled=True).astype(F32)
    gain_own = gains.astype(F32)

    front = gain_full[0] * (1.0 + scale_attn)
    if paired:
        first_all, pre, squares = project(ids, *x_parts, front, w_flat, w_parts[1])
    else:
        w_heads = jnp.concatenate(natural(w_parts), axis=1)
        x_f = jnp.concatenate(x_parts, axis=0).astype(F32)
        first_all = (x_f * inverse_rms(x_f) * front).astype(BF16)
        pre = jnp.stack([dot(first_all, w_heads[j]) for j in range(3)])
        squares = jnp.pad(jnp.sum(pre[:2] * pre[:2], -1), ((0, 6), (0, 0)))
    inverse = lax.rsqrt(row_sum(squares) / D + EPSILON)

    text_part = text_fwd(text_cols, w_text)
    text_pre = scatter_rot(rot_blocks(text_part, 2))
    inv_t = lax.rsqrt(
        pair_sum(jnp.sum(text_pre[0] * text_pre[0], -1, keepdims=True)) / D + EPSILON
    )
    normed_t = text_pre[0] * inv_t
    tk = (normed_t * gain_own[4]).astype(BF16)
    tv = text_pre[1].astype(BF16)

    head_tanh = jnp.tanh(cross_gate.astype(F32))
    gate_row = pad_cols(jnp.repeat(head_tanh, HD)[None], width)
    cosine, sine = rope_tables(places, width)
    gq, gk = pad_cols(gain_own[2:3], width), pad_cols(gain_own[3:4], width)
    pre_p, tkp, tvp = pad_cols(pre, width), pad_cols(tk, width), pad_cols(tv, width)
    q, k, v, mixed_p, so, co, ls, lc = attn_forward(
        caption_lengths, pre_p, inverse, gq, gk, cosine, sine, tkp, tvp, gate_row
    )
    mixed = mixed_p[:, :own_d]

    def rows(value, r):
        return value[r * local : (r + 1) * local]

    parts = [dot(rows(mixed, r), w_out) for r in range(n)]
    attn_branch = scatter_rot([parts[0]] + [p.astype(BF16) for p in parts[1:]])
    x_own = x_bf.astype(F32)
    after_attn = x_own + gate_attn * attn_branch
    inverse_two = inverse_rms(after_attn)
    normed_two = after_attn * inverse_two
    second = (normed_two * gain_full[1] * (1.0 + scale_ffn)).astype(BF16)

    second_all = jnp.concatenate(gather_rot(second), axis=0)
    branch_all = (gate_ffn * dy_all.astype(F32)).astype(BF16)
    wide_keep, wide_send, down_keep, down_send, ffn_own, ffn_rest, back_own, back_rest = ffn(
        ids, second_all, branch_all, w_gate_up, w_down, local, dpn, (bits, late)
    )
    (ffn_own, ffn_rest, back_own, back_rest), text_all = lax.optimization_barrier(
        ((ffn_own, ffn_rest, back_own, back_rest), text_all)
    )
    wide_chain = Halving(bits, wide_keep, wide_send)
    down_chain = Halving(late, down_keep, down_send)
    grad_second = scatter_rot([back_own] + [rows(back_rest, r) for r in range(n - 1)])
    ffn_branch = scatter_rot([ffn_own] + [rows(ffn_rest, r) for r in range(n - 1)])
    output = (after_attn + gate_ffn * ffn_branch).astype(BF16)
    dy = dy_bf.astype(F32)
    d_gate_ffn = jnp.sum(dy * ffn_branch, axis=0) * (1.0 - gate_ffn[0] * gate_ffn[0])

    scaled = grad_second * normed_two
    d_scale_ffn = jnp.sum(scaled * gain_full[1], axis=0)
    gain_two = jnp.sum(scaled * (1.0 + scale_ffn), axis=0)
    grad_after = dy + rms_back(
        grad_second * gain_full[1] * (1.0 + scale_ffn), normed_two, inverse_two
    )
    d_gate_attn = jnp.sum(grad_after * attn_branch, axis=0) * (1.0 - gate_attn[0] * gate_attn[0])
    grad_attn = (gate_attn * grad_after).astype(BF16)
    grad_mixed, *out_halves = out_back(ids, gather_rot(grad_attn), w_out, mixed, dpn, bits)
    out_chain = Halving(bits, *out_halves)
    blocks = pre_p.shape[2] // width
    cut = max(1, 2 * blocks // 3)
    grad_mixed = pad_cols(grad_mixed, width)
    inputs = (so, co, ls, lc, pre_p, inverse, gq, gk, cosine, sine, gate_row)
    part_a = attn_backward(0, cut, caption_lengths, q, k, v, tkp, tvp, grad_mixed, *inputs)
    part_a, grad_mixed = lax.optimization_barrier((part_a, grad_mixed))
    grad_mixed = advance([wide_chain, down_chain], grad_mixed)
    part_b = attn_backward(
        cut, blocks - cut, caption_lengths, q, k, v, tkp, tvp, grad_mixed, *inputs
    )
    means = row_sum(part_a[3] + part_b[3])[:2] / D

    ones, zeros = jnp.ones((1, tokens), F32), jnp.zeros((1, tokens), F32)
    if paired:
        stats = jnp.concatenate([inverse[:2], ones, means, zeros, zeros, zeros], axis=0)
        gain3 = jnp.stack([gain_own[2:3], gain_own[3:4], jnp.ones_like(gain_own[2:3])])
        keep, send, grads = project_grad(
            ids, part_a[0], part_b[0], pre, stats, gain3, first_all, dpn, low_bits
        )
        part_a, part_b, grads = advance(
            [wide_chain, down_chain, out_chain], (part_a[1:], part_b[1:], grads)
        )
        qkv_chain = Halving(low_bits, keep, send)
        parts = project_back(ids, grads, w_flat, w_parts[1])
    else:
        d = jnp.concatenate([part_a[0], part_b[0]], axis=2)[:, :, :own_d]
        part_a, part_b = part_a[1:], part_b[1:]
        inv, mean = inverse[:2, :, None], means[:, :, None]
        hat = d[:2] * gain_own[2:4][:, None] - pre[:2] * inv * mean
        grads = [(inv[0] * hat[0]).astype(BF16), (inv[1] * hat[1]).astype(BF16), d[2].astype(BF16)]
        wide = [dot(g, first_all, 0, 0).astype(BF16) for g in grads]
        wide = [jnp.concatenate(natural(exchange_rot(w_, 1)), axis=0) for w_ in wide]
        wide = relative(jnp.stack([w_.reshape(dpn, share, own_d) for w_ in wide], axis=1))
        wide = jnp.stack([wide[p] for p in sorted(range(dpn), key=lambda p: place_of(p, bits))])
        qkv_chain = Halving(bits, wide[: dpn // 2], wide[dpn // 2 :])
        parts = [
            sum(dot(rows(g, r), w_heads[j], 1, 1) for j, g in enumerate(grads)) for r in range(n)
        ]
        parts = [parts[0]] + [p.astype(BF16) for p in parts[1:]]
    grad_first = scatter_rot(parts)

    dtk, dtv, gain_q, gain_k, gate_g = (
        jnp.concatenate([part_a[i], part_b[i]], axis=1)[:, :own_d] for i in (0, 1, 3, 4, 5)
    )
    gate_total = jnp.sum(gate_g[0].reshape(HEADS // n, HD), axis=1) * (
        1.0 - head_tanh * head_tanh
    )
    text_hat = dtk * gain_own[4]
    gain_text = jnp.sum(dtk * normed_t, axis=0, keepdims=True)
    mean_t = pair_sum(jnp.sum(text_hat * normed_t, -1, keepdims=True)) / D
    grad_tk = (inv_t * (text_hat - normed_t * mean_t)).astype(BF16)
    text_pair = jnp.stack([grad_tk, dtv.astype(BF16)])
    pair_all = jnp.concatenate(natural(gather_rot(text_pair)), axis=-1)
    pair_all = advance([qkv_chain, wide_chain, down_chain, out_chain], pair_all)
    text_in = text_bwd(pair_all, w_text)
    text_in, grad_first = advance([qkv_chain], (text_in, grad_first))
    text_in = jnp.concatenate(natural(exchange_rot(text_in, 0)), axis=1)

    inverse_one = inverse_rms(x_own)
    normed_one = x_own * inverse_one
    scaled = grad_first * normed_one
    d_scale_attn = jnp.sum(scaled * gain_full[0], axis=0)
    gain_one = jnp.sum(scaled * (1.0 + scale_attn), axis=0)
    grad_input = (
        grad_after
        + rms_back(grad_first * gain_full[0] * (1.0 + scale_attn), normed_one, inverse_one)
    ).astype(BF16)


    sums = [d_scale_attn, d_gate_attn, d_scale_ffn, d_gate_ffn, gain_one, gain_two]
    sums = pair_sum(jnp.stack(sums))
    stamp = jnp.full((1, D), timesteps[0].astype(F32))
    gate_pad = jnp.pad(gate_total, (0, own_d - gate_total.shape[0]))[None]
    small = jnp.concatenate([block_of(sums[4:], f, 1), gain_q, gain_k, gain_text, gate_pad], axis=0)
    small = jnp.pad(small.reshape(-1), (0, dpn * SUMS * 128 - small.size))
    mods = jnp.concatenate([sums[:4], stamp], axis=0).reshape(5, dpn, share).transpose(1, 0, 2)
    mods = jnp.pad(mods, ((0, 0), (0, 0), (0, -share % 128)))
    mods = jnp.concatenate([mods, small.reshape(dpn, SUMS, 128)], axis=1)
    outgoing = block_of(pair_all.transpose(0, 2, 1), f, 2)
    outgoing = outgoing.reshape(2, dpn, share, TEXT // n).transpose(1, 0, 2, 3)
    mods = advance([down_chain, out_chain], mods)
    pair_cols, mods, small = swap_all(outgoing, mods)
    chains = [out_chain, down_chain] if paired else [qkv_chain, out_chain, down_chain]
    if paired:
        qkv_got = qkv_chain.got
        (pair_cols, mods, small), qkv_chain.got = lax.optimization_barrier(
            ((pair_cols, mods, small), qkv_got)
        )
        qkv_chain.step()
        own_side = f == (me >> low_bits[-1] + 1)
        mine, got = exchange_rot(qkv_chain.last[0].astype(BF16), 2)
        got, wide_chain.keep = lax.optimization_barrier((got, wide_chain.keep))
        qkv_chain = Halving(
            bits[-1:], jnp.where(own_side, mine, got)[None], jnp.where(own_side, got, mine)[None]
        )
    pair_cols = advance(chains, pair_cols)
    pair_cols = jnp.concatenate(natural(gather_rot(pair_cols)), axis=3)
    pair_cols = pair_cols.transpose(1, 2, 0, 3).reshape(2 * share, dpn * TEXT)
    text_grad = dot(pair_cols, text_all).reshape(2, share, TW // n)
    total = small[:, 5 : 5 + SUMS].reshape(-1)[: 6 * own_d].reshape(6, own_d)
    times = time_embed(mods[:, 4, 0])
    times = lax.dynamic_slice_in_dim(times, f * own_te, own_te, 1).astype(F32)
    ada_grad = lax.dot_general(
        mods[:, :4, :share].reshape(dpn, 4 * share), times, (((0,), (0,)), ((), ())),
        precision=lax.Precision.HIGHEST,
    ).reshape(4, share, own_te)

    for chain in (out_chain, down_chain, wide_chain, qkv_chain):
        while chain.got is not None:
            chain.step()
    return (
        output[None],
        grad_input[None],
        text_in[None],
        ada_grad.transpose(2, 0, 1),
        text_grad.transpose(2, 0, 1),
        qkv_chain.last[0].transpose(2, 0, 1),
        out_chain.last[0].T,
        total[:5],
        total[5, : HEADS // n],
        wide_chain.last[0].transpose(1, 0, 2),
        down_chain.last[0].T,
    )


def solution(mesh):
    return jax.shard_map(
        on_device,
        mesh=mesh,
        in_specs=(
            P("dp", "fsdp", None),
            P("dp", "fsdp", None),
            P("dp"),
            P("dp"),
            P("dp", None, "fsdp"),
            P("dp", "fsdp", None),
            P("fsdp", None, None),
            P("fsdp", None, None),
            P("fsdp", None, None),
            P("fsdp", None),
            P(None, "fsdp"),
            P("fsdp"),
            P(None, None, "fsdp"),
            P("fsdp", None),
        ),
        out_specs=(
            P("dp", "fsdp", None),
            P("dp", "fsdp", None),
            P("dp", "fsdp", None),
            P("fsdp", None, "dp"),
            P("fsdp", None, "dp"),
            P("fsdp", None, "dp"),
            P("fsdp", "dp"),
            P(None, "fsdp"),
            P("fsdp"),
            P("dp", None, "fsdp"),
            P("fsdp", "dp"),
        ),
        check_vma=False,
    )
```

```python
import functools
import math

import jax
import jax.numpy as jnp
from jax import lax
from jax.experimental import pallas as pl
from jax.experimental.pallas import tpu as pltpu
from jax.sharding import PartitionSpec as P

D = 1536
HEADS = 24
HD = 64
TW = 4096
TE = 1024
PATCHES = 1024
TEXT = 256
EPSILON = 1e-06
F32 = jnp.float32
BF16 = jnp.bfloat16
QC = 256


def dot(a, b, ca=1, cb=0):
    return lax.dot_general(a, b, (((ca,), (cb,)), ((), ())), preferred_element_type=F32)


def from_behind(value, step):
    n = lax.axis_size("fsdp")
    return lax.ppermute(value, "fsdp", [(i, (i + step) % n) for i in range(n)])


def gather_rot(value):
    return [value] + [from_behind(value, r) for r in range(1, lax.axis_size("fsdp"))]


def pair_sum(value):
    return functools.reduce(lambda a, b: a + b, gather_rot(value))


def row_sum(value):
    n = lax.axis_size("fsdp")
    rows = value.shape[-1] // n
    total = value
    for r in range(1, n):
        total = total + jnp.roll(from_behind(value, r), r * rows, axis=-1)
    return total


def scatter_rot(blocks):
    n = lax.axis_size("fsdp")
    total = blocks[0].astype(F32)
    for r in range(1, n):
        got = lax.ppermute(blocks[r], "fsdp", [(i, (i - r) % n) for i in range(n)])
        total = total + got.astype(F32)
    return total


def block_of(value, index, axis):
    size = value.shape[axis] // lax.axis_size("fsdp")
    return lax.dynamic_slice_in_dim(value, index * size, size, axis)


def rot_blocks(value, axis):
    n, f = lax.axis_size("fsdp"), lax.axis_index("fsdp")
    return [block_of(value, (f - r) % n, axis) for r in range(n)]


def exchange_rot(value, axis):
    n, f = lax.axis_size("fsdp"), lax.axis_index("fsdp")
    out = [block_of(value, f, axis)]
    for r in range(1, n):
        out.append(from_behind(block_of(value, (f + r) % n, axis), r))
    return out


def natural(got):
    n, f = lax.axis_size("fsdp"), lax.axis_index("fsdp")
    if n == 2:
        return [jnp.where(f == 0, got[0], got[1]), jnp.where(f == 0, got[1], got[0])]
    got = jnp.stack(got)
    return [lax.dynamic_index_in_dim(got, (f - g) % n, 0, keepdims=False) for g in range(n)]


def dp_bits():
    return int(lax.axis_size("dp")).bit_length() - 1


def swapped(p):
    return (p & ~3) | ((p & 1) << 1) | ((p >> 1) & 1)


def turned(p, f):
    return p if dp_bits() < 3 else jnp.where(f % 2 == 0, p, swapped(p))


def dp_swap(value, bit):
    n, dpn = lax.axis_size("fsdp"), lax.axis_size("dp")
    pairs = []
    for i in range(dpn):
        for f in range(n):
            flip = 1 << bit if dp_bits() < 3 or f % 2 == 0 else swapped(1 << bit)
            pairs.append((i * n + f, (i ^ flip) * n + f))
    return lax.ppermute(value, ("dp", "fsdp"), pairs)


def relative(value):
    places = turned(jnp.arange(lax.axis_size("dp")), lax.axis_index("fsdp"))
    return jnp.take(value, lax.axis_index("dp") ^ places, axis=0)


class Halving:
    def __init__(self, order, keep, send):
        self.order = list(order)
        self.keep, self.got = keep, dp_swap(send, self.order.pop(0))

    def step(self):
        if self.got is None:
            return

        def add(part):
            return self.keep[part].astype(F32) + self.got[part].astype(F32)

        if not self.order:
            self.last = add(slice(None))
            self.got = None
            return
        half = self.keep.shape[0] // 2
        send = add(slice(half, None)).astype(BF16)
        self.keep = add(slice(half)).astype(BF16)
        self.got = dp_swap(send, self.order.pop(0))


def place_of(p, order):
    return sum((p >> bit & 1) << i for i, bit in enumerate(reversed(order)))


SUMS = 3


def to_all(source, target, sends, gets):
    me = lax.axis_index("dp")
    return [
        pltpu.make_async_remote_copy(
            src_ref=source(me ^ r), dst_ref=target, send_sem=sends.at[r], recv_sem=gets.at[r],
            device_id={"dp": me ^ r}, device_id_type=pl.DeviceIdType.MESH,
        )
        for r in range(1, lax.axis_size("dp"))
    ]


def small_kernel(mod_ref, mod_out, sum_out, part, sends, gets, own):
    me = lax.axis_index("dp")
    steps = (
        to_all(lambda peer: mod_ref.at[peer], mod_out.at[me], sends.at[0], gets.at[0])
        + [pltpu.make_async_copy(mod_ref.at[me], mod_out.at[me], own.at[0])],
        to_all(lambda peer: part, sum_out.at[me], sends.at[1], gets.at[1])
        + [pltpu.make_async_copy(part, sum_out.at[me], own.at[1])],
    )
    for i, copies in enumerate(steps):
        if i == 1:
            part[...] = jnp.sum(mod_out[...], axis=0)
        for copy in copies:
            copy.start()
        for copy in copies:
            copy.wait()


def small_exchange(mods):
    vmem = pl.BlockSpec(memory_space=pltpu.VMEM)
    count = mods.shape[0]
    return pl.pallas_call(
        small_kernel,
        in_specs=[vmem],
        out_specs=[vmem] * 2,
        out_shape=[jax.ShapeDtypeStruct(mods.shape, mods.dtype)] * 2,
        scratch_shapes=[
            pltpu.VMEM(mods.shape[1:], mods.dtype),
            pltpu.SemaphoreType.DMA((2, count)), pltpu.SemaphoreType.DMA((2, count)),
            pltpu.SemaphoreType.DMA((2,)),
        ],
        compiler_params=pltpu.CompilerParams(has_side_effects=True),
    )(mods)


def advance(chains, value):
    live = [c for c in chains if c.got is not None]
    value, got = lax.optimization_barrier((value, [c.got for c in live]))
    for c, g in zip(live, got):
        c.got = g
        c.step()
    return value


def rope_block(value, cosine, sine, sign):
    width = value.shape[1]
    lane = lax.broadcasted_iota(jnp.int32, value.shape, 1)
    partner = jnp.where(
        lane % 32 < 16, pltpu.roll(value, width - 16, 1), pltpu.roll(value, 16, 1)
    )
    return value * cosine + sign * (partner * sine)


def column(ref, index, width):
    row = ref[index : index + 1, :] if isinstance(index, int) else ref[pl.ds(index, 1), :]
    return jnp.broadcast_to(row, (width, row.shape[1])).T


def masked(value, head):
    lane = lax.broadcasted_iota(jnp.int32, value.shape, 1)
    return jnp.where(lane // HD == head, value, jnp.zeros_like(value))


def attn_fwd_kernel(
    len_ref, pre_ref, inv_ref, gq_ref, gk_ref, cos_ref, sin_ref, tk_ref, tv_ref, gate_ref,
    q_ref, k_ref, v_ref, mixed_ref, so_ref, co_ref, ls_ref, lc_ref,
):
    _, tokens, width = pre_ref.shape
    heads = width // HD
    iq, ik = column(inv_ref, 0, width), column(inv_ref, 1, width)
    q = rope_block(pre_ref[0] * iq * gq_ref[...], cos_ref[...], sin_ref[...], 1.0)
    q_ref[...] = q.astype(BF16)
    k = rope_block(pre_ref[1] * ik * gk_ref[...], cos_ref[...], sin_ref[...], 1.0)
    k_ref[...] = k.astype(BF16)
    v_ref[...] = pre_ref[2].astype(BF16)
    length = len_ref[0]

    def one(keys, values, qm, limit):
        s = dot(qm, keys, 1, 1)
        if limit is not None:
            slot = lax.broadcasted_iota(jnp.int32, s.shape, 1)
            s = jnp.where(slot < limit, s, -1e30)
        peak = jnp.max(s, axis=1, keepdims=True)
        e = jnp.exp(s - peak)
        total = jnp.sum(e, axis=1, keepdims=True)
        o = dot(e.astype(BF16), values)
        return o * (1.0 / total), peak + jnp.log(total)

    lane = lax.broadcasted_iota(jnp.int32, (tokens, width), 1)
    qs = q_ref[...] * jnp.asarray(HD**-0.5, BF16)
    so = co = stats = jnp.zeros((tokens, width), F32)
    for h in range(heads):
        qm = masked(qs, h)
        o, lse = one(k_ref[...], v_ref[...], qm, None)
        so = jnp.where(lane // HD == h, o, so)
        stats = jnp.where(lane == h, lse, stats)
        o, lse = one(tk_ref[...], tv_ref[...], qm, length)
        co = jnp.where(lane // HD == h, o, co)
        stats = jnp.where(lane == heads + h, lse, stats)
    so_ref[...] = so
    co_ref[...] = co
    mixed_ref[...] = (so + gate_ref[...] * co).astype(BF16)
    stats = stats.T
    ls_ref[0] = stats[:heads]
    lc_ref[0] = stats[heads : 2 * heads]


def attn_bwd_kernel(
    len_ref, q_ref, k_ref, v_ref, tk_ref, tv_ref, g_ref, so_ref, co_ref, ls_ref, lc_ref,
    pre_ref, inv_ref, gq_ref, gk_ref, cos_ref, sin_ref, gate_ref,
    d_ref, dtk_ref, dtv_ref, stat_ref, gainq_ref, gaink_ref, gateg_ref,
    gs_ref, gc_ref, ds_ref, dc_ref, kt_ref, tkt_ref, dqt_ref, dk_acc, dv_acc, rq_ref, rk_ref,
):
    tokens, width = q_ref.shape
    heads = width // HD
    scale = jnp.asarray(HD**-0.5, BF16)

    @pl.when(pl.program_id(0) == 0)
    def _():
        rq_ref[...] = jnp.zeros_like(rq_ref)
        rk_ref[...] = jnp.zeros_like(rk_ref)

    g = g_ref[...]
    gs_ref[...] = g.astype(BF16)
    gc_ref[...] = (g * gate_ref[...]).astype(BF16)
    prod_c = g * co_ref[...]
    gateg_ref[...] = jnp.sum(prod_c, axis=0, keepdims=True)
    prod_s = (g * so_ref[...]).T
    prod_c = (prod_c * gate_ref[...]).T
    for h in range(heads):
        ds_ref[h : h + 1, :] = jnp.sum(prod_s[h * HD : (h + 1) * HD], axis=0, keepdims=True)
        dc_ref[h : h + 1, :] = jnp.sum(prod_c[h * HD : (h + 1) * HD], axis=0, keepdims=True)
    kt_ref[...] = k_ref[...].astype(F32).T.astype(BF16)
    tkt_ref[...] = tk_ref[...].astype(F32).T.astype(BF16)
    dk_acc[...] = jnp.zeros_like(dk_acc)
    dv_acc[...] = jnp.zeros_like(dv_acc)
    dtk_ref[...] = jnp.zeros_like(dtk_ref)
    dtv_ref[...] = jnp.zeros_like(dtv_ref)
    length = len_ref[0]

    def one(keys, keys_t, values, qm, gm, lse, delta, head, limit):
        s = dot(keys, qm, 1, 1)
        p = jnp.exp(s - lse)
        if limit is not None:
            slot = lax.broadcasted_iota(jnp.int32, s.shape, 0)
            p = jnp.where(slot < limit, p, 0.0)
        dp = dot(values, gm, 1, 1)
        ds = (p * (dp - delta)).astype(BF16)
        dq = dot(keys_t[head * HD : (head + 1) * HD, :], ds)
        return dq, dot(ds, qm), dot(p.astype(BF16), gm)

    def chunk(c, carry):
        rows = pl.ds(pl.multiple_of(c * QC, QC), QC)
        qc = q_ref[rows, :] * scale
        for h in range(heads):
            qm = masked(qc, h)
            dq, dk, dv = one(
                k_ref[...], kt_ref, v_ref[...], qm, masked(gs_ref[rows, :], h),
                ls_ref[0, h : h + 1, rows], ds_ref[h : h + 1, rows], h, None,
            )
            dk_acc[...] += dk
            dv_acc[...] += dv
            dq2, dk, dv = one(
                tk_ref[...], tkt_ref, tv_ref[...], qm, masked(gc_ref[rows, :], h),
                lc_ref[0, h : h + 1, rows], dc_ref[h : h + 1, rows], h, length,
            )
            dtk_ref[...] += dk
            dtv_ref[...] += dv
            dqt_ref[h * HD : (h + 1) * HD, rows] = (dq + dq2) * HD**-0.5
        return carry

    lax.fori_loop(0, tokens // QC, chunk, 0)
    dq = rope_block(dqt_ref[...].T, cos_ref[...], sin_ref[...], -1.0)
    d_ref[0] = dq
    prod = dq * (pre_ref[0] * column(inv_ref, 0, width))
    gainq_ref[...] = jnp.sum(prod, axis=0, keepdims=True)
    rq_ref[...] += prod * gq_ref[...]
    dk = rope_block(dk_acc[...], cos_ref[...], sin_ref[...], -1.0)
    d_ref[1] = dk
    prod = dk * (pre_ref[1] * column(inv_ref, 1, width))
    gaink_ref[...] = jnp.sum(prod, axis=0, keepdims=True)
    rk_ref[...] += prod * gk_ref[...]
    d_ref[2] = dv_acc[...]

    @pl.when(pl.program_id(0) == pl.num_programs(0) - 1)
    def _():
        stat_ref[...] = jnp.zeros_like(stat_ref)
        for i, ref in enumerate((rq_ref, rk_ref)):
            stat_ref[i : i + 1, :] = jnp.sum(ref[...].T, axis=0, keepdims=True)


def specs(tokens, text, width, heads, at=0):
    col = pl.BlockSpec((tokens, width), lambda i: (0, i + at))
    three = pl.BlockSpec((3, tokens, width), lambda i: (0, 0, i + at))
    tcol = pl.BlockSpec((text, width), lambda i: (0, i + at))
    stat = pl.BlockSpec((8, tokens), lambda i: (0, 0))
    gain = pl.BlockSpec((1, width), lambda i: (0, i + at))
    table = pl.BlockSpec((tokens, width), lambda i: (0, 0))
    lse = pl.BlockSpec((1, heads, tokens), lambda i: (i + at, 0, 0))
    scalar = pl.BlockSpec(memory_space=pltpu.SMEM)
    return col, three, tcol, stat, gain, table, lse, scalar


def sds(shape, dtype=F32):
    return jax.ShapeDtypeStruct(shape, dtype)


def attn_forward(length, pre, inv, gq, gk, cosine, sine, tk, tv, gate):
    _, tokens, columns = pre.shape
    text, width = tk.shape[0], cosine.shape[1]
    heads, blocks = width // HD, columns // width
    col, three, tcol, stat, gain, table, lse, scalar = specs(tokens, text, width, heads)
    flat = (tokens, columns)
    return pl.pallas_call(
        attn_fwd_kernel,
        grid=(blocks,),
        in_specs=[scalar, three, stat, gain, gain, table, table, tcol, tcol, gain],
        out_specs=[col, col, col, col, col, col, lse, lse],
        out_shape=[sds(flat, BF16)] * 4 + [sds(flat)] * 2 + [sds((blocks, heads, tokens))] * 2,
    )(length, pre, inv, gq, gk, cosine, sine, tk, tv, gate)


def attn_backward(at, blocks, length, q, k, v, tk, tv, g, so, co, ls, lc, pre, inv, gq, gk, cosine, sine, gate):
    tokens = q.shape[0]
    text, width = tk.shape[0], cosine.shape[1]
    heads, columns = width // HD, blocks * width
    col, three, tcol, stat, gain, table, lse, scalar = specs(tokens, text, width, heads, at)
    _, three_o, tcol_o, _, gain_o, _, _, _ = specs(tokens, text, width, heads)
    return pl.pallas_call(
        attn_bwd_kernel,
        grid=(blocks,),
        in_specs=[scalar, col, col, col, tcol, tcol, col, col, col, lse, lse,
                  three, stat, gain, gain, table, table, gain],
        out_specs=[three_o, tcol_o, tcol_o, stat, gain_o, gain_o, gain_o],
        out_shape=[
            sds((3, tokens, columns)), sds((text, columns)), sds((text, columns)),
            sds((8, tokens)), sds((1, columns)), sds((1, columns)), sds((1, columns)),
        ],
        scratch_shapes=[
            pltpu.VMEM((tokens, width), BF16), pltpu.VMEM((tokens, width), BF16),
            pltpu.VMEM((heads, tokens), F32), pltpu.VMEM((heads, tokens), F32),
            pltpu.VMEM((width, tokens), BF16), pltpu.VMEM((width, text), BF16),
            pltpu.VMEM((width, tokens), F32),
            pltpu.VMEM((tokens, width), F32), pltpu.VMEM((tokens, width), F32),
            pltpu.VMEM((tokens, width), F32), pltpu.VMEM((tokens, width), F32),
        ],
    )(length, q, k, v, tk, tv, g, so, co, ls, lc, pre, inv, gq, gk, cosine, sine, gate)


def pick(rows, cols, step, part):
    i = lax.broadcasted_iota(jnp.int32, (rows, cols), 0)
    j = lax.broadcasted_iota(jnp.int32, (rows, cols), 1)
    hit = (j == step * i + part) if cols > rows else (i == step * j + part)
    return jnp.where(hit, 1.0, 0.0).astype(BF16)

def text_fwd_kernel(x_ref, w_ref, o_ref):
    @pl.when(pl.program_id(0) == 0)
    def _():
        o_ref[...] = jnp.zeros_like(o_ref)
    for b in range(w_ref.shape[0] // 128):
        rows = slice(b * 128, (b + 1) * 128)
        w = w_ref[rows].reshape(256, w_ref.shape[2])
        x = x_ref[:, rows]
        for j in range(2):
            spread = dot(x, pick(128, 256, 2, j)).astype(BF16)
            o_ref[j] += dot(spread, w)

def text_fwd(x, w):
    depth, _, cols = w.shape
    bk = 256
    return pl.pallas_call(
        text_fwd_kernel, grid=(depth // bk,),
        in_specs=[pl.BlockSpec((x.shape[0], bk), lambda i: (0, i)), pl.BlockSpec((bk, 2, cols), lambda i: (i, 0, 0))],
        out_specs=pl.BlockSpec((2, x.shape[0], cols), lambda i: (0, 0, 0)),
        out_shape=sds((2, x.shape[0], cols)),
    )(x, w)

def text_bwd_kernel(g_ref, w_ref, pair_ref, o_ref, pair_out, sends, gets, own):
    me = lax.axis_index("dp")
    step = pl.program_id(0)
    copies = to_all(lambda peer: pair_ref.at[peer], pair_out.at[me], sends, gets)
    copies.append(pltpu.make_async_copy(pair_ref.at[me], pair_out.at[me], own))

    @pl.when(step == 0)
    def _():
        for copy in copies:
            copy.start()

    for b in range(w_ref.shape[0] // 128):
        rows = slice(b * 128, (b + 1) * 128)
        w = w_ref[rows].reshape(256, w_ref.shape[2])
        total = 0.0
        for j in range(2):
            total = total + dot(g_ref[j], dot(pick(128, 256, 2, j), w).astype(BF16), 1, 1)
        o_ref[:, rows] = total.astype(BF16)

    @pl.when(step == pl.num_programs(0) - 1)
    def _():
        for copy in copies:
            copy.wait()


def text_bwd(g, w, pair):
    depth, _, cols = w.shape
    bk = 256
    count = pair.shape[0]
    return pl.pallas_call(
        text_bwd_kernel,
        grid=(depth // bk,),
        in_specs=[
            pl.BlockSpec(g.shape, lambda i: (0, 0, 0)),
            pl.BlockSpec((bk, 2, cols), lambda i: (i, 0, 0)),
            pl.BlockSpec(memory_space=pl.ANY),
        ],
        out_specs=[
            pl.BlockSpec((g.shape[1], bk), lambda i: (0, i)), pl.BlockSpec(memory_space=pl.ANY),
        ],
        out_shape=[
            sds((g.shape[1], depth), BF16), jax.ShapeDtypeStruct(pair.shape, pair.dtype),
        ],
        scratch_shapes=[
            pltpu.SemaphoreType.DMA((count,)), pltpu.SemaphoreType.DMA((count,)),
            pltpu.SemaphoreType.DMA,
        ],
        compiler_params=pltpu.CompilerParams(has_side_effects=True),
    )(g, w, pair)


def put_relative(dst, src, me, f, count):
    rows = dst.shape[0] // count
    for p in range(count):
        start = pl.multiple_of((me ^ turned(p, f)) * rows, 16)
        dst[p * rows : (p + 1) * rows, :] = src[pl.ds(start, rows), :]


def put_halves(keep, send, value, count, order, slot=None):
    rows = value.shape[0] // count
    for p in range(count):
        place = place_of(p, order[1:])
        where = place if slot is None else (place, slot)
        (send if p >> order[0] & 1 else keep)[where] = value[p * rows : (p + 1) * rows]


def ffn_kernel(
    orders, id_ref, s_ref, b_ref, w_ref, d_ref,
    wk_ref, ws_ref, dk_ref, ds_ref, fo_ref, fp_ref, so_ref, sp_ref,
    st, bt, tmp, wg, wu, facc, sacc,
):
    step = pl.program_id(0)
    depth, _, cols = w_ref.shape
    own = fo_ref.shape[0]
    count = 2 * dk_ref.shape[0]

    @pl.when(step == 0)
    def _():
        for src, dst in ((s_ref, st), (b_ref, bt)):
            for c in range(depth // 256):
                part = slice(c * 256, (c + 1) * 256)
                tmp[part, :] = src[:, part].astype(F32).T.astype(BF16)
            put_relative(dst, tmp, id_ref[0], id_ref[1], count)
        facc[...] = jnp.zeros_like(facc)
        sacc[...] = jnp.zeros_like(sacc)

    for c in range(depth // 128):
        part = slice(c * 128, (c + 1) * 128)
        w = w_ref[part].reshape(256, cols)
        wg[part, :] = dot(pick(128, 256, 2, 0), w).astype(BF16)
        wu[part, :] = dot(pick(128, 256, 2, 1), w).astype(BF16)
    s, b = s_ref[...], b_ref[...]
    gate = dot(s, wg[...])
    up = dot(s, wu[...])
    back = dot(b, d_ref[...], 1, 1)
    sig = jax.nn.sigmoid(gate)
    silu = gate * sig
    hidden = (silu * up).astype(BF16)
    g_gate = (back * up * (sig + silu * (1.0 - sig))).astype(BF16)
    g_up = (back * silu).astype(BF16)
    put_halves(wk_ref, ws_ref, dot(st[...], g_gate).astype(BF16), count, orders[0], 0)
    put_halves(wk_ref, ws_ref, dot(st[...], g_up).astype(BF16), count, orders[0], 1)
    put_halves(dk_ref, ds_ref, dot(bt[...], hidden).astype(BF16), count, orders[1])
    facc[...] += dot(hidden, d_ref[...])
    sacc[...] += dot(g_gate, wg[...], 1, 1) + dot(g_up, wu[...], 1, 1)

    @pl.when(step == pl.num_programs(0) - 1)
    def _():
        fo_ref[...] = facc[:own]
        fp_ref[...] = facc[own:].astype(BF16)
        so_ref[...] = sacc[:own]
        sp_ref[...] = sacc[own:].astype(BF16)


def ffn(ids, s, b, w, d, local, dp, orders):
    tokens, depth = s.shape
    hid = d.shape[0]
    bc = min(256, hid)
    rest = tokens - local
    once = functools.partial(pl.BlockSpec, pipeline_mode=pl.Buffered(1))
    const = lambda i: (0, 0)
    share = depth // dp
    half = pl.BlockSpec((dp // 2, share, bc), lambda i: (0, 0, i))
    halves = pl.BlockSpec((dp // 2, 2, share, bc), lambda i: (0, 0, 0, i))
    return pl.pallas_call(
        functools.partial(ffn_kernel, orders),
        grid=(hid // bc,),
        in_specs=[
            pl.BlockSpec(memory_space=pltpu.SMEM),
            once((tokens, depth), const), once((tokens, depth), const),
            pl.BlockSpec((depth, 2, bc), lambda i: (0, 0, i)),
            pl.BlockSpec((bc, depth), lambda i: (i, 0)),
        ],
        out_specs=[halves] * 2 + [half] * 2 + [
            once((local, depth), const), once((rest, depth), const),
            once((local, depth), const), once((rest, depth), const),
        ],
        out_shape=[sds((dp // 2, 2, share, hid), BF16)] * 2 + [sds((dp // 2, share, hid), BF16)] * 2 + [
            sds((local, depth)), sds((rest, depth), BF16),
            sds((local, depth)), sds((rest, depth), BF16),
        ],
        scratch_shapes=[
            pltpu.VMEM((depth, tokens), BF16), pltpu.VMEM((depth, tokens), BF16),
            pltpu.VMEM((depth, tokens), BF16),
            pltpu.VMEM((depth, bc), BF16), pltpu.VMEM((depth, bc), BF16),
            pltpu.VMEM((tokens, depth), F32), pltpu.VMEM((tokens, depth), F32),
        ],
        compiler_params=pltpu.CompilerParams(vmem_limit_bytes=62 << 20),
    )(ids, s, b, w, d)


def project_kernel(id_ref, xo_ref, xp_ref, front_ref, w_ref, got_ref, first_ref, pre_ref, sq_ref):
    j = pl.program_id(0)
    local, depth = xo_ref.shape
    own = got_ref.shape[2]
    f = id_ref[1]

    @pl.when(j == 0)
    def _():
        for i, ref in enumerate((xo_ref, xp_ref)):
            x = ref[...].astype(F32)
            inv = lax.rsqrt(jnp.sum(x * x, axis=1, keepdims=True) * (1.0 / depth) + EPSILON)
            first_ref[i * local : (i + 1) * local, :] = (x * inv * front_ref[...]).astype(BF16)
        sq_ref[...] = jnp.zeros_like(sq_ref)

    mine = pl.ds(pl.multiple_of(f * own, 128), own)
    other = pl.ds(pl.multiple_of((1 - f) * own, 128), own)
    out = dot(first_ref[:, mine], w_ref[0, :, mine]) + dot(first_ref[:, other], got_ref[0])
    pre_ref[0] = out
    square = out * out
    part = square[:, :128]
    for c in range(1, own // 128):
        part = part + square[:, c * 128 : (c + 1) * 128]
    sq_ref[pl.ds(j, 1), :] = jnp.sum(part.T, axis=0, keepdims=True)


def project(ids, xo, xp, front, w, got):
    local, depth = xo.shape
    own = got.shape[2]
    tokens = 2 * local
    const = lambda j: (0, 0)
    return pl.pallas_call(
        project_kernel,
        grid=(3,),
        in_specs=[
            pl.BlockSpec(memory_space=pltpu.SMEM),
            pl.BlockSpec((local, depth), const), pl.BlockSpec((local, depth), const),
            pl.BlockSpec((1, depth), const),
            pl.BlockSpec((1, own, depth), lambda j: (j, 0, 0)),
            pl.BlockSpec((1, own, own), lambda j: (j, 0, 0)),
        ],
        out_specs=[
            pl.BlockSpec((tokens, depth), const),
            pl.BlockSpec((1, tokens, own), lambda j: (j, 0, 0)),
            pl.BlockSpec((8, tokens), const),
        ],
        out_shape=[sds((tokens, depth), BF16), sds((3, tokens, own)), sds((8, tokens))],
    )(ids, xo, xp, front, w, got)


def project_grad_kernel(
    order, id_ref, da_ref, db_ref, pre_ref, stat_ref, gain_ref, first_ref,
    keep_ref, send_ref, g_ref, gt, tmp,
):
    j = pl.program_id(0)
    own = pre_ref.shape[2]
    cut = da_ref.shape[2]
    count = 2 * keep_ref.shape[0]
    inv, mean = column(stat_ref, j, 128), column(stat_ref, j + 3, 128)
    for c in range(own // 128):
        part = slice(c * 128, (c + 1) * 128)
        here = slice(c * 128 - cut, (c + 1) * 128 - cut) if c * 128 >= cut else part
        d = (db_ref if c * 128 >= cut else da_ref)[0, :, here]
        g = inv * (d * gain_ref[0, :, part] - pre_ref[0, :, part] * inv * mean)
        tmp[part, :] = g.T.astype(BF16)
        g_ref[0, :, part] = g.astype(BF16)
    put_relative(gt, tmp, id_ref[0] % count, id_ref[1], count)
    put_halves(keep_ref, send_ref, dot(gt[...], first_ref[...]).astype(BF16), count, order, j)


def project_grad(ids, da, db, pre, stats, gain, first, dp, order):
    _, tokens, own = pre.shape
    depth = first.shape[1]
    share = depth // dp
    const = lambda j: (0, 0)
    block = lambda j: (j, 0, 0)
    once = functools.partial(pl.BlockSpec, pipeline_mode=pl.Buffered(1))
    half = once((dp // 4, 3, share, depth), lambda j: (0, 0, 0, 0))
    return pl.pallas_call(
        functools.partial(project_grad_kernel, order),
        grid=(3,),
        in_specs=[
            pl.BlockSpec(memory_space=pltpu.SMEM),
            pl.BlockSpec((1,) + da.shape[1:], block), pl.BlockSpec((1,) + db.shape[1:], block),
            pl.BlockSpec((1, tokens, own), block),
            pl.BlockSpec((8, tokens), const),
            pl.BlockSpec((1, 1, own), block),
            once((tokens, depth), const),
        ],
        out_specs=[half, half, pl.BlockSpec((1, tokens, own), block)],
        out_shape=[sds((dp // 4, 3, share, depth), BF16)] * 2
        + [sds((3, tokens, own), BF16)],
        scratch_shapes=[pltpu.VMEM((own, tokens), BF16), pltpu.VMEM((own, tokens), BF16)],
    )(ids, da, db, pre, stats, gain, first)


def project_back_kernel(id_ref, g_ref, w_ref, got_ref, own_ref, peer_ref, acc):
    j = pl.program_id(0)
    own = g_ref.shape[2]
    local = own_ref.shape[0]
    f = id_ref[1]
    mine = pl.ds(pl.multiple_of(f * own, 128), own)
    other = pl.ds(pl.multiple_of((1 - f) * own, 128), own)

    @pl.when(j == 0)
    def _():
        acc[...] = jnp.zeros_like(acc)

    acc[:, mine] += dot(g_ref[0], w_ref[0, :, mine], 1, 1)
    acc[:, other] += dot(g_ref[0], got_ref[0], 1, 1)

    @pl.when(j == 2)
    def _():
        own_ref[...] = acc[:local]
        peer_ref[...] = acc[local:].astype(BF16)


def project_back(ids, g, w, got):
    _, tokens, own = g.shape
    depth = w.shape[2]
    local = tokens // 2
    const = lambda j: (0, 0)
    block = lambda j: (j, 0, 0)
    once = functools.partial(pl.BlockSpec, pipeline_mode=pl.Buffered(1))
    return pl.pallas_call(
        project_back_kernel,
        grid=(3,),
        in_specs=[
            pl.BlockSpec(memory_space=pltpu.SMEM),
            pl.BlockSpec((1, tokens, own), block),
            pl.BlockSpec((1, own, depth), block), pl.BlockSpec((1, own, own), block),
        ],
        out_specs=[once((local, depth), const), once((local, depth), const)],
        out_shape=[sds((local, depth)), sds((local, depth), BF16)],
        scratch_shapes=[pltpu.VMEM((tokens, depth), F32)],
    )(ids, g, w, got)


def out_back_kernel(order, id_ref, *refs):
    n = len(refs) - 8
    blocks, (w_ref, mixed_ref, g_ref, keep_ref, send_ref, all_ref, gt, tmp) = refs[:n], refs[n:]
    local = blocks[0].shape[0]
    for r, ref in enumerate(blocks):
        all_ref[r * local : (r + 1) * local, :] = ref[...]
    grad = all_ref[...]
    g_ref[...] = dot(grad, w_ref[...], 1, 1)
    for c in range(grad.shape[1] // 256):
        part = slice(c * 256, (c + 1) * 256)
        tmp[part, :] = grad[:, part].astype(F32).T.astype(BF16)
    count = 2 * keep_ref.shape[0]
    put_relative(gt, tmp, id_ref[0], id_ref[1], count)
    put_halves(keep_ref, send_ref, dot(gt[...], mixed_ref[...]).astype(BF16), count, order)


def out_back(ids, blocks, w, mixed, dp, order):
    tokens, own = mixed.shape
    depth = w.shape[1]
    vmem = pl.BlockSpec(memory_space=pltpu.VMEM)
    half = sds((dp // 2, depth // dp, own), BF16)
    return pl.pallas_call(
        functools.partial(out_back_kernel, order),
        in_specs=[pl.BlockSpec(memory_space=pltpu.SMEM)] + [vmem] * (len(blocks) + 2),
        out_specs=[vmem] * 3,
        out_shape=[sds((tokens, own)), half, half],
        scratch_shapes=[
            pltpu.VMEM((tokens, depth), BF16),
            pltpu.VMEM((depth, tokens), BF16), pltpu.VMEM((depth, tokens), BF16),
        ],
    )(ids, *blocks, w, mixed)


def time_embed(timesteps):
    half = TE // 2
    frequencies = jnp.exp(-math.log(10000.0) * jnp.arange(half, dtype=F32) / half)
    angles = timesteps.astype(F32)[:, None] * frequencies
    waves = jnp.concatenate([jnp.cos(angles), jnp.sin(angles)], axis=-1)
    return jax.nn.silu(waves).astype(BF16)


def rope_tables(positions, width):
    lane = jnp.arange(width)
    quarter = HD // 4
    frequencies = 10000.0 ** (-(lane % quarter).astype(F32) / quarter)
    place = jnp.where(lane % HD < HD // 2, positions[0][:, None], positions[1][:, None])
    angles = place.astype(F32) * frequencies
    return jnp.cos(angles), jnp.where(lane % 32 < 16, -1.0, 1.0) * jnp.sin(angles)


def inverse_rms(values):
    return lax.rsqrt(jnp.mean(values * values, axis=-1, keepdims=True) + EPSILON)


def rms_back(grad_hat, normed, inverse):
    return inverse * (grad_hat - normed * jnp.mean(grad_hat * normed, axis=-1, keepdims=True))


def pad_cols(value, width):
    extra = -value.shape[-1] % width
    return value if extra == 0 else jnp.pad(value, [(0, 0)] * (value.ndim - 1) + [(0, extra)])


def on_device(
    hidden_in, text_state, caption_lengths, timesteps, patch_positions, cotangent,
    w_ada, w_text, w_qkv, w_out, gains, cross_gate, w_gate_up, w_down,
):
    n, f = lax.axis_size("fsdp"), lax.axis_index("fsdp")
    dpn, me = lax.axis_size("dp"), lax.axis_index("dp")
    bits = list(range(dp_bits()))
    low_bits = bits[:-1]
    late = bits[2:3] + bits[:2] + bits[3:]
    own_d = D // n
    local = hidden_in.shape[1]
    tokens = n * local
    width = 2 * HD
    share = D // dpn
    paired = n == 2 and dpn >= 4
    ids = jnp.stack([me, f]).astype(jnp.int32)
    x_bf, dy_bf = hidden_in[0], cotangent[0]

    time_low = time_embed(timesteps)
    own_te = TE // n
    time_own = lax.dynamic_slice_in_dim(time_low[0], f * own_te, own_te, 0)
    modulation = pair_sum(
        jnp.einsum("k,kjd->jd", time_own, w_ada, preferred_element_type=F32)
    )
    scale_attn, gate_attn = modulation[0:1], jnp.tanh(modulation[1:2])
    scale_ffn, gate_ffn = modulation[2:3], jnp.tanh(modulation[3:4])

    w_flat = jnp.moveaxis(w_qkv, 1, 0)
    w_parts = exchange_rot(w_flat, 2)
    x_parts = gather_rot(x_bf)
    dy_all = jnp.concatenate(gather_rot(dy_bf), axis=0)
    places = jnp.concatenate(gather_rot(patch_positions[0]), axis=1)
    text_cols = jnp.concatenate(natural(exchange_rot(text_state[0], 1)), axis=0)
    text_all = lax.all_gather(text_cols, "dp", axis=0, tiled=True)
    gain_full = lax.all_gather(gains, "fsdp", axis=1, tiled=True).astype(F32)
    gain_own = gains.astype(F32)

    front = gain_full[0] * (1.0 + scale_attn)
    if paired:
        first_all, pre, squares = project(ids, *x_parts, front, w_flat, w_parts[1])
    else:
        w_heads = jnp.concatenate(natural(w_parts), axis=1)
        x_f = jnp.concatenate(x_parts, axis=0).astype(F32)
        first_all = (x_f * inverse_rms(x_f) * front).astype(BF16)
        pre = jnp.stack([dot(first_all, w_heads[j]) for j in range(3)])
        squares = jnp.pad(jnp.sum(pre[:2] * pre[:2], -1), ((0, 6), (0, 0)))
    inverse = lax.rsqrt(row_sum(squares) / D + EPSILON)

    text_part = text_fwd(text_cols, w_text)
    text_pre = scatter_rot(rot_blocks(text_part, 2))
    inv_t = lax.rsqrt(
        pair_sum(jnp.sum(text_pre[0] * text_pre[0], -1, keepdims=True)) / D + EPSILON
    )
    normed_t = text_pre[0] * inv_t
    tk = (normed_t * gain_own[4]).astype(BF16)
    tv = text_pre[1].astype(BF16)

    head_tanh = jnp.tanh(cross_gate.astype(F32))
    gate_row = pad_cols(jnp.repeat(head_tanh, HD)[None], width)
    cosine, sine = rope_tables(places, width)
    gq, gk = pad_cols(gain_own[2:3], width), pad_cols(gain_own[3:4], width)
    pre_p, tkp, tvp = pad_cols(pre, width), pad_cols(tk, width), pad_cols(tv, width)
    q, k, v, mixed_p, so, co, ls, lc = attn_forward(
        caption_lengths, pre_p, inverse, gq, gk, cosine, sine, tkp, tvp, gate_row
    )
    mixed = mixed_p[:, :own_d]

    def rows(value, r):
        return value[r * local : (r + 1) * local]

    parts = [dot(rows(mixed, r), w_out) for r in range(n)]
    attn_branch = scatter_rot([parts[0]] + [p.astype(BF16) for p in parts[1:]])
    x_own = x_bf.astype(F32)
    after_attn = x_own + gate_attn * attn_branch
    inverse_two = inverse_rms(after_attn)
    normed_two = after_attn * inverse_two
    second = (normed_two * gain_full[1] * (1.0 + scale_ffn)).astype(BF16)

    second_all = jnp.concatenate(gather_rot(second), axis=0)
    branch_all = (gate_ffn * dy_all.astype(F32)).astype(BF16)
    wide_keep, wide_send, down_keep, down_send, ffn_own, ffn_rest, back_own, back_rest = ffn(
        ids, second_all, branch_all, w_gate_up, w_down, local, dpn, (bits, late)
    )
    (ffn_own, ffn_rest, back_own, back_rest), text_all = lax.optimization_barrier(
        ((ffn_own, ffn_rest, back_own, back_rest), text_all)
    )
    wide_chain = Halving(bits, wide_keep, wide_send)
    down_chain = Halving(late, down_keep, down_send)
    grad_second = scatter_rot([back_own] + [rows(back_rest, r) for r in range(n - 1)])
    ffn_branch = scatter_rot([ffn_own] + [rows(ffn_rest, r) for r in range(n - 1)])
    output = (after_attn + gate_ffn * ffn_branch).astype(BF16)
    dy = dy_bf.astype(F32)
    d_gate_ffn = jnp.sum(dy * ffn_branch, axis=0) * (1.0 - gate_ffn[0] * gate_ffn[0])

    scaled = grad_second * normed_two
    d_scale_ffn = jnp.sum(scaled * gain_full[1], axis=0)
    gain_two = jnp.sum(scaled * (1.0 + scale_ffn), axis=0)
    grad_after = dy + rms_back(
        grad_second * gain_full[1] * (1.0 + scale_ffn), normed_two, inverse_two
    )
    d_gate_attn = jnp.sum(grad_after * attn_branch, axis=0) * (1.0 - gate_attn[0] * gate_attn[0])
    grad_attn = (gate_attn * grad_after).astype(BF16)
    grad_mixed, *out_halves = out_back(ids, gather_rot(grad_attn), w_out, mixed, dpn, bits)
    out_chain = Halving(bits, *out_halves)
    blocks = pre_p.shape[2] // width
    cut = max(1, 2 * blocks // 3)
    grad_mixed = pad_cols(grad_mixed, width)
    inputs = (so, co, ls, lc, pre_p, inverse, gq, gk, cosine, sine, gate_row)
    part_a = attn_backward(0, cut, caption_lengths, q, k, v, tkp, tvp, grad_mixed, *inputs)
    part_a, grad_mixed = lax.optimization_barrier((part_a, grad_mixed))
    grad_mixed = advance([wide_chain, down_chain], grad_mixed)
    part_b = attn_backward(
        cut, blocks - cut, caption_lengths, q, k, v, tkp, tvp, grad_mixed, *inputs
    )
    means = row_sum(part_a[3] + part_b[3])[:2] / D

    ones, zeros = jnp.ones((1, tokens), F32), jnp.zeros((1, tokens), F32)
    if paired:
        stats = jnp.concatenate([inverse[:2], ones, means, zeros, zeros, zeros], axis=0)
        gain3 = jnp.stack([gain_own[2:3], gain_own[3:4], jnp.ones_like(gain_own[2:3])])
        keep, send, grads = project_grad(
            ids, part_a[0], part_b[0], pre, stats, gain3, first_all, dpn, low_bits
        )
        part_a, part_b, grads = advance(
            [wide_chain, down_chain, out_chain], (part_a[1:], part_b[1:], grads)
        )
        qkv_chain = Halving(low_bits, keep, send)
        parts = project_back(ids, grads, w_flat, w_parts[1])
    else:
        d = jnp.concatenate([part_a[0], part_b[0]], axis=2)[:, :, :own_d]
        part_a, part_b = part_a[1:], part_b[1:]
        inv, mean = inverse[:2, :, None], means[:, :, None]
        hat = d[:2] * gain_own[2:4][:, None] - pre[:2] * inv * mean
        grads = [(inv[0] * hat[0]).astype(BF16), (inv[1] * hat[1]).astype(BF16), d[2].astype(BF16)]
        wide = [dot(g, first_all, 0, 0).astype(BF16) for g in grads]
        wide = [jnp.concatenate(natural(exchange_rot(w_, 1)), axis=0) for w_ in wide]
        wide = relative(jnp.stack([w_.reshape(dpn, share, own_d) for w_ in wide], axis=1))
        wide = jnp.stack([wide[p] for p in sorted(range(dpn), key=lambda p: place_of(p, bits))])
        qkv_chain = Halving(bits, wide[: dpn // 2], wide[dpn // 2 :])
        parts = [
            sum(dot(rows(g, r), w_heads[j], 1, 1) for j, g in enumerate(grads)) for r in range(n)
        ]
        parts = [parts[0]] + [p.astype(BF16) for p in parts[1:]]
    grad_first = scatter_rot(parts)

    dtk, dtv, gain_q, gain_k, gate_g = (
        jnp.concatenate([part_a[i], part_b[i]], axis=1)[:, :own_d] for i in (0, 1, 3, 4, 5)
    )
    text_hat = dtk * gain_own[4]
    gain_text = jnp.sum(dtk * normed_t, axis=0, keepdims=True)
    mean_t = pair_sum(jnp.sum(text_hat * normed_t, -1, keepdims=True)) / D
    grad_tk = (inv_t * (text_hat - normed_t * mean_t)).astype(BF16)
    text_pair = jnp.stack([grad_tk, dtv.astype(BF16)])
    pair_all = jnp.concatenate(natural(gather_rot(text_pair)), axis=-1)
    pair_all = advance([qkv_chain, wide_chain, down_chain, out_chain], pair_all)
    outgoing = block_of(pair_all.transpose(0, 2, 1), f, 2)
    outgoing = outgoing.reshape(2, dpn, share, TEXT // n).transpose(1, 0, 2, 3)
    text_in, pair_cols = text_bwd(pair_all, w_text, outgoing)
    text_in, grad_first = advance([qkv_chain], (text_in, grad_first))
    text_in = jnp.concatenate(natural(exchange_rot(text_in, 0)), axis=1)

    inverse_one = inverse_rms(x_own)
    normed_one = x_own * inverse_one
    scaled = grad_first * normed_one
    d_scale_attn = jnp.sum(scaled * gain_full[0], axis=0)
    gain_one = jnp.sum(scaled * (1.0 + scale_attn), axis=0)
    grad_input = (
        grad_after
        + rms_back(grad_first * gain_full[0] * (1.0 + scale_attn), normed_one, inverse_one)
    ).astype(BF16)


    sums = [d_scale_attn, d_gate_attn, d_scale_ffn, d_gate_ffn, gain_one, gain_two]
    sums = pair_sum(jnp.stack(sums))
    stamp = jnp.full((1, D), timesteps[0].astype(F32))
    small = jnp.concatenate([block_of(sums[4:], f, 1), gain_q, gain_k, gain_text, gate_g], axis=0)
    small = jnp.pad(small.reshape(-1), (0, dpn * SUMS * 128 - small.size))
    mods = jnp.concatenate([sums[:4], stamp], axis=0).reshape(5, dpn, share).transpose(1, 0, 2)
    mods = jnp.pad(mods, ((0, 0), (0, 0), (0, -share % 128)))
    mods = jnp.concatenate([mods, small.reshape(dpn, SUMS, 128)], axis=1)
    mods = advance([down_chain, out_chain], mods)
    mods, small = small_exchange(mods)
    chains = [out_chain, down_chain] if paired else [qkv_chain, out_chain, down_chain]
    if paired:
        qkv_got = qkv_chain.got
        (mods, small), qkv_chain.got = lax.optimization_barrier(((mods, small), qkv_got))
        qkv_chain.step()
        own_side = f == (me >> low_bits[-1] + 1)
        mine, got = exchange_rot(qkv_chain.last[0].astype(BF16), 2)
        got, wide_chain.keep = lax.optimization_barrier((got, wide_chain.keep))
        qkv_chain = Halving(
            bits[-1:], jnp.where(own_side, mine, got)[None], jnp.where(own_side, got, mine)[None]
        )
    mods = advance(chains, mods)
    pair_cols = jnp.concatenate(natural(gather_rot(pair_cols)), axis=3)
    pair_cols = pair_cols.transpose(1, 2, 0, 3).reshape(2 * share, dpn * TEXT)
    text_grad = dot(pair_cols, text_all).reshape(2, share, TW // n)
    total = small[:, 5 : 5 + SUMS].reshape(-1)[: 6 * own_d].reshape(6, own_d)
    gate_total = jnp.sum(total[5].reshape(HEADS // n, HD), axis=1) * (
        1.0 - head_tanh * head_tanh
    )
    times = time_embed(mods[:, 4, 0])
    times = lax.dynamic_slice_in_dim(times, f * own_te, own_te, 1).astype(F32)
    ada_grad = lax.dot_general(
        mods[:, :4, :share].reshape(dpn, 4 * share), times, (((0,), (0,)), ((), ())),
        precision=lax.Precision.HIGHEST,
    ).reshape(4, share, own_te)

    for chain in (out_chain, down_chain, wide_chain, qkv_chain):
        while chain.got is not None:
            chain.step()
    return (
        output[None],
        grad_input[None],
        text_in[None],
        ada_grad.transpose(2, 0, 1),
        text_grad.transpose(2, 0, 1),
        qkv_chain.last[0].transpose(2, 0, 1),
        out_chain.last[0].T,
        total[:5],
        gate_total,
        wide_chain.last[0].transpose(1, 0, 2),
        down_chain.last[0].T,
    )


def solution(mesh):
    return jax.shard_map(
        on_device,
        mesh=mesh,
        in_specs=(
            P("dp", "fsdp", None),
            P("dp", "fsdp", None),
            P("dp"),
            P("dp"),
            P("dp", None, "fsdp"),
            P("dp", "fsdp", None),
            P("fsdp", None, None),
            P("fsdp", None, None),
            P("fsdp", None, None),
            P("fsdp", None),
            P(None, "fsdp"),
            P("fsdp"),
            P(None, None, "fsdp"),
            P("fsdp", None),
        ),
        out_specs=(
            P("dp", "fsdp", None),
            P("dp", "fsdp", None),
            P("dp", "fsdp", None),
            P("fsdp", None, "dp"),
            P("fsdp", None, "dp"),
            P("fsdp", None, "dp"),
            P("fsdp", "dp"),
            P(None, "fsdp"),
            P("fsdp"),
            P("dp", None, "fsdp"),
            P("fsdp", "dp"),
        ),
        check_vma=False,
    )
```

```python
import functools
import math

import jax
import jax.numpy as jnp
from jax import lax
from jax.experimental import pallas as pl
from jax.experimental.pallas import tpu as pltpu
from jax.sharding import PartitionSpec as P

D = 1536
HEADS = 24
HD = 64
TW = 4096
TE = 1024
PATCHES = 1024
TEXT = 256
EPSILON = 1e-06
F32 = jnp.float32
BF16 = jnp.bfloat16
QC = 256


def dot(a, b, ca=1, cb=0):
    return lax.dot_general(a, b, (((ca,), (cb,)), ((), ())), preferred_element_type=F32)


def from_behind(value, step):
    n = lax.axis_size("fsdp")
    return lax.ppermute(value, "fsdp", [(i, (i + step) % n) for i in range(n)])


def gather_rot(value):
    return [value] + [from_behind(value, r) for r in range(1, lax.axis_size("fsdp"))]


def pair_sum(value):
    return functools.reduce(lambda a, b: a + b, gather_rot(value))


def row_sum(value):
    n = lax.axis_size("fsdp")
    rows = value.shape[-1] // n
    total = value
    for r in range(1, n):
        total = total + jnp.roll(from_behind(value, r), r * rows, axis=-1)
    return total


def scatter_rot(blocks):
    n = lax.axis_size("fsdp")
    total = blocks[0].astype(F32)
    for r in range(1, n):
        got = lax.ppermute(blocks[r], "fsdp", [(i, (i - r) % n) for i in range(n)])
        total = total + got.astype(F32)
    return total


def block_of(value, index, axis):
    size = value.shape[axis] // lax.axis_size("fsdp")
    return lax.dynamic_slice_in_dim(value, index * size, size, axis)


def rot_blocks(value, axis):
    n, f = lax.axis_size("fsdp"), lax.axis_index("fsdp")
    return [block_of(value, (f - r) % n, axis) for r in range(n)]


def exchange_rot(value, axis):
    n, f = lax.axis_size("fsdp"), lax.axis_index("fsdp")
    out = [block_of(value, f, axis)]
    for r in range(1, n):
        out.append(from_behind(block_of(value, (f + r) % n, axis), r))
    return out


def natural(got):
    n, f = lax.axis_size("fsdp"), lax.axis_index("fsdp")
    if n == 2:
        return [jnp.where(f == 0, got[0], got[1]), jnp.where(f == 0, got[1], got[0])]
    got = jnp.stack(got)
    return [lax.dynamic_index_in_dim(got, (f - g) % n, 0, keepdims=False) for g in range(n)]


def dp_bits():
    return int(lax.axis_size("dp")).bit_length() - 1


def swapped(p):
    return (p & ~3) | ((p & 1) << 1) | ((p >> 1) & 1)


def turned(p, f):
    return p if dp_bits() < 3 else jnp.where(f % 2 == 0, p, swapped(p))


def dp_swap(value, bit):
    n, dpn = lax.axis_size("fsdp"), lax.axis_size("dp")
    pairs = []
    for i in range(dpn):
        for f in range(n):
            flip = 1 << bit if dp_bits() < 3 or f % 2 == 0 else swapped(1 << bit)
            pairs.append((i * n + f, (i ^ flip) * n + f))
    return lax.ppermute(value, ("dp", "fsdp"), pairs)


def relative(value):
    places = turned(jnp.arange(lax.axis_size("dp")), lax.axis_index("fsdp"))
    return jnp.take(value, lax.axis_index("dp") ^ places, axis=0)


class Halving:
    def __init__(self, order, keep, send):
        self.order = list(order)
        self.keep, self.got = keep, dp_swap(send, self.order.pop(0))

    def step(self):
        if self.got is None:
            return

        def add(part):
            return self.keep[part].astype(F32) + self.got[part].astype(F32)

        if not self.order:
            self.last = add(slice(None))
            self.got = None
            return
        half = self.keep.shape[0] // 2
        send = add(slice(half, None)).astype(BF16)
        self.keep = add(slice(half)).astype(BF16)
        self.got = dp_swap(send, self.order.pop(0))


def place_of(p, order):
    return sum((p >> bit & 1) << i for i, bit in enumerate(reversed(order)))


SUMS = 3


def to_all(source, target, sends, gets):
    me = lax.axis_index("dp")
    return [
        pltpu.make_async_remote_copy(
            src_ref=source(me ^ r), dst_ref=target, send_sem=sends.at[r], recv_sem=gets.at[r],
            device_id={"dp": me ^ r}, device_id_type=pl.DeviceIdType.MESH,
        )
        for r in range(1, lax.axis_size("dp"))
    ]


def small_kernel(mod_ref, mod_out, sum_out, part, sends, gets, own):
    me = lax.axis_index("dp")
    steps = (
        to_all(lambda peer: mod_ref.at[peer], mod_out.at[me], sends.at[0], gets.at[0])
        + [pltpu.make_async_copy(mod_ref.at[me], mod_out.at[me], own.at[0])],
        to_all(lambda peer: part, sum_out.at[me], sends.at[1], gets.at[1])
        + [pltpu.make_async_copy(part, sum_out.at[me], own.at[1])],
    )
    for i, copies in enumerate(steps):
        if i == 1:
            part[...] = jnp.sum(mod_out[...], axis=0)
        for copy in copies:
            copy.start()
        for copy in copies:
            copy.wait()


def small_exchange(mods):
    vmem = pl.BlockSpec(memory_space=pltpu.VMEM)
    count = mods.shape[0]
    return pl.pallas_call(
        small_kernel,
        in_specs=[vmem],
        out_specs=[vmem] * 2,
        out_shape=[jax.ShapeDtypeStruct(mods.shape, mods.dtype)] * 2,
        scratch_shapes=[
            pltpu.VMEM(mods.shape[1:], mods.dtype),
            pltpu.SemaphoreType.DMA((2, count)), pltpu.SemaphoreType.DMA((2, count)),
            pltpu.SemaphoreType.DMA((2,)),
        ],
        compiler_params=pltpu.CompilerParams(has_side_effects=True),
    )(mods)


def settle(chains, value):
    live = [c for c in chains if c.got is not None]
    value, got = lax.optimization_barrier((value, [c.got for c in live]))
    for c, g in zip(live, got):
        c.got = g
    return value


def advance(chains, value):
    value = settle(chains, value)
    for c in chains:
        c.step()
    return value


def rope_block(value, cosine, sine, sign):
    width = value.shape[1]
    lane = lax.broadcasted_iota(jnp.int32, value.shape, 1)
    partner = jnp.where(
        lane % 32 < 16, pltpu.roll(value, width - 16, 1), pltpu.roll(value, 16, 1)
    )
    return value * cosine + sign * (partner * sine)


def column(ref, index, width):
    row = ref[index : index + 1, :] if isinstance(index, int) else ref[pl.ds(index, 1), :]
    return jnp.broadcast_to(row, (width, row.shape[1])).T


def masked(value, head):
    lane = lax.broadcasted_iota(jnp.int32, value.shape, 1)
    return jnp.where(lane // HD == head, value, jnp.zeros_like(value))


def attn_fwd_kernel(
    len_ref, pre_ref, inv_ref, gq_ref, gk_ref, cos_ref, sin_ref, tk_ref, tv_ref, gate_ref,
    q_ref, k_ref, v_ref, mixed_ref, so_ref, co_ref, ls_ref, lc_ref,
):
    _, tokens, width = pre_ref.shape
    heads = width // HD
    iq, ik = column(inv_ref, 0, width), column(inv_ref, 1, width)
    q = rope_block(pre_ref[0] * iq * gq_ref[...], cos_ref[...], sin_ref[...], 1.0)
    q_ref[...] = q.astype(BF16)
    k = rope_block(pre_ref[1] * ik * gk_ref[...], cos_ref[...], sin_ref[...], 1.0)
    k_ref[...] = k.astype(BF16)
    v_ref[...] = pre_ref[2].astype(BF16)
    length = len_ref[0]

    def one(keys, values, qm, limit):
        s = dot(qm, keys, 1, 1)
        if limit is not None:
            slot = lax.broadcasted_iota(jnp.int32, s.shape, 1)
            s = jnp.where(slot < limit, s, -1e30)
        peak = jnp.max(s, axis=1, keepdims=True)
        e = jnp.exp(s - peak)
        total = jnp.sum(e, axis=1, keepdims=True)
        o = dot(e.astype(BF16), values)
        return o * (1.0 / total), peak + jnp.log(total)

    lane = lax.broadcasted_iota(jnp.int32, (tokens, width), 1)
    qs = q_ref[...] * jnp.asarray(HD**-0.5, BF16)
    so = co = stats = jnp.zeros((tokens, width), F32)
    for h in range(heads):
        qm = masked(qs, h)
        o, lse = one(k_ref[...], v_ref[...], qm, None)
        so = jnp.where(lane // HD == h, o, so)
        stats = jnp.where(lane == h, lse, stats)
        o, lse = one(tk_ref[...], tv_ref[...], qm, length)
        co = jnp.where(lane // HD == h, o, co)
        stats = jnp.where(lane == heads + h, lse, stats)
    so_ref[...] = so
    co_ref[...] = co
    mixed_ref[...] = (so + gate_ref[...] * co).astype(BF16)
    stats = stats.T
    ls_ref[0] = stats[:heads]
    lc_ref[0] = stats[heads : 2 * heads]


def attn_bwd_kernel(
    len_ref, q_ref, k_ref, v_ref, tk_ref, tv_ref, g_ref, so_ref, co_ref, ls_ref, lc_ref,
    pre_ref, inv_ref, gq_ref, gk_ref, cos_ref, sin_ref, gate_ref,
    d_ref, dtk_ref, dtv_ref, stat_ref, gainq_ref, gaink_ref, gateg_ref,
    gs_ref, gc_ref, ds_ref, dc_ref, kt_ref, tkt_ref, dqt_ref, dk_acc, dv_acc, rq_ref, rk_ref,
):
    tokens, width = q_ref.shape
    heads = width // HD
    scale = jnp.asarray(HD**-0.5, BF16)

    @pl.when(pl.program_id(0) == 0)
    def _():
        rq_ref[...] = jnp.zeros_like(rq_ref)
        rk_ref[...] = jnp.zeros_like(rk_ref)

    g = g_ref[...]
    gs_ref[...] = g.astype(BF16)
    gc_ref[...] = (g * gate_ref[...]).astype(BF16)
    prod_c = g * co_ref[...]
    gateg_ref[...] = jnp.sum(prod_c, axis=0, keepdims=True)
    prod_s = (g * so_ref[...]).T
    prod_c = (prod_c * gate_ref[...]).T
    for h in range(heads):
        ds_ref[h : h + 1, :] = jnp.sum(prod_s[h * HD : (h + 1) * HD], axis=0, keepdims=True)
        dc_ref[h : h + 1, :] = jnp.sum(prod_c[h * HD : (h + 1) * HD], axis=0, keepdims=True)
    kt_ref[...] = k_ref[...].astype(F32).T.astype(BF16)
    tkt_ref[...] = tk_ref[...].astype(F32).T.astype(BF16)
    dk_acc[...] = jnp.zeros_like(dk_acc)
    dv_acc[...] = jnp.zeros_like(dv_acc)
    dtk_ref[...] = jnp.zeros_like(dtk_ref)
    dtv_ref[...] = jnp.zeros_like(dtv_ref)
    length = len_ref[0]

    def one(keys, keys_t, values, qm, gm, lse, delta, head, limit):
        s = dot(keys, qm, 1, 1)
        p = jnp.exp(s - lse)
        if limit is not None:
            slot = lax.broadcasted_iota(jnp.int32, s.shape, 0)
            p = jnp.where(slot < limit, p, 0.0)
        dp = dot(values, gm, 1, 1)
        ds = (p * (dp - delta)).astype(BF16)
        dq = dot(keys_t[head * HD : (head + 1) * HD, :], ds)
        return dq, dot(ds, qm), dot(p.astype(BF16), gm)

    def chunk(c, carry):
        rows = pl.ds(pl.multiple_of(c * QC, QC), QC)
        qc = q_ref[rows, :] * scale
        for h in range(heads):
            qm = masked(qc, h)
            dq, dk, dv = one(
                k_ref[...], kt_ref, v_ref[...], qm, masked(gs_ref[rows, :], h),
                ls_ref[0, h : h + 1, rows], ds_ref[h : h + 1, rows], h, None,
            )
            dk_acc[...] += dk
            dv_acc[...] += dv
            dq2, dk, dv = one(
                tk_ref[...], tkt_ref, tv_ref[...], qm, masked(gc_ref[rows, :], h),
                lc_ref[0, h : h + 1, rows], dc_ref[h : h + 1, rows], h, length,
            )
            dtk_ref[...] += dk
            dtv_ref[...] += dv
            dqt_ref[h * HD : (h + 1) * HD, rows] = (dq + dq2) * HD**-0.5
        return carry

    lax.fori_loop(0, tokens // QC, chunk, 0)
    dq = rope_block(dqt_ref[...].T, cos_ref[...], sin_ref[...], -1.0)
    d_ref[0] = dq
    prod = dq * (pre_ref[0] * column(inv_ref, 0, width))
    gainq_ref[...] = jnp.sum(prod, axis=0, keepdims=True)
    rq_ref[...] += prod * gq_ref[...]
    dk = rope_block(dk_acc[...], cos_ref[...], sin_ref[...], -1.0)
    d_ref[1] = dk
    prod = dk * (pre_ref[1] * column(inv_ref, 1, width))
    gaink_ref[...] = jnp.sum(prod, axis=0, keepdims=True)
    rk_ref[...] += prod * gk_ref[...]
    d_ref[2] = dv_acc[...]

    @pl.when(pl.program_id(0) == pl.num_programs(0) - 1)
    def _():
        stat_ref[...] = jnp.zeros_like(stat_ref)
        for i, ref in enumerate((rq_ref, rk_ref)):
            stat_ref[i : i + 1, :] = jnp.sum(ref[...].T, axis=0, keepdims=True)


def specs(tokens, text, width, heads, at=0):
    col = pl.BlockSpec((tokens, width), lambda i: (0, i + at))
    three = pl.BlockSpec((3, tokens, width), lambda i: (0, 0, i + at))
    tcol = pl.BlockSpec((text, width), lambda i: (0, i + at))
    stat = pl.BlockSpec((8, tokens), lambda i: (0, 0))
    gain = pl.BlockSpec((1, width), lambda i: (0, i + at))
    table = pl.BlockSpec((tokens, width), lambda i: (0, 0))
    lse = pl.BlockSpec((1, heads, tokens), lambda i: (i + at, 0, 0))
    scalar = pl.BlockSpec(memory_space=pltpu.SMEM)
    return col, three, tcol, stat, gain, table, lse, scalar


def sds(shape, dtype=F32):
    return jax.ShapeDtypeStruct(shape, dtype)


def attn_forward(length, pre, inv, gq, gk, cosine, sine, tk, tv, gate):
    _, tokens, columns = pre.shape
    text, width = tk.shape[0], cosine.shape[1]
    heads, blocks = width // HD, columns // width
    col, three, tcol, stat, gain, table, lse, scalar = specs(tokens, text, width, heads)
    flat = (tokens, columns)
    return pl.pallas_call(
        attn_fwd_kernel,
        grid=(blocks,),
        in_specs=[scalar, three, stat, gain, gain, table, table, tcol, tcol, gain],
        out_specs=[col, col, col, col, col, col, lse, lse],
        out_shape=[sds(flat, BF16)] * 4 + [sds(flat)] * 2 + [sds((blocks, heads, tokens))] * 2,
    )(length, pre, inv, gq, gk, cosine, sine, tk, tv, gate)


def attn_backward(at, blocks, length, q, k, v, tk, tv, g, so, co, ls, lc, pre, inv, gq, gk, cosine, sine, gate):
    tokens = q.shape[0]
    text, width = tk.shape[0], cosine.shape[1]
    heads, columns = width // HD, blocks * width
    col, three, tcol, stat, gain, table, lse, scalar = specs(tokens, text, width, heads, at)
    _, three_o, tcol_o, _, gain_o, _, _, _ = specs(tokens, text, width, heads)
    return pl.pallas_call(
        attn_bwd_kernel,
        grid=(blocks,),
        in_specs=[scalar, col, col, col, tcol, tcol, col, col, col, lse, lse,
                  three, stat, gain, gain, table, table, gain],
        out_specs=[three_o, tcol_o, tcol_o, stat, gain_o, gain_o, gain_o],
        out_shape=[
            sds((3, tokens, columns)), sds((text, columns)), sds((text, columns)),
            sds((8, tokens)), sds((1, columns)), sds((1, columns)), sds((1, columns)),
        ],
        scratch_shapes=[
            pltpu.VMEM((tokens, width), BF16), pltpu.VMEM((tokens, width), BF16),
            pltpu.VMEM((heads, tokens), F32), pltpu.VMEM((heads, tokens), F32),
            pltpu.VMEM((width, tokens), BF16), pltpu.VMEM((width, text), BF16),
            pltpu.VMEM((width, tokens), F32),
            pltpu.VMEM((tokens, width), F32), pltpu.VMEM((tokens, width), F32),
            pltpu.VMEM((tokens, width), F32), pltpu.VMEM((tokens, width), F32),
        ],
    )(length, q, k, v, tk, tv, g, so, co, ls, lc, pre, inv, gq, gk, cosine, sine, gate)


def pick(rows, cols, step, part):
    i = lax.broadcasted_iota(jnp.int32, (rows, cols), 0)
    j = lax.broadcasted_iota(jnp.int32, (rows, cols), 1)
    hit = (j == step * i + part) if cols > rows else (i == step * j + part)
    return jnp.where(hit, 1.0, 0.0).astype(BF16)

def text_fwd_kernel(x_ref, w_ref, o_ref):
    @pl.when(pl.program_id(0) == 0)
    def _():
        o_ref[...] = jnp.zeros_like(o_ref)
    for b in range(w_ref.shape[0] // 128):
        rows = slice(b * 128, (b + 1) * 128)
        w = w_ref[rows].reshape(256, w_ref.shape[2])
        x = x_ref[:, rows]
        for j in range(2):
            spread = dot(x, pick(128, 256, 2, j)).astype(BF16)
            o_ref[j] += dot(spread, w)

def text_fwd(x, w):
    depth, _, cols = w.shape
    bk = 256
    return pl.pallas_call(
        text_fwd_kernel, grid=(depth // bk,),
        in_specs=[pl.BlockSpec((x.shape[0], bk), lambda i: (0, i)), pl.BlockSpec((bk, 2, cols), lambda i: (i, 0, 0))],
        out_specs=pl.BlockSpec((2, x.shape[0], cols), lambda i: (0, 0, 0)),
        out_shape=sds((2, x.shape[0], cols)),
    )(x, w)

def text_bwd_kernel(g_ref, w_ref, pair_ref, o_ref, pair_out, sends, gets, own):
    me = lax.axis_index("dp")
    step = pl.program_id(0)
    copies = to_all(lambda peer: pair_ref.at[peer], pair_out.at[me], sends, gets)
    copies.append(pltpu.make_async_copy(pair_ref.at[me], pair_out.at[me], own))

    @pl.when(step == 0)
    def _():
        for copy in copies:
            copy.start()

    for b in range(w_ref.shape[0] // 128):
        rows = slice(b * 128, (b + 1) * 128)
        w = w_ref[rows].reshape(256, w_ref.shape[2])
        total = 0.0
        for j in range(2):
            total = total + dot(g_ref[j], dot(pick(128, 256, 2, j), w).astype(BF16), 1, 1)
        o_ref[:, rows] = total.astype(BF16)

    @pl.when(step == pl.num_programs(0) - 1)
    def _():
        for copy in copies:
            copy.wait()


def text_bwd(g, w, pair):
    depth, _, cols = w.shape
    bk = 256
    count = pair.shape[0]
    return pl.pallas_call(
        text_bwd_kernel,
        grid=(depth // bk,),
        in_specs=[
            pl.BlockSpec(g.shape, lambda i: (0, 0, 0)),
            pl.BlockSpec((bk, 2, cols), lambda i: (i, 0, 0)),
            pl.BlockSpec(memory_space=pl.ANY),
        ],
        out_specs=[
            pl.BlockSpec((g.shape[1], bk), lambda i: (0, i)), pl.BlockSpec(memory_space=pl.ANY),
        ],
        out_shape=[
            sds((g.shape[1], depth), BF16), jax.ShapeDtypeStruct(pair.shape, pair.dtype),
        ],
        scratch_shapes=[
            pltpu.SemaphoreType.DMA((count,)), pltpu.SemaphoreType.DMA((count,)),
            pltpu.SemaphoreType.DMA,
        ],
        compiler_params=pltpu.CompilerParams(has_side_effects=True),
    )(g, w, pair)


def put_relative(dst, src, me, f, count):
    rows = dst.shape[0] // count
    for p in range(count):
        start = pl.multiple_of((me ^ turned(p, f)) * rows, 16)
        dst[p * rows : (p + 1) * rows, :] = src[pl.ds(start, rows), :]


def put_halves(keep, send, value, count, order, slot=None):
    rows = value.shape[0] // count
    for p in range(count):
        place = place_of(p, order[1:])
        where = place if slot is None else (place, slot)
        (send if p >> order[0] & 1 else keep)[where] = value[p * rows : (p + 1) * rows]


def ffn_kernel(
    orders, id_ref, s_ref, b_ref, w_ref, d_ref,
    wk_ref, ws_ref, dk_ref, ds_ref, fo_ref, fp_ref, so_ref, sp_ref,
    st, bt, tmp, wg, wu, facc, sacc,
):
    step = pl.program_id(0)
    depth, _, cols = w_ref.shape
    own = fo_ref.shape[0]
    count = 2 * dk_ref.shape[0]

    @pl.when(step == 0)
    def _():
        for src, dst in ((s_ref, st), (b_ref, bt)):
            for c in range(depth // 256):
                part = slice(c * 256, (c + 1) * 256)
                tmp[part, :] = src[:, part].astype(F32).T.astype(BF16)
            put_relative(dst, tmp, id_ref[0], id_ref[1], count)
        facc[...] = jnp.zeros_like(facc)
        sacc[...] = jnp.zeros_like(sacc)

    for c in range(depth // 128):
        part = slice(c * 128, (c + 1) * 128)
        w = w_ref[part].reshape(256, cols)
        wg[part, :] = dot(pick(128, 256, 2, 0), w).astype(BF16)
        wu[part, :] = dot(pick(128, 256, 2, 1), w).astype(BF16)
    s, b = s_ref[...], b_ref[...]
    gate = dot(s, wg[...])
    up = dot(s, wu[...])
    back = dot(b, d_ref[...], 1, 1)
    sig = jax.nn.sigmoid(gate)
    silu = gate * sig
    hidden = (silu * up).astype(BF16)
    g_gate = (back * up * (sig + silu * (1.0 - sig))).astype(BF16)
    g_up = (back * silu).astype(BF16)
    put_halves(wk_ref, ws_ref, dot(st[...], g_gate).astype(BF16), count, orders[0], 0)
    put_halves(wk_ref, ws_ref, dot(st[...], g_up).astype(BF16), count, orders[0], 1)
    put_halves(dk_ref, ds_ref, dot(bt[...], hidden).astype(BF16), count, orders[1])
    facc[...] += dot(hidden, d_ref[...])
    sacc[...] += dot(g_gate, wg[...], 1, 1) + dot(g_up, wu[...], 1, 1)

    @pl.when(step == pl.num_programs(0) - 1)
    def _():
        fo_ref[...] = facc[:own]
        fp_ref[...] = facc[own:].astype(BF16)
        so_ref[...] = sacc[:own]
        sp_ref[...] = sacc[own:].astype(BF16)


def ffn(ids, s, b, w, d, local, dp, orders):
    tokens, depth = s.shape
    hid = d.shape[0]
    bc = min(256, hid)
    rest = tokens - local
    once = functools.partial(pl.BlockSpec, pipeline_mode=pl.Buffered(1))
    const = lambda i: (0, 0)
    share = depth // dp
    half = pl.BlockSpec((dp // 2, share, bc), lambda i: (0, 0, i))
    halves = pl.BlockSpec((dp // 2, 2, share, bc), lambda i: (0, 0, 0, i))
    return pl.pallas_call(
        functools.partial(ffn_kernel, orders),
        grid=(hid // bc,),
        in_specs=[
            pl.BlockSpec(memory_space=pltpu.SMEM),
            once((tokens, depth), const), once((tokens, depth), const),
            pl.BlockSpec((depth, 2, bc), lambda i: (0, 0, i)),
            pl.BlockSpec((bc, depth), lambda i: (i, 0)),
        ],
        out_specs=[halves] * 2 + [half] * 2 + [
            once((local, depth), const), once((rest, depth), const),
            once((local, depth), const), once((rest, depth), const),
        ],
        out_shape=[sds((dp // 2, 2, share, hid), BF16)] * 2 + [sds((dp // 2, share, hid), BF16)] * 2 + [
            sds((local, depth)), sds((rest, depth), BF16),
            sds((local, depth)), sds((rest, depth), BF16),
        ],
        scratch_shapes=[
            pltpu.VMEM((depth, tokens), BF16), pltpu.VMEM((depth, tokens), BF16),
            pltpu.VMEM((depth, tokens), BF16),
            pltpu.VMEM((depth, bc), BF16), pltpu.VMEM((depth, bc), BF16),
            pltpu.VMEM((tokens, depth), F32), pltpu.VMEM((tokens, depth), F32),
        ],
        compiler_params=pltpu.CompilerParams(vmem_limit_bytes=62 << 20),
    )(ids, s, b, w, d)


def project_kernel(id_ref, xo_ref, xp_ref, front_ref, w_ref, got_ref, first_ref, pre_ref, sq_ref):
    j = pl.program_id(0)
    local, depth = xo_ref.shape
    own = got_ref.shape[2]
    f = id_ref[1]

    @pl.when(j == 0)
    def _():
        for i, ref in enumerate((xo_ref, xp_ref)):
            x = ref[...].astype(F32)
            inv = lax.rsqrt(jnp.sum(x * x, axis=1, keepdims=True) * (1.0 / depth) + EPSILON)
            first_ref[i * local : (i + 1) * local, :] = (x * inv * front_ref[...]).astype(BF16)
        sq_ref[...] = jnp.zeros_like(sq_ref)

    mine = pl.ds(pl.multiple_of(f * own, 128), own)
    other = pl.ds(pl.multiple_of((1 - f) * own, 128), own)
    out = dot(first_ref[:, mine], w_ref[0, :, mine]) + dot(first_ref[:, other], got_ref[0])
    pre_ref[0] = out
    square = out * out
    part = square[:, :128]
    for c in range(1, own // 128):
        part = part + square[:, c * 128 : (c + 1) * 128]
    sq_ref[pl.ds(j, 1), :] = jnp.sum(part.T, axis=0, keepdims=True)


def project(ids, xo, xp, front, w, got):
    local, depth = xo.shape
    own = got.shape[2]
    tokens = 2 * local
    const = lambda j: (0, 0)
    return pl.pallas_call(
        project_kernel,
        grid=(3,),
        in_specs=[
            pl.BlockSpec(memory_space=pltpu.SMEM),
            pl.BlockSpec((local, depth), const), pl.BlockSpec((local, depth), const),
            pl.BlockSpec((1, depth), const),
            pl.BlockSpec((1, own, depth), lambda j: (j, 0, 0)),
            pl.BlockSpec((1, own, own), lambda j: (j, 0, 0)),
        ],
        out_specs=[
            pl.BlockSpec((tokens, depth), const),
            pl.BlockSpec((1, tokens, own), lambda j: (j, 0, 0)),
            pl.BlockSpec((8, tokens), const),
        ],
        out_shape=[sds((tokens, depth), BF16), sds((3, tokens, own)), sds((8, tokens))],
    )(ids, xo, xp, front, w, got)


def project_grad_kernel(
    order, id_ref, da_ref, db_ref, pre_ref, stat_ref, gain_ref, first_ref,
    keep_ref, send_ref, g_ref, gt, tmp,
):
    j = pl.program_id(0)
    own = pre_ref.shape[2]
    cut = da_ref.shape[2]
    count = 2 * keep_ref.shape[0]
    inv, mean = column(stat_ref, j, 128), column(stat_ref, j + 3, 128)
    for c in range(own // 128):
        part = slice(c * 128, (c + 1) * 128)
        here = slice(c * 128 - cut, (c + 1) * 128 - cut) if c * 128 >= cut else part
        d = (db_ref if c * 128 >= cut else da_ref)[0, :, here]
        g = inv * (d * gain_ref[0, :, part] - pre_ref[0, :, part] * inv * mean)
        tmp[part, :] = g.T.astype(BF16)
        g_ref[0, :, part] = g.astype(BF16)
    put_relative(gt, tmp, id_ref[0] % count, id_ref[1], count)
    put_halves(keep_ref, send_ref, dot(gt[...], first_ref[...]).astype(BF16), count, order, j)


def project_grad(ids, da, db, pre, stats, gain, first, dp, order):
    _, tokens, own = pre.shape
    depth = first.shape[1]
    share = depth // dp
    const = lambda j: (0, 0)
    block = lambda j: (j, 0, 0)
    once = functools.partial(pl.BlockSpec, pipeline_mode=pl.Buffered(1))
    half = once((dp // 4, 3, share, depth), lambda j: (0, 0, 0, 0))
    return pl.pallas_call(
        functools.partial(project_grad_kernel, order),
        grid=(3,),
        in_specs=[
            pl.BlockSpec(memory_space=pltpu.SMEM),
            pl.BlockSpec((1,) + da.shape[1:], block), pl.BlockSpec((1,) + db.shape[1:], block),
            pl.BlockSpec((1, tokens, own), block),
            pl.BlockSpec((8, tokens), const),
            pl.BlockSpec((1, 1, own), block),
            once((tokens, depth), const),
        ],
        out_specs=[half, half, pl.BlockSpec((1, tokens, own), block)],
        out_shape=[sds((dp // 4, 3, share, depth), BF16)] * 2
        + [sds((3, tokens, own), BF16)],
        scratch_shapes=[pltpu.VMEM((own, tokens), BF16), pltpu.VMEM((own, tokens), BF16)],
    )(ids, da, db, pre, stats, gain, first)


def project_back_kernel(id_ref, g_ref, w_ref, got_ref, own_ref, peer_ref, acc):
    j = pl.program_id(0)
    own = g_ref.shape[2]
    local = own_ref.shape[0]
    f = id_ref[1]
    mine = pl.ds(pl.multiple_of(f * own, 128), own)
    other = pl.ds(pl.multiple_of((1 - f) * own, 128), own)

    @pl.when(j == 0)
    def _():
        acc[...] = jnp.zeros_like(acc)

    acc[:, mine] += dot(g_ref[0], w_ref[0, :, mine], 1, 1)
    acc[:, other] += dot(g_ref[0], got_ref[0], 1, 1)

    @pl.when(j == 2)
    def _():
        own_ref[...] = acc[:local]
        peer_ref[...] = acc[local:].astype(BF16)


def project_back(ids, g, w, got):
    _, tokens, own = g.shape
    depth = w.shape[2]
    local = tokens // 2
    const = lambda j: (0, 0)
    block = lambda j: (j, 0, 0)
    once = functools.partial(pl.BlockSpec, pipeline_mode=pl.Buffered(1))
    return pl.pallas_call(
        project_back_kernel,
        grid=(3,),
        in_specs=[
            pl.BlockSpec(memory_space=pltpu.SMEM),
            pl.BlockSpec((1, tokens, own), block),
            pl.BlockSpec((1, own, depth), block), pl.BlockSpec((1, own, own), block),
        ],
        out_specs=[once((local, depth), const), once((local, depth), const)],
        out_shape=[sds((local, depth)), sds((local, depth), BF16)],
        scratch_shapes=[pltpu.VMEM((tokens, depth), F32)],
    )(ids, g, w, got)


def out_back_kernel(order, id_ref, *refs):
    n = len(refs) - 8
    blocks, (w_ref, mixed_ref, g_ref, keep_ref, send_ref, all_ref, gt, tmp) = refs[:n], refs[n:]
    local = blocks[0].shape[0]
    for r, ref in enumerate(blocks):
        all_ref[r * local : (r + 1) * local, :] = ref[...]
    grad = all_ref[...]
    g_ref[...] = dot(grad, w_ref[...], 1, 1)
    for c in range(grad.shape[1] // 256):
        part = slice(c * 256, (c + 1) * 256)
        tmp[part, :] = grad[:, part].astype(F32).T.astype(BF16)
    count = 2 * keep_ref.shape[0]
    put_relative(gt, tmp, id_ref[0], id_ref[1], count)
    put_halves(keep_ref, send_ref, dot(gt[...], mixed_ref[...]).astype(BF16), count, order)


def out_back(ids, blocks, w, mixed, dp, order):
    tokens, own = mixed.shape
    depth = w.shape[1]
    vmem = pl.BlockSpec(memory_space=pltpu.VMEM)
    half = sds((dp // 2, depth // dp, own), BF16)
    return pl.pallas_call(
        functools.partial(out_back_kernel, order),
        in_specs=[pl.BlockSpec(memory_space=pltpu.SMEM)] + [vmem] * (len(blocks) + 2),
        out_specs=[vmem] * 3,
        out_shape=[sds((tokens, own)), half, half],
        scratch_shapes=[
            pltpu.VMEM((tokens, depth), BF16),
            pltpu.VMEM((depth, tokens), BF16), pltpu.VMEM((depth, tokens), BF16),
        ],
    )(ids, *blocks, w, mixed)


def time_embed(timesteps):
    half = TE // 2
    frequencies = jnp.exp(-math.log(10000.0) * jnp.arange(half, dtype=F32) / half)
    angles = timesteps.astype(F32)[:, None] * frequencies
    waves = jnp.concatenate([jnp.cos(angles), jnp.sin(angles)], axis=-1)
    return jax.nn.silu(waves).astype(BF16)


def rope_tables(positions, width):
    lane = jnp.arange(width)
    quarter = HD // 4
    frequencies = 10000.0 ** (-(lane % quarter).astype(F32) / quarter)
    place = jnp.where(lane % HD < HD // 2, positions[0][:, None], positions[1][:, None])
    angles = place.astype(F32) * frequencies
    return jnp.cos(angles), jnp.where(lane % 32 < 16, -1.0, 1.0) * jnp.sin(angles)


def inverse_rms(values):
    return lax.rsqrt(jnp.mean(values * values, axis=-1, keepdims=True) + EPSILON)


def rms_back(grad_hat, normed, inverse):
    return inverse * (grad_hat - normed * jnp.mean(grad_hat * normed, axis=-1, keepdims=True))


def pad_cols(value, width):
    extra = -value.shape[-1] % width
    return value if extra == 0 else jnp.pad(value, [(0, 0)] * (value.ndim - 1) + [(0, extra)])


def on_device(
    hidden_in, text_state, caption_lengths, timesteps, patch_positions, cotangent,
    w_ada, w_text, w_qkv, w_out, gains, cross_gate, w_gate_up, w_down,
):
    n, f = lax.axis_size("fsdp"), lax.axis_index("fsdp")
    dpn, me = lax.axis_size("dp"), lax.axis_index("dp")
    bits = list(range(dp_bits()))
    low_bits = bits[:-1]
    late = bits[2:3] + bits[:2] + bits[3:]
    own_d = D // n
    local = hidden_in.shape[1]
    tokens = n * local
    width = 2 * HD
    share = D // dpn
    paired = n == 2 and dpn >= 4
    ids = jnp.stack([me, f]).astype(jnp.int32)
    x_bf, dy_bf = hidden_in[0], cotangent[0]

    time_low = time_embed(timesteps)
    own_te = TE // n
    time_own = lax.dynamic_slice_in_dim(time_low[0], f * own_te, own_te, 0)
    modulation = pair_sum(
        jnp.einsum("k,kjd->jd", time_own, w_ada, preferred_element_type=F32)
    )
    scale_attn, gate_attn = modulation[0:1], jnp.tanh(modulation[1:2])
    scale_ffn, gate_ffn = modulation[2:3], jnp.tanh(modulation[3:4])

    w_flat = jnp.moveaxis(w_qkv, 1, 0)
    w_parts = exchange_rot(w_flat, 2)
    x_parts = gather_rot(x_bf)
    dy_all = jnp.concatenate(gather_rot(dy_bf), axis=0)
    places = jnp.concatenate(gather_rot(patch_positions[0]), axis=1)
    text_cols = jnp.concatenate(natural(exchange_rot(text_state[0], 1)), axis=0)
    text_all = lax.all_gather(text_cols, "dp", axis=0, tiled=True)
    gain_full = lax.all_gather(gains, "fsdp", axis=1, tiled=True).astype(F32)
    gain_own = gains.astype(F32)

    front = gain_full[0] * (1.0 + scale_attn)
    if paired:
        first_all, pre, squares = project(ids, *x_parts, front, w_flat, w_parts[1])
    else:
        w_heads = jnp.concatenate(natural(w_parts), axis=1)
        x_f = jnp.concatenate(x_parts, axis=0).astype(F32)
        first_all = (x_f * inverse_rms(x_f) * front).astype(BF16)
        pre = jnp.stack([dot(first_all, w_heads[j]) for j in range(3)])
        squares = jnp.pad(jnp.sum(pre[:2] * pre[:2], -1), ((0, 6), (0, 0)))
    inverse = lax.rsqrt(row_sum(squares) / D + EPSILON)

    text_part = text_fwd(text_cols, w_text)
    text_pre = scatter_rot(rot_blocks(text_part, 2))
    inv_t = lax.rsqrt(
        pair_sum(jnp.sum(text_pre[0] * text_pre[0], -1, keepdims=True)) / D + EPSILON
    )
    normed_t = text_pre[0] * inv_t
    tk = (normed_t * gain_own[4]).astype(BF16)
    tv = text_pre[1].astype(BF16)

    head_tanh = jnp.tanh(cross_gate.astype(F32))
    gate_row = pad_cols(jnp.repeat(head_tanh, HD)[None], width)
    cosine, sine = rope_tables(places, width)
    gq, gk = pad_cols(gain_own[2:3], width), pad_cols(gain_own[3:4], width)
    pre_p, tkp, tvp = pad_cols(pre, width), pad_cols(tk, width), pad_cols(tv, width)
    q, k, v, mixed_p, so, co, ls, lc = attn_forward(
        caption_lengths, pre_p, inverse, gq, gk, cosine, sine, tkp, tvp, gate_row
    )
    mixed = mixed_p[:, :own_d]

    def rows(value, r):
        return value[r * local : (r + 1) * local]

    parts = [dot(rows(mixed, r), w_out) for r in range(n)]
    attn_branch = scatter_rot([parts[0]] + [p.astype(BF16) for p in parts[1:]])
    x_own = x_bf.astype(F32)
    after_attn = x_own + gate_attn * attn_branch
    inverse_two = inverse_rms(after_attn)
    normed_two = after_attn * inverse_two
    second = (normed_two * gain_full[1] * (1.0 + scale_ffn)).astype(BF16)

    second_all = jnp.concatenate(gather_rot(second), axis=0)
    branch_all = (gate_ffn * dy_all.astype(F32)).astype(BF16)
    wide_keep, wide_send, down_keep, down_send, ffn_own, ffn_rest, back_own, back_rest = ffn(
        ids, second_all, branch_all, w_gate_up, w_down, local, dpn, (bits, late)
    )
    (ffn_own, ffn_rest, back_own, back_rest), text_all = lax.optimization_barrier(
        ((ffn_own, ffn_rest, back_own, back_rest), text_all)
    )
    wide_chain = Halving(bits, wide_keep, wide_send)
    down_chain = Halving(late, down_keep, down_send)
    grad_second = scatter_rot([back_own] + [rows(back_rest, r) for r in range(n - 1)])
    ffn_branch = scatter_rot([ffn_own] + [rows(ffn_rest, r) for r in range(n - 1)])
    output = (after_attn + gate_ffn * ffn_branch).astype(BF16)
    dy = dy_bf.astype(F32)
    d_gate_ffn = jnp.sum(dy * ffn_branch, axis=0) * (1.0 - gate_ffn[0] * gate_ffn[0])

    scaled = grad_second * normed_two
    d_scale_ffn = jnp.sum(scaled * gain_full[1], axis=0)
    gain_two = jnp.sum(scaled * (1.0 + scale_ffn), axis=0)
    grad_after = dy + rms_back(
        grad_second * gain_full[1] * (1.0 + scale_ffn), normed_two, inverse_two
    )
    d_gate_attn = jnp.sum(grad_after * attn_branch, axis=0) * (1.0 - gate_attn[0] * gate_attn[0])
    grad_attn = (gate_attn * grad_after).astype(BF16)
    grad_mixed, *out_halves = out_back(ids, gather_rot(grad_attn), w_out, mixed, dpn, bits)
    out_chain = Halving(bits, *out_halves)
    blocks = pre_p.shape[2] // width
    cut = max(1, 2 * blocks // 3)
    grad_mixed = pad_cols(grad_mixed, width)
    inputs = (so, co, ls, lc, pre_p, inverse, gq, gk, cosine, sine, gate_row)
    part_a = attn_backward(0, cut, caption_lengths, q, k, v, tkp, tvp, grad_mixed, *inputs)
    part_a, grad_mixed = lax.optimization_barrier((part_a, grad_mixed))
    grad_mixed = advance([wide_chain, down_chain], grad_mixed)
    part_b = attn_backward(
        cut, blocks - cut, caption_lengths, q, k, v, tkp, tvp, grad_mixed, *inputs
    )
    means = row_sum(part_a[3] + part_b[3])[:2] / D

    ones, zeros = jnp.ones((1, tokens), F32), jnp.zeros((1, tokens), F32)
    if paired:
        stats = jnp.concatenate([inverse[:2], ones, means, zeros, zeros, zeros], axis=0)
        gain3 = jnp.stack([gain_own[2:3], gain_own[3:4], jnp.ones_like(gain_own[2:3])])
        keep, send, grads = project_grad(
            ids, part_a[0], part_b[0], pre, stats, gain3, first_all, dpn, low_bits
        )
        part_a, part_b, grads = advance(
            [wide_chain, down_chain, out_chain], (part_a[1:], part_b[1:], grads)
        )
        qkv_chain = Halving(low_bits, keep, send)
        parts = project_back(ids, grads, w_flat, w_parts[1])
    else:
        d = jnp.concatenate([part_a[0], part_b[0]], axis=2)[:, :, :own_d]
        part_a, part_b = part_a[1:], part_b[1:]
        inv, mean = inverse[:2, :, None], means[:, :, None]
        hat = d[:2] * gain_own[2:4][:, None] - pre[:2] * inv * mean
        grads = [(inv[0] * hat[0]).astype(BF16), (inv[1] * hat[1]).astype(BF16), d[2].astype(BF16)]
        wide = [dot(g, first_all, 0, 0).astype(BF16) for g in grads]
        wide = [jnp.concatenate(natural(exchange_rot(w_, 1)), axis=0) for w_ in wide]
        wide = relative(jnp.stack([w_.reshape(dpn, share, own_d) for w_ in wide], axis=1))
        wide = jnp.stack([wide[p] for p in sorted(range(dpn), key=lambda p: place_of(p, bits))])
        qkv_chain = Halving(bits, wide[: dpn // 2], wide[dpn // 2 :])
        parts = [
            sum(dot(rows(g, r), w_heads[j], 1, 1) for j, g in enumerate(grads)) for r in range(n)
        ]
        parts = [parts[0]] + [p.astype(BF16) for p in parts[1:]]
    grad_first = scatter_rot(parts)

    dtk, dtv, gain_q, gain_k, gate_g = (
        jnp.concatenate([part_a[i], part_b[i]], axis=1)[:, :own_d] for i in (0, 1, 3, 4, 5)
    )
    text_hat = dtk * gain_own[4]
    gain_text = jnp.sum(dtk * normed_t, axis=0, keepdims=True)
    mean_t = pair_sum(jnp.sum(text_hat * normed_t, -1, keepdims=True)) / D
    grad_tk = (inv_t * (text_hat - normed_t * mean_t)).astype(BF16)
    text_pair = jnp.stack([grad_tk, dtv.astype(BF16)])
    pair_all = jnp.concatenate(natural(gather_rot(text_pair)), axis=-1)
    pair_all = settle([wide_chain], pair_all)
    outgoing = block_of(pair_all.transpose(0, 2, 1), f, 2)
    outgoing = outgoing.reshape(2, dpn, share, TEXT // n).transpose(1, 0, 2, 3)
    text_in, pair_cols = text_bwd(pair_all, w_text, outgoing)
    text_in, grad_first = advance([qkv_chain, down_chain, out_chain], (text_in, grad_first))
    text_in = jnp.concatenate(natural(exchange_rot(text_in, 0)), axis=1)

    inverse_one = inverse_rms(x_own)
    normed_one = x_own * inverse_one
    scaled = grad_first * normed_one
    d_scale_attn = jnp.sum(scaled * gain_full[0], axis=0)
    gain_one = jnp.sum(scaled * (1.0 + scale_attn), axis=0)
    grad_input = (
        grad_after
        + rms_back(grad_first * gain_full[0] * (1.0 + scale_attn), normed_one, inverse_one)
    ).astype(BF16)


    sums = [d_scale_attn, d_gate_attn, d_scale_ffn, d_gate_ffn, gain_one, gain_two]
    sums = pair_sum(jnp.stack(sums))
    stamp = jnp.full((1, D), timesteps[0].astype(F32))
    small = jnp.concatenate([block_of(sums[4:], f, 1), gain_q, gain_k, gain_text, gate_g], axis=0)
    small = jnp.pad(small.reshape(-1), (0, dpn * SUMS * 128 - small.size))
    mods = jnp.concatenate([sums[:4], stamp], axis=0).reshape(5, dpn, share).transpose(1, 0, 2)
    mods = jnp.pad(mods, ((0, 0), (0, 0), (0, -share % 128)))
    mods = jnp.concatenate([mods, small.reshape(dpn, SUMS, 128)], axis=1)
    mods, small = small_exchange(mods)
    mods = advance([qkv_chain, wide_chain, out_chain, down_chain], mods)
    pair_cols = jnp.concatenate(natural(gather_rot(pair_cols)), axis=3)
    pair_cols = pair_cols.transpose(1, 2, 0, 3).reshape(2 * share, dpn * TEXT)
    text_grad = dot(pair_cols, text_all).reshape(2, share, TW // n)
    total = small[:, 5 : 5 + SUMS].reshape(-1)[: 6 * own_d].reshape(6, own_d)
    gate_total = jnp.sum(total[5].reshape(HEADS // n, HD), axis=1) * (
        1.0 - head_tanh * head_tanh
    )
    times = time_embed(mods[:, 4, 0])
    times = lax.dynamic_slice_in_dim(times, f * own_te, own_te, 1).astype(F32)
    ada_grad = lax.dot_general(
        mods[:, :4, :share].reshape(dpn, 4 * share), times, (((0,), (0,)), ((), ())),
        precision=lax.Precision.HIGHEST,
    ).reshape(4, share, own_te)

    if paired:
        text_grad = advance([qkv_chain], text_grad)
        own_side = f == (me >> low_bits[-1] + 1)
        mine, got = exchange_rot(qkv_chain.last[0].astype(BF16), 2)
        got, wide_chain.keep = lax.optimization_barrier((got, wide_chain.keep))
        qkv_chain = Halving(
            bits[-1:], jnp.where(own_side, mine, got)[None], jnp.where(own_side, got, mine)[None]
        )
    for chain in (out_chain, down_chain, wide_chain, qkv_chain):
        while chain.got is not None:
            chain.step()
    return (
        output[None],
        grad_input[None],
        text_in[None],
        ada_grad.transpose(2, 0, 1),
        text_grad.transpose(2, 0, 1),
        qkv_chain.last[0].transpose(2, 0, 1),
        out_chain.last[0].T,
        total[:5],
        gate_total,
        wide_chain.last[0].transpose(1, 0, 2),
        down_chain.last[0].T,
    )


def solution(mesh):
    return jax.shard_map(
        on_device,
        mesh=mesh,
        in_specs=(
            P("dp", "fsdp", None),
            P("dp", "fsdp", None),
            P("dp"),
            P("dp"),
            P("dp", None, "fsdp"),
            P("dp", "fsdp", None),
            P("fsdp", None, None),
            P("fsdp", None, None),
            P("fsdp", None, None),
            P("fsdp", None),
            P(None, "fsdp"),
            P("fsdp"),
            P(None, None, "fsdp"),
            P("fsdp", None),
        ),
        out_specs=(
            P("dp", "fsdp", None),
            P("dp", "fsdp", None),
            P("dp", "fsdp", None),
            P("fsdp", None, "dp"),
            P("fsdp", None, "dp"),
            P("fsdp", None, "dp"),
            P("fsdp", "dp"),
            P(None, "fsdp"),
            P("fsdp"),
            P("dp", None, "fsdp"),
            P("fsdp", "dp"),
        ),
        check_vma=False,
    )
```

```python
import functools
import math

import jax
import jax.numpy as jnp
from jax import lax
from jax.experimental import pallas as pl
from jax.experimental.pallas import tpu as pltpu
from jax.sharding import PartitionSpec as P

D = 1536
HEADS = 24
HD = 64
TW = 4096
TE = 1024
PATCHES = 1024
TEXT = 256
EPSILON = 1e-06
F32 = jnp.float32
BF16 = jnp.bfloat16
QC = 256


def dot(a, b, ca=1, cb=0):
    return lax.dot_general(a, b, (((ca,), (cb,)), ((), ())), preferred_element_type=F32)


def from_behind(value, step):
    n = lax.axis_size("fsdp")
    return lax.ppermute(value, "fsdp", [(i, (i + step) % n) for i in range(n)])


def gather_rot(value):
    return [value] + [from_behind(value, r) for r in range(1, lax.axis_size("fsdp"))]


def pair_sum(value):
    return functools.reduce(lambda a, b: a + b, gather_rot(value))


def row_sum(value):
    n = lax.axis_size("fsdp")
    rows = value.shape[-1] // n
    total = value
    for r in range(1, n):
        total = total + jnp.roll(from_behind(value, r), r * rows, axis=-1)
    return total


def scatter_rot(blocks):
    n = lax.axis_size("fsdp")
    total = blocks[0].astype(F32)
    for r in range(1, n):
        got = lax.ppermute(blocks[r], "fsdp", [(i, (i - r) % n) for i in range(n)])
        total = total + got.astype(F32)
    return total


def block_of(value, index, axis):
    size = value.shape[axis] // lax.axis_size("fsdp")
    return lax.dynamic_slice_in_dim(value, index * size, size, axis)


def rot_blocks(value, axis):
    n, f = lax.axis_size("fsdp"), lax.axis_index("fsdp")
    return [block_of(value, (f - r) % n, axis) for r in range(n)]


def exchange_rot(value, axis):
    n, f = lax.axis_size("fsdp"), lax.axis_index("fsdp")
    out = [block_of(value, f, axis)]
    for r in range(1, n):
        out.append(from_behind(block_of(value, (f + r) % n, axis), r))
    return out


def natural(got):
    n, f = lax.axis_size("fsdp"), lax.axis_index("fsdp")
    if n == 2:
        return [jnp.where(f == 0, got[0], got[1]), jnp.where(f == 0, got[1], got[0])]
    got = jnp.stack(got)
    return [lax.dynamic_index_in_dim(got, (f - g) % n, 0, keepdims=False) for g in range(n)]


def dp_bits():
    return int(lax.axis_size("dp")).bit_length() - 1


def swapped(p):
    return (p & ~3) | ((p & 1) << 1) | ((p >> 1) & 1)


def turned(p, f):
    return p if dp_bits() < 3 else jnp.where(f % 2 == 0, p, swapped(p))


def dp_swap(value, bit):
    n, dpn = lax.axis_size("fsdp"), lax.axis_size("dp")
    pairs = []
    for i in range(dpn):
        for f in range(n):
            flip = 1 << bit if dp_bits() < 3 or f % 2 == 0 else swapped(1 << bit)
            pairs.append((i * n + f, (i ^ flip) * n + f))
    return lax.ppermute(value, ("dp", "fsdp"), pairs)


def relative(value):
    places = turned(jnp.arange(lax.axis_size("dp")), lax.axis_index("fsdp"))
    return jnp.take(value, lax.axis_index("dp") ^ places, axis=0)


class Halving:
    def __init__(self, order, keep, send):
        self.order = list(order)
        self.keep, self.got = keep, dp_swap(send, self.order.pop(0))

    def step(self):
        if self.got is None:
            return

        def add(part):
            return self.keep[part].astype(F32) + self.got[part].astype(F32)

        if not self.order:
            self.last = add(slice(None))
            self.got = None
            return
        half = self.keep.shape[0] // 2
        send = add(slice(half, None)).astype(BF16)
        self.keep = add(slice(half)).astype(BF16)
        self.got = dp_swap(send, self.order.pop(0))


def place_of(p, order):
    return sum((p >> bit & 1) << i for i, bit in enumerate(reversed(order)))


SUMS = 3


def to_all(source, target, sends, gets):
    me = lax.axis_index("dp")
    return [
        pltpu.make_async_remote_copy(
            src_ref=source(me ^ r), dst_ref=target, send_sem=sends.at[r], recv_sem=gets.at[r],
            device_id={"dp": me ^ r}, device_id_type=pl.DeviceIdType.MESH,
        )
        for r in range(1, lax.axis_size("dp"))
    ]


def small_kernel(mod_ref, mod_out, sum_out, part, sends, gets, own):
    me = lax.axis_index("dp")
    steps = (
        to_all(lambda peer: mod_ref.at[peer], mod_out.at[me], sends.at[0], gets.at[0])
        + [pltpu.make_async_copy(mod_ref.at[me], mod_out.at[me], own.at[0])],
        to_all(lambda peer: part, sum_out.at[me], sends.at[1], gets.at[1])
        + [pltpu.make_async_copy(part, sum_out.at[me], own.at[1])],
    )
    for i, copies in enumerate(steps):
        if i == 1:
            part[...] = jnp.sum(mod_out[...], axis=0)
        for copy in copies:
            copy.start()
        for copy in copies:
            copy.wait()


def small_exchange(mods):
    vmem = pl.BlockSpec(memory_space=pltpu.VMEM)
    count = mods.shape[0]
    return pl.pallas_call(
        small_kernel,
        in_specs=[vmem],
        out_specs=[vmem] * 2,
        out_shape=[jax.ShapeDtypeStruct(mods.shape, mods.dtype)] * 2,
        scratch_shapes=[
            pltpu.VMEM(mods.shape[1:], mods.dtype),
            pltpu.SemaphoreType.DMA((2, count)), pltpu.SemaphoreType.DMA((2, count)),
            pltpu.SemaphoreType.DMA((2,)),
        ],
        compiler_params=pltpu.CompilerParams(has_side_effects=True),
    )(mods)


def settle(chains, value):
    live = [c for c in chains if c.got is not None]
    value, got = lax.optimization_barrier((value, [c.got for c in live]))
    for c, g in zip(live, got):
        c.got = g
    return value


def advance(chains, value):
    value = settle(chains, value)
    for c in chains:
        c.step()
    return value


def rope_block(value, cosine, sine, sign):
    width = value.shape[1]
    lane = lax.broadcasted_iota(jnp.int32, value.shape, 1)
    partner = jnp.where(
        lane % 32 < 16, pltpu.roll(value, width - 16, 1), pltpu.roll(value, 16, 1)
    )
    return value * cosine + sign * (partner * sine)


def column(ref, index, width):
    row = ref[index : index + 1, :] if isinstance(index, int) else ref[pl.ds(index, 1), :]
    return jnp.broadcast_to(row, (width, row.shape[1])).T


def masked(value, head):
    lane = lax.broadcasted_iota(jnp.int32, value.shape, 1)
    return jnp.where(lane // HD == head, value, jnp.zeros_like(value))


def attn_fwd_kernel(
    len_ref, pre_ref, inv_ref, gq_ref, gk_ref, cos_ref, sin_ref, tk_ref, tv_ref, gate_ref,
    q_ref, k_ref, v_ref, mixed_ref, so_ref, co_ref, ls_ref, lc_ref,
):
    _, tokens, width = pre_ref.shape
    heads = width // HD
    iq, ik = column(inv_ref, 0, width), column(inv_ref, 1, width)
    q = rope_block(pre_ref[0] * iq * gq_ref[...], cos_ref[...], sin_ref[...], 1.0)
    q_ref[...] = q.astype(BF16)
    k = rope_block(pre_ref[1] * ik * gk_ref[...], cos_ref[...], sin_ref[...], 1.0)
    k_ref[...] = k.astype(BF16)
    v_ref[...] = pre_ref[2].astype(BF16)
    length = len_ref[0]

    def one(keys, values, qm, limit):
        s = dot(qm, keys, 1, 1)
        if limit is not None:
            slot = lax.broadcasted_iota(jnp.int32, s.shape, 1)
            s = jnp.where(slot < limit, s, -1e30)
        peak = jnp.max(s, axis=1, keepdims=True)
        e = jnp.exp(s - peak)
        total = jnp.sum(e, axis=1, keepdims=True)
        o = dot(e.astype(BF16), values)
        return o * (1.0 / total), peak + jnp.log(total)

    lane = lax.broadcasted_iota(jnp.int32, (tokens, width), 1)
    qs = q_ref[...] * jnp.asarray(HD**-0.5, BF16)
    so = co = stats = jnp.zeros((tokens, width), F32)
    for h in range(heads):
        qm = masked(qs, h)
        o, lse = one(k_ref[...], v_ref[...], qm, None)
        so = jnp.where(lane // HD == h, o, so)
        stats = jnp.where(lane == h, lse, stats)
        o, lse = one(tk_ref[...], tv_ref[...], qm, length)
        co = jnp.where(lane // HD == h, o, co)
        stats = jnp.where(lane == heads + h, lse, stats)
    so_ref[...] = so
    co_ref[...] = co
    mixed_ref[...] = (so + gate_ref[...] * co).astype(BF16)
    stats = stats.T
    ls_ref[0] = stats[:heads]
    lc_ref[0] = stats[heads : 2 * heads]


def attn_bwd_kernel(
    len_ref, q_ref, k_ref, v_ref, tk_ref, tv_ref, g_ref, so_ref, co_ref, ls_ref, lc_ref,
    pre_ref, inv_ref, gq_ref, gk_ref, cos_ref, sin_ref, gate_ref,
    d_ref, dtk_ref, dtv_ref, stat_ref, gainq_ref, gaink_ref, gateg_ref,
    gs_ref, gc_ref, ds_ref, dc_ref, kt_ref, tkt_ref, dqt_ref, dk_acc, dv_acc, rq_ref, rk_ref,
):
    tokens, width = q_ref.shape
    heads = width // HD
    scale = jnp.asarray(HD**-0.5, BF16)

    @pl.when(pl.program_id(0) == 0)
    def _():
        rq_ref[...] = jnp.zeros_like(rq_ref)
        rk_ref[...] = jnp.zeros_like(rk_ref)

    g = g_ref[...]
    gs_ref[...] = g.astype(BF16)
    gc_ref[...] = (g * gate_ref[...]).astype(BF16)
    prod_c = g * co_ref[...]
    gateg_ref[...] = jnp.sum(prod_c, axis=0, keepdims=True)
    prod_s = (g * so_ref[...]).T
    prod_c = (prod_c * gate_ref[...]).T
    for h in range(heads):
        ds_ref[h : h + 1, :] = jnp.sum(prod_s[h * HD : (h + 1) * HD], axis=0, keepdims=True)
        dc_ref[h : h + 1, :] = jnp.sum(prod_c[h * HD : (h + 1) * HD], axis=0, keepdims=True)
    kt_ref[...] = k_ref[...].astype(F32).T.astype(BF16)
    tkt_ref[...] = tk_ref[...].astype(F32).T.astype(BF16)
    dk_acc[...] = jnp.zeros_like(dk_acc)
    dv_acc[...] = jnp.zeros_like(dv_acc)
    dtk_ref[...] = jnp.zeros_like(dtk_ref)
    dtv_ref[...] = jnp.zeros_like(dtv_ref)
    length = len_ref[0]

    def one(keys, keys_t, values, qm, gm, lse, delta, head, limit):
        s = dot(keys, qm, 1, 1)
        p = jnp.exp(s - lse)
        if limit is not None:
            slot = lax.broadcasted_iota(jnp.int32, s.shape, 0)
            p = jnp.where(slot < limit, p, 0.0)
        dp = dot(values, gm, 1, 1)
        ds = (p * (dp - delta)).astype(BF16)
        dq = dot(keys_t[head * HD : (head + 1) * HD, :], ds)
        return dq, dot(ds, qm), dot(p.astype(BF16), gm)

    def chunk(c, carry):
        rows = pl.ds(pl.multiple_of(c * QC, QC), QC)
        qc = q_ref[rows, :] * scale
        for h in range(heads):
            qm = masked(qc, h)
            dq, dk, dv = one(
                k_ref[...], kt_ref, v_ref[...], qm, masked(gs_ref[rows, :], h),
                ls_ref[0, h : h + 1, rows], ds_ref[h : h + 1, rows], h, None,
            )
            dk_acc[...] += dk
            dv_acc[...] += dv
            dq2, dk, dv = one(
                tk_ref[...], tkt_ref, tv_ref[...], qm, masked(gc_ref[rows, :], h),
                lc_ref[0, h : h + 1, rows], dc_ref[h : h + 1, rows], h, length,
            )
            dtk_ref[...] += dk
            dtv_ref[...] += dv
            dqt_ref[h * HD : (h + 1) * HD, rows] = (dq + dq2) * HD**-0.5
        return carry

    lax.fori_loop(0, tokens // QC, chunk, 0)
    dq = rope_block(dqt_ref[...].T, cos_ref[...], sin_ref[...], -1.0)
    d_ref[0] = dq
    prod = dq * (pre_ref[0] * column(inv_ref, 0, width))
    gainq_ref[...] = jnp.sum(prod, axis=0, keepdims=True)
    rq_ref[...] += prod * gq_ref[...]
    dk = rope_block(dk_acc[...], cos_ref[...], sin_ref[...], -1.0)
    d_ref[1] = dk
    prod = dk * (pre_ref[1] * column(inv_ref, 1, width))
    gaink_ref[...] = jnp.sum(prod, axis=0, keepdims=True)
    rk_ref[...] += prod * gk_ref[...]
    d_ref[2] = dv_acc[...]

    @pl.when(pl.program_id(0) == pl.num_programs(0) - 1)
    def _():
        stat_ref[...] = jnp.zeros_like(stat_ref)
        for i, ref in enumerate((rq_ref, rk_ref)):
            stat_ref[i : i + 1, :] = jnp.sum(ref[...].T, axis=0, keepdims=True)


def specs(tokens, text, width, heads, at=0):
    col = pl.BlockSpec((tokens, width), lambda i: (0, i + at))
    three = pl.BlockSpec((3, tokens, width), lambda i: (0, 0, i + at))
    tcol = pl.BlockSpec((text, width), lambda i: (0, i + at))
    stat = pl.BlockSpec((8, tokens), lambda i: (0, 0))
    gain = pl.BlockSpec((1, width), lambda i: (0, i + at))
    table = pl.BlockSpec((tokens, width), lambda i: (0, 0))
    lse = pl.BlockSpec((1, heads, tokens), lambda i: (i + at, 0, 0))
    scalar = pl.BlockSpec(memory_space=pltpu.SMEM)
    return col, three, tcol, stat, gain, table, lse, scalar


def sds(shape, dtype=F32):
    return jax.ShapeDtypeStruct(shape, dtype)


def attn_forward(length, pre, inv, gq, gk, cosine, sine, tk, tv, gate):
    _, tokens, columns = pre.shape
    text, width = tk.shape[0], cosine.shape[1]
    heads, blocks = width // HD, columns // width
    col, three, tcol, stat, gain, table, lse, scalar = specs(tokens, text, width, heads)
    flat = (tokens, columns)
    return pl.pallas_call(
        attn_fwd_kernel,
        grid=(blocks,),
        in_specs=[scalar, three, stat, gain, gain, table, table, tcol, tcol, gain],
        out_specs=[col, col, col, col, col, col, lse, lse],
        out_shape=[sds(flat, BF16)] * 4 + [sds(flat)] * 2 + [sds((blocks, heads, tokens))] * 2,
    )(length, pre, inv, gq, gk, cosine, sine, tk, tv, gate)


def attn_backward(at, blocks, length, q, k, v, tk, tv, g, so, co, ls, lc, pre, inv, gq, gk, cosine, sine, gate):
    tokens = q.shape[0]
    text, width = tk.shape[0], cosine.shape[1]
    heads, columns = width // HD, blocks * width
    col, three, tcol, stat, gain, table, lse, scalar = specs(tokens, text, width, heads, at)
    _, three_o, tcol_o, _, gain_o, _, _, _ = specs(tokens, text, width, heads)
    return pl.pallas_call(
        attn_bwd_kernel,
        grid=(blocks,),
        in_specs=[scalar, col, col, col, tcol, tcol, col, col, col, lse, lse,
                  three, stat, gain, gain, table, table, gain],
        out_specs=[three_o, tcol_o, tcol_o, stat, gain_o, gain_o, gain_o],
        out_shape=[
            sds((3, tokens, columns)), sds((text, columns)), sds((text, columns)),
            sds((8, tokens)), sds((1, columns)), sds((1, columns)), sds((1, columns)),
        ],
        scratch_shapes=[
            pltpu.VMEM((tokens, width), BF16), pltpu.VMEM((tokens, width), BF16),
            pltpu.VMEM((heads, tokens), F32), pltpu.VMEM((heads, tokens), F32),
            pltpu.VMEM((width, tokens), BF16), pltpu.VMEM((width, text), BF16),
            pltpu.VMEM((width, tokens), F32),
            pltpu.VMEM((tokens, width), F32), pltpu.VMEM((tokens, width), F32),
            pltpu.VMEM((tokens, width), F32), pltpu.VMEM((tokens, width), F32),
        ],
    )(length, q, k, v, tk, tv, g, so, co, ls, lc, pre, inv, gq, gk, cosine, sine, gate)


def pick(rows, cols, step, part):
    i = lax.broadcasted_iota(jnp.int32, (rows, cols), 0)
    j = lax.broadcasted_iota(jnp.int32, (rows, cols), 1)
    hit = (j == step * i + part) if cols > rows else (i == step * j + part)
    return jnp.where(hit, 1.0, 0.0).astype(BF16)

def text_fwd_kernel(x_ref, w_ref, o_ref):
    @pl.when(pl.program_id(0) == 0)
    def _():
        o_ref[...] = jnp.zeros_like(o_ref)
    for b in range(w_ref.shape[0] // 128):
        rows = slice(b * 128, (b + 1) * 128)
        w = w_ref[rows].reshape(256, w_ref.shape[2])
        x = x_ref[:, rows]
        for j in range(2):
            spread = dot(x, pick(128, 256, 2, j)).astype(BF16)
            o_ref[j] += dot(spread, w)

def text_fwd(x, w):
    depth, _, cols = w.shape
    bk = 256
    return pl.pallas_call(
        text_fwd_kernel, grid=(depth // bk,),
        in_specs=[pl.BlockSpec((x.shape[0], bk), lambda i: (0, i)), pl.BlockSpec((bk, 2, cols), lambda i: (i, 0, 0))],
        out_specs=pl.BlockSpec((2, x.shape[0], cols), lambda i: (0, 0, 0)),
        out_shape=sds((2, x.shape[0], cols)),
    )(x, w)

def text_bwd_kernel(g_ref, w_ref, pair_ref, o_ref, pair_out, sends, gets, own):
    me = lax.axis_index("dp")
    step = pl.program_id(0)
    copies = to_all(lambda peer: pair_ref.at[peer], pair_out.at[me], sends, gets)
    copies.append(pltpu.make_async_copy(pair_ref.at[me], pair_out.at[me], own))

    @pl.when(step == 0)
    def _():
        for copy in copies:
            copy.start()

    for b in range(w_ref.shape[0] // 128):
        rows = slice(b * 128, (b + 1) * 128)
        w = w_ref[rows].reshape(256, w_ref.shape[2])
        total = 0.0
        for j in range(2):
            total = total + dot(g_ref[j], dot(pick(128, 256, 2, j), w).astype(BF16), 1, 1)
        o_ref[:, rows] = total.astype(BF16)

    @pl.when(step == pl.num_programs(0) - 1)
    def _():
        for copy in copies:
            copy.wait()


def text_bwd(g, w, pair):
    depth, _, cols = w.shape
    bk = 256
    count = pair.shape[0]
    return pl.pallas_call(
        text_bwd_kernel,
        grid=(depth // bk,),
        in_specs=[
            pl.BlockSpec(g.shape, lambda i: (0, 0, 0)),
            pl.BlockSpec((bk, 2, cols), lambda i: (i, 0, 0)),
            pl.BlockSpec(memory_space=pl.ANY),
        ],
        out_specs=[
            pl.BlockSpec((g.shape[1], bk), lambda i: (0, i)), pl.BlockSpec(memory_space=pl.ANY),
        ],
        out_shape=[
            sds((g.shape[1], depth), BF16), jax.ShapeDtypeStruct(pair.shape, pair.dtype),
        ],
        scratch_shapes=[
            pltpu.SemaphoreType.DMA((count,)), pltpu.SemaphoreType.DMA((count,)),
            pltpu.SemaphoreType.DMA,
        ],
        compiler_params=pltpu.CompilerParams(has_side_effects=True),
    )(g, w, pair)


def put_relative(dst, src, me, f, count):
    rows = dst.shape[0] // count
    for p in range(count):
        start = pl.multiple_of((me ^ turned(p, f)) * rows, 16)
        dst[p * rows : (p + 1) * rows, :] = src[pl.ds(start, rows), :]


def put_halves(keep, send, value, count, order, slot=None):
    rows = value.shape[0] // count
    for p in range(count):
        place = place_of(p, order[1:])
        where = place if slot is None else (place, slot)
        (send if p >> order[0] & 1 else keep)[where] = value[p * rows : (p + 1) * rows]


def ffn_kernel(
    orders, id_ref, s_ref, b_ref, w_ref, d_ref,
    wk_ref, ws_ref, dk_ref, ds_ref, fo_ref, fp_ref, so_ref, sp_ref,
    st, bt, tmp, wg, wu, facc, sacc,
):
    step = pl.program_id(0)
    depth, _, cols = w_ref.shape
    own = fo_ref.shape[0]
    count = 2 * dk_ref.shape[0]

    @pl.when(step == 0)
    def _():
        for src, dst in ((s_ref, st), (b_ref, bt)):
            for c in range(depth // 256):
                part = slice(c * 256, (c + 1) * 256)
                tmp[part, :] = src[:, part].astype(F32).T.astype(BF16)
            put_relative(dst, tmp, id_ref[0], id_ref[1], count)
        facc[...] = jnp.zeros_like(facc)
        sacc[...] = jnp.zeros_like(sacc)

    for c in range(depth // 128):
        part = slice(c * 128, (c + 1) * 128)
        w = w_ref[part].reshape(256, cols)
        wg[part, :] = dot(pick(128, 256, 2, 0), w).astype(BF16)
        wu[part, :] = dot(pick(128, 256, 2, 1), w).astype(BF16)
    s, b = s_ref[...], b_ref[...]
    gate = dot(s, wg[...])
    up = dot(s, wu[...])
    back = dot(b, d_ref[...], 1, 1)
    sig = jax.nn.sigmoid(gate)
    silu = gate * sig
    hidden = (silu * up).astype(BF16)
    g_gate = (back * up * (sig + silu * (1.0 - sig))).astype(BF16)
    g_up = (back * silu).astype(BF16)
    put_halves(wk_ref, ws_ref, dot(st[...], g_gate).astype(BF16), count, orders[0], 0)
    put_halves(wk_ref, ws_ref, dot(st[...], g_up).astype(BF16), count, orders[0], 1)
    put_halves(dk_ref, ds_ref, dot(bt[...], hidden).astype(BF16), count, orders[1])
    facc[...] += dot(hidden, d_ref[...])
    sacc[...] += dot(g_gate, wg[...], 1, 1) + dot(g_up, wu[...], 1, 1)

    @pl.when(step == pl.num_programs(0) - 1)
    def _():
        fo_ref[...] = facc[:own]
        fp_ref[...] = facc[own:].astype(BF16)
        so_ref[...] = sacc[:own]
        sp_ref[...] = sacc[own:].astype(BF16)


def ffn(ids, s, b, w, d, local, dp, orders):
    tokens, depth = s.shape
    hid = d.shape[0]
    bc = min(256, hid)
    rest = tokens - local
    once = functools.partial(pl.BlockSpec, pipeline_mode=pl.Buffered(1))
    const = lambda i: (0, 0)
    share = depth // dp
    half = pl.BlockSpec((dp // 2, share, bc), lambda i: (0, 0, i))
    halves = pl.BlockSpec((dp // 2, 2, share, bc), lambda i: (0, 0, 0, i))
    return pl.pallas_call(
        functools.partial(ffn_kernel, orders),
        grid=(hid // bc,),
        in_specs=[
            pl.BlockSpec(memory_space=pltpu.SMEM),
            once((tokens, depth), const), once((tokens, depth), const),
            pl.BlockSpec((depth, 2, bc), lambda i: (0, 0, i)),
            pl.BlockSpec((bc, depth), lambda i: (i, 0)),
        ],
        out_specs=[halves] * 2 + [half] * 2 + [
            once((local, depth), const), once((rest, depth), const),
            once((local, depth), const), once((rest, depth), const),
        ],
        out_shape=[sds((dp // 2, 2, share, hid), BF16)] * 2 + [sds((dp // 2, share, hid), BF16)] * 2 + [
            sds((local, depth)), sds((rest, depth), BF16),
            sds((local, depth)), sds((rest, depth), BF16),
        ],
        scratch_shapes=[
            pltpu.VMEM((depth, tokens), BF16), pltpu.VMEM((depth, tokens), BF16),
            pltpu.VMEM((depth, tokens), BF16),
            pltpu.VMEM((depth, bc), BF16), pltpu.VMEM((depth, bc), BF16),
            pltpu.VMEM((tokens, depth), F32), pltpu.VMEM((tokens, depth), F32),
        ],
        compiler_params=pltpu.CompilerParams(vmem_limit_bytes=62 << 20),
    )(ids, s, b, w, d)


def project_kernel(id_ref, xo_ref, xp_ref, front_ref, w_ref, got_ref, first_ref, pre_ref, sq_ref):
    j = pl.program_id(0)
    local, depth = xo_ref.shape
    own = got_ref.shape[2]
    f = id_ref[1]

    @pl.when(j == 0)
    def _():
        for i, ref in enumerate((xo_ref, xp_ref)):
            x = ref[...].astype(F32)
            inv = lax.rsqrt(jnp.sum(x * x, axis=1, keepdims=True) * (1.0 / depth) + EPSILON)
            first_ref[i * local : (i + 1) * local, :] = (x * inv * front_ref[...]).astype(BF16)
        sq_ref[...] = jnp.zeros_like(sq_ref)

    mine = pl.ds(pl.multiple_of(f * own, 128), own)
    other = pl.ds(pl.multiple_of((1 - f) * own, 128), own)
    out = dot(first_ref[:, mine], w_ref[0, :, mine]) + dot(first_ref[:, other], got_ref[0])
    pre_ref[0] = out
    square = out * out
    part = square[:, :128]
    for c in range(1, own // 128):
        part = part + square[:, c * 128 : (c + 1) * 128]
    sq_ref[pl.ds(j, 1), :] = jnp.sum(part.T, axis=0, keepdims=True)


def project(ids, xo, xp, front, w, got):
    local, depth = xo.shape
    own = got.shape[2]
    tokens = 2 * local
    const = lambda j: (0, 0)
    return pl.pallas_call(
        project_kernel,
        grid=(3,),
        in_specs=[
            pl.BlockSpec(memory_space=pltpu.SMEM),
            pl.BlockSpec((local, depth), const), pl.BlockSpec((local, depth), const),
            pl.BlockSpec((1, depth), const),
            pl.BlockSpec((1, own, depth), lambda j: (j, 0, 0)),
            pl.BlockSpec((1, own, own), lambda j: (j, 0, 0)),
        ],
        out_specs=[
            pl.BlockSpec((tokens, depth), const),
            pl.BlockSpec((1, tokens, own), lambda j: (j, 0, 0)),
            pl.BlockSpec((8, tokens), const),
        ],
        out_shape=[sds((tokens, depth), BF16), sds((3, tokens, own)), sds((8, tokens))],
    )(ids, xo, xp, front, w, got)


def project_grad_kernel(
    order, id_ref, da_ref, db_ref, pre_ref, stat_ref, gain_ref, first_ref,
    keep_ref, send_ref, g_ref, gt, tmp,
):
    j = pl.program_id(0)
    own = pre_ref.shape[2]
    cut = da_ref.shape[2]
    count = 2 * keep_ref.shape[0]
    inv, mean = column(stat_ref, j, 128), column(stat_ref, j + 3, 128)
    for c in range(own // 128):
        part = slice(c * 128, (c + 1) * 128)
        here = slice(c * 128 - cut, (c + 1) * 128 - cut) if c * 128 >= cut else part
        d = (db_ref if c * 128 >= cut else da_ref)[0, :, here]
        g = inv * (d * gain_ref[0, :, part] - pre_ref[0, :, part] * inv * mean)
        tmp[part, :] = g.T.astype(BF16)
        g_ref[0, :, part] = g.astype(BF16)
    put_relative(gt, tmp, id_ref[0] % count, id_ref[1], count)
    put_halves(keep_ref, send_ref, dot(gt[...], first_ref[...]).astype(BF16), count, order, j)


def project_grad(ids, da, db, pre, stats, gain, first, dp, order):
    _, tokens, own = pre.shape
    depth = first.shape[1]
    share = depth // dp
    const = lambda j: (0, 0)
    block = lambda j: (j, 0, 0)
    once = functools.partial(pl.BlockSpec, pipeline_mode=pl.Buffered(1))
    half = once((dp // 4, 3, share, depth), lambda j: (0, 0, 0, 0))
    return pl.pallas_call(
        functools.partial(project_grad_kernel, order),
        grid=(3,),
        in_specs=[
            pl.BlockSpec(memory_space=pltpu.SMEM),
            pl.BlockSpec((1,) + da.shape[1:], block), pl.BlockSpec((1,) + db.shape[1:], block),
            pl.BlockSpec((1, tokens, own), block),
            pl.BlockSpec((8, tokens), const),
            pl.BlockSpec((1, 1, own), block),
            once((tokens, depth), const),
        ],
        out_specs=[half, half, pl.BlockSpec((1, tokens, own), block)],
        out_shape=[sds((dp // 4, 3, share, depth), BF16)] * 2
        + [sds((3, tokens, own), BF16)],
        scratch_shapes=[pltpu.VMEM((own, tokens), BF16), pltpu.VMEM((own, tokens), BF16)],
    )(ids, da, db, pre, stats, gain, first)


def project_back_kernel(id_ref, g_ref, w_ref, got_ref, own_ref, peer_ref, acc):
    j = pl.program_id(0)
    own = g_ref.shape[2]
    local = own_ref.shape[0]
    f = id_ref[1]
    mine = pl.ds(pl.multiple_of(f * own, 128), own)
    other = pl.ds(pl.multiple_of((1 - f) * own, 128), own)

    @pl.when(j == 0)
    def _():
        acc[...] = jnp.zeros_like(acc)

    acc[:, mine] += dot(g_ref[0], w_ref[0, :, mine], 1, 1)
    acc[:, other] += dot(g_ref[0], got_ref[0], 1, 1)

    @pl.when(j == 2)
    def _():
        own_ref[...] = acc[:local]
        peer_ref[...] = acc[local:].astype(BF16)


def project_back(ids, g, w, got):
    _, tokens, own = g.shape
    depth = w.shape[2]
    local = tokens // 2
    const = lambda j: (0, 0)
    block = lambda j: (j, 0, 0)
    once = functools.partial(pl.BlockSpec, pipeline_mode=pl.Buffered(1))
    return pl.pallas_call(
        project_back_kernel,
        grid=(3,),
        in_specs=[
            pl.BlockSpec(memory_space=pltpu.SMEM),
            pl.BlockSpec((1, tokens, own), block),
            pl.BlockSpec((1, own, depth), block), pl.BlockSpec((1, own, own), block),
        ],
        out_specs=[once((local, depth), const), once((local, depth), const)],
        out_shape=[sds((local, depth)), sds((local, depth), BF16)],
        scratch_shapes=[pltpu.VMEM((tokens, depth), F32)],
    )(ids, g, w, got)


def out_back_kernel(order, id_ref, *refs):
    n = len(refs) - 8
    blocks, (w_ref, mixed_ref, g_ref, keep_ref, send_ref, all_ref, gt, tmp) = refs[:n], refs[n:]
    local = blocks[0].shape[0]
    for r, ref in enumerate(blocks):
        all_ref[r * local : (r + 1) * local, :] = ref[...]
    grad = all_ref[...]
    g_ref[...] = dot(grad, w_ref[...], 1, 1)
    for c in range(grad.shape[1] // 256):
        part = slice(c * 256, (c + 1) * 256)
        tmp[part, :] = grad[:, part].astype(F32).T.astype(BF16)
    count = 2 * keep_ref.shape[0]
    put_relative(gt, tmp, id_ref[0], id_ref[1], count)
    put_halves(keep_ref, send_ref, dot(gt[...], mixed_ref[...]).astype(BF16), count, order)


def out_back(ids, blocks, w, mixed, dp, order):
    tokens, own = mixed.shape
    depth = w.shape[1]
    vmem = pl.BlockSpec(memory_space=pltpu.VMEM)
    half = sds((dp // 2, depth // dp, own), BF16)
    return pl.pallas_call(
        functools.partial(out_back_kernel, order),
        in_specs=[pl.BlockSpec(memory_space=pltpu.SMEM)] + [vmem] * (len(blocks) + 2),
        out_specs=[vmem] * 3,
        out_shape=[sds((tokens, own)), half, half],
        scratch_shapes=[
            pltpu.VMEM((tokens, depth), BF16),
            pltpu.VMEM((depth, tokens), BF16), pltpu.VMEM((depth, tokens), BF16),
        ],
    )(ids, *blocks, w, mixed)


def time_embed(timesteps):
    half = TE // 2
    frequencies = jnp.exp(-math.log(10000.0) * jnp.arange(half, dtype=F32) / half)
    angles = timesteps.astype(F32)[:, None] * frequencies
    waves = jnp.concatenate([jnp.cos(angles), jnp.sin(angles)], axis=-1)
    return jax.nn.silu(waves).astype(BF16)


def rope_tables(positions, width):
    lane = jnp.arange(width)
    quarter = HD // 4
    frequencies = 10000.0 ** (-(lane % quarter).astype(F32) / quarter)
    place = jnp.where(lane % HD < HD // 2, positions[0][:, None], positions[1][:, None])
    angles = place.astype(F32) * frequencies
    return jnp.cos(angles), jnp.where(lane % 32 < 16, -1.0, 1.0) * jnp.sin(angles)


def inverse_rms(values):
    return lax.rsqrt(jnp.mean(values * values, axis=-1, keepdims=True) + EPSILON)


def rms_back(grad_hat, normed, inverse):
    return inverse * (grad_hat - normed * jnp.mean(grad_hat * normed, axis=-1, keepdims=True))


def pad_cols(value, width):
    extra = -value.shape[-1] % width
    return value if extra == 0 else jnp.pad(value, [(0, 0)] * (value.ndim - 1) + [(0, extra)])


def on_device(
    hidden_in, text_state, caption_lengths, timesteps, patch_positions, cotangent,
    w_ada, w_text, w_qkv, w_out, gains, cross_gate, w_gate_up, w_down,
):
    n, f = lax.axis_size("fsdp"), lax.axis_index("fsdp")
    dpn, me = lax.axis_size("dp"), lax.axis_index("dp")
    bits = list(range(dp_bits()))
    low_bits = bits[:-1]
    late = bits[2:3] + bits[:2] + bits[3:]
    own_d = D // n
    local = hidden_in.shape[1]
    tokens = n * local
    width = 2 * HD
    share = D // dpn
    paired = n == 2 and dpn >= 4
    ids = jnp.stack([me, f]).astype(jnp.int32)
    x_bf, dy_bf = hidden_in[0], cotangent[0]

    time_low = time_embed(timesteps)
    own_te = TE // n
    time_own = lax.dynamic_slice_in_dim(time_low[0], f * own_te, own_te, 0)
    modulation = pair_sum(
        jnp.einsum("k,kjd->jd", time_own, w_ada, preferred_element_type=F32)
    )
    scale_attn, gate_attn = modulation[0:1], jnp.tanh(modulation[1:2])
    scale_ffn, gate_ffn = modulation[2:3], jnp.tanh(modulation[3:4])

    w_flat = jnp.moveaxis(w_qkv, 1, 0)
    w_parts = exchange_rot(w_flat, 2)
    x_parts = gather_rot(x_bf)
    dy_all = jnp.concatenate(gather_rot(dy_bf), axis=0)
    places = jnp.concatenate(gather_rot(patch_positions[0]), axis=1)
    text_cols = jnp.concatenate(natural(exchange_rot(text_state[0], 1)), axis=0)
    text_all = lax.all_gather(text_cols, "dp", axis=0, tiled=True)
    gain_full = lax.all_gather(gains, "fsdp", axis=1, tiled=True).astype(F32)
    gain_own = gains.astype(F32)

    front = gain_full[0] * (1.0 + scale_attn)
    if paired:
        first_all, pre, squares = project(ids, *x_parts, front, w_flat, w_parts[1])
    else:
        w_heads = jnp.concatenate(natural(w_parts), axis=1)
        x_f = jnp.concatenate(x_parts, axis=0).astype(F32)
        first_all = (x_f * inverse_rms(x_f) * front).astype(BF16)
        pre = jnp.stack([dot(first_all, w_heads[j]) for j in range(3)])
        squares = jnp.pad(jnp.sum(pre[:2] * pre[:2], -1), ((0, 6), (0, 0)))
    inverse = lax.rsqrt(row_sum(squares) / D + EPSILON)

    text_part = text_fwd(text_cols, w_text)
    text_pre = scatter_rot(rot_blocks(text_part, 2))
    inv_t = lax.rsqrt(
        pair_sum(jnp.sum(text_pre[0] * text_pre[0], -1, keepdims=True)) / D + EPSILON
    )
    normed_t = text_pre[0] * inv_t
    tk = (normed_t * gain_own[4]).astype(BF16)
    tv = text_pre[1].astype(BF16)

    head_tanh = jnp.tanh(cross_gate.astype(F32))
    gate_row = pad_cols(jnp.repeat(head_tanh, HD)[None], width)
    cosine, sine = rope_tables(places, width)
    gq, gk = pad_cols(gain_own[2:3], width), pad_cols(gain_own[3:4], width)
    pre_p, tkp, tvp = pad_cols(pre, width), pad_cols(tk, width), pad_cols(tv, width)
    q, k, v, mixed_p, so, co, ls, lc = attn_forward(
        caption_lengths, pre_p, inverse, gq, gk, cosine, sine, tkp, tvp, gate_row
    )
    mixed = mixed_p[:, :own_d]

    def rows(value, r):
        return value[r * local : (r + 1) * local]

    parts = [dot(rows(mixed, r), w_out) for r in range(n)]
    attn_branch = scatter_rot([parts[0]] + [p.astype(BF16) for p in parts[1:]])
    x_own = x_bf.astype(F32)
    after_attn = x_own + gate_attn * attn_branch
    inverse_two = inverse_rms(after_attn)
    normed_two = after_attn * inverse_two
    second = (normed_two * gain_full[1] * (1.0 + scale_ffn)).astype(BF16)

    second_all = jnp.concatenate(gather_rot(second), axis=0)
    branch_all = (gate_ffn * dy_all.astype(F32)).astype(BF16)
    wide_keep, wide_send, down_keep, down_send, ffn_own, ffn_rest, back_own, back_rest = ffn(
        ids, second_all, branch_all, w_gate_up, w_down, local, dpn, (bits, late)
    )
    (ffn_own, ffn_rest, back_own, back_rest), text_all = lax.optimization_barrier(
        ((ffn_own, ffn_rest, back_own, back_rest), text_all)
    )
    wide_chain = Halving(bits, wide_keep, wide_send)
    down_chain = Halving(late, down_keep, down_send)
    grad_second = scatter_rot([back_own] + [rows(back_rest, r) for r in range(n - 1)])
    ffn_branch = scatter_rot([ffn_own] + [rows(ffn_rest, r) for r in range(n - 1)])
    output = (after_attn + gate_ffn * ffn_branch).astype(BF16)
    dy = dy_bf.astype(F32)
    d_gate_ffn = jnp.sum(dy * ffn_branch, axis=0) * (1.0 - gate_ffn[0] * gate_ffn[0])

    scaled = grad_second * normed_two
    d_scale_ffn = jnp.sum(scaled * gain_full[1], axis=0)
    gain_two = jnp.sum(scaled * (1.0 + scale_ffn), axis=0)
    grad_after = dy + rms_back(
        grad_second * gain_full[1] * (1.0 + scale_ffn), normed_two, inverse_two
    )
    d_gate_attn = jnp.sum(grad_after * attn_branch, axis=0) * (1.0 - gate_attn[0] * gate_attn[0])
    grad_attn = (gate_attn * grad_after).astype(BF16)
    grad_mixed, *out_halves = out_back(ids, gather_rot(grad_attn), w_out, mixed, dpn, bits)
    out_chain = Halving(bits, *out_halves)
    blocks = pre_p.shape[2] // width
    cut = max(1, 2 * blocks // 3)
    grad_mixed = pad_cols(grad_mixed, width)
    inputs = (so, co, ls, lc, pre_p, inverse, gq, gk, cosine, sine, gate_row)
    part_a = attn_backward(0, cut, caption_lengths, q, k, v, tkp, tvp, grad_mixed, *inputs)
    part_a, grad_mixed = lax.optimization_barrier((part_a, grad_mixed))
    grad_mixed = advance([wide_chain, down_chain], grad_mixed)
    part_b = attn_backward(
        cut, blocks - cut, caption_lengths, q, k, v, tkp, tvp, grad_mixed, *inputs
    )
    means = row_sum(part_a[3] + part_b[3])[:2] / D

    ones, zeros = jnp.ones((1, tokens), F32), jnp.zeros((1, tokens), F32)
    if paired:
        stats = jnp.concatenate([inverse[:2], ones, means, zeros, zeros, zeros], axis=0)
        gain3 = jnp.stack([gain_own[2:3], gain_own[3:4], jnp.ones_like(gain_own[2:3])])
        keep, send, grads = project_grad(
            ids, part_a[0], part_b[0], pre, stats, gain3, first_all, dpn, low_bits
        )
        part_a, part_b, grads = advance(
            [wide_chain, down_chain, out_chain], (part_a[1:], part_b[1:], grads)
        )
        qkv_chain = Halving(low_bits, keep, send)
        parts = project_back(ids, grads, w_flat, w_parts[1])
    else:
        d = jnp.concatenate([part_a[0], part_b[0]], axis=2)[:, :, :own_d]
        part_a, part_b = part_a[1:], part_b[1:]
        inv, mean = inverse[:2, :, None], means[:, :, None]
        hat = d[:2] * gain_own[2:4][:, None] - pre[:2] * inv * mean
        grads = [(inv[0] * hat[0]).astype(BF16), (inv[1] * hat[1]).astype(BF16), d[2].astype(BF16)]
        wide = [dot(g, first_all, 0, 0).astype(BF16) for g in grads]
        wide = [jnp.concatenate(natural(exchange_rot(w_, 1)), axis=0) for w_ in wide]
        wide = relative(jnp.stack([w_.reshape(dpn, share, own_d) for w_ in wide], axis=1))
        wide = jnp.stack([wide[p] for p in sorted(range(dpn), key=lambda p: place_of(p, bits))])
        qkv_chain = Halving(bits, wide[: dpn // 2], wide[dpn // 2 :])
        parts = [
            sum(dot(rows(g, r), w_heads[j], 1, 1) for j, g in enumerate(grads)) for r in range(n)
        ]
        parts = [parts[0]] + [p.astype(BF16) for p in parts[1:]]
    grad_first = scatter_rot(parts)

    dtk, dtv, gain_q, gain_k, gate_g = (
        jnp.concatenate([part_a[i], part_b[i]], axis=1)[:, :own_d] for i in (0, 1, 3, 4, 5)
    )
    text_hat = dtk * gain_own[4]
    gain_text = jnp.sum(dtk * normed_t, axis=0, keepdims=True)
    mean_t = pair_sum(jnp.sum(text_hat * normed_t, -1, keepdims=True)) / D
    grad_tk = (inv_t * (text_hat - normed_t * mean_t)).astype(BF16)
    text_pair = jnp.stack([grad_tk, dtv.astype(BF16)])
    pair_all = jnp.concatenate(natural(gather_rot(text_pair)), axis=-1)
    pair_all = advance([qkv_chain, wide_chain, down_chain, out_chain], pair_all)
    outgoing = block_of(pair_all.transpose(0, 2, 1), f, 2)
    outgoing = outgoing.reshape(2, dpn, share, TEXT // n).transpose(1, 0, 2, 3)
    text_in, pair_cols = text_bwd(pair_all, w_text, outgoing)
    text_in, grad_first = advance([qkv_chain], (text_in, grad_first))
    pair_cols, qkv_chain.keep = lax.optimization_barrier((pair_cols, qkv_chain.keep))
    text_in = jnp.concatenate(natural(exchange_rot(text_in, 0)), axis=1)

    inverse_one = inverse_rms(x_own)
    normed_one = x_own * inverse_one
    scaled = grad_first * normed_one
    d_scale_attn = jnp.sum(scaled * gain_full[0], axis=0)
    gain_one = jnp.sum(scaled * (1.0 + scale_attn), axis=0)
    grad_input = (
        grad_after
        + rms_back(grad_first * gain_full[0] * (1.0 + scale_attn), normed_one, inverse_one)
    ).astype(BF16)


    sums = [d_scale_attn, d_gate_attn, d_scale_ffn, d_gate_ffn, gain_one, gain_two]
    sums = pair_sum(jnp.stack(sums))
    stamp = jnp.full((1, D), timesteps[0].astype(F32))
    small = jnp.concatenate([block_of(sums[4:], f, 1), gain_q, gain_k, gain_text, gate_g], axis=0)
    small = jnp.pad(small.reshape(-1), (0, dpn * SUMS * 128 - small.size))
    mods = jnp.concatenate([sums[:4], stamp], axis=0).reshape(5, dpn, share).transpose(1, 0, 2)
    mods = jnp.pad(mods, ((0, 0), (0, 0), (0, -share % 128)))
    mods = jnp.concatenate([mods, small.reshape(dpn, SUMS, 128)], axis=1)
    mods = settle([wide_chain], advance([down_chain, out_chain], mods))
    mods, small = small_exchange(mods)
    chains = [out_chain, down_chain] if paired else [qkv_chain, out_chain, down_chain]
    if paired:
        qkv_got = qkv_chain.got
        (mods, small), qkv_chain.got = lax.optimization_barrier(((mods, small), qkv_got))
        qkv_chain.step()
        own_side = f == (me >> low_bits[-1] + 1)
        mine, got = exchange_rot(qkv_chain.last[0].astype(BF16), 2)
        got, wide_chain.keep = lax.optimization_barrier((got, wide_chain.keep))
        qkv_chain = Halving(
            bits[-1:], jnp.where(own_side, mine, got)[None], jnp.where(own_side, got, mine)[None]
        )
    mods = advance(chains, mods)
    pair_cols = jnp.concatenate(natural(gather_rot(pair_cols)), axis=3)
    pair_cols = pair_cols.transpose(1, 2, 0, 3).reshape(2 * share, dpn * TEXT)
    text_grad = dot(pair_cols, text_all).reshape(2, share, TW // n)
    total = small[:, 5 : 5 + SUMS].reshape(-1)[: 6 * own_d].reshape(6, own_d)
    gate_total = jnp.sum(total[5].reshape(HEADS // n, HD), axis=1) * (
        1.0 - head_tanh * head_tanh
    )
    times = time_embed(mods[:, 4, 0])
    times = lax.dynamic_slice_in_dim(times, f * own_te, own_te, 1).astype(F32)
    ada_grad = lax.dot_general(
        mods[:, :4, :share].reshape(dpn, 4 * share), times, (((0,), (0,)), ((), ())),
        precision=lax.Precision.HIGHEST,
    ).reshape(4, share, own_te)

    for chain in (out_chain, down_chain, wide_chain, qkv_chain):
        while chain.got is not None:
            chain.step()
    return (
        output[None],
        grad_input[None],
        text_in[None],
        ada_grad.transpose(2, 0, 1),
        text_grad.transpose(2, 0, 1),
        qkv_chain.last[0].transpose(2, 0, 1),
        out_chain.last[0].T,
        total[:5],
        gate_total,
        wide_chain.last[0].transpose(1, 0, 2),
        down_chain.last[0].T,
    )


def solution(mesh):
    return jax.shard_map(
        on_device,
        mesh=mesh,
        in_specs=(
            P("dp", "fsdp", None),
            P("dp", "fsdp", None),
            P("dp"),
            P("dp"),
            P("dp", None, "fsdp"),
            P("dp", "fsdp", None),
            P("fsdp", None, None),
            P("fsdp", None, None),
            P("fsdp", None, None),
            P("fsdp", None),
            P(None, "fsdp"),
            P("fsdp"),
            P(None, None, "fsdp"),
            P("fsdp", None),
        ),
        out_specs=(
            P("dp", "fsdp", None),
            P("dp", "fsdp", None),
            P("dp", "fsdp", None),
            P("fsdp", None, "dp"),
            P("fsdp", None, "dp"),
            P("fsdp", None, "dp"),
            P("fsdp", "dp"),
            P(None, "fsdp"),
            P("fsdp"),
            P("dp", None, "fsdp"),
            P("fsdp", "dp"),
        ),
        check_vma=False,
    )
```

```python
import functools
import math

import jax
import jax.numpy as jnp
from jax import lax
from jax.experimental import pallas as pl
from jax.experimental.pallas import tpu as pltpu
from jax.sharding import PartitionSpec as P

D = 1536
HEADS = 24
HD = 64
TW = 4096
TE = 1024
PATCHES = 1024
TEXT = 256
EPSILON = 1e-06
F32 = jnp.float32
BF16 = jnp.bfloat16
QC = 256


def dot(a, b, ca=1, cb=0):
    return lax.dot_general(a, b, (((ca,), (cb,)), ((), ())), preferred_element_type=F32)


def from_behind(value, step):
    n = lax.axis_size("fsdp")
    return lax.ppermute(value, "fsdp", [(i, (i + step) % n) for i in range(n)])


def gather_rot(value):
    return [value] + [from_behind(value, r) for r in range(1, lax.axis_size("fsdp"))]


def pair_sum(value):
    return functools.reduce(lambda a, b: a + b, gather_rot(value))


def row_sum(value):
    n = lax.axis_size("fsdp")
    rows = value.shape[-1] // n
    total = value
    for r in range(1, n):
        total = total + jnp.roll(from_behind(value, r), r * rows, axis=-1)
    return total


def scatter_rot(blocks):
    n = lax.axis_size("fsdp")
    total = blocks[0].astype(F32)
    for r in range(1, n):
        got = lax.ppermute(blocks[r], "fsdp", [(i, (i - r) % n) for i in range(n)])
        total = total + got.astype(F32)
    return total


def block_of(value, index, axis):
    size = value.shape[axis] // lax.axis_size("fsdp")
    return lax.dynamic_slice_in_dim(value, index * size, size, axis)


def rot_blocks(value, axis):
    n, f = lax.axis_size("fsdp"), lax.axis_index("fsdp")
    return [block_of(value, (f - r) % n, axis) for r in range(n)]


def exchange_rot(value, axis):
    n, f = lax.axis_size("fsdp"), lax.axis_index("fsdp")
    out = [block_of(value, f, axis)]
    for r in range(1, n):
        out.append(from_behind(block_of(value, (f + r) % n, axis), r))
    return out


def natural(got):
    n, f = lax.axis_size("fsdp"), lax.axis_index("fsdp")
    if n == 2:
        return [jnp.where(f == 0, got[0], got[1]), jnp.where(f == 0, got[1], got[0])]
    got = jnp.stack(got)
    return [lax.dynamic_index_in_dim(got, (f - g) % n, 0, keepdims=False) for g in range(n)]


def dp_bits():
    return int(lax.axis_size("dp")).bit_length() - 1


def swapped(p):
    return (p & ~3) | ((p & 1) << 1) | ((p >> 1) & 1)


def turned(p, f):
    return p if dp_bits() < 3 else jnp.where(f % 2 == 0, p, swapped(p))


def dp_swap(value, bit):
    n, dpn = lax.axis_size("fsdp"), lax.axis_size("dp")
    pairs = []
    for i in range(dpn):
        for f in range(n):
            flip = 1 << bit if dp_bits() < 3 or f % 2 == 0 else swapped(1 << bit)
            pairs.append((i * n + f, (i ^ flip) * n + f))
    return lax.ppermute(value, ("dp", "fsdp"), pairs)


def relative(value):
    places = turned(jnp.arange(lax.axis_size("dp")), lax.axis_index("fsdp"))
    return jnp.take(value, lax.axis_index("dp") ^ places, axis=0)


class Halving:
    def __init__(self, order, keep, send):
        self.order = list(order)
        self.keep, self.got = keep, dp_swap(send, self.order.pop(0))

    def step(self):
        if self.got is None:
            return

        def add(part):
            return self.keep[part].astype(F32) + self.got[part].astype(F32)

        if not self.order:
            self.last = add(slice(None))
            self.got = None
            return
        half = self.keep.shape[0] // 2
        send = add(slice(half, None)).astype(BF16)
        self.keep = add(slice(half)).astype(BF16)
        self.got = dp_swap(send, self.order.pop(0))


def place_of(p, order):
    return sum((p >> bit & 1) << i for i, bit in enumerate(reversed(order)))


SUMS = 3


def to_all(source, target, sends, gets):
    me = lax.axis_index("dp")
    return [
        pltpu.make_async_remote_copy(
            src_ref=source(me ^ r), dst_ref=target, send_sem=sends.at[r], recv_sem=gets.at[r],
            device_id={"dp": me ^ r}, device_id_type=pl.DeviceIdType.MESH,
        )
        for r in range(1, lax.axis_size("dp"))
    ]


def small_kernel(mod_ref, mod_out, sum_out, part, sends, gets, own):
    me = lax.axis_index("dp")
    steps = (
        to_all(lambda peer: mod_ref.at[peer], mod_out.at[me], sends.at[0], gets.at[0])
        + [pltpu.make_async_copy(mod_ref.at[me], mod_out.at[me], own.at[0])],
        to_all(lambda peer: part, sum_out.at[me], sends.at[1], gets.at[1])
        + [pltpu.make_async_copy(part, sum_out.at[me], own.at[1])],
    )
    for i, copies in enumerate(steps):
        if i == 1:
            part[...] = jnp.sum(mod_out[...], axis=0)
        for copy in copies:
            copy.start()
        for copy in copies:
            copy.wait()


def small_exchange(mods):
    vmem = pl.BlockSpec(memory_space=pltpu.VMEM)
    count = mods.shape[0]
    return pl.pallas_call(
        small_kernel,
        in_specs=[vmem],
        out_specs=[vmem] * 2,
        out_shape=[jax.ShapeDtypeStruct(mods.shape, mods.dtype)] * 2,
        scratch_shapes=[
            pltpu.VMEM(mods.shape[1:], mods.dtype),
            pltpu.SemaphoreType.DMA((2, count)), pltpu.SemaphoreType.DMA((2, count)),
            pltpu.SemaphoreType.DMA((2,)),
        ],
        compiler_params=pltpu.CompilerParams(has_side_effects=True),
    )(mods)


def settle(chains, value):
    live = [c for c in chains if c.got is not None]
    value, got = lax.optimization_barrier((value, [c.got for c in live]))
    for c, g in zip(live, got):
        c.got = g
    return value


def advance(chains, value):
    value = settle(chains, value)
    for c in chains:
        c.step()
    return value


def rope_block(value, cosine, sine, sign):
    width = value.shape[1]
    lane = lax.broadcasted_iota(jnp.int32, value.shape, 1)
    partner = jnp.where(
        lane % 32 < 16, pltpu.roll(value, width - 16, 1), pltpu.roll(value, 16, 1)
    )
    return value * cosine + sign * (partner * sine)


def column(ref, index, width):
    row = ref[index : index + 1, :] if isinstance(index, int) else ref[pl.ds(index, 1), :]
    return jnp.broadcast_to(row, (width, row.shape[1])).T


def masked(value, head):
    lane = lax.broadcasted_iota(jnp.int32, value.shape, 1)
    return jnp.where(lane // HD == head, value, jnp.zeros_like(value))


def attn_fwd_kernel(
    len_ref, pre_ref, inv_ref, gq_ref, gk_ref, cos_ref, sin_ref, tk_ref, tv_ref, gate_ref,
    q_ref, k_ref, v_ref, mixed_ref, so_ref, co_ref, ls_ref, lc_ref,
):
    _, tokens, width = pre_ref.shape
    heads = width // HD
    iq, ik = column(inv_ref, 0, width), column(inv_ref, 1, width)
    q = rope_block(pre_ref[0] * iq * gq_ref[...], cos_ref[...], sin_ref[...], 1.0)
    q_ref[...] = q.astype(BF16)
    k = rope_block(pre_ref[1] * ik * gk_ref[...], cos_ref[...], sin_ref[...], 1.0)
    k_ref[...] = k.astype(BF16)
    v_ref[...] = pre_ref[2].astype(BF16)
    length = len_ref[0]

    def one(keys, values, qm, limit):
        s = dot(qm, keys, 1, 1)
        if limit is not None:
            slot = lax.broadcasted_iota(jnp.int32, s.shape, 1)
            s = jnp.where(slot < limit, s, -1e30)
        peak = jnp.max(s, axis=1, keepdims=True)
        e = jnp.exp(s - peak)
        total = jnp.sum(e, axis=1, keepdims=True)
        o = dot(e.astype(BF16), values)
        return o * (1.0 / total), peak + jnp.log(total)

    lane = lax.broadcasted_iota(jnp.int32, (tokens, width), 1)
    qs = q_ref[...] * jnp.asarray(HD**-0.5, BF16)
    so = co = stats = jnp.zeros((tokens, width), F32)
    for h in range(heads):
        qm = masked(qs, h)
        o, lse = one(k_ref[...], v_ref[...], qm, None)
        so = jnp.where(lane // HD == h, o, so)
        stats = jnp.where(lane == h, lse, stats)
        o, lse = one(tk_ref[...], tv_ref[...], qm, length)
        co = jnp.where(lane // HD == h, o, co)
        stats = jnp.where(lane == heads + h, lse, stats)
    so_ref[...] = so
    co_ref[...] = co
    mixed_ref[...] = (so + gate_ref[...] * co).astype(BF16)
    stats = stats.T
    ls_ref[0] = stats[:heads]
    lc_ref[0] = stats[heads : 2 * heads]


def attn_bwd_kernel(
    len_ref, q_ref, k_ref, v_ref, tk_ref, tv_ref, g_ref, so_ref, co_ref, ls_ref, lc_ref,
    pre_ref, inv_ref, gq_ref, gk_ref, cos_ref, sin_ref, gate_ref,
    d_ref, dtk_ref, dtv_ref, stat_ref, gainq_ref, gaink_ref, gateg_ref,
    gs_ref, gc_ref, ds_ref, dc_ref, kt_ref, tkt_ref, dqt_ref, dk_acc, dv_acc, rq_ref, rk_ref,
):
    tokens, width = q_ref.shape
    heads = width // HD
    scale = jnp.asarray(HD**-0.5, BF16)

    @pl.when(pl.program_id(0) == 0)
    def _():
        rq_ref[...] = jnp.zeros_like(rq_ref)
        rk_ref[...] = jnp.zeros_like(rk_ref)

    g = g_ref[...]
    gs_ref[...] = g.astype(BF16)
    gc_ref[...] = (g * gate_ref[...]).astype(BF16)
    prod_c = g * co_ref[...]
    gateg_ref[...] = jnp.sum(prod_c, axis=0, keepdims=True)
    prod_s = (g * so_ref[...]).T
    prod_c = (prod_c * gate_ref[...]).T
    for h in range(heads):
        ds_ref[h : h + 1, :] = jnp.sum(prod_s[h * HD : (h + 1) * HD], axis=0, keepdims=True)
        dc_ref[h : h + 1, :] = jnp.sum(prod_c[h * HD : (h + 1) * HD], axis=0, keepdims=True)
    kt_ref[...] = k_ref[...].astype(F32).T.astype(BF16)
    tkt_ref[...] = tk_ref[...].astype(F32).T.astype(BF16)
    dk_acc[...] = jnp.zeros_like(dk_acc)
    dv_acc[...] = jnp.zeros_like(dv_acc)
    dtk_ref[...] = jnp.zeros_like(dtk_ref)
    dtv_ref[...] = jnp.zeros_like(dtv_ref)
    length = len_ref[0]

    def one(keys, keys_t, values, qm, gm, lse, delta, head, limit):
        s = dot(keys, qm, 1, 1)
        p = jnp.exp(s - lse)
        if limit is not None:
            slot = lax.broadcasted_iota(jnp.int32, s.shape, 0)
            p = jnp.where(slot < limit, p, 0.0)
        dp = dot(values, gm, 1, 1)
        ds = (p * (dp - delta)).astype(BF16)
        dq = dot(keys_t[head * HD : (head + 1) * HD, :], ds)
        return dq, dot(ds, qm), dot(p.astype(BF16), gm)

    def chunk(c, carry):
        rows = pl.ds(pl.multiple_of(c * QC, QC), QC)
        qc = q_ref[rows, :] * scale
        for h in range(heads):
            qm = masked(qc, h)
            dq, dk, dv = one(
                k_ref[...], kt_ref, v_ref[...], qm, masked(gs_ref[rows, :], h),
                ls_ref[0, h : h + 1, rows], ds_ref[h : h + 1, rows], h, None,
            )
            dk_acc[...] += dk
            dv_acc[...] += dv
            dq2, dk, dv = one(
                tk_ref[...], tkt_ref, tv_ref[...], qm, masked(gc_ref[rows, :], h),
                lc_ref[0, h : h + 1, rows], dc_ref[h : h + 1, rows], h, length,
            )
            dtk_ref[...] += dk
            dtv_ref[...] += dv
            dqt_ref[h * HD : (h + 1) * HD, rows] = (dq + dq2) * HD**-0.5
        return carry

    lax.fori_loop(0, tokens // QC, chunk, 0)
    dq = rope_block(dqt_ref[...].T, cos_ref[...], sin_ref[...], -1.0)
    d_ref[0] = dq
    prod = dq * (pre_ref[0] * column(inv_ref, 0, width))
    gainq_ref[...] = jnp.sum(prod, axis=0, keepdims=True)
    rq_ref[...] += prod * gq_ref[...]
    dk = rope_block(dk_acc[...], cos_ref[...], sin_ref[...], -1.0)
    d_ref[1] = dk
    prod = dk * (pre_ref[1] * column(inv_ref, 1, width))
    gaink_ref[...] = jnp.sum(prod, axis=0, keepdims=True)
    rk_ref[...] += prod * gk_ref[...]
    d_ref[2] = dv_acc[...]

    @pl.when(pl.program_id(0) == pl.num_programs(0) - 1)
    def _():
        stat_ref[...] = jnp.zeros_like(stat_ref)
        for i, ref in enumerate((rq_ref, rk_ref)):
            stat_ref[i : i + 1, :] = jnp.sum(ref[...].T, axis=0, keepdims=True)


def specs(tokens, text, width, heads, at=0):
    col = pl.BlockSpec((tokens, width), lambda i: (0, i + at))
    three = pl.BlockSpec((3, tokens, width), lambda i: (0, 0, i + at))
    tcol = pl.BlockSpec((text, width), lambda i: (0, i + at))
    stat = pl.BlockSpec((8, tokens), lambda i: (0, 0))
    gain = pl.BlockSpec((1, width), lambda i: (0, i + at))
    table = pl.BlockSpec((tokens, width), lambda i: (0, 0))
    lse = pl.BlockSpec((1, heads, tokens), lambda i: (i + at, 0, 0))
    scalar = pl.BlockSpec(memory_space=pltpu.SMEM)
    return col, three, tcol, stat, gain, table, lse, scalar


def sds(shape, dtype=F32):
    return jax.ShapeDtypeStruct(shape, dtype)


def attn_forward(length, pre, inv, gq, gk, cosine, sine, tk, tv, gate):
    _, tokens, columns = pre.shape
    text, width = tk.shape[0], cosine.shape[1]
    heads, blocks = width // HD, columns // width
    col, three, tcol, stat, gain, table, lse, scalar = specs(tokens, text, width, heads)
    flat = (tokens, columns)
    return pl.pallas_call(
        attn_fwd_kernel,
        grid=(blocks,),
        in_specs=[scalar, three, stat, gain, gain, table, table, tcol, tcol, gain],
        out_specs=[col, col, col, col, col, col, lse, lse],
        out_shape=[sds(flat, BF16)] * 4 + [sds(flat)] * 2 + [sds((blocks, heads, tokens))] * 2,
    )(length, pre, inv, gq, gk, cosine, sine, tk, tv, gate)


def attn_backward(at, blocks, length, q, k, v, tk, tv, g, so, co, ls, lc, pre, inv, gq, gk, cosine, sine, gate):
    tokens = q.shape[0]
    text, width = tk.shape[0], cosine.shape[1]
    heads, columns = width // HD, blocks * width
    col, three, tcol, stat, gain, table, lse, scalar = specs(tokens, text, width, heads, at)
    _, three_o, tcol_o, _, gain_o, _, _, _ = specs(tokens, text, width, heads)
    return pl.pallas_call(
        attn_bwd_kernel,
        grid=(blocks,),
        in_specs=[scalar, col, col, col, tcol, tcol, col, col, col, lse, lse,
                  three, stat, gain, gain, table, table, gain],
        out_specs=[three_o, tcol_o, tcol_o, stat, gain_o, gain_o, gain_o],
        out_shape=[
            sds((3, tokens, columns)), sds((text, columns)), sds((text, columns)),
            sds((8, tokens)), sds((1, columns)), sds((1, columns)), sds((1, columns)),
        ],
        scratch_shapes=[
            pltpu.VMEM((tokens, width), BF16), pltpu.VMEM((tokens, width), BF16),
            pltpu.VMEM((heads, tokens), F32), pltpu.VMEM((heads, tokens), F32),
            pltpu.VMEM((width, tokens), BF16), pltpu.VMEM((width, text), BF16),
            pltpu.VMEM((width, tokens), F32),
            pltpu.VMEM((tokens, width), F32), pltpu.VMEM((tokens, width), F32),
            pltpu.VMEM((tokens, width), F32), pltpu.VMEM((tokens, width), F32),
        ],
    )(length, q, k, v, tk, tv, g, so, co, ls, lc, pre, inv, gq, gk, cosine, sine, gate)


def pick(rows, cols, step, part):
    i = lax.broadcasted_iota(jnp.int32, (rows, cols), 0)
    j = lax.broadcasted_iota(jnp.int32, (rows, cols), 1)
    hit = (j == step * i + part) if cols > rows else (i == step * j + part)
    return jnp.where(hit, 1.0, 0.0).astype(BF16)

def text_fwd_kernel(x_ref, w_ref, o_ref):
    @pl.when(pl.program_id(0) == 0)
    def _():
        o_ref[...] = jnp.zeros_like(o_ref)
    for b in range(w_ref.shape[0] // 128):
        rows = slice(b * 128, (b + 1) * 128)
        w = w_ref[rows].reshape(256, w_ref.shape[2])
        x = x_ref[:, rows]
        for j in range(2):
            spread = dot(x, pick(128, 256, 2, j)).astype(BF16)
            o_ref[j] += dot(spread, w)

def text_fwd(x, w):
    depth, _, cols = w.shape
    bk = 256
    return pl.pallas_call(
        text_fwd_kernel, grid=(depth // bk,),
        in_specs=[pl.BlockSpec((x.shape[0], bk), lambda i: (0, i)), pl.BlockSpec((bk, 2, cols), lambda i: (i, 0, 0))],
        out_specs=pl.BlockSpec((2, x.shape[0], cols), lambda i: (0, 0, 0)),
        out_shape=sds((2, x.shape[0], cols)),
    )(x, w)

def text_bwd_kernel(g_ref, w_ref, pair_ref, o_ref, pair_out, sends, gets, own):
    me = lax.axis_index("dp")
    step = pl.program_id(0)
    copies = to_all(lambda peer: pair_ref.at[peer], pair_out.at[me], sends, gets)
    copies.append(pltpu.make_async_copy(pair_ref.at[me], pair_out.at[me], own))

    @pl.when(step == 0)
    def _():
        for copy in copies:
            copy.start()

    for b in range(w_ref.shape[0] // 128):
        rows = slice(b * 128, (b + 1) * 128)
        w = w_ref[rows].reshape(256, w_ref.shape[2])
        total = 0.0
        for j in range(2):
            total = total + dot(g_ref[j], dot(pick(128, 256, 2, j), w).astype(BF16), 1, 1)
        o_ref[:, rows] = total.astype(BF16)

    @pl.when(step == pl.num_programs(0) - 1)
    def _():
        for copy in copies:
            copy.wait()


def text_bwd(g, w, pair):
    depth, _, cols = w.shape
    bk = 256
    count = pair.shape[0]
    return pl.pallas_call(
        text_bwd_kernel,
        grid=(depth // bk,),
        in_specs=[
            pl.BlockSpec(g.shape, lambda i: (0, 0, 0)),
            pl.BlockSpec((bk, 2, cols), lambda i: (i, 0, 0)),
            pl.BlockSpec(memory_space=pl.ANY),
        ],
        out_specs=[
            pl.BlockSpec((g.shape[1], bk), lambda i: (0, i)), pl.BlockSpec(memory_space=pl.ANY),
        ],
        out_shape=[
            sds((g.shape[1], depth), BF16), jax.ShapeDtypeStruct(pair.shape, pair.dtype),
        ],
        scratch_shapes=[
            pltpu.SemaphoreType.DMA((count,)), pltpu.SemaphoreType.DMA((count,)),
            pltpu.SemaphoreType.DMA,
        ],
        compiler_params=pltpu.CompilerParams(has_side_effects=True),
    )(g, w, pair)


def put_relative(dst, src, me, f, count):
    rows = dst.shape[0] // count
    for p in range(count):
        start = pl.multiple_of((me ^ turned(p, f)) * rows, 16)
        dst[p * rows : (p + 1) * rows, :] = src[pl.ds(start, rows), :]


def put_halves(keep, send, value, count, order, slot=None):
    rows = value.shape[0] // count
    for p in range(count):
        place = place_of(p, order[1:])
        where = place if slot is None else (place, slot)
        (send if p >> order[0] & 1 else keep)[where] = value[p * rows : (p + 1) * rows]


def ffn_kernel(
    orders, id_ref, s_ref, b_ref, w_ref, d_ref,
    wk_ref, ws_ref, dk_ref, ds_ref, fo_ref, fp_ref, so_ref, sp_ref,
    st, bt, tmp, wg, wu, facc, sacc,
):
    step = pl.program_id(0)
    depth, _, cols = w_ref.shape
    own = fo_ref.shape[0]
    count = 2 * dk_ref.shape[0]

    @pl.when(step == 0)
    def _():
        for src, dst in ((s_ref, st), (b_ref, bt)):
            for c in range(depth // 256):
                part = slice(c * 256, (c + 1) * 256)
                tmp[part, :] = src[:, part].astype(F32).T.astype(BF16)
            put_relative(dst, tmp, id_ref[0], id_ref[1], count)
        facc[...] = jnp.zeros_like(facc)
        sacc[...] = jnp.zeros_like(sacc)

    for c in range(depth // 128):
        part = slice(c * 128, (c + 1) * 128)
        w = w_ref[part].reshape(256, cols)
        wg[part, :] = dot(pick(128, 256, 2, 0), w).astype(BF16)
        wu[part, :] = dot(pick(128, 256, 2, 1), w).astype(BF16)
    s, b = s_ref[...], b_ref[...]
    gate = dot(s, wg[...])
    up = dot(s, wu[...])
    back = dot(b, d_ref[...], 1, 1)
    sig = jax.nn.sigmoid(gate)
    silu = gate * sig
    hidden = (silu * up).astype(BF16)
    g_gate = (back * up * (sig + silu * (1.0 - sig))).astype(BF16)
    g_up = (back * silu).astype(BF16)
    put_halves(wk_ref, ws_ref, dot(st[...], g_gate).astype(BF16), count, orders[0], 0)
    put_halves(wk_ref, ws_ref, dot(st[...], g_up).astype(BF16), count, orders[0], 1)
    put_halves(dk_ref, ds_ref, dot(bt[...], hidden).astype(BF16), count, orders[1])
    facc[...] += dot(hidden, d_ref[...])
    sacc[...] += dot(g_gate, wg[...], 1, 1) + dot(g_up, wu[...], 1, 1)

    @pl.when(step == pl.num_programs(0) - 1)
    def _():
        fo_ref[...] = facc[:own]
        fp_ref[...] = facc[own:].astype(BF16)
        so_ref[...] = sacc[:own]
        sp_ref[...] = sacc[own:].astype(BF16)


def ffn(ids, s, b, w, d, local, dp, orders):
    tokens, depth = s.shape
    hid = d.shape[0]
    bc = min(256, hid)
    rest = tokens - local
    once = functools.partial(pl.BlockSpec, pipeline_mode=pl.Buffered(1))
    const = lambda i: (0, 0)
    share = depth // dp
    half = pl.BlockSpec((dp // 2, share, bc), lambda i: (0, 0, i))
    halves = pl.BlockSpec((dp // 2, 2, share, bc), lambda i: (0, 0, 0, i))
    return pl.pallas_call(
        functools.partial(ffn_kernel, orders),
        grid=(hid // bc,),
        in_specs=[
            pl.BlockSpec(memory_space=pltpu.SMEM),
            once((tokens, depth), const), once((tokens, depth), const),
            pl.BlockSpec((depth, 2, bc), lambda i: (0, 0, i)),
            pl.BlockSpec((bc, depth), lambda i: (i, 0)),
        ],
        out_specs=[halves] * 2 + [half] * 2 + [
            once((local, depth), const), once((rest, depth), const),
            once((local, depth), const), once((rest, depth), const),
        ],
        out_shape=[sds((dp // 2, 2, share, hid), BF16)] * 2 + [sds((dp // 2, share, hid), BF16)] * 2 + [
            sds((local, depth)), sds((rest, depth), BF16),
            sds((local, depth)), sds((rest, depth), BF16),
        ],
        scratch_shapes=[
            pltpu.VMEM((depth, tokens), BF16), pltpu.VMEM((depth, tokens), BF16),
            pltpu.VMEM((depth, tokens), BF16),
            pltpu.VMEM((depth, bc), BF16), pltpu.VMEM((depth, bc), BF16),
            pltpu.VMEM((tokens, depth), F32), pltpu.VMEM((tokens, depth), F32),
        ],
        compiler_params=pltpu.CompilerParams(vmem_limit_bytes=62 << 20),
    )(ids, s, b, w, d)


def project_kernel(id_ref, xo_ref, xp_ref, front_ref, w_ref, got_ref, first_ref, pre_ref, sq_ref):
    j = pl.program_id(0)
    local, depth = xo_ref.shape
    own = got_ref.shape[2]
    f = id_ref[1]

    @pl.when(j == 0)
    def _():
        for i, ref in enumerate((xo_ref, xp_ref)):
            x = ref[...].astype(F32)
            inv = lax.rsqrt(jnp.sum(x * x, axis=1, keepdims=True) * (1.0 / depth) + EPSILON)
            first_ref[i * local : (i + 1) * local, :] = (x * inv * front_ref[...]).astype(BF16)
        sq_ref[...] = jnp.zeros_like(sq_ref)

    mine = pl.ds(pl.multiple_of(f * own, 128), own)
    other = pl.ds(pl.multiple_of((1 - f) * own, 128), own)
    out = dot(first_ref[:, mine], w_ref[0, :, mine]) + dot(first_ref[:, other], got_ref[0])
    pre_ref[0] = out
    square = out * out
    part = square[:, :128]
    for c in range(1, own // 128):
        part = part + square[:, c * 128 : (c + 1) * 128]
    sq_ref[pl.ds(j, 1), :] = jnp.sum(part.T, axis=0, keepdims=True)


def project(ids, xo, xp, front, w, got):
    local, depth = xo.shape
    own = got.shape[2]
    tokens = 2 * local
    const = lambda j: (0, 0)
    return pl.pallas_call(
        project_kernel,
        grid=(3,),
        in_specs=[
            pl.BlockSpec(memory_space=pltpu.SMEM),
            pl.BlockSpec((local, depth), const), pl.BlockSpec((local, depth), const),
            pl.BlockSpec((1, depth), const),
            pl.BlockSpec((1, own, depth), lambda j: (j, 0, 0)),
            pl.BlockSpec((1, own, own), lambda j: (j, 0, 0)),
        ],
        out_specs=[
            pl.BlockSpec((tokens, depth), const),
            pl.BlockSpec((1, tokens, own), lambda j: (j, 0, 0)),
            pl.BlockSpec((8, tokens), const),
        ],
        out_shape=[sds((tokens, depth), BF16), sds((3, tokens, own)), sds((8, tokens))],
    )(ids, xo, xp, front, w, got)


def project_grad_kernel(
    order, id_ref, da_ref, db_ref, pre_ref, stat_ref, gain_ref, first_ref,
    keep_ref, send_ref, g_ref, gt, tmp,
):
    j = pl.program_id(0)
    own = pre_ref.shape[2]
    cut = da_ref.shape[2]
    count = 2 * keep_ref.shape[0]
    inv, mean = column(stat_ref, j, 128), column(stat_ref, j + 3, 128)
    for c in range(own // 128):
        part = slice(c * 128, (c + 1) * 128)
        here = slice(c * 128 - cut, (c + 1) * 128 - cut) if c * 128 >= cut else part
        d = (db_ref if c * 128 >= cut else da_ref)[0, :, here]
        g = inv * (d * gain_ref[0, :, part] - pre_ref[0, :, part] * inv * mean)
        tmp[part, :] = g.T.astype(BF16)
        g_ref[0, :, part] = g.astype(BF16)
    put_relative(gt, tmp, id_ref[0] % count, id_ref[1], count)
    put_halves(keep_ref, send_ref, dot(gt[...], first_ref[...]).astype(BF16), count, order, j)


def project_grad(ids, da, db, pre, stats, gain, first, dp, order):
    _, tokens, own = pre.shape
    depth = first.shape[1]
    share = depth // dp
    const = lambda j: (0, 0)
    block = lambda j: (j, 0, 0)
    once = functools.partial(pl.BlockSpec, pipeline_mode=pl.Buffered(1))
    half = once((dp // 4, 3, share, depth), lambda j: (0, 0, 0, 0))
    return pl.pallas_call(
        functools.partial(project_grad_kernel, order),
        grid=(3,),
        in_specs=[
            pl.BlockSpec(memory_space=pltpu.SMEM),
            pl.BlockSpec((1,) + da.shape[1:], block), pl.BlockSpec((1,) + db.shape[1:], block),
            pl.BlockSpec((1, tokens, own), block),
            pl.BlockSpec((8, tokens), const),
            pl.BlockSpec((1, 1, own), block),
            once((tokens, depth), const),
        ],
        out_specs=[half, half, pl.BlockSpec((1, tokens, own), block)],
        out_shape=[sds((dp // 4, 3, share, depth), BF16)] * 2
        + [sds((3, tokens, own), BF16)],
        scratch_shapes=[pltpu.VMEM((own, tokens), BF16), pltpu.VMEM((own, tokens), BF16)],
    )(ids, da, db, pre, stats, gain, first)


def project_back_kernel(id_ref, g_ref, w_ref, got_ref, own_ref, peer_ref, acc):
    j = pl.program_id(0)
    own = g_ref.shape[2]
    local = own_ref.shape[0]
    f = id_ref[1]
    mine = pl.ds(pl.multiple_of(f * own, 128), own)
    other = pl.ds(pl.multiple_of((1 - f) * own, 128), own)

    @pl.when(j == 0)
    def _():
        acc[...] = jnp.zeros_like(acc)

    acc[:, mine] += dot(g_ref[0], w_ref[0, :, mine], 1, 1)
    acc[:, other] += dot(g_ref[0], got_ref[0], 1, 1)

    @pl.when(j == 2)
    def _():
        own_ref[...] = acc[:local]
        peer_ref[...] = acc[local:].astype(BF16)


def project_back(ids, g, w, got):
    _, tokens, own = g.shape
    depth = w.shape[2]
    local = tokens // 2
    const = lambda j: (0, 0)
    block = lambda j: (j, 0, 0)
    once = functools.partial(pl.BlockSpec, pipeline_mode=pl.Buffered(1))
    return pl.pallas_call(
        project_back_kernel,
        grid=(3,),
        in_specs=[
            pl.BlockSpec(memory_space=pltpu.SMEM),
            pl.BlockSpec((1, tokens, own), block),
            pl.BlockSpec((1, own, depth), block), pl.BlockSpec((1, own, own), block),
        ],
        out_specs=[once((local, depth), const), once((local, depth), const)],
        out_shape=[sds((local, depth)), sds((local, depth), BF16)],
        scratch_shapes=[pltpu.VMEM((tokens, depth), F32)],
    )(ids, g, w, got)


def out_back_kernel(order, id_ref, *refs):
    n = len(refs) - 8
    blocks, (w_ref, mixed_ref, g_ref, keep_ref, send_ref, all_ref, gt, tmp) = refs[:n], refs[n:]
    local = blocks[0].shape[0]
    for r, ref in enumerate(blocks):
        all_ref[r * local : (r + 1) * local, :] = ref[...]
    grad = all_ref[...]
    g_ref[...] = dot(grad, w_ref[...], 1, 1)
    for c in range(grad.shape[1] // 256):
        part = slice(c * 256, (c + 1) * 256)
        tmp[part, :] = grad[:, part].astype(F32).T.astype(BF16)
    count = 2 * keep_ref.shape[0]
    put_relative(gt, tmp, id_ref[0], id_ref[1], count)
    put_halves(keep_ref, send_ref, dot(gt[...], mixed_ref[...]).astype(BF16), count, order)


def out_back(ids, blocks, w, mixed, dp, order):
    tokens, own = mixed.shape
    depth = w.shape[1]
    vmem = pl.BlockSpec(memory_space=pltpu.VMEM)
    half = sds((dp // 2, depth // dp, own), BF16)
    return pl.pallas_call(
        functools.partial(out_back_kernel, order),
        in_specs=[pl.BlockSpec(memory_space=pltpu.SMEM)] + [vmem] * (len(blocks) + 2),
        out_specs=[vmem] * 3,
        out_shape=[sds((tokens, own)), half, half],
        scratch_shapes=[
            pltpu.VMEM((tokens, depth), BF16),
            pltpu.VMEM((depth, tokens), BF16), pltpu.VMEM((depth, tokens), BF16),
        ],
    )(ids, *blocks, w, mixed)


def time_embed(timesteps):
    half = TE // 2
    frequencies = jnp.exp(-math.log(10000.0) * jnp.arange(half, dtype=F32) / half)
    angles = timesteps.astype(F32)[:, None] * frequencies
    waves = jnp.concatenate([jnp.cos(angles), jnp.sin(angles)], axis=-1)
    return jax.nn.silu(waves).astype(BF16)


def rope_tables(positions, width):
    lane = jnp.arange(width)
    quarter = HD // 4
    frequencies = 10000.0 ** (-(lane % quarter).astype(F32) / quarter)
    place = jnp.where(lane % HD < HD // 2, positions[0][:, None], positions[1][:, None])
    angles = place.astype(F32) * frequencies
    return jnp.cos(angles), jnp.where(lane % 32 < 16, -1.0, 1.0) * jnp.sin(angles)


def inverse_rms(values):
    return lax.rsqrt(jnp.mean(values * values, axis=-1, keepdims=True) + EPSILON)


def rms_back(grad_hat, normed, inverse):
    return inverse * (grad_hat - normed * jnp.mean(grad_hat * normed, axis=-1, keepdims=True))


def pad_cols(value, width):
    extra = -value.shape[-1] % width
    return value if extra == 0 else jnp.pad(value, [(0, 0)] * (value.ndim - 1) + [(0, extra)])


def on_device(
    hidden_in, text_state, caption_lengths, timesteps, patch_positions, cotangent,
    w_ada, w_text, w_qkv, w_out, gains, cross_gate, w_gate_up, w_down,
):
    n, f = lax.axis_size("fsdp"), lax.axis_index("fsdp")
    dpn, me = lax.axis_size("dp"), lax.axis_index("dp")
    bits = list(range(dp_bits()))
    low_bits = bits[:-1]
    late = bits[2:3] + bits[:2] + bits[3:]
    own_d = D // n
    local = hidden_in.shape[1]
    tokens = n * local
    width = 2 * HD
    share = D // dpn
    paired = n == 2 and dpn >= 4
    ids = jnp.stack([me, f]).astype(jnp.int32)
    x_bf, dy_bf = hidden_in[0], cotangent[0]

    time_low = time_embed(timesteps)
    own_te = TE // n
    time_own = lax.dynamic_slice_in_dim(time_low[0], f * own_te, own_te, 0)
    modulation = pair_sum(
        jnp.einsum("k,kjd->jd", time_own, w_ada, preferred_element_type=F32)
    )
    scale_attn, gate_attn = modulation[0:1], jnp.tanh(modulation[1:2])
    scale_ffn, gate_ffn = modulation[2:3], jnp.tanh(modulation[3:4])

    w_flat = jnp.moveaxis(w_qkv, 1, 0)
    w_parts = exchange_rot(w_flat, 2)
    x_parts = gather_rot(x_bf)
    dy_all = jnp.concatenate(gather_rot(dy_bf), axis=0)
    places = jnp.concatenate(gather_rot(patch_positions[0]), axis=1)
    text_cols = jnp.concatenate(natural(exchange_rot(text_state[0], 1)), axis=0)
    text_all = lax.all_gather(text_cols, "dp", axis=0, tiled=True)
    gain_full = lax.all_gather(gains, "fsdp", axis=1, tiled=True).astype(F32)
    gain_own = gains.astype(F32)

    front = gain_full[0] * (1.0 + scale_attn)
    if paired:
        first_all, pre, squares = project(ids, *x_parts, front, w_flat, w_parts[1])
    else:
        w_heads = jnp.concatenate(natural(w_parts), axis=1)
        x_f = jnp.concatenate(x_parts, axis=0).astype(F32)
        first_all = (x_f * inverse_rms(x_f) * front).astype(BF16)
        pre = jnp.stack([dot(first_all, w_heads[j]) for j in range(3)])
        squares = jnp.pad(jnp.sum(pre[:2] * pre[:2], -1), ((0, 6), (0, 0)))
    inverse = lax.rsqrt(row_sum(squares) / D + EPSILON)

    text_part = text_fwd(text_cols, w_text)
    text_pre = scatter_rot(rot_blocks(text_part, 2))
    inv_t = lax.rsqrt(
        pair_sum(jnp.sum(text_pre[0] * text_pre[0], -1, keepdims=True)) / D + EPSILON
    )
    normed_t = text_pre[0] * inv_t
    tk = (normed_t * gain_own[4]).astype(BF16)
    tv = text_pre[1].astype(BF16)

    head_tanh = jnp.tanh(cross_gate.astype(F32))
    gate_row = pad_cols(jnp.repeat(head_tanh, HD)[None], width)
    cosine, sine = rope_tables(places, width)
    gq, gk = pad_cols(gain_own[2:3], width), pad_cols(gain_own[3:4], width)
    pre_p, tkp, tvp = pad_cols(pre, width), pad_cols(tk, width), pad_cols(tv, width)
    q, k, v, mixed_p, so, co, ls, lc = attn_forward(
        caption_lengths, pre_p, inverse, gq, gk, cosine, sine, tkp, tvp, gate_row
    )
    mixed = mixed_p[:, :own_d]

    def rows(value, r):
        return value[r * local : (r + 1) * local]

    parts = [dot(rows(mixed, r), w_out) for r in range(n)]
    attn_branch = scatter_rot([parts[0]] + [p.astype(BF16) for p in parts[1:]])
    x_own = x_bf.astype(F32)
    after_attn = x_own + gate_attn * attn_branch
    inverse_two = inverse_rms(after_attn)
    normed_two = after_attn * inverse_two
    second = (normed_two * gain_full[1] * (1.0 + scale_ffn)).astype(BF16)

    second_all = jnp.concatenate(gather_rot(second), axis=0)
    branch_all = (gate_ffn * dy_all.astype(F32)).astype(BF16)
    wide_keep, wide_send, down_keep, down_send, ffn_own, ffn_rest, back_own, back_rest = ffn(
        ids, second_all, branch_all, w_gate_up, w_down, local, dpn, (bits, late)
    )
    (ffn_own, ffn_rest, back_own, back_rest), text_all = lax.optimization_barrier(
        ((ffn_own, ffn_rest, back_own, back_rest), text_all)
    )
    wide_chain = Halving(bits, wide_keep, wide_send)
    down_chain = Halving(late, down_keep, down_send)
    grad_second = scatter_rot([back_own] + [rows(back_rest, r) for r in range(n - 1)])
    ffn_branch = scatter_rot([ffn_own] + [rows(ffn_rest, r) for r in range(n - 1)])
    output = (after_attn + gate_ffn * ffn_branch).astype(BF16)
    dy = dy_bf.astype(F32)
    d_gate_ffn = jnp.sum(dy * ffn_branch, axis=0) * (1.0 - gate_ffn[0] * gate_ffn[0])

    scaled = grad_second * normed_two
    d_scale_ffn = jnp.sum(scaled * gain_full[1], axis=0)
    gain_two = jnp.sum(scaled * (1.0 + scale_ffn), axis=0)
    grad_after = dy + rms_back(
        grad_second * gain_full[1] * (1.0 + scale_ffn), normed_two, inverse_two
    )
    d_gate_attn = jnp.sum(grad_after * attn_branch, axis=0) * (1.0 - gate_attn[0] * gate_attn[0])
    grad_attn = (gate_attn * grad_after).astype(BF16)
    grad_mixed, *out_halves = out_back(ids, gather_rot(grad_attn), w_out, mixed, dpn, bits)
    out_chain = Halving(bits, *out_halves)
    blocks = pre_p.shape[2] // width
    cut = max(1, 2 * blocks // 3)
    grad_mixed = pad_cols(grad_mixed, width)
    inputs = (so, co, ls, lc, pre_p, inverse, gq, gk, cosine, sine, gate_row)
    part_a = attn_backward(0, cut, caption_lengths, q, k, v, tkp, tvp, grad_mixed, *inputs)
    part_a, grad_mixed = lax.optimization_barrier((part_a, grad_mixed))
    grad_mixed = advance([wide_chain, down_chain], grad_mixed)
    part_b = attn_backward(
        cut, blocks - cut, caption_lengths, q, k, v, tkp, tvp, grad_mixed, *inputs
    )
    means = row_sum(part_a[3] + part_b[3])[:2] / D

    ones, zeros = jnp.ones((1, tokens), F32), jnp.zeros((1, tokens), F32)
    if paired:
        stats = jnp.concatenate([inverse[:2], ones, means, zeros, zeros, zeros], axis=0)
        gain3 = jnp.stack([gain_own[2:3], gain_own[3:4], jnp.ones_like(gain_own[2:3])])
        keep, send, grads = project_grad(
            ids, part_a[0], part_b[0], pre, stats, gain3, first_all, dpn, low_bits
        )
        part_a, part_b, grads = advance(
            [wide_chain, down_chain, out_chain], (part_a[1:], part_b[1:], grads)
        )
        qkv_chain = Halving(low_bits, keep, send)
        parts = project_back(ids, grads, w_flat, w_parts[1])
    else:
        d = jnp.concatenate([part_a[0], part_b[0]], axis=2)[:, :, :own_d]
        part_a, part_b = part_a[1:], part_b[1:]
        inv, mean = inverse[:2, :, None], means[:, :, None]
        hat = d[:2] * gain_own[2:4][:, None] - pre[:2] * inv * mean
        grads = [(inv[0] * hat[0]).astype(BF16), (inv[1] * hat[1]).astype(BF16), d[2].astype(BF16)]
        wide = [dot(g, first_all, 0, 0).astype(BF16) for g in grads]
        wide = [jnp.concatenate(natural(exchange_rot(w_, 1)), axis=0) for w_ in wide]
        wide = relative(jnp.stack([w_.reshape(dpn, share, own_d) for w_ in wide], axis=1))
        wide = jnp.stack([wide[p] for p in sorted(range(dpn), key=lambda p: place_of(p, bits))])
        qkv_chain = Halving(bits, wide[: dpn // 2], wide[dpn // 2 :])
        parts = [
            sum(dot(rows(g, r), w_heads[j], 1, 1) for j, g in enumerate(grads)) for r in range(n)
        ]
        parts = [parts[0]] + [p.astype(BF16) for p in parts[1:]]
    grad_first = scatter_rot(parts)

    dtk, dtv, gain_q, gain_k, gate_g = (
        jnp.concatenate([part_a[i], part_b[i]], axis=1)[:, :own_d] for i in (0, 1, 3, 4, 5)
    )
    text_hat = dtk * gain_own[4]
    gain_text = jnp.sum(dtk * normed_t, axis=0, keepdims=True)
    mean_t = pair_sum(jnp.sum(text_hat * normed_t, -1, keepdims=True)) / D
    grad_tk = (inv_t * (text_hat - normed_t * mean_t)).astype(BF16)
    text_pair = jnp.stack([grad_tk, dtv.astype(BF16)])
    pair_all = jnp.concatenate(natural(gather_rot(text_pair)), axis=-1)
    outgoing = block_of(pair_all.transpose(0, 2, 1), f, 2)
    outgoing = outgoing.reshape(2, dpn, share, TEXT // n).transpose(1, 0, 2, 3)
    pair_all, outgoing = settle(
        [qkv_chain, wide_chain, down_chain, out_chain], (pair_all, outgoing)
    )
    for chain in (qkv_chain, down_chain, out_chain):
        chain.step()
    text_in, pair_cols = text_bwd(pair_all, w_text, outgoing)
    text_in, grad_first = advance(
        [qkv_chain, wide_chain, down_chain, out_chain], (text_in, grad_first)
    )
    pair_cols, qkv_chain.keep = lax.optimization_barrier((pair_cols, qkv_chain.keep))
    text_in = jnp.concatenate(natural(exchange_rot(text_in, 0)), axis=1)

    inverse_one = inverse_rms(x_own)
    normed_one = x_own * inverse_one
    scaled = grad_first * normed_one
    d_scale_attn = jnp.sum(scaled * gain_full[0], axis=0)
    gain_one = jnp.sum(scaled * (1.0 + scale_attn), axis=0)
    grad_input = (
        grad_after
        + rms_back(grad_first * gain_full[0] * (1.0 + scale_attn), normed_one, inverse_one)
    ).astype(BF16)


    sums = [d_scale_attn, d_gate_attn, d_scale_ffn, d_gate_ffn, gain_one, gain_two]
    sums = pair_sum(jnp.stack(sums))
    stamp = jnp.full((1, D), timesteps[0].astype(F32))
    small = jnp.concatenate([block_of(sums[4:], f, 1), gain_q, gain_k, gain_text, gate_g], axis=0)
    small = jnp.pad(small.reshape(-1), (0, dpn * SUMS * 128 - small.size))
    mods = jnp.concatenate([sums[:4], stamp], axis=0).reshape(5, dpn, share).transpose(1, 0, 2)
    mods = jnp.pad(mods, ((0, 0), (0, 0), (0, -share % 128)))
    mods = jnp.concatenate([mods, small.reshape(dpn, SUMS, 128)], axis=1)
    pair_cols = jnp.concatenate(natural(gather_rot(pair_cols)), axis=3)
    pair_cols = pair_cols.transpose(1, 2, 0, 3).reshape(2 * share, dpn * TEXT)
    text_grad = dot(pair_cols, text_all).reshape(2, share, TW // n)
    mods, text_grad = settle([wide_chain], (mods, text_grad))
    if paired:
        mods = advance([qkv_chain], mods)
        own_side = f == (me >> low_bits[-1] + 1)
        mine, got = exchange_rot(qkv_chain.last[0].astype(BF16), 2)
        keep, send = jnp.where(own_side, mine, got)[None], jnp.where(own_side, got, mine)[None]
        mods, keep, send = lax.optimization_barrier((mods, keep, send))
        qkv_chain = Halving(bits[-1:], keep, send)
    mods, small = small_exchange(mods)
    mods = settle([qkv_chain], mods)
    total = small[:, 5 : 5 + SUMS].reshape(-1)[: 6 * own_d].reshape(6, own_d)
    gate_total = jnp.sum(total[5].reshape(HEADS // n, HD), axis=1) * (
        1.0 - head_tanh * head_tanh
    )
    times = time_embed(mods[:, 4, 0])
    times = lax.dynamic_slice_in_dim(times, f * own_te, own_te, 1).astype(F32)
    ada_grad = lax.dot_general(
        mods[:, :4, :share].reshape(dpn, 4 * share), times, (((0,), (0,)), ((), ())),
        precision=lax.Precision.HIGHEST,
    ).reshape(4, share, own_te)

    for chain in (out_chain, down_chain, wide_chain, qkv_chain):
        while chain.got is not None:
            chain.step()
    return (
        output[None],
        grad_input[None],
        text_in[None],
        ada_grad.transpose(2, 0, 1),
        text_grad.transpose(2, 0, 1),
        qkv_chain.last[0].transpose(2, 0, 1),
        out_chain.last[0].T,
        total[:5],
        gate_total,
        wide_chain.last[0].transpose(1, 0, 2),
        down_chain.last[0].T,
    )


def solution(mesh):
    return jax.shard_map(
        on_device,
        mesh=mesh,
        in_specs=(
            P("dp", "fsdp", None),
            P("dp", "fsdp", None),
            P("dp"),
            P("dp"),
            P("dp", None, "fsdp"),
            P("dp", "fsdp", None),
            P("fsdp", None, None),
            P("fsdp", None, None),
            P("fsdp", None, None),
            P("fsdp", None),
            P(None, "fsdp"),
            P("fsdp"),
            P(None, None, "fsdp"),
            P("fsdp", None),
        ),
        out_specs=(
            P("dp", "fsdp", None),
            P("dp", "fsdp", None),
            P("dp", "fsdp", None),
            P("fsdp", None, "dp"),
            P("fsdp", None, "dp"),
            P("fsdp", None, "dp"),
            P("fsdp", "dp"),
            P(None, "fsdp"),
            P("fsdp"),
            P("dp", None, "fsdp"),
            P("fsdp", "dp"),
        ),
        check_vma=False,
    )
```

```python
import functools
import math

import jax
import jax.numpy as jnp
from jax import lax
from jax.experimental import pallas as pl
from jax.experimental.pallas import tpu as pltpu
from jax.sharding import PartitionSpec as P

D = 1536
HEADS = 24
HD = 64
TW = 4096
TE = 1024
PATCHES = 1024
TEXT = 256
EPSILON = 1e-06
F32 = jnp.float32
BF16 = jnp.bfloat16
QC = 256


def dot(a, b, ca=1, cb=0):
    return lax.dot_general(a, b, (((ca,), (cb,)), ((), ())), preferred_element_type=F32)


def from_behind(value, step):
    n = lax.axis_size("fsdp")
    return lax.ppermute(value, "fsdp", [(i, (i + step) % n) for i in range(n)])


def gather_rot(value):
    return [value] + [from_behind(value, r) for r in range(1, lax.axis_size("fsdp"))]


def pair_sum(value):
    return functools.reduce(lambda a, b: a + b, gather_rot(value))


def row_sum(value):
    n = lax.axis_size("fsdp")
    rows = value.shape[-1] // n
    total = value
    for r in range(1, n):
        total = total + jnp.roll(from_behind(value, r), r * rows, axis=-1)
    return total


def scatter_rot(blocks):
    n = lax.axis_size("fsdp")
    total = blocks[0].astype(F32)
    for r in range(1, n):
        got = lax.ppermute(blocks[r], "fsdp", [(i, (i - r) % n) for i in range(n)])
        total = total + got.astype(F32)
    return total


def block_of(value, index, axis):
    size = value.shape[axis] // lax.axis_size("fsdp")
    return lax.dynamic_slice_in_dim(value, index * size, size, axis)


def rot_blocks(value, axis):
    n, f = lax.axis_size("fsdp"), lax.axis_index("fsdp")
    return [block_of(value, (f - r) % n, axis) for r in range(n)]


def exchange_rot(value, axis):
    n, f = lax.axis_size("fsdp"), lax.axis_index("fsdp")
    out = [block_of(value, f, axis)]
    for r in range(1, n):
        out.append(from_behind(block_of(value, (f + r) % n, axis), r))
    return out


def natural(got):
    n, f = lax.axis_size("fsdp"), lax.axis_index("fsdp")
    if n == 2:
        return [jnp.where(f == 0, got[0], got[1]), jnp.where(f == 0, got[1], got[0])]
    got = jnp.stack(got)
    return [lax.dynamic_index_in_dim(got, (f - g) % n, 0, keepdims=False) for g in range(n)]


def dp_bits():
    return int(lax.axis_size("dp")).bit_length() - 1


def swapped(p):
    return (p & ~3) | ((p & 1) << 1) | ((p >> 1) & 1)


def turned(p, f):
    return p if dp_bits() < 3 else jnp.where(f % 2 == 0, p, swapped(p))


def dp_swap(value, bit):
    n, dpn = lax.axis_size("fsdp"), lax.axis_size("dp")
    pairs = []
    for i in range(dpn):
        for f in range(n):
            flip = 1 << bit if dp_bits() < 3 or f % 2 == 0 else swapped(1 << bit)
            pairs.append((i * n + f, (i ^ flip) * n + f))
    return lax.ppermute(value, ("dp", "fsdp"), pairs)


def relative(value):
    places = turned(jnp.arange(lax.axis_size("dp")), lax.axis_index("fsdp"))
    return jnp.take(value, lax.axis_index("dp") ^ places, axis=0)


class Halving:
    def __init__(self, order, keep, send):
        self.order = list(order)
        self.keep, self.got = keep, dp_swap(send, self.order.pop(0))

    def step(self):
        if self.got is None:
            return

        def add(part):
            return self.keep[part].astype(F32) + self.got[part].astype(F32)

        if not self.order:
            self.last = add(slice(None))
            self.got = None
            return
        half = self.keep.shape[0] // 2
        send = add(slice(half, None)).astype(BF16)
        self.keep = add(slice(half)).astype(BF16)
        self.got = dp_swap(send, self.order.pop(0))


def place_of(p, order):
    return sum((p >> bit & 1) << i for i, bit in enumerate(reversed(order)))


SUMS = 3


def to_all(source, target, sends, gets):
    me = lax.axis_index("dp")
    return [
        pltpu.make_async_remote_copy(
            src_ref=source(me ^ r), dst_ref=target, send_sem=sends.at[r], recv_sem=gets.at[r],
            device_id={"dp": me ^ r}, device_id_type=pl.DeviceIdType.MESH,
        )
        for r in range(1, lax.axis_size("dp"))
    ]


def small_kernel(mod_ref, mod_out, sum_out, part, sends, gets, own):
    me = lax.axis_index("dp")
    steps = (
        to_all(lambda peer: mod_ref.at[peer], mod_out.at[me], sends.at[0], gets.at[0])
        + [pltpu.make_async_copy(mod_ref.at[me], mod_out.at[me], own.at[0])],
        to_all(lambda peer: part, sum_out.at[me], sends.at[1], gets.at[1])
        + [pltpu.make_async_copy(part, sum_out.at[me], own.at[1])],
    )
    for i, copies in enumerate(steps):
        if i == 1:
            part[...] = jnp.sum(mod_out[...], axis=0)
        for copy in copies:
            copy.start()
        for copy in copies:
            copy.wait()


def small_exchange(mods):
    vmem = pl.BlockSpec(memory_space=pltpu.VMEM)
    count = mods.shape[0]
    return pl.pallas_call(
        small_kernel,
        in_specs=[vmem],
        out_specs=[vmem] * 2,
        out_shape=[jax.ShapeDtypeStruct(mods.shape, mods.dtype)] * 2,
        scratch_shapes=[
            pltpu.VMEM(mods.shape[1:], mods.dtype),
            pltpu.SemaphoreType.DMA((2, count)), pltpu.SemaphoreType.DMA((2, count)),
            pltpu.SemaphoreType.DMA((2,)),
        ],
        compiler_params=pltpu.CompilerParams(has_side_effects=True),
    )(mods)


def settle(chains, value):
    live = [c for c in chains if c.got is not None]
    value, got = lax.optimization_barrier((value, [c.got for c in live]))
    for c, g in zip(live, got):
        c.got = g
    return value


def advance(chains, value):
    value = settle(chains, value)
    for c in chains:
        c.step()
    return value


def rope_block(value, cosine, sine, sign):
    width = value.shape[1]
    lane = lax.broadcasted_iota(jnp.int32, value.shape, 1)
    partner = jnp.where(
        lane % 32 < 16, pltpu.roll(value, width - 16, 1), pltpu.roll(value, 16, 1)
    )
    return value * cosine + sign * (partner * sine)


def column(ref, index, width):
    row = ref[index : index + 1, :] if isinstance(index, int) else ref[pl.ds(index, 1), :]
    return jnp.broadcast_to(row, (width, row.shape[1])).T


def masked(value, head):
    lane = lax.broadcasted_iota(jnp.int32, value.shape, 1)
    return jnp.where(lane // HD == head, value, jnp.zeros_like(value))


def attn_fwd_kernel(
    len_ref, pre_ref, inv_ref, gq_ref, gk_ref, cos_ref, sin_ref, tk_ref, tv_ref, gate_ref,
    q_ref, k_ref, v_ref, mixed_ref, so_ref, co_ref, ls_ref, lc_ref,
):
    _, tokens, width = pre_ref.shape
    heads = width // HD
    iq, ik = column(inv_ref, 0, width), column(inv_ref, 1, width)
    q = rope_block(pre_ref[0] * iq * gq_ref[...], cos_ref[...], sin_ref[...], 1.0)
    q_ref[...] = q.astype(BF16)
    k = rope_block(pre_ref[1] * ik * gk_ref[...], cos_ref[...], sin_ref[...], 1.0)
    k_ref[...] = k.astype(BF16)
    v_ref[...] = pre_ref[2].astype(BF16)
    length = len_ref[0]

    def one(keys, values, qm, limit):
        s = dot(qm, keys, 1, 1)
        if limit is not None:
            slot = lax.broadcasted_iota(jnp.int32, s.shape, 1)
            s = jnp.where(slot < limit, s, -1e30)
        peak = jnp.max(s, axis=1, keepdims=True)
        e = jnp.exp(s - peak)
        total = jnp.sum(e, axis=1, keepdims=True)
        o = dot(e.astype(BF16), values)
        return o * (1.0 / total), peak + jnp.log(total)

    lane = lax.broadcasted_iota(jnp.int32, (tokens, width), 1)
    qs = q_ref[...] * jnp.asarray(HD**-0.5, BF16)
    so = co = stats = jnp.zeros((tokens, width), F32)
    for h in range(heads):
        qm = masked(qs, h)
        o, lse = one(k_ref[...], v_ref[...], qm, None)
        so = jnp.where(lane // HD == h, o, so)
        stats = jnp.where(lane == h, lse, stats)
        o, lse = one(tk_ref[...], tv_ref[...], qm, length)
        co = jnp.where(lane // HD == h, o, co)
        stats = jnp.where(lane == heads + h, lse, stats)
    so_ref[...] = so
    co_ref[...] = co
    mixed_ref[...] = (so + gate_ref[...] * co).astype(BF16)
    stats = stats.T
    ls_ref[0] = stats[:heads]
    lc_ref[0] = stats[heads : 2 * heads]


def attn_bwd_kernel(
    len_ref, q_ref, k_ref, v_ref, tk_ref, tv_ref, g_ref, so_ref, co_ref, ls_ref, lc_ref,
    pre_ref, inv_ref, gq_ref, gk_ref, cos_ref, sin_ref, gate_ref,
    d_ref, dtk_ref, dtv_ref, stat_ref, gainq_ref, gaink_ref, gateg_ref,
    gs_ref, gc_ref, ds_ref, dc_ref, kt_ref, tkt_ref, dqt_ref, dk_acc, dv_acc, rq_ref, rk_ref,
):
    tokens, width = q_ref.shape
    heads = width // HD
    scale = jnp.asarray(HD**-0.5, BF16)

    @pl.when(pl.program_id(0) == 0)
    def _():
        rq_ref[...] = jnp.zeros_like(rq_ref)
        rk_ref[...] = jnp.zeros_like(rk_ref)

    g = g_ref[...]
    gs_ref[...] = g.astype(BF16)
    gc_ref[...] = (g * gate_ref[...]).astype(BF16)
    prod_c = g * co_ref[...]
    gateg_ref[...] = jnp.sum(prod_c, axis=0, keepdims=True)
    prod_s = (g * so_ref[...]).T
    prod_c = (prod_c * gate_ref[...]).T
    for h in range(heads):
        ds_ref[h : h + 1, :] = jnp.sum(prod_s[h * HD : (h + 1) * HD], axis=0, keepdims=True)
        dc_ref[h : h + 1, :] = jnp.sum(prod_c[h * HD : (h + 1) * HD], axis=0, keepdims=True)
    kt_ref[...] = k_ref[...].astype(F32).T.astype(BF16)
    tkt_ref[...] = tk_ref[...].astype(F32).T.astype(BF16)
    dk_acc[...] = jnp.zeros_like(dk_acc)
    dv_acc[...] = jnp.zeros_like(dv_acc)
    dtk_ref[...] = jnp.zeros_like(dtk_ref)
    dtv_ref[...] = jnp.zeros_like(dtv_ref)
    length = len_ref[0]

    def one(keys, keys_t, values, qm, gm, lse, delta, head, limit):
        s = dot(keys, qm, 1, 1)
        p = jnp.exp(s - lse)
        if limit is not None:
            slot = lax.broadcasted_iota(jnp.int32, s.shape, 0)
            p = jnp.where(slot < limit, p, 0.0)
        dp = dot(values, gm, 1, 1)
        ds = (p * (dp - delta)).astype(BF16)
        dq = dot(keys_t[head * HD : (head + 1) * HD, :], ds)
        return dq, dot(ds, qm), dot(p.astype(BF16), gm)

    def chunk(c, carry):
        rows = pl.ds(pl.multiple_of(c * QC, QC), QC)
        qc = q_ref[rows, :] * scale
        for h in range(heads):
            qm = masked(qc, h)
            dq, dk, dv = one(
                k_ref[...], kt_ref, v_ref[...], qm, masked(gs_ref[rows, :], h),
                ls_ref[0, h : h + 1, rows], ds_ref[h : h + 1, rows], h, None,
            )
            dk_acc[...] += dk
            dv_acc[...] += dv
            dq2, dk, dv = one(
                tk_ref[...], tkt_ref, tv_ref[...], qm, masked(gc_ref[rows, :], h),
                lc_ref[0, h : h + 1, rows], dc_ref[h : h + 1, rows], h, length,
            )
            dtk_ref[...] += dk
            dtv_ref[...] += dv
            dqt_ref[h * HD : (h + 1) * HD, rows] = (dq + dq2) * HD**-0.5
        return carry

    lax.fori_loop(0, tokens // QC, chunk, 0)
    dq = rope_block(dqt_ref[...].T, cos_ref[...], sin_ref[...], -1.0)
    d_ref[0] = dq
    prod = dq * (pre_ref[0] * column(inv_ref, 0, width))
    gainq_ref[...] = jnp.sum(prod, axis=0, keepdims=True)
    rq_ref[...] += prod * gq_ref[...]
    dk = rope_block(dk_acc[...], cos_ref[...], sin_ref[...], -1.0)
    d_ref[1] = dk
    prod = dk * (pre_ref[1] * column(inv_ref, 1, width))
    gaink_ref[...] = jnp.sum(prod, axis=0, keepdims=True)
    rk_ref[...] += prod * gk_ref[...]
    d_ref[2] = dv_acc[...]

    @pl.when(pl.program_id(0) == pl.num_programs(0) - 1)
    def _():
        stat_ref[...] = jnp.zeros_like(stat_ref)
        for i, ref in enumerate((rq_ref, rk_ref)):
            stat_ref[i : i + 1, :] = jnp.sum(ref[...].T, axis=0, keepdims=True)


def specs(tokens, text, width, heads, at=0):
    col = pl.BlockSpec((tokens, width), lambda i: (0, i + at))
    three = pl.BlockSpec((3, tokens, width), lambda i: (0, 0, i + at))
    tcol = pl.BlockSpec((text, width), lambda i: (0, i + at))
    stat = pl.BlockSpec((8, tokens), lambda i: (0, 0))
    gain = pl.BlockSpec((1, width), lambda i: (0, i + at))
    table = pl.BlockSpec((tokens, width), lambda i: (0, 0))
    lse = pl.BlockSpec((1, heads, tokens), lambda i: (i + at, 0, 0))
    scalar = pl.BlockSpec(memory_space=pltpu.SMEM)
    return col, three, tcol, stat, gain, table, lse, scalar


def sds(shape, dtype=F32):
    return jax.ShapeDtypeStruct(shape, dtype)


def attn_forward(length, pre, inv, gq, gk, cosine, sine, tk, tv, gate):
    _, tokens, columns = pre.shape
    text, width = tk.shape[0], cosine.shape[1]
    heads, blocks = width // HD, columns // width
    col, three, tcol, stat, gain, table, lse, scalar = specs(tokens, text, width, heads)
    flat = (tokens, columns)
    return pl.pallas_call(
        attn_fwd_kernel,
        grid=(blocks,),
        in_specs=[scalar, three, stat, gain, gain, table, table, tcol, tcol, gain],
        out_specs=[col, col, col, col, col, col, lse, lse],
        out_shape=[sds(flat, BF16)] * 4 + [sds(flat)] * 2 + [sds((blocks, heads, tokens))] * 2,
    )(length, pre, inv, gq, gk, cosine, sine, tk, tv, gate)


def attn_backward(at, blocks, length, q, k, v, tk, tv, g, so, co, ls, lc, pre, inv, gq, gk, cosine, sine, gate):
    tokens = q.shape[0]
    text, width = tk.shape[0], cosine.shape[1]
    heads, columns = width // HD, blocks * width
    col, three, tcol, stat, gain, table, lse, scalar = specs(tokens, text, width, heads, at)
    _, three_o, tcol_o, _, gain_o, _, _, _ = specs(tokens, text, width, heads)
    return pl.pallas_call(
        attn_bwd_kernel,
        grid=(blocks,),
        in_specs=[scalar, col, col, col, tcol, tcol, col, col, col, lse, lse,
                  three, stat, gain, gain, table, table, gain],
        out_specs=[three_o, tcol_o, tcol_o, stat, gain_o, gain_o, gain_o],
        out_shape=[
            sds((3, tokens, columns)), sds((text, columns)), sds((text, columns)),
            sds((8, tokens)), sds((1, columns)), sds((1, columns)), sds((1, columns)),
        ],
        scratch_shapes=[
            pltpu.VMEM((tokens, width), BF16), pltpu.VMEM((tokens, width), BF16),
            pltpu.VMEM((heads, tokens), F32), pltpu.VMEM((heads, tokens), F32),
            pltpu.VMEM((width, tokens), BF16), pltpu.VMEM((width, text), BF16),
            pltpu.VMEM((width, tokens), F32),
            pltpu.VMEM((tokens, width), F32), pltpu.VMEM((tokens, width), F32),
            pltpu.VMEM((tokens, width), F32), pltpu.VMEM((tokens, width), F32),
        ],
    )(length, q, k, v, tk, tv, g, so, co, ls, lc, pre, inv, gq, gk, cosine, sine, gate)


def pick(rows, cols, step, part):
    i = lax.broadcasted_iota(jnp.int32, (rows, cols), 0)
    j = lax.broadcasted_iota(jnp.int32, (rows, cols), 1)
    hit = (j == step * i + part) if cols > rows else (i == step * j + part)
    return jnp.where(hit, 1.0, 0.0).astype(BF16)

def text_fwd_kernel(x_ref, w_ref, o_ref):
    @pl.when(pl.program_id(0) == 0)
    def _():
        o_ref[...] = jnp.zeros_like(o_ref)
    for b in range(w_ref.shape[0] // 128):
        rows = slice(b * 128, (b + 1) * 128)
        w = w_ref[rows].reshape(256, w_ref.shape[2])
        x = x_ref[:, rows]
        for j in range(2):
            spread = dot(x, pick(128, 256, 2, j)).astype(BF16)
            o_ref[j] += dot(spread, w)

def text_fwd(x, w):
    depth, _, cols = w.shape
    bk = 256
    return pl.pallas_call(
        text_fwd_kernel, grid=(depth // bk,),
        in_specs=[pl.BlockSpec((x.shape[0], bk), lambda i: (0, i)), pl.BlockSpec((bk, 2, cols), lambda i: (i, 0, 0))],
        out_specs=pl.BlockSpec((2, x.shape[0], cols), lambda i: (0, 0, 0)),
        out_shape=sds((2, x.shape[0], cols)),
    )(x, w)

def text_bwd_kernel(g_ref, w_ref, pair_ref, o_ref, pair_out, sends, gets, own):
    me = lax.axis_index("dp")
    step = pl.program_id(0)
    copies = to_all(lambda peer: pair_ref.at[peer], pair_out.at[me], sends, gets)
    copies.append(pltpu.make_async_copy(pair_ref.at[me], pair_out.at[me], own))

    @pl.when(step == 0)
    def _():
        for copy in copies:
            copy.start()

    for b in range(w_ref.shape[0] // 128):
        rows = slice(b * 128, (b + 1) * 128)
        w = w_ref[rows].reshape(256, w_ref.shape[2])
        total = 0.0
        for j in range(2):
            total = total + dot(g_ref[j], dot(pick(128, 256, 2, j), w).astype(BF16), 1, 1)
        o_ref[:, rows] = total.astype(BF16)

    @pl.when(step == pl.num_programs(0) - 1)
    def _():
        for copy in copies:
            copy.wait()


def text_bwd(g, w, pair):
    depth, _, cols = w.shape
    bk = 256
    count = pair.shape[0]
    return pl.pallas_call(
        text_bwd_kernel,
        grid=(depth // bk,),
        in_specs=[
            pl.BlockSpec(g.shape, lambda i: (0, 0, 0)),
            pl.BlockSpec((bk, 2, cols), lambda i: (i, 0, 0)),
            pl.BlockSpec(memory_space=pl.ANY),
        ],
        out_specs=[
            pl.BlockSpec((g.shape[1], bk), lambda i: (0, i)), pl.BlockSpec(memory_space=pl.ANY),
        ],
        out_shape=[
            sds((g.shape[1], depth), BF16), jax.ShapeDtypeStruct(pair.shape, pair.dtype),
        ],
        scratch_shapes=[
            pltpu.SemaphoreType.DMA((count,)), pltpu.SemaphoreType.DMA((count,)),
            pltpu.SemaphoreType.DMA,
        ],
        compiler_params=pltpu.CompilerParams(has_side_effects=True),
    )(g, w, pair)


def put_relative(dst, src, me, f, count):
    rows = dst.shape[0] // count
    for p in range(count):
        start = pl.multiple_of((me ^ turned(p, f)) * rows, 16)
        dst[p * rows : (p + 1) * rows, :] = src[pl.ds(start, rows), :]


def put_halves(keep, send, value, count, order, slot=None):
    rows = value.shape[0] // count
    for p in range(count):
        place = place_of(p, order[1:])
        where = place if slot is None else (place, slot)
        (send if p >> order[0] & 1 else keep)[where] = value[p * rows : (p + 1) * rows]


def ffn_kernel(
    orders, id_ref, s_ref, b_ref, w_ref, d_ref,
    wk_ref, ws_ref, dk_ref, ds_ref, fo_ref, fp_ref, so_ref, sp_ref,
    st, bt, tmp, wg, wu, facc, sacc,
):
    step = pl.program_id(0)
    depth, _, cols = w_ref.shape
    own = fo_ref.shape[0]
    count = 2 * dk_ref.shape[0]

    @pl.when(step == 0)
    def _():
        for src, dst in ((s_ref, st), (b_ref, bt)):
            for c in range(depth // 256):
                part = slice(c * 256, (c + 1) * 256)
                tmp[part, :] = src[:, part].astype(F32).T.astype(BF16)
            put_relative(dst, tmp, id_ref[0], id_ref[1], count)
        facc[...] = jnp.zeros_like(facc)
        sacc[...] = jnp.zeros_like(sacc)

    for c in range(depth // 128):
        part = slice(c * 128, (c + 1) * 128)
        w = w_ref[part].reshape(256, cols)
        wg[part, :] = dot(pick(128, 256, 2, 0), w).astype(BF16)
        wu[part, :] = dot(pick(128, 256, 2, 1), w).astype(BF16)
    s, b = s_ref[...], b_ref[...]
    gate = dot(s, wg[...])
    up = dot(s, wu[...])
    back = dot(b, d_ref[...], 1, 1)
    sig = jax.nn.sigmoid(gate)
    silu = gate * sig
    hidden = (silu * up).astype(BF16)
    g_gate = (back * up * (sig + silu * (1.0 - sig))).astype(BF16)
    g_up = (back * silu).astype(BF16)
    put_halves(wk_ref, ws_ref, dot(st[...], g_gate).astype(BF16), count, orders[0], 0)
    put_halves(wk_ref, ws_ref, dot(st[...], g_up).astype(BF16), count, orders[0], 1)
    put_halves(dk_ref, ds_ref, dot(bt[...], hidden).astype(BF16), count, orders[1])
    facc[...] += dot(hidden, d_ref[...])
    sacc[...] += dot(g_gate, wg[...], 1, 1) + dot(g_up, wu[...], 1, 1)

    @pl.when(step == pl.num_programs(0) - 1)
    def _():
        fo_ref[...] = facc[:own]
        fp_ref[...] = facc[own:].astype(BF16)
        so_ref[...] = sacc[:own]
        sp_ref[...] = sacc[own:].astype(BF16)


def ffn(ids, s, b, w, d, local, dp, orders):
    tokens, depth = s.shape
    hid = d.shape[0]
    bc = min(256, hid)
    rest = tokens - local
    once = functools.partial(pl.BlockSpec, pipeline_mode=pl.Buffered(1))
    const = lambda i: (0, 0)
    share = depth // dp
    half = pl.BlockSpec((dp // 2, share, bc), lambda i: (0, 0, i))
    halves = pl.BlockSpec((dp // 2, 2, share, bc), lambda i: (0, 0, 0, i))
    return pl.pallas_call(
        functools.partial(ffn_kernel, orders),
        grid=(hid // bc,),
        in_specs=[
            pl.BlockSpec(memory_space=pltpu.SMEM),
            once((tokens, depth), const), once((tokens, depth), const),
            pl.BlockSpec((depth, 2, bc), lambda i: (0, 0, i)),
            pl.BlockSpec((bc, depth), lambda i: (i, 0)),
        ],
        out_specs=[halves] * 2 + [half] * 2 + [
            once((local, depth), const), once((rest, depth), const),
            once((local, depth), const), once((rest, depth), const),
        ],
        out_shape=[sds((dp // 2, 2, share, hid), BF16)] * 2 + [sds((dp // 2, share, hid), BF16)] * 2 + [
            sds((local, depth)), sds((rest, depth), BF16),
            sds((local, depth)), sds((rest, depth), BF16),
        ],
        scratch_shapes=[
            pltpu.VMEM((depth, tokens), BF16), pltpu.VMEM((depth, tokens), BF16),
            pltpu.VMEM((depth, tokens), BF16),
            pltpu.VMEM((depth, bc), BF16), pltpu.VMEM((depth, bc), BF16),
            pltpu.VMEM((tokens, depth), F32), pltpu.VMEM((tokens, depth), F32),
        ],
        compiler_params=pltpu.CompilerParams(vmem_limit_bytes=62 << 20),
    )(ids, s, b, w, d)


def project_kernel(id_ref, xo_ref, xp_ref, front_ref, w_ref, got_ref, first_ref, pre_ref, sq_ref):
    j = pl.program_id(0)
    local, depth = xo_ref.shape
    own = got_ref.shape[2]
    f = id_ref[1]

    @pl.when(j == 0)
    def _():
        for i, ref in enumerate((xo_ref, xp_ref)):
            x = ref[...].astype(F32)
            inv = lax.rsqrt(jnp.sum(x * x, axis=1, keepdims=True) * (1.0 / depth) + EPSILON)
            first_ref[i * local : (i + 1) * local, :] = (x * inv * front_ref[...]).astype(BF16)
        sq_ref[...] = jnp.zeros_like(sq_ref)

    mine = pl.ds(pl.multiple_of(f * own, 128), own)
    other = pl.ds(pl.multiple_of((1 - f) * own, 128), own)
    out = dot(first_ref[:, mine], w_ref[0, :, mine]) + dot(first_ref[:, other], got_ref[0])
    pre_ref[0] = out
    square = out * out
    part = square[:, :128]
    for c in range(1, own // 128):
        part = part + square[:, c * 128 : (c + 1) * 128]
    sq_ref[pl.ds(j, 1), :] = jnp.sum(part.T, axis=0, keepdims=True)


def project(ids, xo, xp, front, w, got):
    local, depth = xo.shape
    own = got.shape[2]
    tokens = 2 * local
    const = lambda j: (0, 0)
    return pl.pallas_call(
        project_kernel,
        grid=(3,),
        in_specs=[
            pl.BlockSpec(memory_space=pltpu.SMEM),
            pl.BlockSpec((local, depth), const), pl.BlockSpec((local, depth), const),
            pl.BlockSpec((1, depth), const),
            pl.BlockSpec((1, own, depth), lambda j: (j, 0, 0)),
            pl.BlockSpec((1, own, own), lambda j: (j, 0, 0)),
        ],
        out_specs=[
            pl.BlockSpec((tokens, depth), const),
            pl.BlockSpec((1, tokens, own), lambda j: (j, 0, 0)),
            pl.BlockSpec((8, tokens), const),
        ],
        out_shape=[sds((tokens, depth), BF16), sds((3, tokens, own)), sds((8, tokens))],
    )(ids, xo, xp, front, w, got)


def project_grad_kernel(
    order, id_ref, da_ref, db_ref, pre_ref, stat_ref, gain_ref, first_ref,
    keep_ref, send_ref, g_ref, gt, tmp,
):
    j = pl.program_id(0)
    own = pre_ref.shape[2]
    cut = da_ref.shape[2]
    count = 2 * keep_ref.shape[0]
    inv, mean = column(stat_ref, j, 128), column(stat_ref, j + 3, 128)
    for c in range(own // 128):
        part = slice(c * 128, (c + 1) * 128)
        here = slice(c * 128 - cut, (c + 1) * 128 - cut) if c * 128 >= cut else part
        d = (db_ref if c * 128 >= cut else da_ref)[0, :, here]
        g = inv * (d * gain_ref[0, :, part] - pre_ref[0, :, part] * inv * mean)
        tmp[part, :] = g.T.astype(BF16)
        g_ref[0, :, part] = g.astype(BF16)
    put_relative(gt, tmp, id_ref[0] % count, id_ref[1], count)
    put_halves(keep_ref, send_ref, dot(gt[...], first_ref[...]).astype(BF16), count, order, j)


def project_grad(ids, da, db, pre, stats, gain, first, dp, order):
    _, tokens, own = pre.shape
    depth = first.shape[1]
    share = depth // dp
    const = lambda j: (0, 0)
    block = lambda j: (j, 0, 0)
    once = functools.partial(pl.BlockSpec, pipeline_mode=pl.Buffered(1))
    half = once((dp // 4, 3, share, depth), lambda j: (0, 0, 0, 0))
    return pl.pallas_call(
        functools.partial(project_grad_kernel, order),
        grid=(3,),
        in_specs=[
            pl.BlockSpec(memory_space=pltpu.SMEM),
            pl.BlockSpec((1,) + da.shape[1:], block), pl.BlockSpec((1,) + db.shape[1:], block),
            pl.BlockSpec((1, tokens, own), block),
            pl.BlockSpec((8, tokens), const),
            pl.BlockSpec((1, 1, own), block),
            once((tokens, depth), const),
        ],
        out_specs=[half, half, pl.BlockSpec((1, tokens, own), block)],
        out_shape=[sds((dp // 4, 3, share, depth), BF16)] * 2
        + [sds((3, tokens, own), BF16)],
        scratch_shapes=[pltpu.VMEM((own, tokens), BF16), pltpu.VMEM((own, tokens), BF16)],
    )(ids, da, db, pre, stats, gain, first)


def project_back_kernel(id_ref, g_ref, w_ref, got_ref, own_ref, peer_ref, acc):
    j = pl.program_id(0)
    own = g_ref.shape[2]
    local = own_ref.shape[0]
    f = id_ref[1]
    mine = pl.ds(pl.multiple_of(f * own, 128), own)
    other = pl.ds(pl.multiple_of((1 - f) * own, 128), own)

    @pl.when(j == 0)
    def _():
        acc[...] = jnp.zeros_like(acc)

    acc[:, mine] += dot(g_ref[0], w_ref[0, :, mine], 1, 1)
    acc[:, other] += dot(g_ref[0], got_ref[0], 1, 1)

    @pl.when(j == 2)
    def _():
        own_ref[...] = acc[:local]
        peer_ref[...] = acc[local:].astype(BF16)


def project_back(ids, g, w, got):
    _, tokens, own = g.shape
    depth = w.shape[2]
    local = tokens // 2
    const = lambda j: (0, 0)
    block = lambda j: (j, 0, 0)
    once = functools.partial(pl.BlockSpec, pipeline_mode=pl.Buffered(1))
    return pl.pallas_call(
        project_back_kernel,
        grid=(3,),
        in_specs=[
            pl.BlockSpec(memory_space=pltpu.SMEM),
            pl.BlockSpec((1, tokens, own), block),
            pl.BlockSpec((1, own, depth), block), pl.BlockSpec((1, own, own), block),
        ],
        out_specs=[once((local, depth), const), once((local, depth), const)],
        out_shape=[sds((local, depth)), sds((local, depth), BF16)],
        scratch_shapes=[pltpu.VMEM((tokens, depth), F32)],
    )(ids, g, w, got)


def out_back_kernel(order, id_ref, *refs):
    n = len(refs) - 8
    blocks, (w_ref, mixed_ref, g_ref, keep_ref, send_ref, all_ref, gt, tmp) = refs[:n], refs[n:]
    local = blocks[0].shape[0]
    for r, ref in enumerate(blocks):
        all_ref[r * local : (r + 1) * local, :] = ref[...]
    grad = all_ref[...]
    g_ref[...] = dot(grad, w_ref[...], 1, 1)
    for c in range(grad.shape[1] // 256):
        part = slice(c * 256, (c + 1) * 256)
        tmp[part, :] = grad[:, part].astype(F32).T.astype(BF16)
    count = 2 * keep_ref.shape[0]
    put_relative(gt, tmp, id_ref[0], id_ref[1], count)
    put_halves(keep_ref, send_ref, dot(gt[...], mixed_ref[...]).astype(BF16), count, order)


def out_back(ids, blocks, w, mixed, dp, order):
    tokens, own = mixed.shape
    depth = w.shape[1]
    vmem = pl.BlockSpec(memory_space=pltpu.VMEM)
    half = sds((dp // 2, depth // dp, own), BF16)
    return pl.pallas_call(
        functools.partial(out_back_kernel, order),
        in_specs=[pl.BlockSpec(memory_space=pltpu.SMEM)] + [vmem] * (len(blocks) + 2),
        out_specs=[vmem] * 3,
        out_shape=[sds((tokens, own)), half, half],
        scratch_shapes=[
            pltpu.VMEM((tokens, depth), BF16),
            pltpu.VMEM((depth, tokens), BF16), pltpu.VMEM((depth, tokens), BF16),
        ],
    )(ids, *blocks, w, mixed)


def time_embed(timesteps):
    half = TE // 2
    frequencies = jnp.exp(-math.log(10000.0) * jnp.arange(half, dtype=F32) / half)
    angles = timesteps.astype(F32)[:, None] * frequencies
    waves = jnp.concatenate([jnp.cos(angles), jnp.sin(angles)], axis=-1)
    return jax.nn.silu(waves).astype(BF16)


def rope_tables(positions, width):
    lane = jnp.arange(width)
    quarter = HD // 4
    frequencies = 10000.0 ** (-(lane % quarter).astype(F32) / quarter)
    place = jnp.where(lane % HD < HD // 2, positions[0][:, None], positions[1][:, None])
    angles = place.astype(F32) * frequencies
    return jnp.cos(angles), jnp.where(lane % 32 < 16, -1.0, 1.0) * jnp.sin(angles)


def inverse_rms(values):
    return lax.rsqrt(jnp.mean(values * values, axis=-1, keepdims=True) + EPSILON)


def rms_back(grad_hat, normed, inverse):
    return inverse * (grad_hat - normed * jnp.mean(grad_hat * normed, axis=-1, keepdims=True))


def pad_cols(value, width):
    extra = -value.shape[-1] % width
    return value if extra == 0 else jnp.pad(value, [(0, 0)] * (value.ndim - 1) + [(0, extra)])


def on_device(
    hidden_in, text_state, caption_lengths, timesteps, patch_positions, cotangent,
    w_ada, w_text, w_qkv, w_out, gains, cross_gate, w_gate_up, w_down,
):
    n, f = lax.axis_size("fsdp"), lax.axis_index("fsdp")
    dpn, me = lax.axis_size("dp"), lax.axis_index("dp")
    bits = list(range(dp_bits()))
    low_bits = bits[:-1]
    late = bits[2:3] + bits[:2] + bits[3:]
    own_d = D // n
    local = hidden_in.shape[1]
    tokens = n * local
    width = 2 * HD
    share = D // dpn
    paired = n == 2 and dpn >= 4
    ids = jnp.stack([me, f]).astype(jnp.int32)
    x_bf, dy_bf = hidden_in[0], cotangent[0]

    time_low = time_embed(timesteps)
    own_te = TE // n
    time_own = lax.dynamic_slice_in_dim(time_low[0], f * own_te, own_te, 0)
    modulation = pair_sum(
        jnp.einsum("k,kjd->jd", time_own, w_ada, preferred_element_type=F32)
    )
    scale_attn, gate_attn = modulation[0:1], jnp.tanh(modulation[1:2])
    scale_ffn, gate_ffn = modulation[2:3], jnp.tanh(modulation[3:4])

    w_flat = jnp.moveaxis(w_qkv, 1, 0)
    w_parts = exchange_rot(w_flat, 2)
    x_parts = gather_rot(x_bf)
    dy_all = jnp.concatenate(gather_rot(dy_bf), axis=0)
    places = jnp.concatenate(gather_rot(patch_positions[0]), axis=1)
    text_cols = jnp.concatenate(natural(exchange_rot(text_state[0], 1)), axis=0)
    text_all = lax.all_gather(text_cols, "dp", axis=0, tiled=True)
    gain_full = lax.all_gather(gains, "fsdp", axis=1, tiled=True).astype(F32)
    gain_own = gains.astype(F32)

    front = gain_full[0] * (1.0 + scale_attn)
    if paired:
        first_all, pre, squares = project(ids, *x_parts, front, w_flat, w_parts[1])
    else:
        w_heads = jnp.concatenate(natural(w_parts), axis=1)
        x_f = jnp.concatenate(x_parts, axis=0).astype(F32)
        first_all = (x_f * inverse_rms(x_f) * front).astype(BF16)
        pre = jnp.stack([dot(first_all, w_heads[j]) for j in range(3)])
        squares = jnp.pad(jnp.sum(pre[:2] * pre[:2], -1), ((0, 6), (0, 0)))
    inverse = lax.rsqrt(row_sum(squares) / D + EPSILON)

    text_part = text_fwd(text_cols, w_text)
    text_pre = scatter_rot(rot_blocks(text_part, 2))
    inv_t = lax.rsqrt(
        pair_sum(jnp.sum(text_pre[0] * text_pre[0], -1, keepdims=True)) / D + EPSILON
    )
    normed_t = text_pre[0] * inv_t
    tk = (normed_t * gain_own[4]).astype(BF16)
    tv = text_pre[1].astype(BF16)

    head_tanh = jnp.tanh(cross_gate.astype(F32))
    gate_row = pad_cols(jnp.repeat(head_tanh, HD)[None], width)
    cosine, sine = rope_tables(places, width)
    gq, gk = pad_cols(gain_own[2:3], width), pad_cols(gain_own[3:4], width)
    pre_p, tkp, tvp = pad_cols(pre, width), pad_cols(tk, width), pad_cols(tv, width)
    q, k, v, mixed_p, so, co, ls, lc = attn_forward(
        caption_lengths, pre_p, inverse, gq, gk, cosine, sine, tkp, tvp, gate_row
    )
    mixed = mixed_p[:, :own_d]

    def rows(value, r):
        return value[r * local : (r + 1) * local]

    parts = [dot(rows(mixed, r), w_out) for r in range(n)]
    attn_branch = scatter_rot([parts[0]] + [p.astype(BF16) for p in parts[1:]])
    x_own = x_bf.astype(F32)
    after_attn = x_own + gate_attn * attn_branch
    inverse_two = inverse_rms(after_attn)
    normed_two = after_attn * inverse_two
    second = (normed_two * gain_full[1] * (1.0 + scale_ffn)).astype(BF16)

    second_all = jnp.concatenate(gather_rot(second), axis=0)
    branch_all = (gate_ffn * dy_all.astype(F32)).astype(BF16)
    wide_keep, wide_send, down_keep, down_send, ffn_own, ffn_rest, back_own, back_rest = ffn(
        ids, second_all, branch_all, w_gate_up, w_down, local, dpn, (bits, late)
    )
    (ffn_own, ffn_rest, back_own, back_rest), text_all = lax.optimization_barrier(
        ((ffn_own, ffn_rest, back_own, back_rest), text_all)
    )
    wide_chain = Halving(bits, wide_keep, wide_send)
    down_chain = Halving(late, down_keep, down_send)
    grad_second = scatter_rot([back_own] + [rows(back_rest, r) for r in range(n - 1)])
    ffn_branch = scatter_rot([ffn_own] + [rows(ffn_rest, r) for r in range(n - 1)])
    output = (after_attn + gate_ffn * ffn_branch).astype(BF16)
    dy = dy_bf.astype(F32)
    d_gate_ffn = jnp.sum(dy * ffn_branch, axis=0) * (1.0 - gate_ffn[0] * gate_ffn[0])

    scaled = grad_second * normed_two
    d_scale_ffn = jnp.sum(scaled * gain_full[1], axis=0)
    gain_two = jnp.sum(scaled * (1.0 + scale_ffn), axis=0)
    grad_after = dy + rms_back(
        grad_second * gain_full[1] * (1.0 + scale_ffn), normed_two, inverse_two
    )
    d_gate_attn = jnp.sum(grad_after * attn_branch, axis=0) * (1.0 - gate_attn[0] * gate_attn[0])
    grad_attn = (gate_attn * grad_after).astype(BF16)
    grad_mixed, *out_halves = out_back(ids, gather_rot(grad_attn), w_out, mixed, dpn, bits)
    out_chain = Halving(bits, *out_halves)
    blocks = pre_p.shape[2] // width
    cut = max(1, 2 * blocks // 3)
    grad_mixed = pad_cols(grad_mixed, width)
    inputs = (so, co, ls, lc, pre_p, inverse, gq, gk, cosine, sine, gate_row)
    part_a = attn_backward(0, cut, caption_lengths, q, k, v, tkp, tvp, grad_mixed, *inputs)
    part_a, grad_mixed = lax.optimization_barrier((part_a, grad_mixed))
    grad_mixed = advance([wide_chain, down_chain], grad_mixed)
    part_b = attn_backward(
        cut, blocks - cut, caption_lengths, q, k, v, tkp, tvp, grad_mixed, *inputs
    )
    means = row_sum(part_a[3] + part_b[3])[:2] / D

    ones, zeros = jnp.ones((1, tokens), F32), jnp.zeros((1, tokens), F32)
    if paired:
        stats = jnp.concatenate([inverse[:2], ones, means, zeros, zeros, zeros], axis=0)
        gain3 = jnp.stack([gain_own[2:3], gain_own[3:4], jnp.ones_like(gain_own[2:3])])
        keep, send, grads = project_grad(
            ids, part_a[0], part_b[0], pre, stats, gain3, first_all, dpn, low_bits
        )
        part_a, part_b, grads = advance(
            [wide_chain, down_chain], (part_a[1:], part_b[1:], grads)
        )
        qkv_chain = Halving(low_bits, keep, send)
        parts = project_back(ids, grads, w_flat, w_parts[1])
    else:
        d = jnp.concatenate([part_a[0], part_b[0]], axis=2)[:, :, :own_d]
        part_a, part_b = part_a[1:], part_b[1:]
        inv, mean = inverse[:2, :, None], means[:, :, None]
        hat = d[:2] * gain_own[2:4][:, None] - pre[:2] * inv * mean
        grads = [(inv[0] * hat[0]).astype(BF16), (inv[1] * hat[1]).astype(BF16), d[2].astype(BF16)]
        wide = [dot(g, first_all, 0, 0).astype(BF16) for g in grads]
        wide = [jnp.concatenate(natural(exchange_rot(w_, 1)), axis=0) for w_ in wide]
        wide = relative(jnp.stack([w_.reshape(dpn, share, own_d) for w_ in wide], axis=1))
        wide = jnp.stack([wide[p] for p in sorted(range(dpn), key=lambda p: place_of(p, bits))])
        qkv_chain = Halving(bits, wide[: dpn // 2], wide[dpn // 2 :])
        parts = [
            sum(dot(rows(g, r), w_heads[j], 1, 1) for j, g in enumerate(grads)) for r in range(n)
        ]
        parts = [parts[0]] + [p.astype(BF16) for p in parts[1:]]
    grad_first = scatter_rot(parts)

    dtk, dtv, gain_q, gain_k, gate_g = (
        jnp.concatenate([part_a[i], part_b[i]], axis=1)[:, :own_d] for i in (0, 1, 3, 4, 5)
    )
    text_hat = dtk * gain_own[4]
    gain_text = jnp.sum(dtk * normed_t, axis=0, keepdims=True)
    mean_t = pair_sum(jnp.sum(text_hat * normed_t, -1, keepdims=True)) / D
    grad_tk = (inv_t * (text_hat - normed_t * mean_t)).astype(BF16)
    text_pair = jnp.stack([grad_tk, dtv.astype(BF16)])
    pair_all = jnp.concatenate(natural(gather_rot(text_pair)), axis=-1)
    outgoing = block_of(pair_all.transpose(0, 2, 1), f, 2)
    outgoing = outgoing.reshape(2, dpn, share, TEXT // n).transpose(1, 0, 2, 3)
    pair_all, outgoing = settle(
        [qkv_chain, wide_chain, down_chain, out_chain], (pair_all, outgoing)
    )
    for chain in (qkv_chain, down_chain, out_chain):
        chain.step()
    text_in, pair_cols = text_bwd(pair_all, w_text, outgoing)
    text_in, grad_first = advance(
        [qkv_chain, wide_chain, down_chain, out_chain], (text_in, grad_first)
    )
    pair_cols, qkv_chain.keep = lax.optimization_barrier((pair_cols, qkv_chain.keep))
    text_in = jnp.concatenate(natural(exchange_rot(text_in, 0)), axis=1)

    inverse_one = inverse_rms(x_own)
    normed_one = x_own * inverse_one
    scaled = grad_first * normed_one
    d_scale_attn = jnp.sum(scaled * gain_full[0], axis=0)
    gain_one = jnp.sum(scaled * (1.0 + scale_attn), axis=0)
    grad_input = (
        grad_after
        + rms_back(grad_first * gain_full[0] * (1.0 + scale_attn), normed_one, inverse_one)
    ).astype(BF16)


    sums = [d_scale_attn, d_gate_attn, d_scale_ffn, d_gate_ffn, gain_one, gain_two]
    sums = pair_sum(jnp.stack(sums))
    stamp = jnp.full((1, D), timesteps[0].astype(F32))
    small = jnp.concatenate([block_of(sums[4:], f, 1), gain_q, gain_k, gain_text, gate_g], axis=0)
    small = jnp.pad(small.reshape(-1), (0, dpn * SUMS * 128 - small.size))
    mods = jnp.concatenate([sums[:4], stamp], axis=0).reshape(5, dpn, share).transpose(1, 0, 2)
    mods = jnp.pad(mods, ((0, 0), (0, 0), (0, -share % 128)))
    mods = jnp.concatenate([mods, small.reshape(dpn, SUMS, 128)], axis=1)
    pair_cols = jnp.concatenate(natural(gather_rot(pair_cols)), axis=3)
    pair_cols = pair_cols.transpose(1, 2, 0, 3).reshape(2 * share, dpn * TEXT)
    text_grad = dot(pair_cols, text_all).reshape(2, share, TW // n)
    mods, text_grad = settle([wide_chain], (mods, text_grad))
    if paired:
        mods = advance([qkv_chain, out_chain], mods)
        own_side = f == (me >> low_bits[-1] + 1)
        mine, got = exchange_rot(qkv_chain.last[0].astype(BF16), 2)
        keep, send = jnp.where(own_side, mine, got)[None], jnp.where(own_side, got, mine)[None]
        mods, keep, send = lax.optimization_barrier((mods, keep, send))
        qkv_chain = Halving(bits[-1:], keep, send)
    mods, small = small_exchange(mods)
    mods = settle([qkv_chain, out_chain], mods)
    total = small[:, 5 : 5 + SUMS].reshape(-1)[: 6 * own_d].reshape(6, own_d)
    gate_total = jnp.sum(total[5].reshape(HEADS // n, HD), axis=1) * (
        1.0 - head_tanh * head_tanh
    )
    times = time_embed(mods[:, 4, 0])
    times = lax.dynamic_slice_in_dim(times, f * own_te, own_te, 1).astype(F32)
    ada_grad = lax.dot_general(
        mods[:, :4, :share].reshape(dpn, 4 * share), times, (((0,), (0,)), ((), ())),
        precision=lax.Precision.HIGHEST,
    ).reshape(4, share, own_te)

    for chain in (out_chain, down_chain, wide_chain, qkv_chain):
        while chain.got is not None:
            chain.step()
    return (
        output[None],
        grad_input[None],
        text_in[None],
        ada_grad.transpose(2, 0, 1),
        text_grad.transpose(2, 0, 1),
        qkv_chain.last[0].transpose(2, 0, 1),
        out_chain.last[0].T,
        total[:5],
        gate_total,
        wide_chain.last[0].transpose(1, 0, 2),
        down_chain.last[0].T,
    )


def solution(mesh):
    return jax.shard_map(
        on_device,
        mesh=mesh,
        in_specs=(
            P("dp", "fsdp", None),
            P("dp", "fsdp", None),
            P("dp"),
            P("dp"),
            P("dp", None, "fsdp"),
            P("dp", "fsdp", None),
            P("fsdp", None, None),
            P("fsdp", None, None),
            P("fsdp", None, None),
            P("fsdp", None),
            P(None, "fsdp"),
            P("fsdp"),
            P(None, None, "fsdp"),
            P("fsdp", None),
        ),
        out_specs=(
            P("dp", "fsdp", None),
            P("dp", "fsdp", None),
            P("dp", "fsdp", None),
            P("fsdp", None, "dp"),
            P("fsdp", None, "dp"),
            P("fsdp", None, "dp"),
            P("fsdp", "dp"),
            P(None, "fsdp"),
            P("fsdp"),
            P("dp", None, "fsdp"),
            P("fsdp", "dp"),
        ),
        check_vma=False,
    )
```

```python
import functools
import math

import jax
import jax.numpy as jnp
from jax import lax
from jax.experimental import pallas as pl
from jax.experimental.pallas import tpu as pltpu
from jax.sharding import PartitionSpec as P

D = 1536
HEADS = 24
HD = 64
TW = 4096
TE = 1024
PATCHES = 1024
TEXT = 256
EPSILON = 1e-06
F32 = jnp.float32
BF16 = jnp.bfloat16
QC = 256


def dot(a, b, ca=1, cb=0):
    return lax.dot_general(a, b, (((ca,), (cb,)), ((), ())), preferred_element_type=F32)


def from_behind(value, step):
    n = lax.axis_size("fsdp")
    return lax.ppermute(value, "fsdp", [(i, (i + step) % n) for i in range(n)])


def gather_rot(value):
    return [value] + [from_behind(value, r) for r in range(1, lax.axis_size("fsdp"))]


def pair_sum(value):
    return functools.reduce(lambda a, b: a + b, gather_rot(value))


def row_sum(value):
    n = lax.axis_size("fsdp")
    rows = value.shape[-1] // n
    total = value
    for r in range(1, n):
        total = total + jnp.roll(from_behind(value, r), r * rows, axis=-1)
    return total


def scatter_rot(blocks):
    n = lax.axis_size("fsdp")
    total = blocks[0].astype(F32)
    for r in range(1, n):
        got = lax.ppermute(blocks[r], "fsdp", [(i, (i - r) % n) for i in range(n)])
        total = total + got.astype(F32)
    return total


def block_of(value, index, axis):
    size = value.shape[axis] // lax.axis_size("fsdp")
    return lax.dynamic_slice_in_dim(value, index * size, size, axis)


def rot_blocks(value, axis):
    n, f = lax.axis_size("fsdp"), lax.axis_index("fsdp")
    return [block_of(value, (f - r) % n, axis) for r in range(n)]


def exchange_rot(value, axis):
    n, f = lax.axis_size("fsdp"), lax.axis_index("fsdp")
    out = [block_of(value, f, axis)]
    for r in range(1, n):
        out.append(from_behind(block_of(value, (f + r) % n, axis), r))
    return out


def natural(got):
    n, f = lax.axis_size("fsdp"), lax.axis_index("fsdp")
    if n == 2:
        return [jnp.where(f == 0, got[0], got[1]), jnp.where(f == 0, got[1], got[0])]
    got = jnp.stack(got)
    return [lax.dynamic_index_in_dim(got, (f - g) % n, 0, keepdims=False) for g in range(n)]


def dp_bits():
    return int(lax.axis_size("dp")).bit_length() - 1


def swapped(p):
    return (p & ~3) | ((p & 1) << 1) | ((p >> 1) & 1)


def turned(p, f):
    return p if dp_bits() < 3 else jnp.where(f % 2 == 0, p, swapped(p))


def dp_swap(value, bit):
    n, dpn = lax.axis_size("fsdp"), lax.axis_size("dp")
    pairs = []
    for i in range(dpn):
        for f in range(n):
            flip = 1 << bit if dp_bits() < 3 or f % 2 == 0 else swapped(1 << bit)
            pairs.append((i * n + f, (i ^ flip) * n + f))
    return lax.ppermute(value, ("dp", "fsdp"), pairs)


def relative(value):
    places = turned(jnp.arange(lax.axis_size("dp")), lax.axis_index("fsdp"))
    return jnp.take(value, lax.axis_index("dp") ^ places, axis=0)


class Halving:
    def __init__(self, order, keep, send):
        self.order = list(order)
        self.keep, self.got = keep, dp_swap(send, self.order.pop(0))

    def step(self):
        if self.got is None:
            return

        def add(part):
            return self.keep[part].astype(F32) + self.got[part].astype(F32)

        if not self.order:
            self.last = add(slice(None))
            self.got = None
            return
        half = self.keep.shape[0] // 2
        send = add(slice(half, None)).astype(BF16)
        self.keep = add(slice(half)).astype(BF16)
        self.got = dp_swap(send, self.order.pop(0))


def place_of(p, order):
    return sum((p >> bit & 1) << i for i, bit in enumerate(reversed(order)))


SUMS = 3


def swap_all_kernel(text_ref, mod_ref, text_out, mod_out, sum_out, part, sends, gets, own):
    dpn, me = lax.axis_size("dp"), lax.axis_index("dp")

    def to_all(kind, source, target):
        copies = []
        for r in range(1, dpn):
            peer = me ^ r
            copies.append(
                pltpu.make_async_remote_copy(
                    src_ref=source(peer), dst_ref=target,
                    send_sem=sends.at[kind, r], recv_sem=gets.at[kind, r],
                    device_id={"dp": peer}, device_id_type=pl.DeviceIdType.MESH,
                )
            )
            copies[-1].start()
        return copies

    mods = to_all(0, lambda peer: mod_ref.at[peer], mod_out.at[me])
    texts = to_all(1, lambda peer: text_ref.at[peer], text_out.at[me])
    local = (
        pltpu.make_async_copy(text_ref.at[me], text_out.at[me], own.at[0]),
        pltpu.make_async_copy(mod_ref.at[me], mod_out.at[me], own.at[1]),
    )
    for copy in local:
        copy.start()
    for copy in (*local, *mods):
        copy.wait()
    part[...] = jnp.sum(mod_out[...], axis=0)
    sums = to_all(2, lambda peer: part, sum_out.at[me])
    mine = pltpu.make_async_copy(part, sum_out.at[me], own.at[2])
    mine.start()
    for copy in (mine, *sums, *texts):
        copy.wait()


def swap_all(text, mods):
    vmem = pl.BlockSpec(memory_space=pltpu.VMEM)
    count = text.shape[0]
    return pl.pallas_call(
        swap_all_kernel,
        in_specs=[vmem] * 2,
        out_specs=[vmem] * 3,
        out_shape=[
            jax.ShapeDtypeStruct(v.shape, v.dtype) for v in (text, mods, mods)
        ],
        scratch_shapes=[
            pltpu.VMEM(mods.shape[1:], mods.dtype),
            pltpu.SemaphoreType.DMA((3, count)), pltpu.SemaphoreType.DMA((3, count)),
            pltpu.SemaphoreType.DMA((3,)),
        ],
        compiler_params=pltpu.CompilerParams(has_side_effects=True),
    )(text, mods)


def settle(chains, value):
    live = [c for c in chains if c.got is not None]
    value, got = lax.optimization_barrier((value, [c.got for c in live]))
    for c, g in zip(live, got):
        c.got = g
    return value


def advance(chains, value):
    value = settle(chains, value)
    for c in chains:
        c.step()
    return value


def rope_block(value, cosine, sine, sign):
    width = value.shape[1]
    lane = lax.broadcasted_iota(jnp.int32, value.shape, 1)
    partner = jnp.where(
        lane % 32 < 16, pltpu.roll(value, width - 16, 1), pltpu.roll(value, 16, 1)
    )
    return value * cosine + sign * (partner * sine)


def column(ref, index, width):
    row = ref[index : index + 1, :] if isinstance(index, int) else ref[pl.ds(index, 1), :]
    return jnp.broadcast_to(row, (width, row.shape[1])).T


def masked(value, head):
    lane = lax.broadcasted_iota(jnp.int32, value.shape, 1)
    return jnp.where(lane // HD == head, value, jnp.zeros_like(value))


def attn_fwd_kernel(
    len_ref, pre_ref, inv_ref, gq_ref, gk_ref, cos_ref, sin_ref, tk_ref, tv_ref, gate_ref,
    q_ref, k_ref, v_ref, mixed_ref, so_ref, co_ref, ls_ref, lc_ref,
):
    _, tokens, width = pre_ref.shape
    heads = width // HD
    iq, ik = column(inv_ref, 0, width), column(inv_ref, 1, width)
    q = rope_block(pre_ref[0] * iq * gq_ref[...], cos_ref[...], sin_ref[...], 1.0)
    q_ref[...] = q.astype(BF16)
    k = rope_block(pre_ref[1] * ik * gk_ref[...], cos_ref[...], sin_ref[...], 1.0)
    k_ref[...] = k.astype(BF16)
    v_ref[...] = pre_ref[2].astype(BF16)
    length = len_ref[0]

    def one(keys, values, qm, limit):
        s = dot(qm, keys, 1, 1)
        if limit is not None:
            slot = lax.broadcasted_iota(jnp.int32, s.shape, 1)
            s = jnp.where(slot < limit, s, -1e30)
        peak = jnp.max(s, axis=1, keepdims=True)
        e = jnp.exp(s - peak)
        total = jnp.sum(e, axis=1, keepdims=True)
        o = dot(e.astype(BF16), values)
        return o * (1.0 / total), peak + jnp.log(total)

    lane = lax.broadcasted_iota(jnp.int32, (tokens, width), 1)
    qs = q_ref[...] * jnp.asarray(HD**-0.5, BF16)
    so = co = stats = jnp.zeros((tokens, width), F32)
    for h in range(heads):
        qm = masked(qs, h)
        o, lse = one(k_ref[...], v_ref[...], qm, None)
        so = jnp.where(lane // HD == h, o, so)
        stats = jnp.where(lane == h, lse, stats)
        o, lse = one(tk_ref[...], tv_ref[...], qm, length)
        co = jnp.where(lane // HD == h, o, co)
        stats = jnp.where(lane == heads + h, lse, stats)
    so_ref[...] = so
    co_ref[...] = co
    mixed_ref[...] = (so + gate_ref[...] * co).astype(BF16)
    stats = stats.T
    ls_ref[0] = stats[:heads]
    lc_ref[0] = stats[heads : 2 * heads]


def attn_bwd_kernel(
    len_ref, q_ref, k_ref, v_ref, tk_ref, tv_ref, g_ref, so_ref, co_ref, ls_ref, lc_ref,
    pre_ref, inv_ref, gq_ref, gk_ref, cos_ref, sin_ref, gate_ref,
    d_ref, dtk_ref, dtv_ref, stat_ref, gainq_ref, gaink_ref, gateg_ref,
    gs_ref, gc_ref, ds_ref, dc_ref, kt_ref, tkt_ref, dqt_ref, dk_acc, dv_acc, rq_ref, rk_ref,
):
    tokens, width = q_ref.shape
    heads = width // HD
    scale = jnp.asarray(HD**-0.5, BF16)

    @pl.when(pl.program_id(0) == 0)
    def _():
        rq_ref[...] = jnp.zeros_like(rq_ref)
        rk_ref[...] = jnp.zeros_like(rk_ref)

    g = g_ref[...]
    gs_ref[...] = g.astype(BF16)
    gc_ref[...] = (g * gate_ref[...]).astype(BF16)
    prod_c = g * co_ref[...]
    gateg_ref[...] = jnp.sum(prod_c, axis=0, keepdims=True)
    prod_s = (g * so_ref[...]).T
    prod_c = (prod_c * gate_ref[...]).T
    for h in range(heads):
        ds_ref[h : h + 1, :] = jnp.sum(prod_s[h * HD : (h + 1) * HD], axis=0, keepdims=True)
        dc_ref[h : h + 1, :] = jnp.sum(prod_c[h * HD : (h + 1) * HD], axis=0, keepdims=True)
    kt_ref[...] = k_ref[...].astype(F32).T.astype(BF16)
    tkt_ref[...] = tk_ref[...].astype(F32).T.astype(BF16)
    dk_acc[...] = jnp.zeros_like(dk_acc)
    dv_acc[...] = jnp.zeros_like(dv_acc)
    dtk_ref[...] = jnp.zeros_like(dtk_ref)
    dtv_ref[...] = jnp.zeros_like(dtv_ref)
    length = len_ref[0]

    def one(keys, keys_t, values, qm, gm, lse, delta, head, limit):
        s = dot(keys, qm, 1, 1)
        p = jnp.exp(s - lse)
        if limit is not None:
            slot = lax.broadcasted_iota(jnp.int32, s.shape, 0)
            p = jnp.where(slot < limit, p, 0.0)
        dp = dot(values, gm, 1, 1)
        ds = (p * (dp - delta)).astype(BF16)
        dq = dot(keys_t[head * HD : (head + 1) * HD, :], ds)
        return dq, dot(ds, qm), dot(p.astype(BF16), gm)

    def chunk(c, carry):
        rows = pl.ds(pl.multiple_of(c * QC, QC), QC)
        qc = q_ref[rows, :] * scale
        for h in range(heads):
            qm = masked(qc, h)
            dq, dk, dv = one(
                k_ref[...], kt_ref, v_ref[...], qm, masked(gs_ref[rows, :], h),
                ls_ref[0, h : h + 1, rows], ds_ref[h : h + 1, rows], h, None,
            )
            dk_acc[...] += dk
            dv_acc[...] += dv
            dq2, dk, dv = one(
                tk_ref[...], tkt_ref, tv_ref[...], qm, masked(gc_ref[rows, :], h),
                lc_ref[0, h : h + 1, rows], dc_ref[h : h + 1, rows], h, length,
            )
            dtk_ref[...] += dk
            dtv_ref[...] += dv
            dqt_ref[h * HD : (h + 1) * HD, rows] = (dq + dq2) * HD**-0.5
        return carry

    lax.fori_loop(0, tokens // QC, chunk, 0)
    dq = rope_block(dqt_ref[...].T, cos_ref[...], sin_ref[...], -1.0)
    d_ref[0] = dq
    prod = dq * (pre_ref[0] * column(inv_ref, 0, width))
    gainq_ref[...] = jnp.sum(prod, axis=0, keepdims=True)
    rq_ref[...] += prod * gq_ref[...]
    dk = rope_block(dk_acc[...], cos_ref[...], sin_ref[...], -1.0)
    d_ref[1] = dk
    prod = dk * (pre_ref[1] * column(inv_ref, 1, width))
    gaink_ref[...] = jnp.sum(prod, axis=0, keepdims=True)
    rk_ref[...] += prod * gk_ref[...]
    d_ref[2] = dv_acc[...]

    @pl.when(pl.program_id(0) == pl.num_programs(0) - 1)
    def _():
        stat_ref[...] = jnp.zeros_like(stat_ref)
        for i, ref in enumerate((rq_ref, rk_ref)):
            stat_ref[i : i + 1, :] = jnp.sum(ref[...].T, axis=0, keepdims=True)


def specs(tokens, text, width, heads, at=0):
    col = pl.BlockSpec((tokens, width), lambda i: (0, i + at))
    three = pl.BlockSpec((3, tokens, width), lambda i: (0, 0, i + at))
    tcol = pl.BlockSpec((text, width), lambda i: (0, i + at))
    stat = pl.BlockSpec((8, tokens), lambda i: (0, 0))
    gain = pl.BlockSpec((1, width), lambda i: (0, i + at))
    table = pl.BlockSpec((tokens, width), lambda i: (0, 0))
    lse = pl.BlockSpec((1, heads, tokens), lambda i: (i + at, 0, 0))
    scalar = pl.BlockSpec(memory_space=pltpu.SMEM)
    return col, three, tcol, stat, gain, table, lse, scalar


def sds(shape, dtype=F32):
    return jax.ShapeDtypeStruct(shape, dtype)


def attn_forward(length, pre, inv, gq, gk, cosine, sine, tk, tv, gate):
    _, tokens, columns = pre.shape
    text, width = tk.shape[0], cosine.shape[1]
    heads, blocks = width // HD, columns // width
    col, three, tcol, stat, gain, table, lse, scalar = specs(tokens, text, width, heads)
    flat = (tokens, columns)
    return pl.pallas_call(
        attn_fwd_kernel,
        grid=(blocks,),
        in_specs=[scalar, three, stat, gain, gain, table, table, tcol, tcol, gain],
        out_specs=[col, col, col, col, col, col, lse, lse],
        out_shape=[sds(flat, BF16)] * 4 + [sds(flat)] * 2 + [sds((blocks, heads, tokens))] * 2,
    )(length, pre, inv, gq, gk, cosine, sine, tk, tv, gate)


def attn_backward(at, blocks, length, q, k, v, tk, tv, g, so, co, ls, lc, pre, inv, gq, gk, cosine, sine, gate):
    tokens = q.shape[0]
    text, width = tk.shape[0], cosine.shape[1]
    heads, columns = width // HD, blocks * width
    col, three, tcol, stat, gain, table, lse, scalar = specs(tokens, text, width, heads, at)
    _, three_o, tcol_o, _, gain_o, _, _, _ = specs(tokens, text, width, heads)
    return pl.pallas_call(
        attn_bwd_kernel,
        grid=(blocks,),
        in_specs=[scalar, col, col, col, tcol, tcol, col, col, col, lse, lse,
                  three, stat, gain, gain, table, table, gain],
        out_specs=[three_o, tcol_o, tcol_o, stat, gain_o, gain_o, gain_o],
        out_shape=[
            sds((3, tokens, columns)), sds((text, columns)), sds((text, columns)),
            sds((8, tokens)), sds((1, columns)), sds((1, columns)), sds((1, columns)),
        ],
        scratch_shapes=[
            pltpu.VMEM((tokens, width), BF16), pltpu.VMEM((tokens, width), BF16),
            pltpu.VMEM((heads, tokens), F32), pltpu.VMEM((heads, tokens), F32),
            pltpu.VMEM((width, tokens), BF16), pltpu.VMEM((width, text), BF16),
            pltpu.VMEM((width, tokens), F32),
            pltpu.VMEM((tokens, width), F32), pltpu.VMEM((tokens, width), F32),
            pltpu.VMEM((tokens, width), F32), pltpu.VMEM((tokens, width), F32),
        ],
    )(length, q, k, v, tk, tv, g, so, co, ls, lc, pre, inv, gq, gk, cosine, sine, gate)


def pick(rows, cols, step, part):
    i = lax.broadcasted_iota(jnp.int32, (rows, cols), 0)
    j = lax.broadcasted_iota(jnp.int32, (rows, cols), 1)
    hit = (j == step * i + part) if cols > rows else (i == step * j + part)
    return jnp.where(hit, 1.0, 0.0).astype(BF16)

def text_fwd_kernel(x_ref, w_ref, o_ref):
    @pl.when(pl.program_id(0) == 0)
    def _():
        o_ref[...] = jnp.zeros_like(o_ref)
    for b in range(w_ref.shape[0] // 128):
        rows = slice(b * 128, (b + 1) * 128)
        w = w_ref[rows].reshape(256, w_ref.shape[2])
        x = x_ref[:, rows]
        for j in range(2):
            spread = dot(x, pick(128, 256, 2, j)).astype(BF16)
            o_ref[j] += dot(spread, w)

def text_fwd(x, w):
    depth, _, cols = w.shape
    bk = 256
    return pl.pallas_call(
        text_fwd_kernel, grid=(depth // bk,),
        in_specs=[pl.BlockSpec((x.shape[0], bk), lambda i: (0, i)), pl.BlockSpec((bk, 2, cols), lambda i: (i, 0, 0))],
        out_specs=pl.BlockSpec((2, x.shape[0], cols), lambda i: (0, 0, 0)),
        out_shape=sds((2, x.shape[0], cols)),
    )(x, w)

def text_bwd_kernel(g_ref, w_ref, o_ref):
    for b in range(w_ref.shape[0] // 128):
        rows = slice(b * 128, (b + 1) * 128)
        w = w_ref[rows].reshape(256, w_ref.shape[2])
        total = 0.0
        for j in range(2):
            total = total + dot(g_ref[j], dot(pick(128, 256, 2, j), w).astype(BF16), 1, 1)
        o_ref[:, rows] = total.astype(BF16)

def text_bwd(g, w):
    depth, _, cols = w.shape
    bk = 256
    return pl.pallas_call(
        text_bwd_kernel, grid=(depth // bk,),
        in_specs=[pl.BlockSpec(g.shape, lambda i: (0, 0, 0)), pl.BlockSpec((bk, 2, cols), lambda i: (i, 0, 0))],
        out_specs=pl.BlockSpec((g.shape[1], bk), lambda i: (0, i)),
        out_shape=sds((g.shape[1], depth), BF16),
    )(g, w)

def put_relative(dst, src, me, f, count):
    rows = dst.shape[0] // count
    for p in range(count):
        start = pl.multiple_of((me ^ turned(p, f)) * rows, 16)
        dst[p * rows : (p + 1) * rows, :] = src[pl.ds(start, rows), :]


def put_halves(keep, send, value, count, order, slot=None):
    rows = value.shape[0] // count
    for p in range(count):
        place = place_of(p, order[1:])
        where = place if slot is None else (place, slot)
        (send if p >> order[0] & 1 else keep)[where] = value[p * rows : (p + 1) * rows]


def ffn_kernel(
    orders, id_ref, s_ref, b_ref, w_ref, d_ref,
    wk_ref, ws_ref, dk_ref, ds_ref, fo_ref, fp_ref, so_ref, sp_ref,
    st, bt, tmp, wg, wu, facc, sacc,
):
    step = pl.program_id(0)
    depth, _, cols = w_ref.shape
    own = fo_ref.shape[0]
    count = 2 * dk_ref.shape[0]

    @pl.when(step == 0)
    def _():
        for src, dst in ((s_ref, st), (b_ref, bt)):
            for c in range(depth // 256):
                part = slice(c * 256, (c + 1) * 256)
                tmp[part, :] = src[:, part].astype(F32).T.astype(BF16)
            put_relative(dst, tmp, id_ref[0], id_ref[1], count)
        facc[...] = jnp.zeros_like(facc)
        sacc[...] = jnp.zeros_like(sacc)

    for c in range(depth // 128):
        part = slice(c * 128, (c + 1) * 128)
        w = w_ref[part].reshape(256, cols)
        wg[part, :] = dot(pick(128, 256, 2, 0), w).astype(BF16)
        wu[part, :] = dot(pick(128, 256, 2, 1), w).astype(BF16)
    s, b = s_ref[...], b_ref[...]
    gate = dot(s, wg[...])
    up = dot(s, wu[...])
    back = dot(b, d_ref[...], 1, 1)
    sig = jax.nn.sigmoid(gate)
    silu = gate * sig
    hidden = (silu * up).astype(BF16)
    g_gate = (back * up * (sig + silu * (1.0 - sig))).astype(BF16)
    g_up = (back * silu).astype(BF16)
    put_halves(wk_ref, ws_ref, dot(st[...], g_gate).astype(BF16), count, orders[0], 0)
    put_halves(wk_ref, ws_ref, dot(st[...], g_up).astype(BF16), count, orders[0], 1)
    put_halves(dk_ref, ds_ref, dot(bt[...], hidden).astype(BF16), count, orders[1])
    facc[...] += dot(hidden, d_ref[...])
    sacc[...] += dot(g_gate, wg[...], 1, 1) + dot(g_up, wu[...], 1, 1)

    @pl.when(step == pl.num_programs(0) - 1)
    def _():
        fo_ref[...] = facc[:own]
        fp_ref[...] = facc[own:].astype(BF16)
        so_ref[...] = sacc[:own]
        sp_ref[...] = sacc[own:].astype(BF16)


def ffn(ids, s, b, w, d, local, dp, orders):
    tokens, depth = s.shape
    hid = d.shape[0]
    bc = min(256, hid)
    rest = tokens - local
    once = functools.partial(pl.BlockSpec, pipeline_mode=pl.Buffered(1))
    const = lambda i: (0, 0)
    share = depth // dp
    half = pl.BlockSpec((dp // 2, share, bc), lambda i: (0, 0, i))
    halves = pl.BlockSpec((dp // 2, 2, share, bc), lambda i: (0, 0, 0, i))
    return pl.pallas_call(
        functools.partial(ffn_kernel, orders),
        grid=(hid // bc,),
        in_specs=[
            pl.BlockSpec(memory_space=pltpu.SMEM),
            once((tokens, depth), const), once((tokens, depth), const),
            pl.BlockSpec((depth, 2, bc), lambda i: (0, 0, i)),
            pl.BlockSpec((bc, depth), lambda i: (i, 0)),
        ],
        out_specs=[halves] * 2 + [half] * 2 + [
            once((local, depth), const), once((rest, depth), const),
            once((local, depth), const), once((rest, depth), const),
        ],
        out_shape=[sds((dp // 2, 2, share, hid), BF16)] * 2 + [sds((dp // 2, share, hid), BF16)] * 2 + [
            sds((local, depth)), sds((rest, depth), BF16),
            sds((local, depth)), sds((rest, depth), BF16),
        ],
        scratch_shapes=[
            pltpu.VMEM((depth, tokens), BF16), pltpu.VMEM((depth, tokens), BF16),
            pltpu.VMEM((depth, tokens), BF16),
            pltpu.VMEM((depth, bc), BF16), pltpu.VMEM((depth, bc), BF16),
            pltpu.VMEM((tokens, depth), F32), pltpu.VMEM((tokens, depth), F32),
        ],
        compiler_params=pltpu.CompilerParams(vmem_limit_bytes=62 << 20),
    )(ids, s, b, w, d)


def project_kernel(id_ref, xo_ref, xp_ref, front_ref, w_ref, got_ref, first_ref, pre_ref, sq_ref):
    j = pl.program_id(0)
    local, depth = xo_ref.shape
    own = got_ref.shape[2]
    f = id_ref[1]

    @pl.when(j == 0)
    def _():
        for i, ref in enumerate((xo_ref, xp_ref)):
            x = ref[...].astype(F32)
            inv = lax.rsqrt(jnp.sum(x * x, axis=1, keepdims=True) * (1.0 / depth) + EPSILON)
            first_ref[i * local : (i + 1) * local, :] = (x * inv * front_ref[...]).astype(BF16)
        sq_ref[...] = jnp.zeros_like(sq_ref)

    mine = pl.ds(pl.multiple_of(f * own, 128), own)
    other = pl.ds(pl.multiple_of((1 - f) * own, 128), own)
    out = dot(first_ref[:, mine], w_ref[0, :, mine]) + dot(first_ref[:, other], got_ref[0])
    pre_ref[0] = out
    square = out * out
    part = square[:, :128]
    for c in range(1, own // 128):
        part = part + square[:, c * 128 : (c + 1) * 128]
    sq_ref[pl.ds(j, 1), :] = jnp.sum(part.T, axis=0, keepdims=True)


def project(ids, xo, xp, front, w, got):
    local, depth = xo.shape
    own = got.shape[2]
    tokens = 2 * local
    const = lambda j: (0, 0)
    return pl.pallas_call(
        project_kernel,
        grid=(3,),
        in_specs=[
            pl.BlockSpec(memory_space=pltpu.SMEM),
            pl.BlockSpec((local, depth), const), pl.BlockSpec((local, depth), const),
            pl.BlockSpec((1, depth), const),
            pl.BlockSpec((1, own, depth), lambda j: (j, 0, 0)),
            pl.BlockSpec((1, own, own), lambda j: (j, 0, 0)),
        ],
        out_specs=[
            pl.BlockSpec((tokens, depth), const),
            pl.BlockSpec((1, tokens, own), lambda j: (j, 0, 0)),
            pl.BlockSpec((8, tokens), const),
        ],
        out_shape=[sds((tokens, depth), BF16), sds((3, tokens, own)), sds((8, tokens))],
    )(ids, xo, xp, front, w, got)


def project_grad_kernel(
    order, id_ref, da_ref, db_ref, pre_ref, stat_ref, gain_ref, first_ref,
    keep_ref, send_ref, g_ref, gt, tmp,
):
    j = pl.program_id(0)
    own = pre_ref.shape[2]
    cut = da_ref.shape[2]
    count = 2 * keep_ref.shape[0]
    inv, mean = column(stat_ref, j, 128), column(stat_ref, j + 3, 128)
    for c in range(own // 128):
        part = slice(c * 128, (c + 1) * 128)
        here = slice(c * 128 - cut, (c + 1) * 128 - cut) if c * 128 >= cut else part
        d = (db_ref if c * 128 >= cut else da_ref)[0, :, here]
        g = inv * (d * gain_ref[0, :, part] - pre_ref[0, :, part] * inv * mean)
        tmp[part, :] = g.T.astype(BF16)
        g_ref[0, :, part] = g.astype(BF16)
    put_relative(gt, tmp, id_ref[0] % count, id_ref[1], count)
    put_halves(keep_ref, send_ref, dot(gt[...], first_ref[...]).astype(BF16), count, order, j)


def project_grad(ids, da, db, pre, stats, gain, first, dp, order):
    _, tokens, own = pre.shape
    depth = first.shape[1]
    share = depth // dp
    const = lambda j: (0, 0)
    block = lambda j: (j, 0, 0)
    once = functools.partial(pl.BlockSpec, pipeline_mode=pl.Buffered(1))
    half = once((dp // 4, 3, share, depth), lambda j: (0, 0, 0, 0))
    return pl.pallas_call(
        functools.partial(project_grad_kernel, order),
        grid=(3,),
        in_specs=[
            pl.BlockSpec(memory_space=pltpu.SMEM),
            pl.BlockSpec((1,) + da.shape[1:], block), pl.BlockSpec((1,) + db.shape[1:], block),
            pl.BlockSpec((1, tokens, own), block),
            pl.BlockSpec((8, tokens), const),
            pl.BlockSpec((1, 1, own), block),
            once((tokens, depth), const),
        ],
        out_specs=[half, half, pl.BlockSpec((1, tokens, own), block)],
        out_shape=[sds((dp // 4, 3, share, depth), BF16)] * 2
        + [sds((3, tokens, own), BF16)],
        scratch_shapes=[pltpu.VMEM((own, tokens), BF16), pltpu.VMEM((own, tokens), BF16)],
    )(ids, da, db, pre, stats, gain, first)


def project_back_kernel(id_ref, g_ref, w_ref, got_ref, own_ref, peer_ref, acc):
    j = pl.program_id(0)
    own = g_ref.shape[2]
    local = own_ref.shape[0]
    f = id_ref[1]
    mine = pl.ds(pl.multiple_of(f * own, 128), own)
    other = pl.ds(pl.multiple_of((1 - f) * own, 128), own)

    @pl.when(j == 0)
    def _():
        acc[...] = jnp.zeros_like(acc)

    acc[:, mine] += dot(g_ref[0], w_ref[0, :, mine], 1, 1)
    acc[:, other] += dot(g_ref[0], got_ref[0], 1, 1)

    @pl.when(j == 2)
    def _():
        own_ref[...] = acc[:local]
        peer_ref[...] = acc[local:].astype(BF16)


def project_back(ids, g, w, got):
    _, tokens, own = g.shape
    depth = w.shape[2]
    local = tokens // 2
    const = lambda j: (0, 0)
    block = lambda j: (j, 0, 0)
    once = functools.partial(pl.BlockSpec, pipeline_mode=pl.Buffered(1))
    return pl.pallas_call(
        project_back_kernel,
        grid=(3,),
        in_specs=[
            pl.BlockSpec(memory_space=pltpu.SMEM),
            pl.BlockSpec((1, tokens, own), block),
            pl.BlockSpec((1, own, depth), block), pl.BlockSpec((1, own, own), block),
        ],
        out_specs=[once((local, depth), const), once((local, depth), const)],
        out_shape=[sds((local, depth)), sds((local, depth), BF16)],
        scratch_shapes=[pltpu.VMEM((tokens, depth), F32)],
    )(ids, g, w, got)


def out_back_kernel(order, id_ref, *refs):
    n = len(refs) - 8
    blocks, (w_ref, mixed_ref, g_ref, keep_ref, send_ref, all_ref, gt, tmp) = refs[:n], refs[n:]
    local = blocks[0].shape[0]
    for r, ref in enumerate(blocks):
        all_ref[r * local : (r + 1) * local, :] = ref[...]
    grad = all_ref[...]
    g_ref[...] = dot(grad, w_ref[...], 1, 1)
    for c in range(grad.shape[1] // 256):
        part = slice(c * 256, (c + 1) * 256)
        tmp[part, :] = grad[:, part].astype(F32).T.astype(BF16)
    count = 2 * keep_ref.shape[0]
    put_relative(gt, tmp, id_ref[0], id_ref[1], count)
    put_halves(keep_ref, send_ref, dot(gt[...], mixed_ref[...]).astype(BF16), count, order)


def out_back(ids, blocks, w, mixed, dp, order):
    tokens, own = mixed.shape
    depth = w.shape[1]
    vmem = pl.BlockSpec(memory_space=pltpu.VMEM)
    half = sds((dp // 2, depth // dp, own), BF16)
    return pl.pallas_call(
        functools.partial(out_back_kernel, order),
        in_specs=[pl.BlockSpec(memory_space=pltpu.SMEM)] + [vmem] * (len(blocks) + 2),
        out_specs=[vmem] * 3,
        out_shape=[sds((tokens, own)), half, half],
        scratch_shapes=[
            pltpu.VMEM((tokens, depth), BF16),
            pltpu.VMEM((depth, tokens), BF16), pltpu.VMEM((depth, tokens), BF16),
        ],
    )(ids, *blocks, w, mixed)


def time_embed(timesteps):
    half = TE // 2
    frequencies = jnp.exp(-math.log(10000.0) * jnp.arange(half, dtype=F32) / half)
    angles = timesteps.astype(F32)[:, None] * frequencies
    waves = jnp.concatenate([jnp.cos(angles), jnp.sin(angles)], axis=-1)
    return jax.nn.silu(waves).astype(BF16)


def rope_tables(positions, width):
    lane = jnp.arange(width)
    quarter = HD // 4
    frequencies = 10000.0 ** (-(lane % quarter).astype(F32) / quarter)
    place = jnp.where(lane % HD < HD // 2, positions[0][:, None], positions[1][:, None])
    angles = place.astype(F32) * frequencies
    return jnp.cos(angles), jnp.where(lane % 32 < 16, -1.0, 1.0) * jnp.sin(angles)


def inverse_rms(values):
    return lax.rsqrt(jnp.mean(values * values, axis=-1, keepdims=True) + EPSILON)


def rms_back(grad_hat, normed, inverse):
    return inverse * (grad_hat - normed * jnp.mean(grad_hat * normed, axis=-1, keepdims=True))


def pad_cols(value, width):
    extra = -value.shape[-1] % width
    return value if extra == 0 else jnp.pad(value, [(0, 0)] * (value.ndim - 1) + [(0, extra)])


def on_device(
    hidden_in, text_state, caption_lengths, timesteps, patch_positions, cotangent,
    w_ada, w_text, w_qkv, w_out, gains, cross_gate, w_gate_up, w_down,
):
    n, f = lax.axis_size("fsdp"), lax.axis_index("fsdp")
    dpn, me = lax.axis_size("dp"), lax.axis_index("dp")
    bits = list(range(dp_bits()))
    low_bits = bits[:-1]
    late = bits[2:3] + bits[:2] + bits[3:]
    own_d = D // n
    local = hidden_in.shape[1]
    tokens = n * local
    width = 2 * HD
    share = D // dpn
    paired = n == 2 and dpn >= 4
    ids = jnp.stack([me, f]).astype(jnp.int32)
    x_bf, dy_bf = hidden_in[0], cotangent[0]

    time_low = time_embed(timesteps)
    own_te = TE // n
    time_own = lax.dynamic_slice_in_dim(time_low[0], f * own_te, own_te, 0)
    modulation = pair_sum(
        jnp.einsum("k,kjd->jd", time_own, w_ada, preferred_element_type=F32)
    )
    scale_attn, gate_attn = modulation[0:1], jnp.tanh(modulation[1:2])
    scale_ffn, gate_ffn = modulation[2:3], jnp.tanh(modulation[3:4])

    w_flat = jnp.moveaxis(w_qkv, 1, 0)
    w_parts = exchange_rot(w_flat, 2)
    x_parts = gather_rot(x_bf)
    dy_all = jnp.concatenate(gather_rot(dy_bf), axis=0)
    places = jnp.concatenate(gather_rot(patch_positions[0]), axis=1)
    text_cols = jnp.concatenate(natural(exchange_rot(text_state[0], 1)), axis=0)
    text_all = lax.all_gather(text_cols, "dp", axis=0, tiled=True)
    gain_full = lax.all_gather(gains, "fsdp", axis=1, tiled=True).astype(F32)
    gain_own = gains.astype(F32)

    front = gain_full[0] * (1.0 + scale_attn)
    if paired:
        first_all, pre, squares = project(ids, *x_parts, front, w_flat, w_parts[1])
    else:
        w_heads = jnp.concatenate(natural(w_parts), axis=1)
        x_f = jnp.concatenate(x_parts, axis=0).astype(F32)
        first_all = (x_f * inverse_rms(x_f) * front).astype(BF16)
        pre = jnp.stack([dot(first_all, w_heads[j]) for j in range(3)])
        squares = jnp.pad(jnp.sum(pre[:2] * pre[:2], -1), ((0, 6), (0, 0)))
    inverse = lax.rsqrt(row_sum(squares) / D + EPSILON)

    text_part = text_fwd(text_cols, w_text)
    text_pre = scatter_rot(rot_blocks(text_part, 2))
    inv_t = lax.rsqrt(
        pair_sum(jnp.sum(text_pre[0] * text_pre[0], -1, keepdims=True)) / D + EPSILON
    )
    normed_t = text_pre[0] * inv_t
    tk = (normed_t * gain_own[4]).astype(BF16)
    tv = text_pre[1].astype(BF16)

    head_tanh = jnp.tanh(cross_gate.astype(F32))
    gate_row = pad_cols(jnp.repeat(head_tanh, HD)[None], width)
    cosine, sine = rope_tables(places, width)
    gq, gk = pad_cols(gain_own[2:3], width), pad_cols(gain_own[3:4], width)
    pre_p, tkp, tvp = pad_cols(pre, width), pad_cols(tk, width), pad_cols(tv, width)
    q, k, v, mixed_p, so, co, ls, lc = attn_forward(
        caption_lengths, pre_p, inverse, gq, gk, cosine, sine, tkp, tvp, gate_row
    )
    mixed = mixed_p[:, :own_d]

    def rows(value, r):
        return value[r * local : (r + 1) * local]

    parts = [dot(rows(mixed, r), w_out) for r in range(n)]
    attn_branch = scatter_rot([parts[0]] + [p.astype(BF16) for p in parts[1:]])
    x_own = x_bf.astype(F32)
    after_attn = x_own + gate_attn * attn_branch
    inverse_two = inverse_rms(after_attn)
    normed_two = after_attn * inverse_two
    second = (normed_two * gain_full[1] * (1.0 + scale_ffn)).astype(BF16)

    second_all = jnp.concatenate(gather_rot(second), axis=0)
    branch_all = (gate_ffn * dy_all.astype(F32)).astype(BF16)
    wide_keep, wide_send, down_keep, down_send, ffn_own, ffn_rest, back_own, back_rest = ffn(
        ids, second_all, branch_all, w_gate_up, w_down, local, dpn, (bits, late)
    )
    (ffn_own, ffn_rest, back_own, back_rest), text_all = lax.optimization_barrier(
        ((ffn_own, ffn_rest, back_own, back_rest), text_all)
    )
    wide_chain = Halving(bits, wide_keep, wide_send)
    down_chain = Halving(late, down_keep, down_send)
    grad_second = scatter_rot([back_own] + [rows(back_rest, r) for r in range(n - 1)])
    ffn_branch = scatter_rot([ffn_own] + [rows(ffn_rest, r) for r in range(n - 1)])
    output = (after_attn + gate_ffn * ffn_branch).astype(BF16)
    dy = dy_bf.astype(F32)
    d_gate_ffn = jnp.sum(dy * ffn_branch, axis=0) * (1.0 - gate_ffn[0] * gate_ffn[0])

    scaled = grad_second * normed_two
    d_scale_ffn = jnp.sum(scaled * gain_full[1], axis=0)
    gain_two = jnp.sum(scaled * (1.0 + scale_ffn), axis=0)
    grad_after = dy + rms_back(
        grad_second * gain_full[1] * (1.0 + scale_ffn), normed_two, inverse_two
    )
    d_gate_attn = jnp.sum(grad_after * attn_branch, axis=0) * (1.0 - gate_attn[0] * gate_attn[0])
    grad_attn = (gate_attn * grad_after).astype(BF16)
    grad_mixed, *out_halves = out_back(ids, gather_rot(grad_attn), w_out, mixed, dpn, bits)
    out_chain = Halving(bits, *out_halves)
    blocks = pre_p.shape[2] // width
    cut = max(1, 2 * blocks // 3)
    grad_mixed = pad_cols(grad_mixed, width)
    inputs = (so, co, ls, lc, pre_p, inverse, gq, gk, cosine, sine, gate_row)
    part_a = attn_backward(0, cut, caption_lengths, q, k, v, tkp, tvp, grad_mixed, *inputs)
    part_a, grad_mixed = lax.optimization_barrier((part_a, grad_mixed))
    grad_mixed = advance([wide_chain, down_chain], grad_mixed)
    part_b = attn_backward(
        cut, blocks - cut, caption_lengths, q, k, v, tkp, tvp, grad_mixed, *inputs
    )
    means = row_sum(part_a[3] + part_b[3])[:2] / D

    ones, zeros = jnp.ones((1, tokens), F32), jnp.zeros((1, tokens), F32)
    if paired:
        stats = jnp.concatenate([inverse[:2], ones, means, zeros, zeros, zeros], axis=0)
        gain3 = jnp.stack([gain_own[2:3], gain_own[3:4], jnp.ones_like(gain_own[2:3])])
        keep, send, grads = project_grad(
            ids, part_a[0], part_b[0], pre, stats, gain3, first_all, dpn, low_bits
        )
        part_a, part_b, grads = advance(
            [wide_chain, down_chain, out_chain], (part_a[1:], part_b[1:], grads)
        )
        qkv_chain = Halving(low_bits, keep, send)
        parts = project_back(ids, grads, w_flat, w_parts[1])
    else:
        d = jnp.concatenate([part_a[0], part_b[0]], axis=2)[:, :, :own_d]
        part_a, part_b = part_a[1:], part_b[1:]
        inv, mean = inverse[:2, :, None], means[:, :, None]
        hat = d[:2] * gain_own[2:4][:, None] - pre[:2] * inv * mean
        grads = [(inv[0] * hat[0]).astype(BF16), (inv[1] * hat[1]).astype(BF16), d[2].astype(BF16)]
        wide = [dot(g, first_all, 0, 0).astype(BF16) for g in grads]
        wide = [jnp.concatenate(natural(exchange_rot(w_, 1)), axis=0) for w_ in wide]
        wide = relative(jnp.stack([w_.reshape(dpn, share, own_d) for w_ in wide], axis=1))
        wide = jnp.stack([wide[p] for p in sorted(range(dpn), key=lambda p: place_of(p, bits))])
        qkv_chain = Halving(bits, wide[: dpn // 2], wide[dpn // 2 :])
        parts = [
            sum(dot(rows(g, r), w_heads[j], 1, 1) for j, g in enumerate(grads)) for r in range(n)
        ]
        parts = [parts[0]] + [p.astype(BF16) for p in parts[1:]]
    grad_first = scatter_rot(parts)

    dtk, dtv, gain_q, gain_k, gate_g = (
        jnp.concatenate([part_a[i], part_b[i]], axis=1)[:, :own_d] for i in (0, 1, 3, 4, 5)
    )
    gate_total = jnp.sum(gate_g[0].reshape(HEADS // n, HD), axis=1) * (
        1.0 - head_tanh * head_tanh
    )
    text_hat = dtk * gain_own[4]
    gain_text = jnp.sum(dtk * normed_t, axis=0, keepdims=True)
    mean_t = pair_sum(jnp.sum(text_hat * normed_t, -1, keepdims=True)) / D
    grad_tk = (inv_t * (text_hat - normed_t * mean_t)).astype(BF16)
    text_pair = jnp.stack([grad_tk, dtv.astype(BF16)])
    pair_all = jnp.concatenate(natural(gather_rot(text_pair)), axis=-1)
    pair_all = advance([qkv_chain, wide_chain, down_chain, out_chain], pair_all)
    pair_all, wide_chain.keep = lax.optimization_barrier((pair_all, wide_chain.keep))
    text_in = text_bwd(pair_all, w_text)
    text_in, grad_first = advance([qkv_chain], (text_in, grad_first))
    text_in = jnp.concatenate(natural(exchange_rot(text_in, 0)), axis=1)

    inverse_one = inverse_rms(x_own)
    normed_one = x_own * inverse_one
    scaled = grad_first * normed_one
    d_scale_attn = jnp.sum(scaled * gain_full[0], axis=0)
    gain_one = jnp.sum(scaled * (1.0 + scale_attn), axis=0)
    grad_input = (
        grad_after
        + rms_back(grad_first * gain_full[0] * (1.0 + scale_attn), normed_one, inverse_one)
    ).astype(BF16)


    sums = [d_scale_attn, d_gate_attn, d_scale_ffn, d_gate_ffn, gain_one, gain_two]
    sums = pair_sum(jnp.stack(sums))
    stamp = jnp.full((1, D), timesteps[0].astype(F32))
    gate_pad = jnp.pad(gate_total, (0, own_d - gate_total.shape[0]))[None]
    small = jnp.concatenate([block_of(sums[4:], f, 1), gain_q, gain_k, gain_text, gate_pad], axis=0)
    small = jnp.pad(small.reshape(-1), (0, dpn * SUMS * 128 - small.size))
    mods = jnp.concatenate([sums[:4], stamp], axis=0).reshape(5, dpn, share).transpose(1, 0, 2)
    mods = jnp.pad(mods, ((0, 0), (0, 0), (0, -share % 128)))
    mods = jnp.concatenate([mods, small.reshape(dpn, SUMS, 128)], axis=1)
    outgoing = block_of(pair_all.transpose(0, 2, 1), f, 2)
    outgoing = outgoing.reshape(2, dpn, share, TEXT // n).transpose(1, 0, 2, 3)
    mods = settle([wide_chain], advance([down_chain, out_chain], mods))
    pair_cols, mods, small = swap_all(outgoing, mods)
    chains = [out_chain, down_chain] if paired else [qkv_chain, out_chain, down_chain]
    if paired:
        qkv_got = qkv_chain.got
        (pair_cols, mods, small), qkv_chain.got = lax.optimization_barrier(
            ((pair_cols, mods, small), qkv_got)
        )
        qkv_chain.step()
        own_side = f == (me >> low_bits[-1] + 1)
        mine, got = exchange_rot(qkv_chain.last[0].astype(BF16), 2)
        got, wide_chain.keep = lax.optimization_barrier((got, wide_chain.keep))
        qkv_chain = Halving(
            bits[-1:], jnp.where(own_side, mine, got)[None], jnp.where(own_side, got, mine)[None]
        )
    pair_cols = advance(chains, pair_cols)
    pair_cols = jnp.concatenate(natural(gather_rot(pair_cols)), axis=3)
    pair_cols = pair_cols.transpose(1, 2, 0, 3).reshape(2 * share, dpn * TEXT)
    text_grad = dot(pair_cols, text_all).reshape(2, share, TW // n)
    total = small[:, 5 : 5 + SUMS].reshape(-1)[: 6 * own_d].reshape(6, own_d)
    times = time_embed(mods[:, 4, 0])
    times = lax.dynamic_slice_in_dim(times, f * own_te, own_te, 1).astype(F32)
    ada_grad = lax.dot_general(
        mods[:, :4, :share].reshape(dpn, 4 * share), times, (((0,), (0,)), ((), ())),
        precision=lax.Precision.HIGHEST,
    ).reshape(4, share, own_te)

    for chain in (out_chain, down_chain, wide_chain, qkv_chain):
        while chain.got is not None:
            chain.step()
    return (
        output[None],
        grad_input[None],
        text_in[None],
        ada_grad.transpose(2, 0, 1),
        text_grad.transpose(2, 0, 1),
        qkv_chain.last[0].transpose(2, 0, 1),
        out_chain.last[0].T,
        total[:5],
        total[5, : HEADS // n],
        wide_chain.last[0].transpose(1, 0, 2),
        down_chain.last[0].T,
    )


def solution(mesh):
    return jax.shard_map(
        on_device,
        mesh=mesh,
        in_specs=(
            P("dp", "fsdp", None),
            P("dp", "fsdp", None),
            P("dp"),
            P("dp"),
            P("dp", None, "fsdp"),
            P("dp", "fsdp", None),
            P("fsdp", None, None),
            P("fsdp", None, None),
            P("fsdp", None, None),
            P("fsdp", None),
            P(None, "fsdp"),
            P("fsdp"),
            P(None, None, "fsdp"),
            P("fsdp", None),
        ),
        out_specs=(
            P("dp", "fsdp", None),
            P("dp", "fsdp", None),
            P("dp", "fsdp", None),
            P("fsdp", None, "dp"),
            P("fsdp", None, "dp"),
            P("fsdp", None, "dp"),
            P("fsdp", "dp"),
            P(None, "fsdp"),
            P("fsdp"),
            P("dp", None, "fsdp"),
            P("fsdp", "dp"),
        ),
        check_vma=False,
    )
```
